32 devices in a mesh: narrow: 4 (over y, x), wide: 8 (over z, core).
Axes of the slice: x: 2, y: 2, z: 4, core: 2. Of those that a mesh axis runs over, the one named last changes fastest.
Arguments:
- token_ids: int32 [2, 32, 512], P(None, ('narrow', 'wide')), may hold values from 0 to 30591
- seq_lengths: int32 [2, 32, 4], P(None, ('narrow', 'wide')), may hold values from 1 to 384, 512 in all within a row
- task_ids: int32 [2, 32, 4], P(None, ('narrow', 'wide')), may hold values from 0 to 1
- labels: int32 [2, 32, 4], P(None, ('narrow', 'wide')), may hold values from 0 to 2
- negatives: int32 [2, 32, 4, 4], P(None, ('narrow', 'wide')), may hold values from 0 to 127
- step_count: int32 [1], replicated, may hold values from 2 to 20
- hidden_master: float32 [9216, 768], P('wide')
- hidden_momentum: float32 [9216, 768], P('wide'), may hold values from -2.3841858e-06 to 2.3841858e-06
- table_master: float32 [768, 30592], P('wide'), may hold values from -0.125 to 0.125
- table_first: float32 [768, 30592], P('wide'), may hold values from -2.3841858e-07 to 2.3841858e-07
- table_second: float32 [768, 30592], P('wide'), may hold values from 1.3e-16 to 5.2e-16
- pos_types: float32 [514, 768], replicated, may hold values from -0.125 to 0.125
- pos_first: float32 [514, 768], replicated, may hold values from -2.3841858e-07 to 2.3841858e-07
- pos_second: float32 [514, 768], replicated, may hold values from 1.3e-16 to 5.2e-16
- vectors: float32 [18, 768], replicated
- vec_first: float32 [18, 768], replicated, may hold values from -1.1920929e-06 to 1.1920929e-06
- vec_second: float32 [18, 768], replicated, may hold values from 4e-15 to 1.6e-14
Outputs:
- loss: float32 [], replicated
- clip_norm: float32 [], replicated
- momentum_new: float32 [9216, 768], P('wide')
- hidden_new: float32 [9216, 768], P('wide')
- hidden_copy: bfloat16 [9216, 768], P('wide')
- table_new: float32 [768, 30592], P('wide')
- table_first_new: float32 [768, 30592], P('wide')
- table_second_new: float32 [768, 30592], P('wide')
- table_copy: bfloat16 [768, 30592], P('wide')
- pos_new: float32 [514, 768], replicated
- pos_first_new: float32 [514, 768], replicated
- pos_second_new: float32 [514, 768], replicated
- vectors_new: float32 [18, 768], replicated
- vec_first_new: float32 [18, 768], replicated
- vec_second_new: float32 [18, 768], replicated
The draws below stay inside these ranges and needn't reach their ends.
Inputs may be any that keep to these rules, and one draw needn't show every extreme that they name: `seq_lengths`: the 4 lengths of each batch row sum to 512. `task_ids`: 0 marks a classification pair, 1 a ranking pair. `labels`: read only for task 0. `negatives`: index of a pair of the same micro-batch, counted by batch row, then slot; read only for task 1.
All inputs are finite; a program needn't handle non-finite values.
Results may differ from the reference program's by a relative error of at most 0.014.
Values may be sent and summed in bfloat16 or wider, within the bound.
No kernel may reach another device: no remote copies, remote signals or barrier semaphores. Data moves between devices by JAX's collectives and lax.ppermute only.
A program may use at most 320 MiB of HBM per device.

```python
import math
import jax
import jax.numpy as jnp
import numpy as np
from jax import lax

D = 768
HEADS = 12
HEAD = 64
FF = 3072
VOCAB = 30592
SEQ = 512
SLOTS = 4
MOST = 384
NEG = 4
MICRO = 2
NS_TURNS = 5
BR = 32
NSEQ = 128
HR = 9216
VR = 18


def draw_hidden_master(key, part):
    total_rows = 4 * D + 2 * FF
    noise = jnp.clip(jax.random.normal(key, (total_rows, D), jnp.float32), -6.0, 6.0)
    row_ids = jnp.arange(total_rows)
    factor = jnp.where(row_ids < 3 * D, 1.0, jnp.where(row_ids < 4 * D, 3.0, jnp.where(row_ids < 4 * D + FF, 1.0, math.sqrt(D / FF))))
    return noise * factor[:, None] / math.sqrt(D)


def draw_vectors(key, part):
    row_count = 14 + FF // D
    noise = jnp.clip(jax.random.normal(key, (row_count, D), jnp.float32), -6.0, 6.0)
    row_ids = jnp.arange(row_count)
    is_gain = (row_ids == 0) | (row_ids == 2) | (row_ids == 4)
    is_head = (row_ids >= 10) & (row_ids < 14)
    return jnp.where(is_gain[:, None], 1.0 + 0.1 * noise, jnp.where(is_head[:, None], 0.2 * noise, 0.1 * noise))


def place_ends(result, key, least, largest):
    index_at = [jax.random.randint(jax.random.fold_in(key, axis), (), 0, length) for axis, length in enumerate(result.shape)]
    main_axis = result.shape.index(max(result.shape))
    neighbour = index_at[:main_axis] + [(index_at[main_axis] + 1) % result.shape[main_axis]] + index_at[main_axis + 1:]
    return result.at[tuple(index_at)].set(least).at[tuple(neighbour)].set(largest)


def block_levels(own_key, shape, pieces, smallest, largest):
    def one(axis_at, shards_of):
        heights = jax.random.uniform(jax.random.fold_in(jax.random.fold_in(own_key, 6), axis_at), (shards_of,), jnp.float32, smallest / len(pieces), largest / len(pieces))
        return jnp.repeat(jnp.exp(heights), shape[axis_at] // shards_of).reshape((-1,) + (1,) * (len(shape) - axis_at - 1))

    level = one(*pieces[0])
    for cut in pieces[1:]:
        level = level * one(*cut)
    return level


def rank_bounds(amount, lean):
    weights = [(1 << 20) // math.isqrt(standing ** lean) + 1 for standing in range(1, amount + 1)]
    width = 1 + sum(weights) // (1 << 30)
    return np.cumsum(np.array([max(1, weight // width) for weight in weights]))


def ranked(rng, extent, count, skew):
    listing = rank_bounds(count, skew)
    pick = jax.random.randint(jax.random.fold_in(rng, 1), extent, 0, int(listing[count - 1]))
    rank = jnp.searchsorted(jnp.asarray(listing, jnp.int32), pick, side="right")
    return jax.random.permutation(jax.random.fold_in(rng, 2), count)[rank].astype(jnp.int32)


def profile(count, total, limit, slope):
    portions = [(1 << 20) // math.isqrt(rank ** slope) + 1 for rank in range(2, count + 1)]
    spare, given = total - limit - (count - 1), [1] * (count - 1)
    while spare > 0:
        movable = [i for i in range(count - 1) if given[i] < limit]
        mass, left = sum([portions[i] for i in movable]), spare
        for i in movable:
            addition = min(limit - given[i], max(1, left * portions[i] // mass), spare)
            given[i] = given[i] + addition
            spare = spare - addition
    return np.array([limit] + given)


def uneven(key, amount, total, bound, slope):
    if amount == 2:
        one = jax.random.randint(key, (), max(1, total - bound), min(bound, total - 1) + 1)
        return jnp.stack([one, total - one])
    tallies = jnp.asarray(profile(amount, total, bound, slope), jnp.int32)
    pairs = (amount - 1) // 2
    giver, taker = tallies[1:1 + 2 * pairs:2], tallies[2:2 + 2 * pairs:2]
    room = jnp.minimum(giver - 1, bound - taker)
    shifted = jax.random.randint(jax.random.fold_in(key, 1), (pairs,), 0, 1 << 20) % (room + 1)
    tallies = tallies.at[1:1 + 2 * pairs:2].set(giver - shifted).at[2:2 + 2 * pairs:2].set(taker + shifted)
    return tallies[jax.random.permutation(jax.random.fold_in(key, 2), amount)]


def scatter_about(own_key, dims, deviation, limit, cuts=(), kind=jnp.bfloat16):
    loudness = block_levels(own_key, dims, cuts, -0.22, 0.18) if cuts else 1.0
    array = jax.random.normal(own_key, dims, jnp.float32) * deviation * loudness
    return jnp.minimum(jnp.maximum(array, -limit), limit).astype(kind)


def setup_inputs(seed: int = 0) -> dict:
    streams_of = jax.random.split(jax.random.key(seed), 18)
    return {
        "token_ids": place_ends(ranked(streams_of[0], (MICRO, BR, SEQ), VOCAB, 2), jax.random.fold_in(streams_of[0], 3), 0, VOCAB - 1).astype(jnp.int32),
        "seq_lengths": jax.vmap(lambda own: uneven(own, SLOTS, SEQ, MOST, 2))(jax.random.split(streams_of[1], MICRO * BR)).reshape((MICRO, BR, SLOTS)).astype(jnp.int32),
        "task_ids": place_ends(jax.random.randint(streams_of[2], (MICRO, BR, SLOTS), 0, 2), jax.random.fold_in(streams_of[2], 1), 0, 1).astype(jnp.int32),
        "labels": place_ends(jax.random.randint(streams_of[3], (MICRO, BR, SLOTS), 0, 3), jax.random.fold_in(streams_of[3], 1), 0, 2).astype(jnp.int32),
        "negatives": place_ends(jax.random.randint(streams_of[4], (MICRO, BR, SLOTS, NEG), 0, NSEQ), jax.random.fold_in(streams_of[4], 1), 0, NSEQ - 1).astype(jnp.int32),
        "step_count": jax.random.randint(streams_of[5], (1,), 2, 21).astype(jnp.int32),
        "hidden_master": draw_hidden_master(jax.random.fold_in(streams_of[17], 71), 0),
        "hidden_momentum": scatter_about(streams_of[7], (HR, D), (4e-7), 2.384185791015625e-06, ((0, 8),), jnp.float32),
        "table_master": scatter_about(streams_of[8], (D, VOCAB), 0.02, 0.125, ((0, 8),), jnp.float32),
        "table_first": scatter_about(streams_of[9], (D, VOCAB), (4e-8), 2.384185791015625e-07, ((0, 8),), jnp.float32),
        "table_second": jnp.clip(jnp.exp(math.log(5.199999849456378e-16) - 1.3862944 * jax.random.uniform(streams_of[10], (D, VOCAB), jnp.float32) ** block_levels(streams_of[10], (D, VOCAB), ((0, 8),), -0.2, 0.2)), 1.2999999623640945e-16, 5.199999849456378e-16),
        "pos_types": scatter_about(streams_of[11], (SEQ + 2, D), 0.02, 0.125, (), jnp.float32),
        "pos_first": scatter_about(streams_of[12], (SEQ + 2, D), (4e-8), 2.384185791015625e-07, (), jnp.float32),
        "pos_second": jnp.clip(jnp.exp(jax.random.uniform(streams_of[13], (SEQ + 2, D), jnp.float32, math.log(1.2999999623640945e-16), math.log(5.199999849456378e-16))), 1.2999999623640945e-16, 5.199999849456378e-16),
        "vectors": draw_vectors(jax.random.fold_in(streams_of[17], 71), 0),
        "vec_first": scatter_about(streams_of[15], (VR, D), (2e-7), 1.1920928955078125e-06, (), jnp.float32),
        "vec_second": jnp.clip(jnp.exp(jax.random.uniform(streams_of[16], (VR, D), jnp.float32, math.log(4.000000014509975e-15), math.log(1.60000000580399e-14))), 4.000000014509975e-15, 1.60000000580399e-14),
    }


highest = lax.Precision.HIGHEST
clip_bound = 0.002
norm_eps = 1e-06
muon_beta = 0.95
muon_rate = 0.1
muon_decay = 0.01
beta_one = 0.9
beta_two = 0.999
adam_eps = 1e-08
adam_decay = 0.01

@jax.custom_vjp
def low(v):
    return lax.optimization_barrier(v.astype(jnp.bfloat16)).astype(jnp.float32)

@jax.custom_vjp
def low_back(v):
    return v

def low_keep(v):
    return (low(v), None)

def low_pass(kept, grad):
    return (grad,)

def back_keep(v):
    return (v, None)

def back_low(kept, grad):
    return (low(grad),)
low.defvjp(low_keep, low_pass)
low_back.defvjp(back_keep, back_low)

def layout(lengths):
    row_ends = jnp.cumsum(lengths).astype(jnp.int32)
    starts = (row_ends - lengths).astype(jnp.int32)
    places = jnp.arange(SEQ, dtype=jnp.int32)
    segment = lax.optimization_barrier(jnp.sum((places[:, None] >= row_ends[None, :]).astype(jnp.int32), axis=1)).astype(jnp.int32)
    chosen = segment[:, None] == jnp.arange(SLOTS, dtype=jnp.int32)[None, :]
    start_at = lax.optimization_barrier(jnp.sum(jnp.where(chosen, starts[None, :], 0), axis=1)).astype(jnp.int32)
    length_at = lax.optimization_barrier(jnp.sum(jnp.where(chosen, lengths[None, :], 0), axis=1)).astype(jnp.int32)
    position = (places - start_at).astype(jnp.int32)
    second = (2 * position >= length_at).astype(jnp.int32)
    return (chosen.astype(jnp.float32), position, second, segment)

def layer_norm(hidden, gain, bias):
    center = hidden - lax.optimization_barrier(jnp.mean(hidden, axis=-1, keepdims=True))
    spread = lax.optimization_barrier(jnp.mean(center * center, axis=-1, keepdims=True))
    return center * lax.rsqrt(spread + norm_eps) * gain + bias

def matmul(left, right):
    return jnp.dot(left, right, precision=highest, preferred_element_type=jnp.float32)

def row_forward(weights, table_low, pos_types, vectors, token_row, lengths):
    member, position, second, segment = layout(lengths)
    embed = low_back(table_low[:, token_row].T) + pos_types[position] + pos_types[SEQ + second]
    normed0 = layer_norm(embed, vectors[0], vectors[1])
    qkv_bias = jnp.concatenate([vectors[6], jnp.zeros_like(vectors[6]), vectors[7]])
    mixed = low(low_back(matmul(low(normed0), weights[:3 * D].T) + qkv_bias))
    split = mixed.reshape(SEQ, 3, HEADS, HEAD)
    raw = low_back(jnp.einsum('qhd,khd->hqk', split[:, 0], split[:, 1], precision=highest))
    same = segment[:, None] == segment[None, :]
    scores = jnp.where(same[None], raw * (1.0 / math.sqrt(HEAD)), -1e+30)
    probs = jax.nn.softmax(scores, axis=-1)
    context = jnp.einsum('hqk,khd->qhd', low(probs), split[:, 2], precision=highest).reshape(SEQ, D)
    attended = low_back(matmul(low(low_back(context)), weights[3 * D:4 * D].T) + vectors[8])
    normed1 = layer_norm(normed0 + attended, vectors[2], vectors[3])
    inner = low_back(matmul(low(normed1), weights[4 * D:4 * D + FF].T) + vectors[14:].reshape(-1))
    branch = low_back(matmul(low(jax.nn.gelu(inner, approximate=False)), weights[4 * D + FF:]) + vectors[9])
    normed2 = layer_norm(normed1 + branch, vectors[4], vectors[5])
    return matmul(member.T, normed2) / lengths.astype(jnp.float32)[:, None]

def task_loss(logits, own, scores_all, tasks, labels, negatives, counts):
    logprob = jax.nn.log_softmax(logits, axis=-1)
    picked = lax.optimization_barrier(jnp.sum(jnp.where(labels[:, None] == jnp.arange(3, dtype=jnp.int32)[None, :], logprob, 0.0), axis=1))
    rivals = scores_all[negatives]
    together = jnp.concatenate([own[:, None], rivals], axis=1)
    ranking = jax.nn.logsumexp(together, axis=1) - own
    first_part = jnp.sum(jnp.where(tasks == 0, -picked, 0.0)) / counts[0]
    return first_part + jnp.sum(jnp.where(tasks == 1, ranking, 0.0)) / counts[1]

def newton(moment):
    gram = matmul(moment.T, moment)
    scale = jnp.sqrt(jnp.trace(gram)) + 1e-07
    iterate = moment / scale
    gram = gram / (scale * scale)
    for turn in range(NS_TURNS):
        if turn > 0:
            gram = matmul(iterate.T, iterate)
        first = matmul(iterate, gram)
        second = matmul(first, gram)
        iterate = 3.4445 * iterate - 4.775 * first + 2.0315 * second
    return iterate

def adam(weight, grad, first, second, step, rate):
    first = beta_one * first + (1.0 - beta_one) * grad
    second = beta_two * second + (1.0 - beta_two) * grad * grad
    unbiased = first / (1.0 - beta_one ** step)
    spread = second / (1.0 - beta_two ** step)
    return (weight - rate * (unbiased / (jnp.sqrt(spread) + adam_eps) + adam_decay * weight), first, second)

def reference(token_ids, seq_lengths, task_ids, labels, negatives, step_count, hidden_master, hidden_momentum, table_master, table_first, table_second, pos_types, pos_first, pos_second, vectors, vec_first, vec_second):
    counts = jnp.stack([jnp.sum((task_ids == 0).astype(jnp.float32)), jnp.sum((task_ids == 1).astype(jnp.float32))])

    def objective(hidden, table, pos_table, vec_table):
        weights = low(hidden)
        table_low = low(table)
        row_fn = jax.checkpoint(lambda inputs: row_forward(weights, table_low, pos_table, vec_table, inputs[0], inputs[1]))
        total = jnp.zeros((), jnp.float32)
        for micro_at in range(MICRO):
            pooled = lax.map(row_fn, (token_ids[micro_at], seq_lengths[micro_at])).reshape(-1, D)
            logits = matmul(pooled, vec_table[10:13].T)
            scores = matmul(pooled, vec_table[13])
            total = total + task_loss(logits, scores, scores, task_ids[micro_at].reshape(-1), labels[micro_at].reshape(-1), negatives[micro_at].reshape(-1, NEG), counts)
        return total
    loss, pullback = jax.vjp(objective, hidden_master, table_master, pos_types, vectors)
    grads = pullback(jnp.ones_like(loss))
    clip_norm = jnp.sqrt(sum((jnp.sum(entry * entry) for entry in grads)))
    factor = jnp.minimum(1.0, clip_bound / clip_norm)
    hidden_grad, table_grad, pos_grad, vec_grad = [entry * factor for entry in grads]
    moment = muon_beta * hidden_momentum + hidden_grad
    bounds = [(0, 3 * D), (3 * D, 4 * D), (4 * D, 4 * D + FF), (4 * D + FF, 4 * D + 2 * FF)]
    ortho = jnp.concatenate([newton(moment[lower:upper]) * (0.2 * math.sqrt(upper - lower)) for lower, upper in bounds])
    hidden_new = hidden_master * (1.0 - muon_rate * muon_decay) - muon_rate * ortho
    step = step_count[0].astype(jnp.float32)
    table_new, table_first_new, table_second_new = adam(table_master, table_grad, table_first, table_second, step, 0.02)
    pos_new, pos_first_new, pos_second_new = adam(pos_types, pos_grad, pos_first, pos_second, step, 0.02)
    vectors_new, vec_first_new, vec_second_new = adam(vectors, vec_grad, vec_first, vec_second, step, 0.2)
    return (loss, clip_norm, moment, hidden_new, hidden_new.astype(jnp.bfloat16), table_new, table_first_new, table_second_new, table_new.astype(jnp.bfloat16), pos_new, pos_first_new, pos_second_new, vectors_new, vec_first_new, vec_second_new)
```

```python
from functools import partial
import math

import jax
import jax.numpy as jnp
from jax import lax
from jax.experimental import pallas as pl
from jax.experimental.pallas import tpu as pltpu
from jax.sharding import PartitionSpec as P

D = 768
HEADS = 12
HEAD = 64
FF = 3072
SEQ = 512
SLOTS = 4
NEG = 4
NS_TURNS = 5
LANES = 128
GROUPS = 4
WIDTH = LANES // GROUPS

BOTH = ("narrow", "wide")
highest = lax.Precision.HIGHEST
clip_bound = 0.002
norm_eps = 1e-06
muon_beta = 0.95
muon_rate = 0.1
muon_decay = 0.01
beta_one = 0.9
beta_two = 0.999
adam_eps = 1e-08
adam_decay = 0.01
BOUNDS = (0, 3 * D, 4 * D, 4 * D + FF, 4 * D + 2 * FF)

low = jnp.bfloat16
full = jnp.float32


def dims(left, right):
    return (((left,), (right,)), ((), ()))


def dot32(left, right, left_dim, right_dim):
    return lax.dot_general(left, right, dims(left_dim, right_dim), preferred_element_type=full)


def halves(x):
    high = x.astype(low)
    return high, (x - high.astype(full)).astype(low)


def dot_split(left, right, left_dim=1, right_dim=0):
    (lh, ll), (rh, rl) = left, right
    return dot32(lh, rh, left_dim, right_dim) + (
        dot32(lh, rl, left_dim, right_dim) + dot32(ll, rh, left_dim, right_dim)
    )


def params(mib):
    return pltpu.CompilerParams(vmem_limit_bytes=mib << 20)


def vmem():
    return pl.BlockSpec(memory_space=pltpu.VMEM)


def smem():
    return pl.BlockSpec(memory_space=pltpu.SMEM)


def attend_kernel(mixed_ref, seg_col_ref, seg_row_ref, context_ref, logsum_ref):
    same = seg_col_ref[0] == seg_row_ref[0]

    def pair(step, carry):
        at = pl.multiple_of(step * LANES, LANES)
        queries = mixed_ref[:, pl.ds(at, LANES)]
        keys = mixed_ref[:, pl.ds(D + at, LANES)]
        values = mixed_ref[:, pl.ds(2 * D + at, LANES)]
        outs = []
        for half in range(2):
            cut = slice(half * HEAD, (half + 1) * HEAD)
            raw = dot32(keys[:, cut], queries[:, cut], 1, 1)
            scores = jnp.where(same, raw * (1.0 / math.sqrt(HEAD)), -1e30)
            peak = jnp.max(scores, axis=0, keepdims=True)
            lifted = jnp.exp(scores - peak)
            total = jnp.sum(lifted, axis=0, keepdims=True)
            probs = (lifted * (1.0 / total)).astype(low)
            outs.append(dot32(values[:, cut], probs, 0, 0))
            logsum_ref[0, pl.ds(2 * step + half, 1), :] = peak + jnp.log(total)
        context_ref[:, pl.ds(at, LANES)] = jnp.concatenate(outs, axis=0).T.astype(low)
        return carry

    lax.fori_loop(0, HEADS // 2, pair, 0)


def attend(mixed, segment):
    rows = segment.shape[0]
    return pl.pallas_call(
        attend_kernel,
        grid=(rows,),
        in_specs=[
            pl.BlockSpec((SEQ, 3 * D), lambda b: (b, 0)),
            pl.BlockSpec((1, SEQ, 1), lambda b: (b, 0, 0)),
            pl.BlockSpec((1, 1, SEQ), lambda b: (b, 0, 0)),
        ],
        out_specs=[
            pl.BlockSpec((SEQ, D), lambda b: (b, 0)),
            pl.BlockSpec((1, 16, SEQ), lambda b: (b, 0, 0)),
        ],
        out_shape=[
            jax.ShapeDtypeStruct((rows * SEQ, D), low),
            jax.ShapeDtypeStruct((rows, 16, SEQ), full),
        ],
        compiler_params=params(48),
        name="attend",
    )(mixed, segment[:, :, None], segment[:, None, :])


def attend_back_kernel(mixed_ref, grad_ref, logsum_ref, seg_col_ref, seg_row_ref, out_ref):
    same = seg_col_ref[0] == seg_row_ref[0]
    scale = 1.0 / math.sqrt(HEAD)

    def pair(step, carry):
        at = pl.multiple_of(step * LANES, LANES)
        queries = mixed_ref[:, pl.ds(at, LANES)]
        keys = mixed_ref[:, pl.ds(D + at, LANES)]
        values = mixed_ref[:, pl.ds(2 * D + at, LANES)]
        upstream = grad_ref[:, pl.ds(at, LANES)]
        query_grads, key_grads, value_grads = [], [], []
        for half in range(2):
            cut = slice(half * HEAD, (half + 1) * HEAD)
            logsum = logsum_ref[0, pl.ds(2 * step + half, 1), :]
            raw = dot32(keys[:, cut], queries[:, cut], 1, 1)
            probs = jnp.exp(jnp.where(same, raw * scale, -1e30) - logsum)
            prob_grads = dot32(values[:, cut], upstream[:, cut], 1, 1)
            value_grads.append(dot32(probs.astype(low), upstream[:, cut], 1, 0))
            moved = jnp.sum(prob_grads * probs, axis=0, keepdims=True)
            back = (probs * (prob_grads - moved) * scale).astype(low)
            key_grads.append(dot32(back, queries[:, cut], 1, 0))
            query_grads.append(dot32(keys[:, cut], back, 0, 0))
        out_ref[:, pl.ds(at, LANES)] = jnp.concatenate(query_grads, axis=0).T.astype(low)
        out_ref[:, pl.ds(D + at, LANES)] = jnp.concatenate(key_grads, axis=1).astype(low)
        out_ref[:, pl.ds(2 * D + at, LANES)] = jnp.concatenate(value_grads, axis=1).astype(low)
        return carry

    lax.fori_loop(0, HEADS // 2, pair, 0)


def attend_back(mixed, context_grad, logsum, segment):
    rows = segment.shape[0]
    return pl.pallas_call(
        attend_back_kernel,
        grid=(rows,),
        in_specs=[
            pl.BlockSpec((SEQ, 3 * D), lambda b: (b, 0)),
            pl.BlockSpec((SEQ, D), lambda b: (b, 0)),
            pl.BlockSpec((1, 16, SEQ), lambda b: (b, 0, 0)),
            pl.BlockSpec((1, SEQ, 1), lambda b: (b, 0, 0)),
            pl.BlockSpec((1, 1, SEQ), lambda b: (b, 0, 0)),
        ],
        out_specs=pl.BlockSpec((SEQ, 3 * D), lambda b: (b, 0)),
        out_shape=jax.ShapeDtypeStruct((rows * SEQ, 3 * D), low),
        compiler_params=params(56),
        name="attend_back",
    )(mixed, context_grad, logsum, segment[:, :, None], segment[:, None, :])


def collect_kernel(place_ref, ids_ref, grads_ref, out_ref, small_ref, square_ref, acc_ref, rows_ref,
                   *, span, tokens, features, vocab):
    step = pl.program_id(0)
    last = pl.num_programs(0) - 1
    streams = acc_ref.shape[0]

    @pl.when(step == 0)
    def _():
        acc_ref[...] = jnp.zeros_like(acc_ref)
        small_ref[...] = jnp.zeros_like(small_ref)

    small_ref[...] += grads_ref[0, :, tokens:].astype(full)
    group = ids_ref[0] // span
    grads = grads_ref[0, :, :tokens].astype(full)
    pad = jnp.zeros((WIDTH - features, tokens), full)
    pieces = []
    for at in range(GROUPS):
        pieces += [jnp.where(group == at, grads, 0.0), pad]
    spread = jnp.concatenate(pieces, axis=0)
    rows_ref[...] = spread.T

    def body(i, carry):
        base = i * 16
        for j in range(16):
            place = place_ref[0, 0, base + j]
            k = j % streams
            acc_ref[k, pl.ds(place, 1), :] += rows_ref[pl.ds(base + j, 1), :]
        return carry

    lax.fori_loop(0, tokens // 16, body, 0)

    @pl.when(step == last)
    def _():
        def flush(b, total):
            at = pl.multiple_of(b * LANES, LANES)
            block = acc_ref[0, pl.ds(at, LANES), :]
            for k in range(1, streams):
                block += acc_ref[k, pl.ds(at, LANES), :]
            turned = block.T
            for g in range(GROUPS):
                piece = turned[g * WIDTH:g * WIDTH + features]

                @pl.when(g * span + at < vocab)
                def _():
                    out_ref[:, pl.ds(pl.multiple_of(g * span + at, LANES), LANES)] = piece.astype(low)
            return total + block * block

        total = lax.fori_loop(0, span // LANES, flush, jnp.zeros((LANES, LANES), full))
        square_ref[...] = jnp.broadcast_to(jnp.sum(total, keepdims=True), square_ref.shape)


def collect(ids, grads, vocab, tokens):
    sources, features, width = grads.shape
    span = -(-vocab // (GROUPS * LANES)) * LANES
    return pl.pallas_call(
        partial(collect_kernel, span=span, tokens=tokens, features=features, vocab=vocab),
        grid=(sources,),
        in_specs=[
            pl.BlockSpec((1, 1, tokens), lambda s: (s, 0, 0), memory_space=pltpu.SMEM),
            pl.BlockSpec((1, 1, tokens), lambda s: (s, 0, 0)),
            pl.BlockSpec((1, features, width), lambda s: (s, 0, 0)),
        ],
        out_specs=[
            pl.BlockSpec((features, vocab), lambda s: (0, 0)),
            pl.BlockSpec((features, width - tokens), lambda s: (0, 0)),
            pl.BlockSpec((8, LANES), lambda s: (0, 0)),
        ],
        out_shape=[
            jax.ShapeDtypeStruct((features, vocab), low),
            jax.ShapeDtypeStruct((features, width - tokens), full),
            jax.ShapeDtypeStruct((8, LANES), full),
        ],
        scratch_shapes=[
            pltpu.VMEM((4, span, LANES), full),
            pltpu.VMEM((tokens, LANES), full),
        ],
        compiler_params=params(56),
        name="collect",
    )((ids % span)[:, None, :], ids[:, None, :], grads)


def moment_kernel(info_ref, factor_ref, grad_ref, old_ref, moment_ref, gram_ref, *, piece, block):
    factor = factor_ref[0]
    for at in range(old_ref.shape[0] // piece):
        source = pl.multiple_of(info_ref[2 + at] * piece, piece)
        rows = slice(at * piece, (at + 1) * piece)
        moment_ref[rows] = muon_beta * old_ref[rows] + factor * grad_ref[pl.ds(source, piece)].astype(full)
    gram_ref[...] = jnp.zeros_like(gram_ref)

    def body(b, carry):
        slot = (b * block >= info_ref[0]).astype(jnp.int32)
        rows = halves(moment_ref[pl.ds(pl.multiple_of(b * block, block), block)])
        gram_ref[slot] += dot_split(rows, rows, 0, 0)
        return carry

    lax.fori_loop(0, old_ref.shape[0] // block, body, 0)


def moment_and_gram(info, factor, grad, old, piece, block):
    return pl.pallas_call(
        partial(moment_kernel, piece=piece, block=block),
        in_specs=[smem(), smem(), vmem(), vmem(), vmem()][:4],
        out_specs=[vmem(), vmem()],
        out_shape=[
            jax.ShapeDtypeStruct(old.shape, full),
            jax.ShapeDtypeStruct((2, D, D), full),
        ],
        compiler_params=params(56),
        name="moment",
    )(info, factor, grad, old)


def newton_kernel(info_ref, gain_ref, gram0_ref, gram1_ref, moment_ref, master_ref, new_ref, copy_ref,
                  a_ref, q_ref, p_ref, *, block):
    rows_total = moment_ref.shape[0]
    diagonal = lax.broadcasted_iota(jnp.int32, (D, D), 0) == lax.broadcasted_iota(jnp.int32, (D, D), 1)

    def chain(gram_ref, slot, first, last):
        gram = gram_ref[...]
        scale = jnp.sqrt(jnp.sum(jnp.where(diagonal, gram, 0.0))) + 1e-07
        a_ref[...] = gram * (1.0 / (scale * scale))

        def turn(k, carry):
            a = halves(a_ref[...])
            square = dot_split(a, a)
            q_ref[...] = jnp.where(diagonal, 3.4445, 0.0) - 4.775 * a_ref[...] + 2.0315 * square
            q = halves(q_ref[...])

            @pl.when(k == 0)
            def _():
                p_ref[...] = q_ref[...]

            @pl.when(k > 0)
            def _():
                p_ref[...] = dot_split(halves(p_ref[...]), q)

            @pl.when(k < NS_TURNS - 1)
            def _():
                a_ref[...] = dot_split(a, q)
                a_ref[...] = dot_split(halves(a_ref[...]), q)

            return carry

        lax.fori_loop(0, NS_TURNS, turn, 0)
        p = halves(p_ref[...])
        gain = gain_ref[slot] * muon_rate

        def body(b, carry):
            rows = pl.ds(pl.multiple_of(b * block, block), block)
            ortho = dot_split(halves(moment_ref[rows] * (1.0 / scale)), p)
            new = master_ref[rows] * (1.0 - muon_rate * muon_decay) - gain * ortho
            new_ref[rows] = new
            copy_ref[rows] = new.astype(low)
            return carry

        lax.fori_loop(first, last, body, 0)

    split = info_ref[0] // block
    chain(gram0_ref, 0, 0, split)

    @pl.when(split < rows_total // block)
    def _():
        chain(gram1_ref, 1, split, rows_total // block)


def newton(info, gains, gram0, gram1, moment, master, block):
    return pl.pallas_call(
        partial(newton_kernel, block=block),
        in_specs=[smem(), smem(), vmem(), vmem(), vmem(), vmem()],
        out_specs=[vmem(), vmem()],
        out_shape=[
            jax.ShapeDtypeStruct(moment.shape, full),
            jax.ShapeDtypeStruct(moment.shape, low),
        ],
        scratch_shapes=[pltpu.VMEM((D, D), full)] * 3,
        compiler_params=params(60),
        name="newton",
    )(info, gains, gram0, gram1, moment, master)


def share_grams(grams, wide_at, first_matrix, second_matrix):
    wide = lax.axis_size("wide")
    if wide != 8:
        which = jnp.arange(4)
        slots = (which == first_matrix).astype(full)[:, None, None] * grams[0]
        slots = slots + (which == second_matrix).astype(full)[:, None, None] * grams[1]
        total = lax.psum(slots, "wide")
        return (
            lax.dynamic_index_in_dim(total, first_matrix, 0, keepdims=False),
            lax.dynamic_index_in_dim(total, second_matrix, 0, keepdims=False),
        )
    half = D // 2
    gram0, gram1 = grams[0], grams[1]
    pairs = [(i, i ^ 1) for i in range(8)]
    lower = wide_at % 2 == 0
    mine = jnp.where(wide_at == 2, gram1, gram0)
    moved = lax.ppermute(gram1[:half], "wide", [(5, 4)])
    chip = mine + lax.ppermute(mine, "wide", pairs)
    up_send = jnp.where(lower, chip[:half], chip[half:])
    down_send = jnp.where(wide_at == 4, moved, jnp.where(wide_at == 5, gram1[half:], up_send))
    up = up_send + lax.ppermute(up_send, "wide", [(2, 4), (4, 2), (3, 5), (5, 3)])
    down = down_send + lax.ppermute(down_send, "wide", [(4, 6), (6, 4), (5, 7), (7, 5)])
    done = jnp.where(wide_at <= 5, up, down)
    other = lax.ppermute(done, "wide", pairs)
    extra = lax.ppermute(down, "wide", [(4, 5)])
    whole = jnp.concatenate([jnp.where(lower, done, other), jnp.where(lower, other, done)])
    first = jnp.where(wide_at < 2, chip, jnp.where(wide_at == 2, gram0, whole))
    second = jnp.where(wide_at == 5, jnp.concatenate([extra, down]), whole)
    return first, second


def layout(lengths):
    row_ends = jnp.cumsum(lengths)
    starts = row_ends - lengths
    places = jnp.arange(SEQ, dtype=jnp.int32)
    segment = jnp.sum((places[:, None] >= row_ends[None, :]).astype(jnp.int32), axis=1)
    chosen = segment[:, None] == jnp.arange(SLOTS, dtype=jnp.int32)[None, :]
    start_at = jnp.sum(jnp.where(chosen, starts[None, :], 0), axis=1)
    length_at = jnp.sum(jnp.where(chosen, lengths[None, :], 0), axis=1)
    position = places - start_at
    second = (2 * position >= length_at).astype(jnp.int32)
    return (chosen.astype(full), position, second, segment)


def norm_forward(hidden, gain, bias):
    center = hidden - jnp.mean(hidden, axis=-1, keepdims=True)
    inverse = lax.rsqrt(jnp.mean(center * center, axis=-1, keepdims=True) + norm_eps)
    scaled = center * inverse
    return (scaled * gain + bias, scaled, inverse)


def norm_backward(upstream, scaled, inverse, gain):
    weighted = upstream * gain
    back = inverse * (
        weighted
        - jnp.mean(weighted, axis=-1, keepdims=True)
        - scaled * jnp.mean(weighted * scaled, axis=-1, keepdims=True)
    )
    return (back, jnp.sum(upstream * scaled, axis=0), jnp.sum(upstream, axis=0))


def project(left, right):
    return jnp.dot(left, right, preferred_element_type=full)


def task_loss(logits, scores, tasks, labels, negatives, counts):
    logprob = jax.nn.log_softmax(logits, axis=-1)
    picked = jnp.sum(
        jnp.where(labels[:, :, None] == jnp.arange(3, dtype=jnp.int32), logprob, 0.0), axis=2
    )
    chosen = negatives[:, :, :, None] == jnp.arange(scores.shape[1], dtype=jnp.int32)
    rivals = jnp.sum(jnp.where(chosen, scores[:, None, None, :], 0.0), axis=3)
    together = jnp.concatenate([scores[:, :, None], rivals], axis=2)
    ranking = jax.nn.logsumexp(together, axis=2) - scores
    first_part = jnp.sum(jnp.where(tasks == 0, -picked, 0.0)) / counts[0]
    return first_part + jnp.sum(jnp.where(tasks == 1, ranking, 0.0)) / counts[1]


def adam(weight, grad, first, second, step, rate):
    first = beta_one * first + (1.0 - beta_one) * grad
    second = beta_two * second + (1.0 - beta_two) * grad * grad
    unbiased = first / (1.0 - beta_one**step)
    spread = second / (1.0 - beta_two**step)
    return (
        weight - rate * (unbiased / (jnp.sqrt(spread) + adam_eps) + adam_decay * weight),
        first,
        second,
    )


def broadcast_all(x):
    count = lax.axis_size("narrow") * lax.axis_size("wide")
    return lax.all_to_all(
        jnp.broadcast_to(x[None], (count,) + x.shape), BOTH, split_axis=0, concat_axis=0, tiled=True
    )


def by_owner(grad, spans, parts):
    pieces = [
        grad[lo:hi].reshape(parts, (hi - lo) // parts, D) for lo, hi in spans
    ]
    return jnp.concatenate(pieces, axis=1).reshape(-1, D).astype(low)


def shards(
    token_ids,
    seq_lengths,
    task_ids,
    labels,
    negatives,
    step_count,
    hidden_master,
    hidden_momentum,
    table_master,
    table_first,
    table_second,
    pos_types,
    pos_first,
    pos_second,
    vectors,
    vec_first,
    vec_second,
):
    wide_at = lax.axis_index("wide")
    narrow_at = lax.axis_index("narrow")
    wide = lax.axis_size("wide")
    narrow = lax.axis_size("narrow")
    count = wide * narrow
    device_at = narrow_at * wide + wide_at
    micro_count, rows_each = token_ids.shape[:2]
    batch = micro_count * rows_each
    tokens = batch * SEQ
    shard = hidden_master.shape[0]
    vocab = table_master.shape[1]
    features = table_master.shape[0] // narrow
    pairs_each = rows_each * SLOTS

    parts = [token_ids, task_ids, labels, negatives]
    sizes = [part.size for part in parts]
    packed = jnp.concatenate([part.reshape(-1) for part in parts])
    packed = jnp.pad(packed, (0, -packed.size % LANES))
    gathered = broadcast_all(packed)
    ends = [sum(sizes[: i + 1]) for i in range(len(sizes))]
    ids_all = gathered[:, : ends[0]]

    def pairs_of(lo, hi, tail):
        block = gathered[:, lo:hi].reshape((count, micro_count, pairs_each) + tail)
        return jnp.moveaxis(block, 1, 0).reshape((micro_count, count * pairs_each) + tail)

    tasks_all = pairs_of(ends[0], ends[1], ())
    labels_all = pairs_of(ends[1], ends[2], ())
    negatives_all = pairs_of(ends[2], ends[3], (NEG,))
    counts = jnp.stack(
        [jnp.sum((tasks_all == 0).astype(full)), jnp.sum((tasks_all == 1).astype(full))]
    )

    weights = lax.all_gather(hidden_master.astype(low), "wide", axis=0, tiled=True)

    group_ids = lax.dynamic_slice_in_dim(ids_all, narrow_at * wide, wide, 0).reshape(-1)
    pieces = jnp.take(table_master.astype(low), group_ids, axis=1)
    arrived = lax.all_to_all(pieces, "wide", split_axis=1, concat_axis=0, tiled=True)
    token_rows = arrived.T

    lengths = seq_lengths.reshape(batch, SLOTS)
    member, position, second, segment = jax.vmap(layout)(lengths)
    flat_position = position.reshape(-1)
    flat_second = second.reshape(-1)
    embed = token_rows.astype(full) + pos_types[flat_position]
    embed = embed + jnp.where(flat_second[:, None] == 1, pos_types[SEQ + 1], pos_types[SEQ])
    normed0, scaled0, inverse0 = norm_forward(embed, vectors[0], vectors[1])
    input0 = normed0.astype(low)
    qkv_bias = jnp.concatenate([vectors[6], jnp.zeros_like(vectors[6]), vectors[7]])
    mixed = (project(input0, weights[: 3 * D].T) + qkv_bias).astype(low)
    context_low, logsum = attend(mixed, segment)
    attended = project(context_low, weights[3 * D : 4 * D].T) + vectors[8]
    normed1, scaled1, inverse1 = norm_forward(normed0 + attended, vectors[2], vectors[3])
    input1 = normed1.astype(low)
    inner = project(input1, weights[4 * D : 4 * D + FF].T) + vectors[14:].reshape(-1)
    cdf = 0.5 * (1.0 + lax.erf(inner * math.sqrt(0.5)))
    active = (inner * cdf).astype(low)
    slope = cdf + inner * (jnp.exp(-0.5 * inner * inner) * (1.0 / math.sqrt(2.0 * math.pi)))
    branch = project(active, weights[4 * D + FF :]) + vectors[9]
    normed2, scaled2, inverse2 = norm_forward(normed1 + branch, vectors[4], vectors[5])
    share = member / lengths.astype(full)[:, None, :]
    pooled = jnp.einsum("rps,rpd->rsd", share, normed2.reshape(batch, SEQ, D), precision=highest)
    flat_pooled = pooled.reshape(-1, D)
    heads = vectors[10:14]
    head_out = jnp.dot(flat_pooled, heads.T, precision=highest)

    sent = jnp.pad(head_out.reshape(-1), (0, -head_out.size % LANES))
    head_all = broadcast_all(sent)[:, : head_out.size]
    head_all = head_all.reshape(count, micro_count, pairs_each, 4)
    head_all = jnp.moveaxis(head_all, 1, 0).reshape(micro_count, count * pairs_each, 4)

    def objective(every):
        return task_loss(every[:, :, :3], every[:, :, 3], tasks_all, labels_all, negatives_all, counts)

    loss, pullback = jax.vjp(objective, head_all)
    head_grads = pullback(jnp.ones_like(loss))[0]
    output_grads = lax.dynamic_slice_in_dim(head_grads, device_at * pairs_each, pairs_each, 1)
    output_grads = output_grads.reshape(-1, 4)
    heads_grad = jnp.dot(output_grads.T, flat_pooled, precision=highest)
    pooled_grads = jnp.dot(output_grads, heads, precision=highest).reshape(pooled.shape)

    spread = jnp.einsum("rps,rsd->rpd", share, pooled_grads, precision=highest).reshape(-1, D)
    sum2_grad, gain2, bias2 = norm_backward(spread, scaled2, inverse2, vectors[4])
    branch_grad = sum2_grad.astype(low)
    down_grad = project(active.T, branch_grad)
    simple = wide != 8
    spans_down = [(0, 768), (768, 1920), (1920, 3072)]
    spans_up = [(0, 384), (384, 1536), (1536, 2688), (2688, 3072)]
    spans_front = [(0, 1152), (1152, 2304), (2304, 3072)]

    def first_stage(grad, spans):
        if simple:
            return grad.astype(low)
        return lax.psum_scatter(by_owner(grad, spans, narrow), "narrow", scatter_dimension=0, tiled=True)

    down_part = first_stage(down_grad, spans_down)
    active_grad = project(branch_grad, weights[4 * D + FF :].T)
    inner_grad = (active_grad * slope).astype(low)
    up_grad = project(inner_grad.T, input1)
    up_part = first_stage(up_grad, spans_up)
    normed1_grad = sum2_grad + project(inner_grad, weights[4 * D : 4 * D + FF])
    sum1_grad, gain1, bias1 = norm_backward(normed1_grad, scaled1, inverse1, vectors[2])
    attended_grad = sum1_grad.astype(low)
    out_grad = project(attended_grad.T, context_low)
    context_grad = project(attended_grad, weights[3 * D : 4 * D]).astype(low)
    mixed_grad = attend_back(mixed, context_grad, logsum, segment)
    qkv_grad = project(mixed_grad.T, input0)
    front_part = first_stage(jnp.concatenate([qkv_grad, out_grad]), spans_front)
    normed0_grad = sum1_grad + project(mixed_grad, weights[: 3 * D])
    embed_grad, gain0, bias0 = norm_backward(normed0_grad, scaled0, inverse0, vectors[0])
    mixed_sum = jnp.sum(mixed_grad.astype(full), axis=0)
    small_rows = jnp.stack(
        [
            gain0,
            bias0,
            gain1,
            bias1,
            gain2,
            bias2,
            mixed_sum[:D],
            mixed_sum[2 * D :],
            jnp.sum(attended_grad.astype(full), axis=0),
            jnp.sum(branch_grad.astype(full), axis=0),
        ]
    )
    up_rows = jnp.sum(inner_grad.astype(full), axis=0).reshape(-1, D)

    places = jnp.arange(SEQ, dtype=jnp.int32)[:, None]
    row_hot = jnp.concatenate(
        [
            flat_position[None] == places,
            jnp.stack([flat_second == 0, flat_second == 1]),
        ]
    ).astype(low)
    high_part, low_part = halves(embed_grad)
    pos_grad = project(jnp.concatenate([row_hot, row_hot], axis=1), jnp.concatenate([high_part, low_part]))
    small = jnp.concatenate([pos_grad, small_rows, heads_grad, up_rows])
    small_count = small.shape[0]
    small = jnp.pad(small, ((0, count * features - small_count), (0, 0)))

    table_send = embed_grad.astype(low).T.reshape(wide, narrow, features, tokens)
    table_send = jnp.moveaxis(table_send, 1, 0).reshape(count, features, tokens)
    small_send = small.astype(low).reshape(count, features, D)
    table_come = lax.all_to_all(
        jnp.concatenate([table_send, small_send], axis=2), BOTH, split_axis=0, concat_axis=0, tiled=True
    )
    table_part, small_part, table_square = collect(ids_all, table_come, vocab, tokens)

    joined = jnp.concatenate([front_part, up_part, down_part])
    hidden_part = lax.psum_scatter(joined, "wide", scatter_dimension=0, tiled=True)
    if simple:
        hidden_part = lax.psum_scatter(hidden_part, "narrow", scatter_dimension=0, tiled=True)
    hidden_all = lax.all_gather(hidden_part, "narrow", axis=0, tiled=True)
    table_grad = lax.all_gather(table_part, "narrow", axis=0, tiled=True)
    small_all = lax.all_gather(small_part, BOTH, axis=0, tiled=True)[:small_count]

    hidden_wide = hidden_part.astype(full)
    square = jnp.sum(hidden_wide * hidden_wide) + table_square[0, 0] + jnp.sum(small_part * small_part)
    squares = broadcast_all(jnp.broadcast_to(square, (LANES,)))
    clip_norm = jnp.sqrt(jnp.sum(squares[:, 0]))
    factor = jnp.minimum(1.0, clip_bound / clip_norm)

    start = wide_at * shard
    bounds = jnp.array(BOUNDS, jnp.int32)
    first_matrix = jnp.sum((start >= bounds[1:4]).astype(jnp.int32))
    second_matrix = jnp.sum((start + shard - 1 >= bounds[1:4]).astype(jnp.int32))
    split = jnp.minimum(bounds[first_matrix + 1] - start, shard)
    block = shard // 3
    piece = shard // 12
    at = jnp.arange(12, dtype=jnp.int32)
    if simple:
        source = at
    else:
        lead = split // piece
        each = lead // narrow
        rest = (12 - lead) // narrow
        in_first = at < lead
        inside = jnp.where(in_first, at, at - lead)
        width = jnp.maximum(jnp.where(in_first, each, rest), 1)
        source = (inside // width) * (12 // narrow) + jnp.where(in_first, 0, each) + inside % width
    info = jnp.concatenate([jnp.stack([split, split]), source]).astype(jnp.int32)
    gains = jnp.array([0.2 * math.sqrt(hi - lo) for lo, hi in zip(BOUNDS, BOUNDS[1:])], full)
    moment, grams = moment_and_gram(info, factor[None], hidden_all, hidden_momentum, piece, block)
    gram0, gram1 = share_grams(grams, wide_at, first_matrix, second_matrix)
    slot_gains = jnp.stack([gains[first_matrix], gains[second_matrix]])
    hidden_new, hidden_copy = newton(info, slot_gains, gram0, gram1, moment, hidden_master, block)

    step = step_count[0].astype(full)
    table_new, table_first_new, table_second_new = adam(
        table_master, factor * table_grad.astype(full), table_first, table_second, step, 0.02
    )
    pos_new, pos_first_new, pos_second_new = adam(
        pos_types, factor * small_all[: SEQ + 2], pos_first, pos_second, step, 0.02
    )
    vectors_new, vec_first_new, vec_second_new = adam(
        vectors, factor * small_all[SEQ + 2 :], vec_first, vec_second, step, 0.2
    )
    return (
        loss,
        clip_norm,
        moment,
        hidden_new,
        hidden_copy,
        table_new,
        table_first_new,
        table_second_new,
        table_new.astype(low),
        pos_new,
        pos_first_new,
        pos_second_new,
        vectors_new,
        vec_first_new,
        vec_second_new,
    )


def solution(mesh):
    rows = P(None, BOTH, None)
    owned = P("wide", None)
    return jax.shard_map(
        shards,
        mesh=mesh,
        in_specs=(rows, rows, rows, rows, P(None, BOTH, None, None), P())
        + (owned,) * 5
        + (P(),) * 6,
        out_specs=(P(), P()) + (owned,) * 7 + (P(),) * 6,
        check_vma=False,
    )
```

```python
from functools import partial
import math

import jax
import jax.numpy as jnp
from jax import lax
from jax.experimental import pallas as pl
from jax.experimental.pallas import tpu as pltpu
from jax.sharding import PartitionSpec as P

D = 768
HEADS = 12
HEAD = 64
FF = 3072
SEQ = 512
SLOTS = 4
NEG = 4
NS_TURNS = 5
LANES = 128
GROUPS = 4
WIDTH = LANES // GROUPS
BLOCK = 256

BOTH = ("narrow", "wide")
highest = lax.Precision.HIGHEST
clip_bound = 0.002
norm_eps = 1e-06
muon_beta = 0.95
muon_rate = 0.1
muon_decay = 0.01
beta_one = 0.9
beta_two = 0.999
adam_eps = 1e-08
adam_decay = 0.01
BOUNDS = (0, 3 * D, 4 * D, 4 * D + FF, 4 * D + 2 * FF)

low = jnp.bfloat16
full = jnp.float32


def dims(left, right):
    return (((left,), (right,)), ((), ()))


def dot32(left, right, left_dim, right_dim):
    return lax.dot_general(left, right, dims(left_dim, right_dim), preferred_element_type=full)


def halves(x):
    high = x.astype(low)
    return high, (x - high.astype(full)).astype(low)


def dot_split(left, right, left_dim=1, right_dim=0):
    (lh, ll), (rh, rl) = left, right
    return dot32(lh, rh, left_dim, right_dim) + (
        dot32(lh, rl, left_dim, right_dim) + dot32(ll, rh, left_dim, right_dim)
    )


def params(mib):
    return pltpu.CompilerParams(vmem_limit_bytes=mib << 20)


def vmem():
    return pl.BlockSpec(memory_space=pltpu.VMEM)


def smem():
    return pl.BlockSpec(memory_space=pltpu.SMEM)


def attend_kernel(mixed_ref, seg_col_ref, seg_row_ref, context_ref, logsum_ref):
    same = seg_col_ref[0] == seg_row_ref[0]

    def pair(step, carry):
        at = pl.multiple_of(step * LANES, LANES)
        queries = mixed_ref[:, pl.ds(at, LANES)]
        keys = mixed_ref[:, pl.ds(D + at, LANES)]
        values = mixed_ref[:, pl.ds(2 * D + at, LANES)]
        outs = []
        for half in range(2):
            cut = slice(half * HEAD, (half + 1) * HEAD)
            raw = dot32(keys[:, cut], queries[:, cut], 1, 1)
            scores = jnp.where(same, raw * (1.0 / math.sqrt(HEAD)), -1e30)
            peak = jnp.max(scores, axis=0, keepdims=True)
            lifted = jnp.exp(scores - peak)
            total = jnp.sum(lifted, axis=0, keepdims=True)
            probs = (lifted * (1.0 / total)).astype(low)
            outs.append(dot32(values[:, cut], probs, 0, 0))
            logsum_ref[0, pl.ds(2 * step + half, 1), :] = peak + jnp.log(total)
        context_ref[:, pl.ds(at, LANES)] = jnp.concatenate(outs, axis=0).T.astype(low)
        return carry

    lax.fori_loop(0, HEADS // 2, pair, 0)


def attend(mixed, segment):
    rows = segment.shape[0]
    return pl.pallas_call(
        attend_kernel,
        grid=(rows,),
        in_specs=[
            pl.BlockSpec((SEQ, 3 * D), lambda b: (b, 0)),
            pl.BlockSpec((1, SEQ, 1), lambda b: (b, 0, 0)),
            pl.BlockSpec((1, 1, SEQ), lambda b: (b, 0, 0)),
        ],
        out_specs=[
            pl.BlockSpec((SEQ, D), lambda b: (b, 0)),
            pl.BlockSpec((1, 16, SEQ), lambda b: (b, 0, 0)),
        ],
        out_shape=[
            jax.ShapeDtypeStruct((rows * SEQ, D), low),
            jax.ShapeDtypeStruct((rows, 16, SEQ), full),
        ],
        compiler_params=params(48),
        name="attend",
    )(mixed, segment[:, :, None], segment[:, None, :])


def attend_back_kernel(mixed_ref, grad_ref, logsum_ref, seg_col_ref, seg_row_ref, out_ref):
    same = seg_col_ref[0] == seg_row_ref[0]
    scale = 1.0 / math.sqrt(HEAD)

    def pair(step, carry):
        at = pl.multiple_of(step * LANES, LANES)
        queries = mixed_ref[:, pl.ds(at, LANES)]
        keys = mixed_ref[:, pl.ds(D + at, LANES)]
        values = mixed_ref[:, pl.ds(2 * D + at, LANES)]
        upstream = grad_ref[:, pl.ds(at, LANES)]
        query_grads, key_grads, value_grads = [], [], []
        for half in range(2):
            cut = slice(half * HEAD, (half + 1) * HEAD)
            logsum = logsum_ref[0, pl.ds(2 * step + half, 1), :]
            raw = dot32(keys[:, cut], queries[:, cut], 1, 1)
            probs = jnp.exp(jnp.where(same, raw * scale, -1e30) - logsum)
            prob_grads = dot32(values[:, cut], upstream[:, cut], 1, 1)
            value_grads.append(dot32(probs.astype(low), upstream[:, cut], 1, 0))
            moved = jnp.sum(prob_grads * probs, axis=0, keepdims=True)
            back = (probs * (prob_grads - moved) * scale).astype(low)
            key_grads.append(dot32(back, queries[:, cut], 1, 0))
            query_grads.append(dot32(keys[:, cut], back, 0, 0))
        out_ref[:, pl.ds(at, LANES)] = jnp.concatenate(query_grads, axis=0).T.astype(low)
        out_ref[:, pl.ds(D + at, LANES)] = jnp.concatenate(key_grads, axis=1).astype(low)
        out_ref[:, pl.ds(2 * D + at, LANES)] = jnp.concatenate(value_grads, axis=1).astype(low)
        return carry

    lax.fori_loop(0, HEADS // 2, pair, 0)


def attend_back(mixed, context_grad, logsum, segment):
    rows = segment.shape[0]
    return pl.pallas_call(
        attend_back_kernel,
        grid=(rows,),
        in_specs=[
            pl.BlockSpec((SEQ, 3 * D), lambda b: (b, 0)),
            pl.BlockSpec((SEQ, D), lambda b: (b, 0)),
            pl.BlockSpec((1, 16, SEQ), lambda b: (b, 0, 0)),
            pl.BlockSpec((1, SEQ, 1), lambda b: (b, 0, 0)),
            pl.BlockSpec((1, 1, SEQ), lambda b: (b, 0, 0)),
        ],
        out_specs=pl.BlockSpec((SEQ, 3 * D), lambda b: (b, 0)),
        out_shape=jax.ShapeDtypeStruct((rows * SEQ, 3 * D), low),
        compiler_params=params(56),
        name="attend_back",
    )(mixed, context_grad, logsum, segment[:, :, None], segment[:, None, :])


def collect_kernel(place_ref, ids_ref, grads_ref, out_ref, square_ref, *scratch,
                   span, tokens, features, vocab):
    sums, rows_ref = scratch[:-1], scratch[-1]
    step = pl.program_id(0)
    last = pl.num_programs(0) - 1
    streams = len(sums)
    batch = 4 * streams

    @pl.when(step == 0)
    def _():
        for total in sums:
            total[...] = jnp.zeros_like(total)

    group = ids_ref[0] // span
    grads = grads_ref[0].astype(full)
    pad = jnp.zeros((WIDTH - features, tokens), full)
    pieces = []
    for at in range(GROUPS):
        pieces += [jnp.where(group == at, grads, 0.0), pad]
    rows_ref[...] = jnp.concatenate(pieces, axis=0).T

    def body(i, carry):
        for base in range(0, batch, streams):
            at = i * batch + base
            places = [pl.ds(place_ref[0, 0, at + k], 1) for k in range(streams)]
            olds = [sums[k][places[k], :] for k in range(streams)]
            news = [rows_ref[pl.ds(at + k, 1), :] for k in range(streams)]
            for k in range(streams):
                sums[k][places[k], :] = olds[k] + news[k]
        return carry

    lax.fori_loop(0, tokens // batch, body, 0)

    @pl.when(step == last)
    def _():
        def flush(b, total):
            at = pl.multiple_of(b * LANES, LANES)
            block = sums[0][pl.ds(at, LANES), :]
            for k in range(1, streams):
                block += sums[k][pl.ds(at, LANES), :]
            turned = block.T
            for g in range(GROUPS):
                piece = turned[g * WIDTH:g * WIDTH + features]

                @pl.when(g * span + at < vocab)
                def _():
                    out_ref[:, pl.ds(pl.multiple_of(g * span + at, LANES), LANES)] = piece.astype(low)

            return total + block * block

        total = lax.fori_loop(0, span // LANES, flush, jnp.zeros((LANES, LANES), full))
        square_ref[...] = jnp.broadcast_to(jnp.sum(total, keepdims=True), square_ref.shape)


def collect(ids, grads, vocab):
    sources, features, tokens = grads.shape
    span = -(-vocab // (GROUPS * LANES)) * LANES
    return pl.pallas_call(
        partial(collect_kernel, span=span, tokens=tokens, features=features, vocab=vocab),
        grid=(sources,),
        in_specs=[
            pl.BlockSpec((1, 1, tokens), lambda s: (s, 0, 0), memory_space=pltpu.SMEM),
            pl.BlockSpec((1, 1, tokens), lambda s: (s, 0, 0)),
            pl.BlockSpec((1, features, tokens), lambda s: (s, 0, 0)),
        ],
        out_specs=[
            pl.BlockSpec((features, vocab), lambda s: (0, 0)),
            pl.BlockSpec((8, LANES), lambda s: (0, 0)),
        ],
        out_shape=[
            jax.ShapeDtypeStruct((features, vocab), low),
            jax.ShapeDtypeStruct((8, LANES), full),
        ],
        scratch_shapes=[pltpu.VMEM((span, LANES), full)] * 8 + [pltpu.VMEM((tokens, LANES), full)],
        compiler_params=params(56),
        name="collect",
    )((ids % span)[:, None, :], ids[:, None, :], grads)


def moment_kernel(info_ref, factor_ref, grad_ref, old_ref, moment_ref, gram_ref, *, piece, block):
    factor = factor_ref[0]
    for at in range(old_ref.shape[0] // piece):
        source = pl.multiple_of(info_ref[2 + at] * piece, piece)
        rows = slice(at * piece, (at + 1) * piece)
        moment_ref[rows] = muon_beta * old_ref[rows] + factor * grad_ref[pl.ds(source, piece)].astype(full)
    gram_ref[...] = jnp.zeros_like(gram_ref)

    def body(b, carry):
        slot = (b * block >= info_ref[0]).astype(jnp.int32)
        rows = halves(moment_ref[pl.ds(pl.multiple_of(b * block, block), block)])
        gram_ref[slot] += dot_split(rows, rows, 0, 0)
        return carry

    lax.fori_loop(0, old_ref.shape[0] // block, body, 0)


def moment_and_gram(info, factor, grad, old, piece, block):
    return pl.pallas_call(
        partial(moment_kernel, piece=piece, block=block),
        in_specs=[smem(), smem(), vmem(), vmem(), vmem()][:4],
        out_specs=[vmem(), vmem()],
        out_shape=[
            jax.ShapeDtypeStruct(old.shape, full),
            jax.ShapeDtypeStruct((2, D, D), full),
        ],
        compiler_params=params(56),
        name="moment",
    )(info, factor, grad, old)


def even_product(left, right, put):
    (lh, ll), (rh, rl) = left, right
    for i in range(D // BLOCK):
        rows = slice(i * BLOCK, (i + 1) * BLOCK)
        panel = jnp.concatenate([lh[rows], lh[rows], ll[rows]], axis=1)
        for j in range(i, D // BLOCK):
            cols = slice(j * BLOCK, (j + 1) * BLOCK)
            other = jnp.concatenate([rh[:, cols], rl[:, cols], rh[:, cols]], axis=0)
            put(rows, cols, dot32(panel, other, 1, 0))


def keep(pair):
    def put(rows, cols, value):
        pair[0][rows, cols], pair[1][rows, cols] = halves(value)
        if rows != cols:
            pair[0][cols, rows], pair[1][cols, rows] = halves(value.T)

    return put


def chain_kernel(gram_ref, out_ref, a_ref, *parts):
    a, q, p, t = [parts[2 * i:2 * i + 2] for i in range(4)]

    def diagonal(size):
        shape = (size, size)
        return lax.broadcasted_iota(jnp.int32, shape, 0) == lax.broadcasted_iota(jnp.int32, shape, 1)

    gram = gram_ref[...]
    scale = jnp.sqrt(jnp.sum(jnp.where(diagonal(D), gram, 0.0))) + 1e-07
    a_ref[...] = gram * (1.0 / (scale * scale))
    a[0][...], a[1][...] = halves(a_ref[...])
    once = diagonal(BLOCK)

    def put_q(rows, cols, value):
        new = 2.0315 * value - 4.775 * a_ref[rows, cols]
        keep(q)(rows, cols, new + jnp.where(once, 3.4445, 0.0) if rows == cols else new)

    def put_a(rows, cols, value):
        a_ref[rows, cols] = value
        keep(a)(rows, cols, value)

    def put_out(rows, cols, value):
        value = value * (1.0 / scale)
        out_ref[rows, cols] = value
        if rows != cols:
            out_ref[cols, rows] = value.T

    def turn(k, carry):
        even_product(a, a, put_q)

        @pl.when(k == 0)
        def _():
            p[0][...], p[1][...] = q[0][...], q[1][...]

        @pl.when((k > 0) & (k < NS_TURNS - 1))
        def _():
            even_product(p, q, keep(t))
            p[0][...], p[1][...] = t[0][...], t[1][...]

        @pl.when(k == NS_TURNS - 1)
        def _():
            even_product(p, q, put_out)

        @pl.when(k < NS_TURNS - 1)
        def _():
            even_product(a, q, keep(t))
            even_product(t, q, put_a)

        return carry

    lax.fori_loop(0, NS_TURNS, turn, 0)


def chain(gram):
    return pl.pallas_call(
        chain_kernel,
        in_specs=[vmem()],
        out_specs=vmem(),
        out_shape=jax.ShapeDtypeStruct((D, D), full),
        scratch_shapes=[pltpu.VMEM((D, D), full)] + [pltpu.VMEM((D, D), low)] * 8,
        compiler_params=params(40),
        name="chain",
    )(gram)


def apply_kernel(info_ref, gain_ref, first_ref, second_ref, moment_ref, master_ref, new_ref, copy_ref,
                 *, block):
    split = info_ref[0] // block

    def over(slot, p_ref, start, stop):
        p = halves(p_ref[...])
        gain = gain_ref[slot] * muon_rate

        def body(b, carry):
            rows = pl.ds(pl.multiple_of(b * block, block), block)
            ortho = dot_split(halves(moment_ref[rows]), p)
            new = master_ref[rows] * (1.0 - muon_rate * muon_decay) - gain * ortho
            new_ref[rows] = new
            copy_ref[rows] = new.astype(low)
            return carry

        lax.fori_loop(start, stop, body, 0)

    over(0, first_ref, 0, split)
    total = moment_ref.shape[0] // block

    @pl.when(split < total)
    def _():
        over(1, second_ref, split, total)


def apply_chain(info, gains, first, second, moment, master, block):
    return pl.pallas_call(
        partial(apply_kernel, block=block),
        in_specs=[smem(), smem(), vmem(), vmem(), vmem(), vmem()],
        out_specs=[vmem(), vmem()],
        out_shape=[
            jax.ShapeDtypeStruct(moment.shape, full),
            jax.ShapeDtypeStruct(moment.shape, low),
        ],
        compiler_params=params(48),
        name="apply",
    )(info, gains, first, second, moment, master)


def chains(grams, wide_at, first_matrix, second_matrix):
    wide = lax.axis_size("wide")
    if wide != 8:
        which = jnp.arange(4)
        slots = (which == first_matrix).astype(full)[:, None, None] * grams[0]
        slots = slots + (which == second_matrix).astype(full)[:, None, None] * grams[1]
        total = lax.psum(slots, "wide")
        return (
            chain(lax.dynamic_index_in_dim(total, first_matrix, 0, keepdims=False)),
            chain(lax.dynamic_index_in_dim(total, second_matrix, 0, keepdims=False)),
        )
    half = D // 2
    gram0, gram1 = grams[0], grams[1]
    pairs = [(i, i ^ 1) for i in range(8)]
    lower = wide_at % 2 == 0
    mine = jnp.where(wide_at == 2, gram1, gram0)
    moved = lax.ppermute(gram1[:half], "wide", [(5, 4)])
    chip = mine + lax.ppermute(mine, "wide", pairs)
    up_send = jnp.where(lower, chip[:half], chip[half:])
    down_send = jnp.where(wide_at == 4, moved, jnp.where(wide_at == 5, gram1[half:], up_send))
    up = up_send + lax.ppermute(up_send, "wide", [(2, 4), (4, 2), (3, 5), (5, 3)])
    down = down_send + lax.ppermute(down_send, "wide", [(4, 6), (6, 4), (5, 7), (7, 5)])
    send = jnp.where((wide_at == 4), down, up)
    send = jnp.where(wide_at >= 6, down, send)
    swap = lax.ppermute(send, "wide", [(2, 3), (4, 5), (6, 7), (7, 6)])
    back = lax.ppermute(up, "wide", [(5, 4)])
    kept = jnp.where(wide_at >= 5, down, up)
    other = jnp.where(wide_at == 4, back, swap)
    whole = jnp.concatenate([jnp.where(lower, kept, other), jnp.where(lower, other, kept)])
    own = chain(jnp.where(wide_at < 2, chip, jnp.where(wide_at == 2, gram0, whole)))
    come = lax.ppermute(own, "wide", [(3, 2), (4, 5)])
    return jnp.where(wide_at == 5, come, own), jnp.where(wide_at == 5, own, come)


def layout(lengths):
    row_ends = jnp.cumsum(lengths)
    starts = row_ends - lengths
    places = jnp.arange(SEQ, dtype=jnp.int32)
    segment = jnp.sum((places[:, None] >= row_ends[None, :]).astype(jnp.int32), axis=1)
    chosen = segment[:, None] == jnp.arange(SLOTS, dtype=jnp.int32)[None, :]
    start_at = jnp.sum(jnp.where(chosen, starts[None, :], 0), axis=1)
    length_at = jnp.sum(jnp.where(chosen, lengths[None, :], 0), axis=1)
    position = places - start_at
    second = (2 * position >= length_at).astype(jnp.int32)
    return (chosen.astype(full), position, second, segment)


def norm_forward(hidden, gain, bias):
    center = hidden - jnp.mean(hidden, axis=-1, keepdims=True)
    inverse = lax.rsqrt(jnp.mean(center * center, axis=-1, keepdims=True) + norm_eps)
    scaled = center * inverse
    return (scaled * gain + bias, scaled, inverse)


def norm_backward(upstream, scaled, inverse, gain):
    weighted = upstream * gain
    back = inverse * (
        weighted
        - jnp.mean(weighted, axis=-1, keepdims=True)
        - scaled * jnp.mean(weighted * scaled, axis=-1, keepdims=True)
    )
    return (back, jnp.sum(upstream * scaled, axis=0), jnp.sum(upstream, axis=0))


def project(left, right):
    return jnp.dot(left, right, preferred_element_type=full)


def task_loss(logits, scores, tasks, labels, negatives, counts):
    logprob = jax.nn.log_softmax(logits, axis=-1)
    picked = jnp.sum(
        jnp.where(labels[:, :, None] == jnp.arange(3, dtype=jnp.int32), logprob, 0.0), axis=2
    )
    chosen = negatives[:, :, :, None] == jnp.arange(scores.shape[1], dtype=jnp.int32)
    rivals = jnp.sum(jnp.where(chosen, scores[:, None, None, :], 0.0), axis=3)
    together = jnp.concatenate([scores[:, :, None], rivals], axis=2)
    ranking = jax.nn.logsumexp(together, axis=2) - scores
    first_part = jnp.sum(jnp.where(tasks == 0, -picked, 0.0)) / counts[0]
    return first_part + jnp.sum(jnp.where(tasks == 1, ranking, 0.0)) / counts[1]


def adam(weight, grad, first, second, step, rate):
    first = beta_one * first + (1.0 - beta_one) * grad
    second = beta_two * second + (1.0 - beta_two) * grad * grad
    unbiased = first / (1.0 - beta_one**step)
    spread = second / (1.0 - beta_two**step)
    return (
        weight - rate * (unbiased / (jnp.sqrt(spread) + adam_eps) + adam_decay * weight),
        first,
        second,
    )


def broadcast_all(x):
    count = lax.axis_size("narrow") * lax.axis_size("wide")
    return lax.all_to_all(
        jnp.broadcast_to(x[None], (count,) + x.shape), BOTH, split_axis=0, concat_axis=0, tiled=True
    )


def sides(wide):
    return [list(range(0, wide, 2)), list(range(1, wide, 2))]


def chip_mates(wide):
    return [(i, i ^ 1) for i in range(wide)]


def scatter_sum(x):
    narrow_bits = lax.axis_size("narrow").bit_length() - 1
    wide_bits = lax.axis_size("wide").bit_length() - 1
    turns = [("wide", 0)] + [("narrow", b) for b in range(narrow_bits)]
    turns += [("wide", b) for b in range(1, wide_bits)]
    for axis, bit in turns:
        upper = (lax.axis_index(axis) >> bit) & 1
        half = x.shape[0] // 2
        stays = jnp.where(upper == 1, x[half:], x[:half])
        leaves = jnp.where(upper == 1, x[:half], x[half:])
        pairs = [(i, i ^ (1 << bit)) for i in range(lax.axis_size(axis))]
        x = stays + lax.ppermute(leaves, axis, pairs)
    order = [("narrow", b) for b in reversed(range(narrow_bits))]
    order += [("wide", b) for b in reversed(range(wide_bits))]
    return x, [order.index(turn) for turn in turns]


def join_pieces(piece, places):
    whole = lax.all_gather(piece, BOTH, axis=0, tiled=False)
    whole = whole.reshape((2,) * len(places) + piece.shape)
    whole = whole.transpose(places + [len(places), len(places) + 1])
    return whole.reshape(-1, piece.shape[1])


def by_owner(grad, spans, parts):
    pieces = [
        grad[lo:hi].reshape(parts, (hi - lo) // parts, D) for lo, hi in spans
    ]
    return jnp.concatenate(pieces, axis=1).reshape(-1, D).astype(low)


def gather_weights(master, narrow_at, wide_at, first):
    wide = lax.axis_size("wide")
    if wide != 8:
        whole = lax.all_gather(master.astype(low), "wide", axis=0, tiled=True)
        return [whole[lo:hi] for lo, hi in zip(BOUNDS, BOUNDS[1:])]
    share = master.shape[0] // lax.axis_size("narrow")
    mine = lax.dynamic_slice_in_dim(master, narrow_at * share, share, 0).astype(low)
    near = lax.all_gather(mine, "wide", axis=0, tiled=False, axis_index_groups=sides(wide))
    near, _ = lax.optimization_barrier((near, first))
    owners = []
    for part in (near[: wide // 4], near[wide // 4 :]):
        held = lax.all_gather(part, "narrow", axis=1, tiled=True)
        other = lax.ppermute(held, "wide", chip_mates(wide))
        side = wide_at % 2
        even = jnp.where(side == 0, held, other)
        odd = jnp.where(side == 0, other, held)
        for at in range(wide // 4):
            owners += [even[at], odd[at]]
    rows = master.shape[0]
    matrices = []
    for lo, hi in zip(BOUNDS, BOUNDS[1:]):
        pieces = []
        for at in range(lo // rows, -(-hi // rows)):
            pieces.append(owners[at][max(lo - at * rows, 0) : min(hi - at * rows, rows)])
        matrices.append(jnp.concatenate(pieces) if len(pieces) > 1 else pieces[0])
    return matrices


def shards(
    token_ids,
    seq_lengths,
    task_ids,
    labels,
    negatives,
    step_count,
    hidden_master,
    hidden_momentum,
    table_master,
    table_first,
    table_second,
    pos_types,
    pos_first,
    pos_second,
    vectors,
    vec_first,
    vec_second,
):
    wide_at = lax.axis_index("wide")
    narrow_at = lax.axis_index("narrow")
    wide = lax.axis_size("wide")
    narrow = lax.axis_size("narrow")
    count = wide * narrow
    device_at = narrow_at * wide + wide_at
    micro_count, rows_each = token_ids.shape[:2]
    batch = micro_count * rows_each
    tokens = batch * SEQ
    shard = hidden_master.shape[0]
    vocab = table_master.shape[1]
    features = table_master.shape[0] // narrow
    pairs_each = rows_each * SLOTS

    parts = [token_ids, task_ids, labels, negatives]
    sizes = [part.size for part in parts]
    packed = jnp.concatenate([part.reshape(-1) for part in parts])
    packed = jnp.pad(packed, (0, -packed.size % LANES))
    gathered = broadcast_all(packed)
    ends = [sum(sizes[: i + 1]) for i in range(len(sizes))]
    ids_all = gathered[:, : ends[0]]

    def pairs_of(lo, hi, tail):
        block = gathered[:, lo:hi].reshape((count, micro_count, pairs_each) + tail)
        return jnp.moveaxis(block, 1, 0).reshape((micro_count, count * pairs_each) + tail)

    tasks_all = pairs_of(ends[0], ends[1], ())
    labels_all = pairs_of(ends[1], ends[2], ())
    negatives_all = pairs_of(ends[2], ends[3], (NEG,))
    counts = jnp.stack(
        [jnp.sum((tasks_all == 0).astype(full)), jnp.sum((tasks_all == 1).astype(full))]
    )


    group_ids = lax.dynamic_slice_in_dim(ids_all, narrow_at * wide, wide, 0).reshape(-1)
    table_low = table_master.astype(low)
    weights = gather_weights(hidden_master, narrow_at, wide_at, (gathered, table_low))
    pieces = jnp.take(table_low, group_ids, axis=1)
    arrived = lax.all_to_all(pieces, "wide", split_axis=1, concat_axis=0, tiled=True)
    token_rows = arrived.T

    lengths = seq_lengths.reshape(batch, SLOTS)
    member, position, second, segment = jax.vmap(layout)(lengths)
    flat_position = position.reshape(-1)
    flat_second = second.reshape(-1)
    embed = token_rows.astype(full) + pos_types[flat_position]
    embed = embed + jnp.where(flat_second[:, None] == 1, pos_types[SEQ + 1], pos_types[SEQ])
    normed0, scaled0, inverse0 = norm_forward(embed, vectors[0], vectors[1])
    input0 = normed0.astype(low)
    qkv_bias = jnp.concatenate([vectors[6], jnp.zeros_like(vectors[6]), vectors[7]])
    mixed = (project(input0, weights[0].T) + qkv_bias).astype(low)
    context_low, logsum = attend(mixed, segment)
    attended = project(context_low, weights[1].T) + vectors[8]
    normed1, scaled1, inverse1 = norm_forward(normed0 + attended, vectors[2], vectors[3])
    input1 = normed1.astype(low)
    inner = project(input1, weights[2].T) + vectors[14:].reshape(-1)
    cdf = 0.5 * (1.0 + lax.erf(inner * math.sqrt(0.5)))
    active = (inner * cdf).astype(low)
    slope = cdf + inner * (jnp.exp(-0.5 * inner * inner) * (1.0 / math.sqrt(2.0 * math.pi)))
    branch = project(active, weights[3]) + vectors[9]
    normed2, scaled2, inverse2 = norm_forward(normed1 + branch, vectors[4], vectors[5])
    share = member / lengths.astype(full)[:, None, :]
    pooled = jnp.einsum("rps,rpd->rsd", share, normed2.reshape(batch, SEQ, D), precision=highest)
    flat_pooled = pooled.reshape(-1, D)
    heads = vectors[10:14]
    head_out = jnp.dot(flat_pooled, heads.T, precision=highest)

    sent = jnp.pad(head_out.reshape(-1), (0, -head_out.size % LANES))
    head_all = broadcast_all(sent)[:, : head_out.size]
    head_all = head_all.reshape(count, micro_count, pairs_each, 4)
    head_all = jnp.moveaxis(head_all, 1, 0).reshape(micro_count, count * pairs_each, 4)

    def objective(every):
        return task_loss(every[:, :, :3], every[:, :, 3], tasks_all, labels_all, negatives_all, counts)

    loss, pullback = jax.vjp(objective, head_all)
    head_grads = pullback(jnp.ones_like(loss))[0]
    output_grads = lax.dynamic_slice_in_dim(head_grads, device_at * pairs_each, pairs_each, 1)
    output_grads = output_grads.reshape(-1, 4)
    heads_grad = jnp.dot(output_grads.T, flat_pooled, precision=highest)
    pooled_grads = jnp.dot(output_grads, heads, precision=highest).reshape(pooled.shape)

    spread = jnp.einsum("rps,rsd->rpd", share, pooled_grads, precision=highest).reshape(-1, D)
    sum2_grad, gain2, bias2 = norm_backward(spread, scaled2, inverse2, vectors[4])
    branch_grad = sum2_grad.astype(low)
    down_grad = project(active.T, branch_grad)
    simple = wide != 8
    spans_down = [(0, 768), (768, 1920), (1920, 3072)]
    spans_up = [(0, 384), (384, 1536), (1536, 2688), (2688, 3072)]
    spans_front = [(0, 1152), (1152, 2304), (2304, 3072)]

    side = wide_at % 2

    def ready(grad, spans):
        if simple:
            return grad.astype(low)
        grad = by_owner(grad, spans, narrow)
        left, right = grad[:, : D // 2], grad[:, D // 2 :]
        stays = jnp.where(side == 0, left, right)
        leaves = jnp.where(side == 0, right, left)
        return stays, leaves

    def first_stage(grad):
        if simple:
            return grad
        stays, leaves = grad
        comes = lax.ppermute(leaves, "wide", chip_mates(wide))
        chip = (stays.astype(full) + comes.astype(full)).astype(low)
        return lax.psum_scatter(chip, "narrow", scatter_dimension=0, tiled=True)

    down_send, after_down = lax.optimization_barrier((ready(down_grad, spans_down), branch_grad))
    down_part = first_stage(down_send)
    active_grad = project(after_down, weights[3].T)
    inner_grad = (active_grad * slope).astype(low)
    up_grad = project(inner_grad.T, input1)
    up_send, after_up = lax.optimization_barrier((ready(up_grad, spans_up), inner_grad))
    up_part = first_stage(up_send)
    normed1_grad = sum2_grad + project(after_up, weights[2])
    sum1_grad, gain1, bias1 = norm_backward(normed1_grad, scaled1, inverse1, vectors[2])
    attended_grad = sum1_grad.astype(low)
    out_grad = project(attended_grad.T, context_low)
    context_grad = project(attended_grad, weights[1]).astype(low)
    mixed_grad = attend_back(mixed, context_grad, logsum, segment)
    qkv_grad = project(mixed_grad.T, input0)
    front_grad = jnp.concatenate([qkv_grad.astype(low), out_grad.astype(low)])
    front_send, after_front = lax.optimization_barrier((ready(front_grad, spans_front), mixed_grad))
    normed0_grad = sum1_grad + project(after_front, weights[0])
    embed_grad, gain0, bias0 = norm_backward(normed0_grad, scaled0, inverse0, vectors[0])
    mixed_sum = jnp.sum(mixed_grad.astype(full), axis=0)
    small_rows = jnp.stack(
        [
            gain0,
            bias0,
            gain1,
            bias1,
            gain2,
            bias2,
            mixed_sum[:D],
            mixed_sum[2 * D :],
            jnp.sum(attended_grad.astype(full), axis=0),
            jnp.sum(branch_grad.astype(full), axis=0),
        ]
    )
    up_rows = jnp.sum(inner_grad.astype(full), axis=0).reshape(-1, D)

    places = jnp.arange(SEQ, dtype=jnp.int32)[:, None]
    row_hot = jnp.concatenate(
        [
            flat_position[None] == places,
            jnp.stack([flat_second == 0, flat_second == 1]),
        ]
    ).astype(low)
    high_part, low_part = halves(embed_grad)
    pos_grad = project(jnp.concatenate([row_hot, row_hot], axis=1), jnp.concatenate([high_part, low_part]))
    small = jnp.concatenate([pos_grad, small_rows, heads_grad, up_rows])
    small_count = small.shape[0]
    small = jnp.pad(small, ((0, count * features - small_count), (0, 0)))

    table_send = embed_grad.astype(low).T.reshape(wide, narrow, features, tokens)
    table_send = jnp.moveaxis(table_send, 1, 0).reshape(count, features, tokens)
    table_come = lax.all_to_all(table_send, BOTH, split_axis=0, concat_axis=0, tiled=True)
    small_part, small_places = scatter_sum(small)

    front_part = first_stage(front_send)
    joined = jnp.concatenate([front_part, up_part, down_part])
    joined, _ = lax.optimization_barrier((joined, table_send))
    table_come, _, _ = lax.optimization_barrier((table_come, joined, small_part))
    table_part, table_square = collect(ids_all, table_come, vocab)
    if simple:
        hidden_part = lax.psum_scatter(joined, "wide", scatter_dimension=0, tiled=True)
        hidden_part = lax.psum_scatter(hidden_part, "narrow", scatter_dimension=0, tiled=True)
    else:
        owned = lax.psum_scatter(
            joined, "wide", scatter_dimension=0, tiled=True, axis_index_groups=sides(wide)
        )
        owned, _ = lax.optimization_barrier((owned, table_part))
        half = owned.shape[0] // 2
        stays = jnp.where(side == 0, owned[:half], owned[half:])
        leaves = jnp.where(side == 0, owned[half:], owned[:half])
        comes = lax.ppermute(leaves, "wide", chip_mates(wide))
        hidden_part = jnp.concatenate(
            [jnp.where(side == 0, stays, comes), jnp.where(side == 0, comes, stays)], axis=1
        )
    hidden_all = lax.all_gather(hidden_part, "narrow", axis=0, tiled=True)
    table_grad = lax.all_gather(table_part, "narrow", axis=0, tiled=True)
    late_small, _ = lax.optimization_barrier((small_part, table_grad))
    small_all = join_pieces(late_small, small_places)[:small_count]

    hidden_wide = hidden_part.astype(full)
    square = jnp.sum(hidden_wide * hidden_wide) + table_square[0, 0] + jnp.sum(small_part * small_part)
    squares = broadcast_all(jnp.broadcast_to(square, (LANES,)))
    clip_norm = jnp.sqrt(jnp.sum(squares[:, 0]))
    factor = jnp.minimum(1.0, clip_bound / clip_norm)

    start = wide_at * shard
    bounds = jnp.array(BOUNDS, jnp.int32)
    first_matrix = jnp.sum((start >= bounds[1:4]).astype(jnp.int32))
    second_matrix = jnp.sum((start + shard - 1 >= bounds[1:4]).astype(jnp.int32))
    split = jnp.minimum(bounds[first_matrix + 1] - start, shard)
    block = shard // 3
    piece = shard // 12
    at = jnp.arange(12, dtype=jnp.int32)
    if simple:
        source = at
    else:
        lead = split // piece
        each = lead // narrow
        rest = (12 - lead) // narrow
        in_first = at < lead
        inside = jnp.where(in_first, at, at - lead)
        width = jnp.maximum(jnp.where(in_first, each, rest), 1)
        source = (inside // width) * (12 // narrow) + jnp.where(in_first, 0, each) + inside % width
    info = jnp.concatenate([jnp.stack([split, split]), source]).astype(jnp.int32)
    gains = jnp.array([0.2 * math.sqrt(hi - lo) for lo, hi in zip(BOUNDS, BOUNDS[1:])], full)
    moment, grams = moment_and_gram(info, factor[None], hidden_all, hidden_momentum, piece, block)
    chain0, chain1 = chains(grams, wide_at, first_matrix, second_matrix)
    slot_gains = jnp.stack([gains[first_matrix], gains[second_matrix]])
    hidden_new, hidden_copy = apply_chain(info, slot_gains, chain0, chain1, moment, hidden_master, block)

    step = step_count[0].astype(full)
    table_new, table_first_new, table_second_new = adam(
        table_master, factor * table_grad.astype(full), table_first, table_second, step, 0.02
    )
    pos_new, pos_first_new, pos_second_new = adam(
        pos_types, factor * small_all[: SEQ + 2], pos_first, pos_second, step, 0.02
    )
    vectors_new, vec_first_new, vec_second_new = adam(
        vectors, factor * small_all[SEQ + 2 :], vec_first, vec_second, step, 0.2
    )
    return (
        loss,
        clip_norm,
        moment,
        hidden_new,
        hidden_copy,
        table_new,
        table_first_new,
        table_second_new,
        table_new.astype(low),
        pos_new,
        pos_first_new,
        pos_second_new,
        vectors_new,
        vec_first_new,
        vec_second_new,
    )


def solution(mesh):
    rows = P(None, BOTH, None)
    owned = P("wide", None)
    return jax.shard_map(
        shards,
        mesh=mesh,
        in_specs=(rows, rows, rows, rows, P(None, BOTH, None, None), P())
        + (owned,) * 5
        + (P(),) * 6,
        out_specs=(P(), P()) + (owned,) * 7 + (P(),) * 6,
        check_vma=False,
    )
```

```python
from functools import partial
import math

import jax
import jax.numpy as jnp
from jax import lax
from jax.experimental import pallas as pl
from jax.experimental.pallas import tpu as pltpu
from jax.sharding import PartitionSpec as P

D = 768
HEADS = 12
HEAD = 64
FF = 3072
SEQ = 512
SLOTS = 4
NEG = 4
NS_TURNS = 5
LANES = 128
GROUPS = 4
WIDTH = LANES // GROUPS
BLOCK = 256

BOTH = ("narrow", "wide")
highest = lax.Precision.HIGHEST
clip_bound = 0.002
norm_eps = 1e-06
muon_beta = 0.95
muon_rate = 0.1
muon_decay = 0.01
beta_one = 0.9
beta_two = 0.999
adam_eps = 1e-08
adam_decay = 0.01
BOUNDS = (0, 3 * D, 4 * D, 4 * D + FF, 4 * D + 2 * FF)

low = jnp.bfloat16
full = jnp.float32


def dims(left, right):
    return (((left,), (right,)), ((), ()))


def dot32(left, right, left_dim, right_dim):
    return lax.dot_general(left, right, dims(left_dim, right_dim), preferred_element_type=full)


def halves(x):
    high = x.astype(low)
    return high, (x - high.astype(full)).astype(low)


def dot_split(left, right, left_dim=1, right_dim=0):
    (lh, ll), (rh, rl) = left, right
    return dot32(lh, rh, left_dim, right_dim) + (
        dot32(lh, rl, left_dim, right_dim) + dot32(ll, rh, left_dim, right_dim)
    )


def params(mib):
    return pltpu.CompilerParams(vmem_limit_bytes=mib << 20)


def vmem():
    return pl.BlockSpec(memory_space=pltpu.VMEM)


def smem():
    return pl.BlockSpec(memory_space=pltpu.SMEM)


def attend_kernel(mixed_ref, seg_col_ref, seg_row_ref, context_ref, logsum_ref):
    same = seg_col_ref[0] == seg_row_ref[0]

    def pair(step, carry):
        at = pl.multiple_of(step * LANES, LANES)
        queries = mixed_ref[:, pl.ds(at, LANES)]
        keys = mixed_ref[:, pl.ds(D + at, LANES)]
        values = mixed_ref[:, pl.ds(2 * D + at, LANES)]
        outs = []
        for half in range(2):
            cut = slice(half * HEAD, (half + 1) * HEAD)
            raw = dot32(keys[:, cut], queries[:, cut], 1, 1)
            scores = jnp.where(same, raw * (1.0 / math.sqrt(HEAD)), -1e30)
            peak = jnp.max(scores, axis=0, keepdims=True)
            lifted = jnp.exp(scores - peak)
            total = jnp.sum(lifted, axis=0, keepdims=True)
            probs = (lifted * (1.0 / total)).astype(low)
            outs.append(dot32(values[:, cut], probs, 0, 0))
            logsum_ref[0, pl.ds(2 * step + half, 1), :] = peak + jnp.log(total)
        context_ref[:, pl.ds(at, LANES)] = jnp.concatenate(outs, axis=0).T.astype(low)
        return carry

    lax.fori_loop(0, HEADS // 2, pair, 0)


def attend(mixed, segment):
    rows = segment.shape[0]
    return pl.pallas_call(
        attend_kernel,
        grid=(rows,),
        in_specs=[
            pl.BlockSpec((SEQ, 3 * D), lambda b: (b, 0)),
            pl.BlockSpec((1, SEQ, 1), lambda b: (b, 0, 0)),
            pl.BlockSpec((1, 1, SEQ), lambda b: (b, 0, 0)),
        ],
        out_specs=[
            pl.BlockSpec((SEQ, D), lambda b: (b, 0)),
            pl.BlockSpec((1, 16, SEQ), lambda b: (b, 0, 0)),
        ],
        out_shape=[
            jax.ShapeDtypeStruct((rows * SEQ, D), low),
            jax.ShapeDtypeStruct((rows, 16, SEQ), full),
        ],
        compiler_params=params(48),
        name="attend",
    )(mixed, segment[:, :, None], segment[:, None, :])


def attend_back_kernel(mixed_ref, grad_ref, logsum_ref, seg_col_ref, seg_row_ref, out_ref):
    same = seg_col_ref[0] == seg_row_ref[0]
    scale = 1.0 / math.sqrt(HEAD)

    def pair(step, carry):
        at = pl.multiple_of(step * LANES, LANES)
        queries = mixed_ref[:, pl.ds(at, LANES)]
        keys = mixed_ref[:, pl.ds(D + at, LANES)]
        values = mixed_ref[:, pl.ds(2 * D + at, LANES)]
        upstream = grad_ref[:, pl.ds(at, LANES)]
        query_grads, key_grads, value_grads = [], [], []
        for half in range(2):
            cut = slice(half * HEAD, (half + 1) * HEAD)
            logsum = logsum_ref[0, pl.ds(2 * step + half, 1), :]
            raw = dot32(keys[:, cut], queries[:, cut], 1, 1)
            probs = jnp.exp(jnp.where(same, raw * scale, -1e30) - logsum)
            prob_grads = dot32(values[:, cut], upstream[:, cut], 1, 1)
            value_grads.append(dot32(probs.astype(low), upstream[:, cut], 1, 0))
            moved = jnp.sum(prob_grads * probs, axis=0, keepdims=True)
            back = (probs * (prob_grads - moved) * scale).astype(low)
            key_grads.append(dot32(back, queries[:, cut], 1, 0))
            query_grads.append(dot32(keys[:, cut], back, 0, 0))
        out_ref[:, pl.ds(at, LANES)] = jnp.concatenate(query_grads, axis=0).T.astype(low)
        out_ref[:, pl.ds(D + at, LANES)] = jnp.concatenate(key_grads, axis=1).astype(low)
        out_ref[:, pl.ds(2 * D + at, LANES)] = jnp.concatenate(value_grads, axis=1).astype(low)
        return carry

    lax.fori_loop(0, HEADS // 2, pair, 0)


def attend_back(mixed, context_grad, logsum, segment):
    rows = segment.shape[0]
    return pl.pallas_call(
        attend_back_kernel,
        grid=(rows,),
        in_specs=[
            pl.BlockSpec((SEQ, 3 * D), lambda b: (b, 0)),
            pl.BlockSpec((SEQ, D), lambda b: (b, 0)),
            pl.BlockSpec((1, 16, SEQ), lambda b: (b, 0, 0)),
            pl.BlockSpec((1, SEQ, 1), lambda b: (b, 0, 0)),
            pl.BlockSpec((1, 1, SEQ), lambda b: (b, 0, 0)),
        ],
        out_specs=pl.BlockSpec((SEQ, 3 * D), lambda b: (b, 0)),
        out_shape=jax.ShapeDtypeStruct((rows * SEQ, 3 * D), low),
        compiler_params=params(56),
        name="attend_back",
    )(mixed, context_grad, logsum, segment[:, :, None], segment[:, None, :])


def collect_kernel(place_ref, ids_ref, grads_ref, out_ref, square_ref, *scratch,
                   span, tokens, features, vocab):
    sums, rows_ref = scratch[:-1], scratch[-1]
    step = pl.program_id(0)
    last = pl.num_programs(0) - 1
    streams = len(sums)
    batch = 4 * streams

    @pl.when(step == 0)
    def _():
        for total in sums:
            total[...] = jnp.zeros_like(total)

    group = ids_ref[0] // span
    grads = grads_ref[0].astype(full)
    pad = jnp.zeros((WIDTH - features, tokens), full)
    pieces = []
    for at in range(GROUPS):
        pieces += [jnp.where(group == at, grads, 0.0), pad]
    rows_ref[...] = jnp.concatenate(pieces, axis=0).T

    def body(i, carry):
        for base in range(0, batch, streams):
            at = i * batch + base
            places = [pl.ds(place_ref[0, 0, at + k], 1) for k in range(streams)]
            olds = [sums[k][places[k], :] for k in range(streams)]
            news = [rows_ref[pl.ds(at + k, 1), :] for k in range(streams)]
            for k in range(streams):
                sums[k][places[k], :] = olds[k] + news[k]
        return carry

    lax.fori_loop(0, tokens // batch, body, 0)

    @pl.when(step == last)
    def _():
        def flush(b, total):
            at = pl.multiple_of(b * LANES, LANES)
            block = sums[0][pl.ds(at, LANES), :]
            for k in range(1, streams):
                block += sums[k][pl.ds(at, LANES), :]
            turned = block.T
            for g in range(GROUPS):
                piece = turned[g * WIDTH:g * WIDTH + features]

                @pl.when(g * span + at < vocab)
                def _():
                    out_ref[:, pl.ds(pl.multiple_of(g * span + at, LANES), LANES)] = piece.astype(low)

            return total + block * block

        total = lax.fori_loop(0, span // LANES, flush, jnp.zeros((LANES, LANES), full))
        square_ref[...] = jnp.broadcast_to(jnp.sum(total, keepdims=True), square_ref.shape)


def collect(ids, grads, vocab, tokens):
    sources, features = grads.shape[:2]
    span = -(-vocab // (GROUPS * LANES)) * LANES
    return pl.pallas_call(
        partial(collect_kernel, span=span, tokens=tokens, features=features, vocab=vocab),
        grid=(sources,),
        in_specs=[
            pl.BlockSpec((1, 1, tokens), lambda s: (s, 0, 0), memory_space=pltpu.SMEM),
            pl.BlockSpec((1, 1, tokens), lambda s: (s, 0, 0)),
            pl.BlockSpec((1, features, tokens), lambda s: (s, 0, 0)),
        ],
        out_specs=[
            pl.BlockSpec((features, vocab), lambda s: (0, 0)),
            pl.BlockSpec((8, LANES), lambda s: (0, 0)),
        ],
        out_shape=[
            jax.ShapeDtypeStruct((features, vocab), low),
            jax.ShapeDtypeStruct((8, LANES), full),
        ],
        scratch_shapes=[pltpu.VMEM((span, LANES), full)] * 8 + [pltpu.VMEM((tokens, LANES), full)],
        compiler_params=params(56),
        name="collect",
    )((ids % span)[:, None, :], ids[:, None, :], grads)


def moment_kernel(info_ref, factor_ref, grad_ref, old_ref, moment_ref, gram_ref, *, piece, block):
    factor = factor_ref[0]
    for at in range(old_ref.shape[0] // piece):
        source = pl.multiple_of(info_ref[2 + at] * piece, piece)
        rows = slice(at * piece, (at + 1) * piece)
        moment_ref[rows] = muon_beta * old_ref[rows] + factor * grad_ref[pl.ds(source, piece)].astype(full)
    gram_ref[...] = jnp.zeros_like(gram_ref)

    def body(b, carry):
        slot = (b * block >= info_ref[0]).astype(jnp.int32)
        rows = halves(moment_ref[pl.ds(pl.multiple_of(b * block, block), block)])
        gram_ref[slot] += dot_split(rows, rows, 0, 0)
        return carry

    lax.fori_loop(0, old_ref.shape[0] // block, body, 0)


def moment_and_gram(info, factor, grad, old, piece, block):
    return pl.pallas_call(
        partial(moment_kernel, piece=piece, block=block),
        in_specs=[smem(), smem(), vmem(), vmem(), vmem()][:4],
        out_specs=[vmem(), vmem()],
        out_shape=[
            jax.ShapeDtypeStruct(old.shape, full),
            jax.ShapeDtypeStruct((2, D, D), full),
        ],
        compiler_params=params(56),
        name="moment",
    )(info, factor, grad, old)


def even_product(left, right, put):
    (lh, ll), (rh, rl) = left, right
    for i in range(D // BLOCK):
        rows = slice(i * BLOCK, (i + 1) * BLOCK)
        panel = jnp.concatenate([lh[rows], lh[rows], ll[rows]], axis=1)
        for j in range(i, D // BLOCK):
            cols = slice(j * BLOCK, (j + 1) * BLOCK)
            other = jnp.concatenate([rh[:, cols], rl[:, cols], rh[:, cols]], axis=0)
            put(rows, cols, dot32(panel, other, 1, 0))


def keep(pair):
    def put(rows, cols, value):
        pair[0][rows, cols], pair[1][rows, cols] = halves(value)
        if rows != cols:
            pair[0][cols, rows], pair[1][cols, rows] = halves(value.T)

    return put


def chain_kernel(gram_ref, out_ref, a_ref, *parts):
    a, q, p, t = [parts[2 * i:2 * i + 2] for i in range(4)]

    def diagonal(size):
        shape = (size, size)
        return lax.broadcasted_iota(jnp.int32, shape, 0) == lax.broadcasted_iota(jnp.int32, shape, 1)

    gram = gram_ref[...]
    scale = jnp.sqrt(jnp.sum(jnp.where(diagonal(D), gram, 0.0))) + 1e-07
    a_ref[...] = gram * (1.0 / (scale * scale))
    a[0][...], a[1][...] = halves(a_ref[...])
    once = diagonal(BLOCK)

    def put_q(rows, cols, value):
        new = 2.0315 * value - 4.775 * a_ref[rows, cols]
        keep(q)(rows, cols, new + jnp.where(once, 3.4445, 0.0) if rows == cols else new)

    def put_a(rows, cols, value):
        a_ref[rows, cols] = value
        keep(a)(rows, cols, value)

    def put_out(rows, cols, value):
        value = value * (1.0 / scale)
        out_ref[rows, cols] = value
        if rows != cols:
            out_ref[cols, rows] = value.T

    def turn(k, carry):
        even_product(a, a, put_q)

        @pl.when(k == 0)
        def _():
            p[0][...], p[1][...] = q[0][...], q[1][...]

        @pl.when((k > 0) & (k < NS_TURNS - 1))
        def _():
            even_product(p, q, keep(t))
            p[0][...], p[1][...] = t[0][...], t[1][...]

        @pl.when(k == NS_TURNS - 1)
        def _():
            even_product(p, q, put_out)

        @pl.when(k < NS_TURNS - 1)
        def _():
            even_product(a, q, keep(t))
            even_product(t, q, put_a)

        return carry

    lax.fori_loop(0, NS_TURNS, turn, 0)


def chain(gram):
    return pl.pallas_call(
        chain_kernel,
        in_specs=[vmem()],
        out_specs=vmem(),
        out_shape=jax.ShapeDtypeStruct((D, D), full),
        scratch_shapes=[pltpu.VMEM((D, D), full)] + [pltpu.VMEM((D, D), low)] * 8,
        compiler_params=params(40),
        name="chain",
    )(gram)


def apply_kernel(info_ref, gain_ref, first_ref, second_ref, moment_ref, master_ref, new_ref, copy_ref,
                 *, block):
    split = info_ref[0] // block

    def over(slot, p_ref, start, stop):
        p = halves(p_ref[...])
        gain = gain_ref[slot] * muon_rate

        def body(b, carry):
            rows = pl.ds(pl.multiple_of(b * block, block), block)
            ortho = dot_split(halves(moment_ref[rows]), p)
            new = master_ref[rows] * (1.0 - muon_rate * muon_decay) - gain * ortho
            new_ref[rows] = new
            copy_ref[rows] = new.astype(low)
            return carry

        lax.fori_loop(start, stop, body, 0)

    over(0, first_ref, 0, split)
    total = moment_ref.shape[0] // block

    @pl.when(split < total)
    def _():
        over(1, second_ref, split, total)


def apply_chain(info, gains, first, second, moment, master, block):
    return pl.pallas_call(
        partial(apply_kernel, block=block),
        in_specs=[smem(), smem(), vmem(), vmem(), vmem(), vmem()],
        out_specs=[vmem(), vmem()],
        out_shape=[
            jax.ShapeDtypeStruct(moment.shape, full),
            jax.ShapeDtypeStruct(moment.shape, low),
        ],
        compiler_params=params(48),
        name="apply",
    )(info, gains, first, second, moment, master)


def chains(grams, wide_at, first_matrix, second_matrix, rider):
    wide = lax.axis_size("wide")
    if wide != 8:
        which = jnp.arange(4)
        slots = (which == first_matrix).astype(full)[:, None, None] * grams[0]
        slots = slots + (which == second_matrix).astype(full)[:, None, None] * grams[1]
        total = lax.psum(slots, "wide")
        return (
            chain(lax.dynamic_index_in_dim(total, first_matrix, 0, keepdims=False)),
            chain(lax.dynamic_index_in_dim(total, second_matrix, 0, keepdims=False)),
            rider,
        )
    half = D // 2
    gram0, gram1 = grams[0], grams[1]
    pairs = [(i, i ^ 1) for i in range(8)]
    lower = wide_at % 2 == 0
    mine = jnp.where(wide_at == 2, gram1, gram0)
    moved = lax.ppermute(gram1[:half], "wide", [(5, 4)])
    chip = mine + lax.ppermute(mine, "wide", pairs)
    up_send = jnp.where(lower, chip[:half], chip[half:])
    down_send = jnp.where(wide_at == 4, moved, jnp.where(wide_at == 5, gram1[half:], up_send))
    up = up_send + lax.ppermute(up_send, "wide", [(2, 4), (4, 2), (3, 5), (5, 3)])
    down = down_send + lax.ppermute(down_send, "wide", [(4, 6), (6, 4), (5, 7), (7, 5)])
    send = jnp.where((wide_at == 4), down, up)
    send = jnp.where(wide_at >= 6, down, send)
    swap = lax.ppermute(send, "wide", [(2, 3), (4, 5), (6, 7), (7, 6)])
    back = lax.ppermute(up, "wide", [(5, 4)])
    kept = jnp.where(wide_at >= 5, down, up)
    other = jnp.where(wide_at == 4, back, swap)
    whole = jnp.concatenate([jnp.where(lower, kept, other), jnp.where(lower, other, kept)])
    gram = jnp.where(wide_at < 2, chip, jnp.where(wide_at == 2, gram0, whole))
    gram, rider = lax.optimization_barrier((gram, rider))
    own = chain(gram)
    come = lax.ppermute(own, "wide", [(3, 2), (4, 5)])
    return jnp.where(wide_at == 5, come, own), jnp.where(wide_at == 5, own, come), rider


def layout(lengths):
    row_ends = jnp.cumsum(lengths)
    starts = row_ends - lengths
    places = jnp.arange(SEQ, dtype=jnp.int32)
    segment = jnp.sum((places[:, None] >= row_ends[None, :]).astype(jnp.int32), axis=1)
    chosen = segment[:, None] == jnp.arange(SLOTS, dtype=jnp.int32)[None, :]
    start_at = jnp.sum(jnp.where(chosen, starts[None, :], 0), axis=1)
    length_at = jnp.sum(jnp.where(chosen, lengths[None, :], 0), axis=1)
    position = places - start_at
    second = (2 * position >= length_at).astype(jnp.int32)
    return (chosen.astype(full), position, second, segment)


def norm_forward(hidden, gain, bias):
    center = hidden - jnp.mean(hidden, axis=-1, keepdims=True)
    inverse = lax.rsqrt(jnp.mean(center * center, axis=-1, keepdims=True) + norm_eps)
    scaled = center * inverse
    return (scaled * gain + bias, scaled, inverse)


def norm_backward(upstream, scaled, inverse, gain):
    weighted = upstream * gain
    back = inverse * (
        weighted
        - jnp.mean(weighted, axis=-1, keepdims=True)
        - scaled * jnp.mean(weighted * scaled, axis=-1, keepdims=True)
    )
    return (back, jnp.sum(upstream * scaled, axis=0), jnp.sum(upstream, axis=0))


def project(left, right):
    return jnp.dot(left, right, preferred_element_type=full)


def task_loss(logits, scores, tasks, labels, negatives, counts):
    logprob = jax.nn.log_softmax(logits, axis=-1)
    picked = jnp.sum(
        jnp.where(labels[:, :, None] == jnp.arange(3, dtype=jnp.int32), logprob, 0.0), axis=2
    )
    chosen = negatives[:, :, :, None] == jnp.arange(scores.shape[1], dtype=jnp.int32)
    rivals = jnp.sum(jnp.where(chosen, scores[:, None, None, :], 0.0), axis=3)
    together = jnp.concatenate([scores[:, :, None], rivals], axis=2)
    ranking = jax.nn.logsumexp(together, axis=2) - scores
    first_part = jnp.sum(jnp.where(tasks == 0, -picked, 0.0)) / counts[0]
    return first_part + jnp.sum(jnp.where(tasks == 1, ranking, 0.0)) / counts[1]


def adam(weight, grad, first, second, step, rate):
    first = beta_one * first + (1.0 - beta_one) * grad
    second = beta_two * second + (1.0 - beta_two) * grad * grad
    unbiased = first / (1.0 - beta_one**step)
    spread = second / (1.0 - beta_two**step)
    return (
        weight - rate * (unbiased / (jnp.sqrt(spread) + adam_eps) + adam_decay * weight),
        first,
        second,
    )


def broadcast_all(x):
    count = lax.axis_size("narrow") * lax.axis_size("wide")
    return lax.all_to_all(
        jnp.broadcast_to(x[None], (count,) + x.shape), BOTH, split_axis=0, concat_axis=0, tiled=True
    )


def sides(wide):
    return [list(range(0, wide, 2)), list(range(1, wide, 2))]


def chip_mates(wide):
    return [(i, i ^ 1) for i in range(wide)]


def by_owner(grad, spans, parts):
    pieces = [
        grad[lo:hi].reshape(parts, (hi - lo) // parts, D) for lo, hi in spans
    ]
    return jnp.concatenate(pieces, axis=1).reshape(-1, D).astype(low)


def gather_weights(master, narrow_at, wide_at, first):
    wide = lax.axis_size("wide")
    if wide != 8:
        whole = lax.all_gather(master.astype(low), "wide", axis=0, tiled=True)
        return first, list(whole.reshape(wide, -1, D))
    share = master.shape[0] // lax.axis_size("narrow")
    mine = lax.dynamic_slice_in_dim(master, narrow_at * share, share, 0).astype(low)
    near = lax.all_gather(mine, "wide", axis=0, tiled=False, axis_index_groups=sides(wide))
    near, first = lax.optimization_barrier((near, first))
    return first, [
        lax.all_gather(part, "narrow", axis=1, tiled=True)
        for part in (near[: wide // 4], near[wide // 4 :])
    ]


def both_cores(held, wide_at):
    owners = []
    other = lax.ppermute(held, "wide", chip_mates(lax.axis_size("wide")))
    side = wide_at % 2
    even = jnp.where(side == 0, held, other)
    odd = jnp.where(side == 0, other, held)
    for at in range(held.shape[0]):
        owners += [even[at], odd[at]]
    return owners


def rows_of(owners, matrix):
    rows = owners[0].shape[0]
    lo, hi = BOUNDS[matrix], BOUNDS[matrix + 1]
    pieces = []
    for at in range(lo // rows, -(-hi // rows)):
        pieces.append(owners[at][max(lo - at * rows, 0) : min(hi - at * rows, rows)])
    return jnp.concatenate(pieces) if len(pieces) > 1 else pieces[0]


def shards(
    token_ids,
    seq_lengths,
    task_ids,
    labels,
    negatives,
    step_count,
    hidden_master,
    hidden_momentum,
    table_master,
    table_first,
    table_second,
    pos_types,
    pos_first,
    pos_second,
    vectors,
    vec_first,
    vec_second,
):
    wide_at = lax.axis_index("wide")
    narrow_at = lax.axis_index("narrow")
    wide = lax.axis_size("wide")
    narrow = lax.axis_size("narrow")
    count = wide * narrow
    device_at = narrow_at * wide + wide_at
    micro_count, rows_each = token_ids.shape[:2]
    batch = micro_count * rows_each
    tokens = batch * SEQ
    shard = hidden_master.shape[0]
    vocab = table_master.shape[1]
    features = table_master.shape[0] // narrow
    pairs_each = rows_each * SLOTS

    parts = [token_ids, task_ids, labels, negatives]
    sizes = [part.size for part in parts]
    packed = jnp.concatenate([part.reshape(-1) for part in parts])
    packed = jnp.pad(packed, (0, -packed.size % LANES))
    gathered = broadcast_all(packed)
    ends = [sum(sizes[: i + 1]) for i in range(len(sizes))]
    ids_all = gathered[:, : ends[0]]

    def pairs_of(lo, hi, tail):
        block = gathered[:, lo:hi].reshape((count, micro_count, pairs_each) + tail)
        return jnp.moveaxis(block, 1, 0).reshape((micro_count, count * pairs_each) + tail)

    tasks_all = pairs_of(ends[0], ends[1], ())
    labels_all = pairs_of(ends[1], ends[2], ())
    negatives_all = pairs_of(ends[2], ends[3], (NEG,))
    counts = jnp.stack(
        [jnp.sum((tasks_all == 0).astype(full)), jnp.sum((tasks_all == 1).astype(full))]
    )


    group_ids = lax.dynamic_slice_in_dim(ids_all, narrow_at * wide, wide, 0).reshape(-1)
    table_low = table_master.astype(low)
    pieces = jnp.take(table_low, group_ids, axis=1)
    pieces, gathers = gather_weights(hidden_master, narrow_at, wide_at, pieces)
    simple = wide != 8
    owners = gathers if simple else both_cores(gathers[0], wide_at)
    arrived = lax.all_to_all(pieces, "wide", split_axis=1, concat_axis=0, tiled=True)
    token_rows = arrived.T

    lengths = seq_lengths.reshape(batch, SLOTS)
    member, position, second, segment = jax.vmap(layout)(lengths)
    flat_position = position.reshape(-1)
    flat_second = second.reshape(-1)
    embed = token_rows.astype(full) + pos_types[flat_position]
    embed = embed + jnp.where(flat_second[:, None] == 1, pos_types[SEQ + 1], pos_types[SEQ])
    normed0, scaled0, inverse0 = norm_forward(embed, vectors[0], vectors[1])
    input0 = normed0.astype(low)
    qkv_bias = jnp.concatenate([vectors[6], jnp.zeros_like(vectors[6]), vectors[7]])
    weight_qkv, weight_out = rows_of(owners, 0), rows_of(owners, 1)
    mixed = (project(input0, weight_qkv.T) + qkv_bias).astype(low)
    if not simple:
        rest, mixed = lax.optimization_barrier((gathers[1], mixed))
        owners = owners + both_cores(rest, wide_at)
    weight_up, weight_down = rows_of(owners, 2), rows_of(owners, 3)
    context_low, logsum = attend(mixed, segment)
    attended = project(context_low, weight_out.T) + vectors[8]
    normed1, scaled1, inverse1 = norm_forward(normed0 + attended, vectors[2], vectors[3])
    input1 = normed1.astype(low)
    inner = project(input1, weight_up.T) + vectors[14:].reshape(-1)
    cdf = 0.5 * (1.0 + lax.erf(inner * math.sqrt(0.5)))
    active = (inner * cdf).astype(low)
    slope = cdf + inner * (jnp.exp(-0.5 * inner * inner) * (1.0 / math.sqrt(2.0 * math.pi)))
    branch = project(active, weight_down) + vectors[9]
    normed2, scaled2, inverse2 = norm_forward(normed1 + branch, vectors[4], vectors[5])
    share = member / lengths.astype(full)[:, None, :]
    pooled = jnp.einsum("rps,rpd->rsd", share, normed2.reshape(batch, SEQ, D), precision=highest)
    flat_pooled = pooled.reshape(-1, D)
    heads = vectors[10:14]
    head_out = jnp.dot(flat_pooled, heads.T, precision=highest)

    sent = jnp.pad(head_out.reshape(-1), (0, -head_out.size % LANES))
    head_all = broadcast_all(sent)[:, : head_out.size]
    head_all = head_all.reshape(count, micro_count, pairs_each, 4)
    head_all = jnp.moveaxis(head_all, 1, 0).reshape(micro_count, count * pairs_each, 4)

    def objective(every):
        return task_loss(every[:, :, :3], every[:, :, 3], tasks_all, labels_all, negatives_all, counts)

    loss, pullback = jax.vjp(objective, head_all)
    head_grads = pullback(jnp.ones_like(loss))[0]
    output_grads = lax.dynamic_slice_in_dim(head_grads, device_at * pairs_each, pairs_each, 1)
    output_grads = output_grads.reshape(-1, 4)
    heads_grad = jnp.dot(output_grads.T, flat_pooled, precision=highest)
    pooled_grads = jnp.dot(output_grads, heads, precision=highest).reshape(pooled.shape)

    spread = jnp.einsum("rps,rsd->rpd", share, pooled_grads, precision=highest).reshape(-1, D)
    sum2_grad, gain2, bias2 = norm_backward(spread, scaled2, inverse2, vectors[4])
    branch_grad = sum2_grad.astype(low)
    down_grad = project(active.T, branch_grad)
    spans_down = [(0, 768), (768, 1920), (1920, 3072)]
    spans_up = [(0, 384), (384, 1536), (1536, 2688), (2688, 3072)]
    spans_front = [(0, 1152), (1152, 2304), (2304, 3072)]

    side = wide_at % 2

    def ready(grad, spans):
        if simple:
            return grad.astype(low)
        grad = by_owner(grad, spans, narrow)
        left, right = grad[:, : D // 2], grad[:, D // 2 :]
        stays = jnp.where(side == 0, left, right)
        leaves = jnp.where(side == 0, right, left)
        return stays, leaves

    def between_cores(grad):
        if simple:
            return grad
        stays, leaves = grad
        return stays, lax.ppermute(leaves, "wide", chip_mates(wide))

    def slices(grad):
        if simple:
            return [grad]
        stays, comes = grad
        chip = (stays.astype(full) + comes.astype(full)).astype(low).reshape(narrow, -1, D // 2)
        return [chip[narrow_at ^ turn] for turn in range(narrow)]

    def over_narrow(parts):
        return parts[:1] + [
            lax.ppermute(part, "narrow", [(i, i ^ (turn + 1)) for i in range(narrow)])
            for turn, part in enumerate(parts[1:])
        ]

    together = lax.optimization_barrier
    down_send, after_down = together((ready(down_grad, spans_down), branch_grad))
    down_pair = between_cores(down_send)
    active_grad = project(after_down, weight_down.T)
    inner_grad = (active_grad * slope).astype(low)
    up_grad = project(inner_grad.T, input1)
    up_send, down_pair, after_up = together((ready(up_grad, spans_up), down_pair, inner_grad))
    up_pair = between_cores(up_send)
    down_cut, after_up = together((slices(down_pair), after_up))
    down_part = over_narrow(down_cut)
    normed1_grad = sum2_grad + project(after_up, weight_up)
    sum1_grad, gain1, bias1 = norm_backward(normed1_grad, scaled1, inverse1, vectors[2])
    attended_grad = sum1_grad.astype(low)
    up_pair, attended_grad = together((up_pair, attended_grad))
    out_grad = project(attended_grad.T, context_low)
    context_grad = project(attended_grad, weight_out).astype(low)
    up_cut, context_grad = together((slices(up_pair), context_grad))
    up_part = over_narrow(up_cut)
    mixed_grad = attend_back(mixed, context_grad, logsum, segment)
    qkv_grad = project(mixed_grad.T, input0)
    front_grad = jnp.concatenate([qkv_grad.astype(low), out_grad.astype(low)])
    front_send, down_part, after_front = together(
        (ready(front_grad, spans_front), down_part, mixed_grad)
    )
    front_pair = between_cores(front_send)
    normed0_grad = sum1_grad + project(after_front, weight_qkv)
    embed_grad, gain0, bias0 = norm_backward(normed0_grad, scaled0, inverse0, vectors[0])
    mixed_sum = jnp.sum(mixed_grad.astype(full), axis=0)
    small_rows = jnp.stack(
        [
            gain0,
            bias0,
            gain1,
            bias1,
            gain2,
            bias2,
            mixed_sum[:D],
            mixed_sum[2 * D :],
            jnp.sum(attended_grad.astype(full), axis=0),
            jnp.sum(branch_grad.astype(full), axis=0),
        ]
    )
    up_rows = jnp.sum(inner_grad.astype(full), axis=0).reshape(-1, D)

    places = jnp.arange(SEQ, dtype=jnp.int32)[:, None]
    row_hot = jnp.concatenate(
        [
            flat_position[None] == places,
            jnp.stack([flat_second == 0, flat_second == 1]),
        ]
    ).astype(low)
    high_part, low_part = halves(embed_grad)
    pos_grad = project(jnp.concatenate([row_hot, row_hot], axis=1), jnp.concatenate([high_part, low_part]))
    small = jnp.concatenate([pos_grad, small_rows, heads_grad, up_rows])
    small_count = small.shape[0]
    small = jnp.pad(small, ((0, count * features - small_count), (0, 0)))

    embed_low, front_pair = together((embed_grad.astype(low), front_pair))
    front_part = over_narrow(slices(front_pair))
    table_send = embed_low.T.reshape(wide, narrow, features, tokens)
    table_send = jnp.moveaxis(table_send, 1, 0).reshape(count, features, tokens)
    small_send = small.astype(low).reshape(count, features, D)
    come = lax.all_to_all(
        jnp.concatenate([table_send, small_send], axis=2), BOTH, split_axis=0, concat_axis=0, tiled=True
    )

    def added(parts):
        return sum(part.astype(full) for part in parts).astype(low)

    joined = jnp.concatenate([added(front_part), added(up_part), added(down_part)])
    joined, come = together((joined, come))
    small_part = jnp.sum(come[:, :, tokens:].astype(full), axis=0)
    table_part, table_square = collect(ids_all, come, vocab, tokens)
    if simple:
        hidden_part = lax.psum_scatter(joined, "wide", scatter_dimension=0, tiled=True)
        hidden_part = lax.psum_scatter(hidden_part, "narrow", scatter_dimension=0, tiled=True)
    else:
        owned = lax.psum_scatter(
            joined, "wide", scatter_dimension=0, tiled=True, axis_index_groups=sides(wide)
        )
        owned, table_square = together((owned, table_square))
        half = owned.shape[0] // 2
        stays = jnp.where(side == 0, owned[:half], owned[half:])
        leaves = jnp.where(side == 0, owned[half:], owned[:half])
        comes = lax.ppermute(leaves, "wide", chip_mates(wide))
        hidden_part = jnp.concatenate(
            [jnp.where(side == 0, stays, comes), jnp.where(side == 0, comes, stays)], axis=1
        )
    if simple:
        hidden_all = lax.all_gather(hidden_part, "narrow", axis=0, tiled=True)
    else:
        hidden_all = jnp.concatenate(
            [hidden_part]
            + [
                lax.ppermute(hidden_part, "narrow", [(i, i ^ turn) for i in range(narrow)])
                for turn in range(1, narrow)
            ]
        )
    table_grad = lax.all_gather(table_part, "narrow", axis=0, tiled=True)

    hidden_wide = hidden_part.astype(full)
    square = jnp.sum(hidden_wide * hidden_wide) + table_square[0, 0] + jnp.sum(small_part * small_part)
    squares = broadcast_all(jnp.broadcast_to(square, (LANES,)))
    clip_norm = jnp.sqrt(jnp.sum(squares[:, 0]))
    factor = jnp.minimum(1.0, clip_bound / clip_norm)

    start = wide_at * shard
    bounds = jnp.array(BOUNDS, jnp.int32)
    first_matrix = jnp.sum((start >= bounds[1:4]).astype(jnp.int32))
    second_matrix = jnp.sum((start + shard - 1 >= bounds[1:4]).astype(jnp.int32))
    split = jnp.minimum(bounds[first_matrix + 1] - start, shard)
    block = shard // 3
    piece = shard // 12
    at = jnp.arange(12, dtype=jnp.int32)
    if simple:
        source = at
    else:
        lead = split // piece
        each = lead // narrow
        rest = (12 - lead) // narrow
        in_first = at < lead
        inside = jnp.where(in_first, at, at - lead)
        width = jnp.maximum(jnp.where(in_first, each, rest), 1)
        origin = (inside // width) ^ narrow_at
        source = origin * (12 // narrow) + jnp.where(in_first, 0, each) + inside % width
    info = jnp.concatenate([jnp.stack([split, split]), source]).astype(jnp.int32)
    gains = jnp.array([0.2 * math.sqrt(hi - lo) for lo, hi in zip(BOUNDS, BOUNDS[1:])], full)
    moment, grams = moment_and_gram(info, factor[None], hidden_all, hidden_momentum, piece, block)
    chain0, chain1, late_small = chains(grams, wide_at, first_matrix, second_matrix, small_part)
    small_all = lax.all_gather(late_small, BOTH, axis=0, tiled=True)[:small_count]
    slot_gains = jnp.stack([gains[first_matrix], gains[second_matrix]])
    hidden_new, hidden_copy = apply_chain(info, slot_gains, chain0, chain1, moment, hidden_master, block)

    step = step_count[0].astype(full)
    table_new, table_first_new, table_second_new = adam(
        table_master, factor * table_grad.astype(full), table_first, table_second, step, 0.02
    )
    pos_new, pos_first_new, pos_second_new = adam(
        pos_types, factor * small_all[: SEQ + 2], pos_first, pos_second, step, 0.02
    )
    vectors_new, vec_first_new, vec_second_new = adam(
        vectors, factor * small_all[SEQ + 2 :], vec_first, vec_second, step, 0.2
    )
    return (
        loss,
        clip_norm,
        moment,
        hidden_new,
        hidden_copy,
        table_new,
        table_first_new,
        table_second_new,
        table_new.astype(low),
        pos_new,
        pos_first_new,
        pos_second_new,
        vectors_new,
        vec_first_new,
        vec_second_new,
    )


def solution(mesh):
    rows = P(None, BOTH, None)
    owned = P("wide", None)
    return jax.shard_map(
        shards,
        mesh=mesh,
        in_specs=(rows, rows, rows, rows, P(None, BOTH, None, None), P())
        + (owned,) * 5
        + (P(),) * 6,
        out_specs=(P(), P()) + (owned,) * 7 + (P(),) * 6,
        check_vma=False,
    )
```

```python
from functools import partial
import math

import jax
import jax.numpy as jnp
from jax import lax
from jax.experimental import pallas as pl
from jax.experimental.pallas import tpu as pltpu
from jax.sharding import PartitionSpec as P

D = 768
HEADS = 12
HEAD = 64
FF = 3072
SEQ = 512
SLOTS = 4
NEG = 4
NS_TURNS = 5
LANES = 128
GROUPS = 4
WIDTH = LANES // GROUPS
BLOCK = 256
TILES = [(i, j) for i in range(D // BLOCK) for j in range(i, D // BLOCK)]

BOTH = ("narrow", "wide")
highest = lax.Precision.HIGHEST
clip_bound = 0.002
norm_eps = 1e-06
muon_beta = 0.95
muon_rate = 0.1
muon_decay = 0.01
beta_one = 0.9
beta_two = 0.999
adam_eps = 1e-08
adam_decay = 0.01
BOUNDS = (0, 3 * D, 4 * D, 4 * D + FF, 4 * D + 2 * FF)

low = jnp.bfloat16
full = jnp.float32


def dims(left, right):
    return (((left,), (right,)), ((), ()))


def dot32(left, right, left_dim, right_dim):
    return lax.dot_general(left, right, dims(left_dim, right_dim), preferred_element_type=full)


def halves(x):
    high = x.astype(low)
    return high, (x - high.astype(full)).astype(low)


def dot_split(left, right, left_dim=1, right_dim=0):
    (lh, ll), (rh, rl) = left, right
    return dot32(lh, rh, left_dim, right_dim) + (
        dot32(lh, rl, left_dim, right_dim) + dot32(ll, rh, left_dim, right_dim)
    )


def params(mib):
    return pltpu.CompilerParams(vmem_limit_bytes=mib << 20)


def cost(micros):
    return pl.CostEstimate(flops=micros * 10**9, transcendentals=0, bytes_accessed=1 << 20)


def vmem():
    return pl.BlockSpec(memory_space=pltpu.VMEM)


def smem():
    return pl.BlockSpec(memory_space=pltpu.SMEM)


def attend_kernel(mixed_ref, seg_col_ref, seg_row_ref, context_ref, logsum_ref):
    same = seg_col_ref[0] == seg_row_ref[0]

    def pair(step, carry):
        at = pl.multiple_of(step * LANES, LANES)
        queries = mixed_ref[:, pl.ds(at, LANES)]
        keys = mixed_ref[:, pl.ds(D + at, LANES)]
        values = mixed_ref[:, pl.ds(2 * D + at, LANES)]
        outs = []
        for half in range(2):
            cut = slice(half * HEAD, (half + 1) * HEAD)
            raw = dot32(keys[:, cut], queries[:, cut], 1, 1)
            scores = jnp.where(same, raw * (1.0 / math.sqrt(HEAD)), -1e30)
            peak = jnp.max(scores, axis=0, keepdims=True)
            lifted = jnp.exp(scores - peak)
            total = jnp.sum(lifted, axis=0, keepdims=True)
            probs = (lifted * (1.0 / total)).astype(low)
            outs.append(dot32(values[:, cut], probs, 0, 0))
            logsum_ref[0, pl.ds(2 * step + half, 1), :] = peak + jnp.log(total)
        context_ref[:, pl.ds(at, LANES)] = jnp.concatenate(outs, axis=0).T.astype(low)
        return carry

    lax.fori_loop(0, HEADS // 2, pair, 0)


def attend(mixed, segment):
    rows = segment.shape[0]
    return pl.pallas_call(
        attend_kernel,
        grid=(rows,),
        in_specs=[
            pl.BlockSpec((SEQ, 3 * D), lambda b: (b, 0)),
            pl.BlockSpec((1, SEQ, 1), lambda b: (b, 0, 0)),
            pl.BlockSpec((1, 1, SEQ), lambda b: (b, 0, 0)),
        ],
        out_specs=[
            pl.BlockSpec((SEQ, D), lambda b: (b, 0)),
            pl.BlockSpec((1, 16, SEQ), lambda b: (b, 0, 0)),
        ],
        out_shape=[
            jax.ShapeDtypeStruct((rows * SEQ, D), low),
            jax.ShapeDtypeStruct((rows, 16, SEQ), full),
        ],
        compiler_params=params(48),
        cost_estimate=cost(19),
        name="attend",
    )(mixed, segment[:, :, None], segment[:, None, :])


def attend_back_kernel(mixed_ref, grad_ref, logsum_ref, seg_col_ref, seg_row_ref, out_ref):
    same = seg_col_ref[0] == seg_row_ref[0]
    scale = 1.0 / math.sqrt(HEAD)

    def pair(step, carry):
        at = pl.multiple_of(step * LANES, LANES)
        queries = mixed_ref[:, pl.ds(at, LANES)]
        keys = mixed_ref[:, pl.ds(D + at, LANES)]
        values = mixed_ref[:, pl.ds(2 * D + at, LANES)]
        upstream = grad_ref[:, pl.ds(at, LANES)]
        query_grads, key_grads, value_grads = [], [], []
        for half in range(2):
            cut = slice(half * HEAD, (half + 1) * HEAD)
            logsum = logsum_ref[0, pl.ds(2 * step + half, 1), :]
            raw = dot32(keys[:, cut], queries[:, cut], 1, 1)
            probs = jnp.exp(jnp.where(same, raw * scale, -1e30) - logsum)
            prob_grads = dot32(values[:, cut], upstream[:, cut], 1, 1)
            value_grads.append(dot32(probs.astype(low), upstream[:, cut], 1, 0))
            moved = jnp.sum(prob_grads * probs, axis=0, keepdims=True)
            back = (probs * (prob_grads - moved) * scale).astype(low)
            key_grads.append(dot32(back, queries[:, cut], 1, 0))
            query_grads.append(dot32(keys[:, cut], back, 0, 0))
        out_ref[:, pl.ds(at, LANES)] = jnp.concatenate(query_grads, axis=0).T.astype(low)
        out_ref[:, pl.ds(D + at, LANES)] = jnp.concatenate(key_grads, axis=1).astype(low)
        out_ref[:, pl.ds(2 * D + at, LANES)] = jnp.concatenate(value_grads, axis=1).astype(low)
        return carry

    lax.fori_loop(0, HEADS // 2, pair, 0)


def attend_back(mixed, context_grad, logsum, segment):
    rows = segment.shape[0]
    return pl.pallas_call(
        attend_back_kernel,
        grid=(rows,),
        in_specs=[
            pl.BlockSpec((SEQ, 3 * D), lambda b: (b, 0)),
            pl.BlockSpec((SEQ, D), lambda b: (b, 0)),
            pl.BlockSpec((1, 16, SEQ), lambda b: (b, 0, 0)),
            pl.BlockSpec((1, SEQ, 1), lambda b: (b, 0, 0)),
            pl.BlockSpec((1, 1, SEQ), lambda b: (b, 0, 0)),
        ],
        out_specs=pl.BlockSpec((SEQ, 3 * D), lambda b: (b, 0)),
        out_shape=jax.ShapeDtypeStruct((rows * SEQ, 3 * D), low),
        compiler_params=params(56),
        cost_estimate=cost(28),
        name="attend_back",
    )(mixed, context_grad, logsum, segment[:, :, None], segment[:, None, :])


def collect_kernel(place_ref, ids_ref, grads_ref, out_ref, square_ref, *scratch,
                   span, tokens, features, vocab):
    sums, rows_ref = scratch[:-1], scratch[-1]
    step = pl.program_id(0)
    last = pl.num_programs(0) - 1
    streams = len(sums)
    batch = 4 * streams

    @pl.when(step == 0)
    def _():
        for total in sums:
            total[...] = jnp.zeros_like(total)

    group = ids_ref[0] // span
    grads = grads_ref[0].astype(full)
    pad = jnp.zeros((WIDTH - features, tokens), full)
    pieces = []
    for at in range(GROUPS):
        pieces += [jnp.where(group == at, grads, 0.0), pad]
    rows_ref[...] = jnp.concatenate(pieces, axis=0).T

    def body(i, carry):
        for base in range(0, batch, streams):
            at = i * batch + base
            places = [pl.ds(place_ref[0, 0, at + k], 1) for k in range(streams)]
            olds = [sums[k][places[k], :] for k in range(streams)]
            news = [rows_ref[pl.ds(at + k, 1), :] for k in range(streams)]
            for k in range(streams):
                sums[k][places[k], :] = olds[k] + news[k]
        return carry

    lax.fori_loop(0, tokens // batch, body, 0)

    @pl.when(step == last)
    def _():
        def flush(b, total):
            at = pl.multiple_of(b * LANES, LANES)
            block = sums[0][pl.ds(at, LANES), :]
            for k in range(1, streams):
                block += sums[k][pl.ds(at, LANES), :]
            turned = block.T
            for g in range(GROUPS):
                piece = turned[g * WIDTH:g * WIDTH + features]

                @pl.when(g * span + at < vocab)
                def _():
                    out_ref[:, pl.ds(pl.multiple_of(g * span + at, LANES), LANES)] = piece.astype(low)

            return total + block * block

        total = lax.fori_loop(0, span // LANES, flush, jnp.zeros((LANES, LANES), full))
        square_ref[...] = jnp.broadcast_to(jnp.sum(total, keepdims=True), square_ref.shape)


def collect(ids, grads, vocab, tokens):
    sources, features = grads.shape[:2]
    span = -(-vocab // (GROUPS * LANES)) * LANES
    return pl.pallas_call(
        partial(collect_kernel, span=span, tokens=tokens, features=features, vocab=vocab),
        grid=(sources,),
        in_specs=[
            pl.BlockSpec((1, 1, tokens), lambda s: (s, 0, 0), memory_space=pltpu.SMEM),
            pl.BlockSpec((1, 1, tokens), lambda s: (s, 0, 0)),
            pl.BlockSpec((1, features, tokens), lambda s: (s, 0, 0)),
        ],
        out_specs=[
            pl.BlockSpec((features, vocab), lambda s: (0, 0)),
            pl.BlockSpec((8, LANES), lambda s: (0, 0)),
        ],
        out_shape=[
            jax.ShapeDtypeStruct((features, vocab), low),
            jax.ShapeDtypeStruct((8, LANES), full),
        ],
        scratch_shapes=[pltpu.VMEM((span, LANES), full)] * 8 + [pltpu.VMEM((tokens, LANES), full)],
        compiler_params=params(56),
        cost_estimate=cost(49),
        name="collect",
    )((ids % span)[:, None, :], ids[:, None, :], grads)


def moment_kernel(info_ref, factor_ref, grad_ref, old_ref, moment_ref, gram_ref, *, piece, block):
    factor = factor_ref[0]
    for at in range(old_ref.shape[0] // piece):
        source = pl.multiple_of(info_ref[2 + at] * piece, piece)
        rows = slice(at * piece, (at + 1) * piece)
        moment_ref[rows] = muon_beta * old_ref[rows] + factor * grad_ref[pl.ds(source, piece)].astype(full)
    gram_ref[...] = jnp.zeros_like(gram_ref)

    def body(b, carry):
        slot = (b * block >= info_ref[0]).astype(jnp.int32)
        high, small = halves(moment_ref[pl.ds(pl.multiple_of(b * block, block), block)])
        for at, (i, j) in enumerate(TILES):
            left, right = slice(i * BLOCK, (i + 1) * BLOCK), slice(j * BLOCK, (j + 1) * BLOCK)
            gram_ref[slot, at] += dot32(
                jnp.concatenate([high[:, left], high[:, left], small[:, left]], axis=0),
                jnp.concatenate([high[:, right], small[:, right], high[:, right]], axis=0),
                0,
                0,
            )
        return carry

    lax.fori_loop(0, old_ref.shape[0] // block, body, 0)


def moment_and_gram(info, factor, grad, old, piece, block):
    return pl.pallas_call(
        partial(moment_kernel, piece=piece, block=block),
        in_specs=[smem(), smem(), vmem(), vmem(), vmem()][:4],
        out_specs=[vmem(), vmem()],
        out_shape=[
            jax.ShapeDtypeStruct(old.shape, full),
            jax.ShapeDtypeStruct((2, len(TILES), BLOCK, BLOCK), full),
        ],
        compiler_params=params(56),
        cost_estimate=cost(10),
        name="moment",
    )(info, factor, grad, old)


def even_product(left, right, put):
    (lh, ll), (rh, rl) = left, right
    for i in range(D // BLOCK):
        rows = slice(i * BLOCK, (i + 1) * BLOCK)
        panel = jnp.concatenate([lh[rows], lh[rows], ll[rows]], axis=1)
        for j in range(i, D // BLOCK):
            cols = slice(j * BLOCK, (j + 1) * BLOCK)
            other = jnp.concatenate([rh[:, cols], rl[:, cols], rh[:, cols]], axis=0)
            put(rows, cols, dot32(panel, other, 1, 0))


def keep(pair):
    def put(rows, cols, value):
        pair[0][rows, cols], pair[1][rows, cols] = halves(value)
        if rows != cols:
            pair[0][cols, rows], pair[1][cols, rows] = halves(value.T)

    return put


def chain_kernel(gram_ref, out_ref, a_ref, *parts):
    a, q, p, t = [parts[2 * i:2 * i + 2] for i in range(4)]

    def diagonal(size):
        shape = (size, size)
        return lax.broadcasted_iota(jnp.int32, shape, 0) == lax.broadcasted_iota(jnp.int32, shape, 1)

    def put_a(rows, cols, value):
        a_ref[rows, cols] = value
        keep(a)(rows, cols, value)

    once = diagonal(BLOCK)
    trace = 0.0
    for at, (i, j) in enumerate(TILES):
        if i == j:
            trace = trace + jnp.sum(jnp.where(once, gram_ref[at], 0.0))
    scale = jnp.sqrt(trace) + 1e-07
    for at, (i, j) in enumerate(TILES):
        rows, cols = slice(i * BLOCK, (i + 1) * BLOCK), slice(j * BLOCK, (j + 1) * BLOCK)
        put_a(rows, cols, gram_ref[at] * (1.0 / (scale * scale)))

    def put_q(rows, cols, value):
        new = 2.0315 * value - 4.775 * a_ref[rows, cols]
        keep(q)(rows, cols, new + jnp.where(once, 3.4445, 0.0) if rows == cols else new)

    def put_out(rows, cols, value):
        value = value * (1.0 / scale)
        out_ref[rows, cols] = value
        if rows != cols:
            out_ref[cols, rows] = value.T

    def turn(k, carry):
        even_product(a, a, put_q)

        @pl.when(k == 0)
        def _():
            p[0][...], p[1][...] = q[0][...], q[1][...]

        @pl.when((k > 0) & (k < NS_TURNS - 1))
        def _():
            even_product(p, q, keep(t))
            p[0][...], p[1][...] = t[0][...], t[1][...]

        @pl.when(k == NS_TURNS - 1)
        def _():
            even_product(p, q, put_out)

        @pl.when(k < NS_TURNS - 1)
        def _():
            even_product(a, q, keep(t))
            even_product(t, q, put_a)

        return carry

    lax.fori_loop(0, NS_TURNS, turn, 0)


def chain(gram):
    return pl.pallas_call(
        chain_kernel,
        in_specs=[vmem()],
        out_specs=vmem(),
        out_shape=jax.ShapeDtypeStruct((D, D), full),
        scratch_shapes=[pltpu.VMEM((D, D), full)] + [pltpu.VMEM((D, D), low)] * 8,
        compiler_params=params(40),
        cost_estimate=cost(36),
        name="chain",
    )(gram)


def apply_kernel(info_ref, gain_ref, first_ref, second_ref, moment_ref, master_ref, new_ref, copy_ref,
                 *, block):
    split = info_ref[0] // block

    def over(slot, p_ref, start, stop):
        p = halves(p_ref[...])
        gain = gain_ref[slot] * muon_rate

        def body(b, carry):
            rows = pl.ds(pl.multiple_of(b * block, block), block)
            ortho = dot_split(halves(moment_ref[rows]), p)
            new = master_ref[rows] * (1.0 - muon_rate * muon_decay) - gain * ortho
            new_ref[rows] = new
            copy_ref[rows] = new.astype(low)
            return carry

        lax.fori_loop(start, stop, body, 0)

    over(0, first_ref, 0, split)
    total = moment_ref.shape[0] // block

    @pl.when(split < total)
    def _():
        over(1, second_ref, split, total)


def apply_chain(info, gains, first, second, moment, master, block):
    return pl.pallas_call(
        partial(apply_kernel, block=block),
        in_specs=[smem(), smem(), vmem(), vmem(), vmem(), vmem()],
        out_specs=[vmem(), vmem()],
        out_shape=[
            jax.ShapeDtypeStruct(moment.shape, full),
            jax.ShapeDtypeStruct(moment.shape, low),
        ],
        compiler_params=params(48),
        cost_estimate=cost(10),
        name="apply",
    )(info, gains, first, second, moment, master)


def chains(grams, wide_at, first_matrix, second_matrix, rider):
    wide = lax.axis_size("wide")
    if wide != 8:
        which = jnp.arange(4)
        slots = (which == first_matrix).astype(full)[:, None, None, None] * grams[0]
        slots = slots + (which == second_matrix).astype(full)[:, None, None, None] * grams[1]
        total = lax.psum(slots, "wide")
        return (
            chain(lax.dynamic_index_in_dim(total, first_matrix, 0, keepdims=False)),
            chain(lax.dynamic_index_in_dim(total, second_matrix, 0, keepdims=False)),
            rider,
        )
    half = len(TILES) // 2
    gram0, gram1 = grams[0], grams[1]
    pairs = [(i, i ^ 1) for i in range(8)]
    lower = wide_at % 2 == 0
    mine = jnp.where(wide_at == 2, gram1, gram0)
    moved = lax.ppermute(gram1[:half], "wide", [(5, 4)])
    chip = mine + lax.ppermute(mine, "wide", pairs)
    up_send = jnp.where(lower, chip[:half], chip[half:])
    down_send = jnp.where(wide_at == 4, moved, jnp.where(wide_at == 5, gram1[half:], up_send))
    up = up_send + lax.ppermute(up_send, "wide", [(2, 4), (4, 2), (3, 5), (5, 3)])
    down = down_send + lax.ppermute(down_send, "wide", [(4, 6), (6, 4), (5, 7), (7, 5)])
    send = jnp.where((wide_at == 4), down, up)
    send = jnp.where(wide_at >= 6, down, send)
    swap = lax.ppermute(send, "wide", [(2, 3), (4, 5), (6, 7), (7, 6)])
    back = lax.ppermute(up, "wide", [(5, 4)])
    kept = jnp.where(wide_at >= 5, down, up)
    other = jnp.where(wide_at == 4, back, swap)
    whole = jnp.concatenate([jnp.where(lower, kept, other), jnp.where(lower, other, kept)])
    gram = jnp.where(wide_at < 2, chip, jnp.where(wide_at == 2, gram0, whole))
    gram, rider = lax.optimization_barrier((gram, rider))
    own = chain(gram)
    come = lax.ppermute(own, "wide", [(3, 2), (4, 5)])
    return jnp.where(wide_at == 5, come, own), jnp.where(wide_at == 5, own, come), rider


def layout(lengths):
    row_ends = jnp.cumsum(lengths)
    starts = row_ends - lengths
    places = jnp.arange(SEQ, dtype=jnp.int32)
    segment = jnp.sum((places[:, None] >= row_ends[None, :]).astype(jnp.int32), axis=1)
    chosen = segment[:, None] == jnp.arange(SLOTS, dtype=jnp.int32)[None, :]
    start_at = jnp.sum(jnp.where(chosen, starts[None, :], 0), axis=1)
    length_at = jnp.sum(jnp.where(chosen, lengths[None, :], 0), axis=1)
    position = places - start_at
    second = (2 * position >= length_at).astype(jnp.int32)
    return (chosen.astype(full), position, second, segment)


def norm_forward(hidden, gain, bias):
    center = hidden - jnp.mean(hidden, axis=-1, keepdims=True)
    inverse = lax.rsqrt(jnp.mean(center * center, axis=-1, keepdims=True) + norm_eps)
    scaled = center * inverse
    return (scaled * gain + bias, scaled, inverse)


def norm_backward(upstream, scaled, inverse, gain):
    weighted = upstream * gain
    back = inverse * (
        weighted
        - jnp.mean(weighted, axis=-1, keepdims=True)
        - scaled * jnp.mean(weighted * scaled, axis=-1, keepdims=True)
    )
    return (back, jnp.sum(upstream * scaled, axis=0), jnp.sum(upstream, axis=0))


def project(left, right):
    return jnp.dot(left, right, preferred_element_type=full)


def task_loss(logits, scores, tasks, labels, negatives, counts):
    logprob = jax.nn.log_softmax(logits, axis=-1)
    picked = jnp.sum(
        jnp.where(labels[:, :, None] == jnp.arange(3, dtype=jnp.int32), logprob, 0.0), axis=2
    )
    chosen = negatives[:, :, :, None] == jnp.arange(scores.shape[1], dtype=jnp.int32)
    rivals = jnp.sum(jnp.where(chosen, scores[:, None, None, :], 0.0), axis=3)
    together = jnp.concatenate([scores[:, :, None], rivals], axis=2)
    ranking = jax.nn.logsumexp(together, axis=2) - scores
    first_part = jnp.sum(jnp.where(tasks == 0, -picked, 0.0)) / counts[0]
    return first_part + jnp.sum(jnp.where(tasks == 1, ranking, 0.0)) / counts[1]


def adam(weight, grad, first, second, step, rate):
    first = beta_one * first + (1.0 - beta_one) * grad
    second = beta_two * second + (1.0 - beta_two) * grad * grad
    unbiased = first / (1.0 - beta_one**step)
    spread = second / (1.0 - beta_two**step)
    return (
        weight - rate * (unbiased / (jnp.sqrt(spread) + adam_eps) + adam_decay * weight),
        first,
        second,
    )


def broadcast_all(x):
    count = lax.axis_size("narrow") * lax.axis_size("wide")
    return lax.all_to_all(
        jnp.broadcast_to(x[None], (count,) + x.shape), BOTH, split_axis=0, concat_axis=0, tiled=True
    )


def sides(wide):
    return [list(range(0, wide, 2)), list(range(1, wide, 2))]


def chip_mates(wide):
    return [(i, i ^ 1) for i in range(wide)]


def by_owner(grad, spans, parts):
    pieces = [
        grad[lo:hi].reshape(parts, (hi - lo) // parts, D) for lo, hi in spans
    ]
    return jnp.concatenate(pieces, axis=1).reshape(-1, D).astype(low)


def gather_weights(master, narrow_at, wide_at, first):
    wide = lax.axis_size("wide")
    if wide != 8:
        whole = lax.all_gather(master.astype(low), "wide", axis=0, tiled=True)
        return first, list(whole.reshape(wide, -1, D))
    share = master.shape[0] // lax.axis_size("narrow")
    mine = lax.dynamic_slice_in_dim(master, narrow_at * share, share, 0).astype(low)
    near = lax.all_gather(mine, "wide", axis=0, tiled=False, axis_index_groups=sides(wide))
    near, first = lax.optimization_barrier((near, first))
    return first, [
        lax.all_gather(part, "narrow", axis=1, tiled=True)
        for part in (near[: wide // 4], near[wide // 4 :])
    ]


def both_cores(held, wide_at):
    owners = []
    other = lax.ppermute(held, "wide", chip_mates(lax.axis_size("wide")))
    side = wide_at % 2
    even = jnp.where(side == 0, held, other)
    odd = jnp.where(side == 0, other, held)
    for at in range(held.shape[0]):
        owners += [even[at], odd[at]]
    return owners


def rows_of(owners, matrix):
    rows = owners[0].shape[0]
    lo, hi = BOUNDS[matrix], BOUNDS[matrix + 1]
    pieces = []
    for at in range(lo // rows, -(-hi // rows)):
        pieces.append(owners[at][max(lo - at * rows, 0) : min(hi - at * rows, rows)])
    return jnp.concatenate(pieces) if len(pieces) > 1 else pieces[0]


def shards(
    token_ids,
    seq_lengths,
    task_ids,
    labels,
    negatives,
    step_count,
    hidden_master,
    hidden_momentum,
    table_master,
    table_first,
    table_second,
    pos_types,
    pos_first,
    pos_second,
    vectors,
    vec_first,
    vec_second,
):
    wide_at = lax.axis_index("wide")
    narrow_at = lax.axis_index("narrow")
    wide = lax.axis_size("wide")
    narrow = lax.axis_size("narrow")
    count = wide * narrow
    device_at = narrow_at * wide + wide_at
    micro_count, rows_each = token_ids.shape[:2]
    batch = micro_count * rows_each
    tokens = batch * SEQ
    shard = hidden_master.shape[0]
    vocab = table_master.shape[1]
    features = table_master.shape[0] // narrow
    pairs_each = rows_each * SLOTS

    parts = [token_ids, task_ids, labels, negatives]
    sizes = [part.size for part in parts]
    packed = jnp.concatenate([part.reshape(-1) for part in parts])
    packed = jnp.pad(packed, (0, -packed.size % LANES))
    gathered = broadcast_all(packed)
    ends = [sum(sizes[: i + 1]) for i in range(len(sizes))]
    ids_all = gathered[:, : ends[0]]

    def pairs_of(lo, hi, tail):
        block = gathered[:, lo:hi].reshape((count, micro_count, pairs_each) + tail)
        return jnp.moveaxis(block, 1, 0).reshape((micro_count, count * pairs_each) + tail)

    tasks_all = pairs_of(ends[0], ends[1], ())
    labels_all = pairs_of(ends[1], ends[2], ())
    negatives_all = pairs_of(ends[2], ends[3], (NEG,))
    counts = jnp.stack(
        [jnp.sum((tasks_all == 0).astype(full)), jnp.sum((tasks_all == 1).astype(full))]
    )


    group_ids = lax.dynamic_slice_in_dim(ids_all, narrow_at * wide, wide, 0).reshape(-1)
    table_low = table_master.astype(low)
    pieces = jnp.take(table_low, group_ids, axis=1, mode="clip")
    pieces, gathers = gather_weights(hidden_master, narrow_at, wide_at, pieces)
    simple = wide != 8
    owners = gathers if simple else both_cores(gathers[0], wide_at)
    arrived = lax.all_to_all(pieces, "wide", split_axis=1, concat_axis=0, tiled=True)
    token_rows = arrived.T

    lengths = seq_lengths.reshape(batch, SLOTS)
    member, position, second, segment = jax.vmap(layout)(lengths)
    flat_position = position.reshape(-1)
    flat_second = second.reshape(-1)
    embed = token_rows.astype(full) + pos_types[flat_position]
    embed = embed + jnp.where(flat_second[:, None] == 1, pos_types[SEQ + 1], pos_types[SEQ])
    normed0, scaled0, inverse0 = norm_forward(embed, vectors[0], vectors[1])
    input0 = normed0.astype(low)
    qkv_bias = jnp.concatenate([vectors[6], jnp.zeros_like(vectors[6]), vectors[7]])
    weight_qkv, weight_out = rows_of(owners, 0), rows_of(owners, 1)
    mixed = (project(input0, weight_qkv.T) + qkv_bias).astype(low)
    context_low, logsum = attend(mixed, segment)
    if not simple:
        rest, context_low = lax.optimization_barrier((gathers[1], context_low))
        owners = owners + both_cores(rest, wide_at)
    weight_up, weight_down = rows_of(owners, 2), rows_of(owners, 3)
    attended = project(context_low, weight_out.T) + vectors[8]
    normed1, scaled1, inverse1 = norm_forward(normed0 + attended, vectors[2], vectors[3])
    input1 = normed1.astype(low)
    inner = project(input1, weight_up.T) + vectors[14:].reshape(-1)
    cdf = 0.5 * (1.0 + lax.erf(inner * math.sqrt(0.5)))
    active = (inner * cdf).astype(low)
    slope = cdf + inner * (jnp.exp(-0.5 * inner * inner) * (1.0 / math.sqrt(2.0 * math.pi)))
    branch = project(active, weight_down) + vectors[9]
    normed2, scaled2, inverse2 = norm_forward(normed1 + branch, vectors[4], vectors[5])
    share = member / lengths.astype(full)[:, None, :]
    pooled = jnp.einsum("rps,rpd->rsd", share, normed2.reshape(batch, SEQ, D), precision=highest)
    flat_pooled = pooled.reshape(-1, D)
    heads = vectors[10:14]
    head_out = jnp.dot(flat_pooled, heads.T, precision=highest)

    sent = jnp.pad(head_out.reshape(-1), (0, -head_out.size % LANES))
    head_all = broadcast_all(sent)[:, : head_out.size]
    head_all = head_all.reshape(count, micro_count, pairs_each, 4)
    head_all = jnp.moveaxis(head_all, 1, 0).reshape(micro_count, count * pairs_each, 4)

    def objective(every):
        return task_loss(every[:, :, :3], every[:, :, 3], tasks_all, labels_all, negatives_all, counts)

    loss, pullback = jax.vjp(objective, head_all)
    head_grads = pullback(jnp.ones_like(loss))[0]
    output_grads = lax.dynamic_slice_in_dim(head_grads, device_at * pairs_each, pairs_each, 1)
    output_grads = output_grads.reshape(-1, 4)
    heads_grad = jnp.dot(output_grads.T, flat_pooled, precision=highest)
    pooled_grads = jnp.dot(output_grads, heads, precision=highest).reshape(pooled.shape)

    spread = jnp.einsum("rps,rsd->rpd", share, pooled_grads, precision=highest).reshape(-1, D)
    sum2_grad, gain2, bias2 = norm_backward(spread, scaled2, inverse2, vectors[4])
    branch_grad = sum2_grad.astype(low)
    down_grad = project(active.T, branch_grad)
    spans_down = [(0, 768), (768, 1920), (1920, 3072)]
    spans_up = [(0, 384), (384, 1536), (1536, 2688), (2688, 3072)]
    spans_front = [(0, 1152), (1152, 2304), (2304, 3072)]

    side = wide_at % 2

    def ready(grad, spans):
        if simple:
            return grad.astype(low)
        grad = by_owner(grad, spans, narrow)
        left, right = grad[:, : D // 2], grad[:, D // 2 :]
        stays = jnp.where(side == 0, left, right)
        leaves = jnp.where(side == 0, right, left)
        return stays, leaves

    def between_cores(grad):
        if simple:
            return grad
        stays, leaves = grad
        return stays, lax.ppermute(leaves, "wide", chip_mates(wide))

    def slices(grad):
        if simple:
            return [grad]
        stays, comes = grad
        chip = (stays.astype(full) + comes.astype(full)).astype(low).reshape(narrow, -1, D // 2)
        return [chip[narrow_at ^ turn] for turn in range(narrow)]

    def over_narrow(parts):
        return parts[:1] + [
            lax.ppermute(part, "narrow", [(i, i ^ (turn + 1)) for i in range(narrow)])
            for turn, part in enumerate(parts[1:])
        ]

    together = lax.optimization_barrier
    down_send, after_down = together((ready(down_grad, spans_down), branch_grad))
    down_pair = between_cores(down_send)
    active_grad = project(after_down, weight_down.T)
    inner_grad = (active_grad * slope).astype(low)
    up_grad = project(inner_grad.T, input1)
    up_send, down_pair, after_up = together((ready(up_grad, spans_up), down_pair, inner_grad))
    up_pair = between_cores(up_send)
    down_cut, after_up = together((slices(down_pair), after_up))
    down_part = over_narrow(down_cut)
    normed1_grad = sum2_grad + project(after_up, weight_up)
    sum1_grad, gain1, bias1 = norm_backward(normed1_grad, scaled1, inverse1, vectors[2])
    attended_grad = sum1_grad.astype(low)
    up_pair, attended_grad = together((up_pair, attended_grad))
    out_grad = project(attended_grad.T, context_low)
    context_grad = project(attended_grad, weight_out).astype(low)
    up_cut, context_grad = together((slices(up_pair), context_grad))
    up_part = over_narrow(up_cut)
    mixed_grad = attend_back(mixed, context_grad, logsum, segment)
    mixed_grad, up_part, down_part = together((mixed_grad, up_part, down_part))
    qkv_grad = project(mixed_grad.T, input0)
    front_grad = jnp.concatenate([qkv_grad.astype(low), out_grad.astype(low)])
    front_send, after_front = together((ready(front_grad, spans_front), mixed_grad))
    front_pair = between_cores(front_send)
    normed0_grad = sum1_grad + project(after_front, weight_qkv)
    embed_grad, gain0, bias0 = norm_backward(normed0_grad, scaled0, inverse0, vectors[0])
    mixed_sum = jnp.sum(mixed_grad.astype(full), axis=0)
    small_rows = jnp.stack(
        [
            gain0,
            bias0,
            gain1,
            bias1,
            gain2,
            bias2,
            mixed_sum[:D],
            mixed_sum[2 * D :],
            jnp.sum(attended_grad.astype(full), axis=0),
            jnp.sum(branch_grad.astype(full), axis=0),
        ]
    )
    up_rows = jnp.sum(inner_grad.astype(full), axis=0).reshape(-1, D)

    places = jnp.arange(SEQ, dtype=jnp.int32)[:, None]
    row_hot = jnp.concatenate(
        [
            flat_position[None] == places,
            jnp.stack([flat_second == 0, flat_second == 1]),
        ]
    ).astype(low)
    high_part, low_part = halves(embed_grad)
    pos_grad = project(jnp.concatenate([row_hot, row_hot], axis=1), jnp.concatenate([high_part, low_part]))
    small = jnp.concatenate([pos_grad, small_rows, heads_grad, up_rows])
    small_count = small.shape[0]
    small = jnp.pad(small, ((0, count * features - small_count), (0, 0)))

    embed_low, front_pair = together((embed_grad.astype(low), front_pair))
    front_part = over_narrow(slices(front_pair))
    table_send = embed_low.T.reshape(wide, narrow, features, tokens)
    table_send = jnp.moveaxis(table_send, 1, 0).reshape(count, features, tokens)
    small_send = small.astype(low).reshape(count, features, D)
    come = lax.all_to_all(
        jnp.concatenate([table_send, small_send], axis=2), BOTH, split_axis=0, concat_axis=0, tiled=True
    )

    def added(parts):
        return sum(part.astype(full) for part in parts).astype(low)

    joined = jnp.concatenate([added(front_part), added(up_part), added(down_part)])
    joined, come = together((joined, come))
    small_part = jnp.sum(come[:, :, tokens:].astype(full), axis=0)
    small_square = jnp.sum(small_part * small_part)
    small_square, come = together((small_square, come))
    table_part, table_square = collect(ids_all, come, vocab, tokens)
    if simple:
        hidden_part = lax.psum_scatter(joined, "wide", scatter_dimension=0, tiled=True)
        hidden_part = lax.psum_scatter(hidden_part, "narrow", scatter_dimension=0, tiled=True)
        hidden_square = jnp.sum(jnp.square(hidden_part.astype(full)))
    else:
        owned = lax.psum_scatter(
            joined, "wide", scatter_dimension=0, tiled=True, axis_index_groups=sides(wide)
        )
        owned, table_square = together((owned, table_square))
        hidden_square = jnp.sum(jnp.square(owned.astype(full)))
        half = owned.shape[0] // 2
        stays = jnp.where(side == 0, owned[:half], owned[half:])
        leaves = jnp.where(side == 0, owned[half:], owned[:half])
        comes = lax.ppermute(leaves, "wide", chip_mates(wide))
        hidden_part = jnp.concatenate(
            [jnp.where(side == 0, stays, comes), jnp.where(side == 0, comes, stays)], axis=1
        )
    if simple:
        hidden_all = lax.all_gather(hidden_part, "narrow", axis=0, tiled=True)
    else:
        hidden_all = jnp.concatenate(
            [hidden_part]
            + [
                lax.ppermute(hidden_part, "narrow", [(i, i ^ turn) for i in range(narrow)])
                for turn in range(1, narrow)
            ]
        )
    square = hidden_square + table_square[0, 0] + small_square
    squares = broadcast_all(jnp.broadcast_to(square, (LANES,)))
    squares, table_part = together((squares, table_part))
    table_grad = lax.all_gather(table_part, "narrow", axis=0, tiled=True)
    clip_norm = jnp.sqrt(jnp.sum(squares[:, 0]))
    factor = jnp.minimum(1.0, clip_bound / clip_norm)

    start = wide_at * shard
    bounds = jnp.array(BOUNDS, jnp.int32)
    first_matrix = jnp.sum((start >= bounds[1:4]).astype(jnp.int32))
    second_matrix = jnp.sum((start + shard - 1 >= bounds[1:4]).astype(jnp.int32))
    split = jnp.minimum(bounds[first_matrix + 1] - start, shard)
    block = shard // 3
    piece = shard // 12
    at = jnp.arange(12, dtype=jnp.int32)
    if simple:
        source = at
    else:
        lead = split // piece
        each = lead // narrow
        rest = (12 - lead) // narrow
        in_first = at < lead
        inside = jnp.where(in_first, at, at - lead)
        width = jnp.maximum(jnp.where(in_first, each, rest), 1)
        origin = (inside // width) ^ narrow_at
        source = origin * (12 // narrow) + jnp.where(in_first, 0, each) + inside % width
    info = jnp.concatenate([jnp.stack([split, split]), source]).astype(jnp.int32)
    gains = jnp.array([0.2 * math.sqrt(hi - lo) for lo, hi in zip(BOUNDS, BOUNDS[1:])], full)
    moment, grams = moment_and_gram(info, factor[None], hidden_all, hidden_momentum, piece, block)
    chain0, chain1, late_small = chains(grams, wide_at, first_matrix, second_matrix, small_part)
    small_all = lax.all_gather(late_small.astype(low), BOTH, axis=0, tiled=True)
    small_all = small_all[:small_count].astype(full)
    slot_gains = jnp.stack([gains[first_matrix], gains[second_matrix]])
    hidden_new, hidden_copy = apply_chain(info, slot_gains, chain0, chain1, moment, hidden_master, block)

    step = step_count[0].astype(full)
    table_new, table_first_new, table_second_new = adam(
        table_master, factor * table_grad.astype(full), table_first, table_second, step, 0.02
    )
    pos_new, pos_first_new, pos_second_new = adam(
        pos_types, factor * small_all[: SEQ + 2], pos_first, pos_second, step, 0.02
    )
    vectors_new, vec_first_new, vec_second_new = adam(
        vectors, factor * small_all[SEQ + 2 :], vec_first, vec_second, step, 0.2
    )
    return (
        loss,
        clip_norm,
        moment,
        hidden_new,
        hidden_copy,
        table_new,
        table_first_new,
        table_second_new,
        table_new.astype(low),
        pos_new,
        pos_first_new,
        pos_second_new,
        vectors_new,
        vec_first_new,
        vec_second_new,
    )


def solution(mesh):
    rows = P(None, BOTH, None)
    owned = P("wide", None)
    return jax.shard_map(
        shards,
        mesh=mesh,
        in_specs=(rows, rows, rows, rows, P(None, BOTH, None, None), P())
        + (owned,) * 5
        + (P(),) * 6,
        out_specs=(P(), P()) + (owned,) * 7 + (P(),) * 6,
        check_vma=False,
    )
```

```python
from functools import partial
import math

import jax
import jax.numpy as jnp
from jax import lax
from jax.experimental import pallas as pl
from jax.experimental.pallas import tpu as pltpu
from jax.sharding import PartitionSpec as P

D = 768
HEADS = 12
HEAD = 64
FF = 3072
SEQ = 512
SLOTS = 4
NEG = 4
NS_TURNS = 5
LANES = 128
GROUPS = 4
WIDTH = LANES // GROUPS
BLOCK = 256
TILES = [(i, j) for i in range(D // BLOCK) for j in range(i, D // BLOCK)]

BOTH = ("narrow", "wide")
highest = lax.Precision.HIGHEST
clip_bound = 0.002
norm_eps = 1e-06
muon_beta = 0.95
muon_rate = 0.1
muon_decay = 0.01
beta_one = 0.9
beta_two = 0.999
adam_eps = 1e-08
adam_decay = 0.01
BOUNDS = (0, 3 * D, 4 * D, 4 * D + FF, 4 * D + 2 * FF)

low = jnp.bfloat16
full = jnp.float32


def dims(left, right):
    return (((left,), (right,)), ((), ()))


def dot32(left, right, left_dim, right_dim):
    return lax.dot_general(left, right, dims(left_dim, right_dim), preferred_element_type=full)


def halves(x):
    high = x.astype(low)
    return high, (x - high.astype(full)).astype(low)


def dot_split(left, right, left_dim=1, right_dim=0):
    (lh, ll), (rh, rl) = left, right
    return dot32(lh, rh, left_dim, right_dim) + (
        dot32(lh, rl, left_dim, right_dim) + dot32(ll, rh, left_dim, right_dim)
    )


def params(mib):
    return pltpu.CompilerParams(vmem_limit_bytes=mib << 20)


def cost(micros):
    return pl.CostEstimate(flops=micros * 10**9, transcendentals=0, bytes_accessed=1 << 20)


def vmem():
    return pl.BlockSpec(memory_space=pltpu.VMEM)


def smem():
    return pl.BlockSpec(memory_space=pltpu.SMEM)


def attend_kernel(mixed_ref, seg_col_ref, seg_row_ref, context_ref, logsum_ref):
    same = seg_col_ref[0] == seg_row_ref[0]

    def pair(step, carry):
        at = pl.multiple_of(step * LANES, LANES)
        queries = mixed_ref[:, pl.ds(at, LANES)]
        keys = mixed_ref[:, pl.ds(D + at, LANES)]
        values = mixed_ref[:, pl.ds(2 * D + at, LANES)]
        outs = []
        for half in range(2):
            cut = slice(half * HEAD, (half + 1) * HEAD)
            raw = dot32(keys[:, cut], queries[:, cut], 1, 1)
            scores = jnp.where(same, raw * (1.0 / math.sqrt(HEAD)), -1e30)
            peak = jnp.max(scores, axis=0, keepdims=True)
            lifted = jnp.exp(scores - peak)
            total = jnp.sum(lifted, axis=0, keepdims=True)
            probs = (lifted * (1.0 / total)).astype(low)
            outs.append(dot32(values[:, cut], probs, 0, 0))
            logsum_ref[0, pl.ds(2 * step + half, 1), :] = peak + jnp.log(total)
        context_ref[:, pl.ds(at, LANES)] = jnp.concatenate(outs, axis=0).T.astype(low)
        return carry

    lax.fori_loop(0, HEADS // 2, pair, 0)


def attend(mixed, segment):
    rows = segment.shape[0]
    return pl.pallas_call(
        attend_kernel,
        grid=(rows,),
        in_specs=[
            pl.BlockSpec((SEQ, 3 * D), lambda b: (b, 0)),
            pl.BlockSpec((1, SEQ, 1), lambda b: (b, 0, 0)),
            pl.BlockSpec((1, 1, SEQ), lambda b: (b, 0, 0)),
        ],
        out_specs=[
            pl.BlockSpec((SEQ, D), lambda b: (b, 0)),
            pl.BlockSpec((1, 16, SEQ), lambda b: (b, 0, 0)),
        ],
        out_shape=[
            jax.ShapeDtypeStruct((rows * SEQ, D), low),
            jax.ShapeDtypeStruct((rows, 16, SEQ), full),
        ],
        compiler_params=params(48),
        cost_estimate=cost(19),
        name="attend",
    )(mixed, segment[:, :, None], segment[:, None, :])


def attend_back_kernel(mixed_ref, grad_ref, logsum_ref, seg_col_ref, seg_row_ref, out_ref):
    same = seg_col_ref[0] == seg_row_ref[0]
    scale = 1.0 / math.sqrt(HEAD)

    def pair(step, carry):
        at = pl.multiple_of(step * LANES, LANES)
        queries = mixed_ref[:, pl.ds(at, LANES)]
        keys = mixed_ref[:, pl.ds(D + at, LANES)]
        values = mixed_ref[:, pl.ds(2 * D + at, LANES)]
        upstream = grad_ref[:, pl.ds(at, LANES)]
        query_grads, key_grads, value_grads = [], [], []
        for half in range(2):
            cut = slice(half * HEAD, (half + 1) * HEAD)
            logsum = logsum_ref[0, pl.ds(2 * step + half, 1), :]
            raw = dot32(keys[:, cut], queries[:, cut], 1, 1)
            probs = jnp.exp(jnp.where(same, raw * scale, -1e30) - logsum)
            prob_grads = dot32(values[:, cut], upstream[:, cut], 1, 1)
            value_grads.append(dot32(probs.astype(low), upstream[:, cut], 1, 0))
            moved = jnp.sum(prob_grads * probs, axis=0, keepdims=True)
            back = (probs * (prob_grads - moved) * scale).astype(low)
            key_grads.append(dot32(back, queries[:, cut], 1, 0))
            query_grads.append(dot32(keys[:, cut], back, 0, 0))
        out_ref[:, pl.ds(at, LANES)] = jnp.concatenate(query_grads, axis=0).T.astype(low)
        out_ref[:, pl.ds(D + at, LANES)] = jnp.concatenate(key_grads, axis=1).astype(low)
        out_ref[:, pl.ds(2 * D + at, LANES)] = jnp.concatenate(value_grads, axis=1).astype(low)
        return carry

    lax.fori_loop(0, HEADS // 2, pair, 0)


def attend_back(mixed, context_grad, logsum, segment):
    rows = segment.shape[0]
    return pl.pallas_call(
        attend_back_kernel,
        grid=(rows,),
        in_specs=[
            pl.BlockSpec((SEQ, 3 * D), lambda b: (b, 0)),
            pl.BlockSpec((SEQ, D), lambda b: (b, 0)),
            pl.BlockSpec((1, 16, SEQ), lambda b: (b, 0, 0)),
            pl.BlockSpec((1, SEQ, 1), lambda b: (b, 0, 0)),
            pl.BlockSpec((1, 1, SEQ), lambda b: (b, 0, 0)),
        ],
        out_specs=pl.BlockSpec((SEQ, 3 * D), lambda b: (b, 0)),
        out_shape=jax.ShapeDtypeStruct((rows * SEQ, 3 * D), low),
        compiler_params=params(56),
        cost_estimate=cost(28),
        name="attend_back",
    )(mixed, context_grad, logsum, segment[:, :, None], segment[:, None, :])


def lookup_kernel(ids_ref, table_ref, out_ref, turned_ref, rows_ref):
    step = pl.program_id(0)
    features, width = table_ref.shape
    tokens, chunk = out_ref.shape[0], rows_ref.shape[0]
    block = table_ref[...].astype(low).astype(full)
    block = jnp.concatenate([block, jnp.zeros((LANES - features, width), full)], axis=0)
    turned_ref[pl.ds(pl.multiple_of(step * width, width), width), :] = block.T

    @pl.when(step == pl.num_programs(0) - 1)
    def _():
        def piece(c, carry):
            def body(i, inner):
                at = i * 32
                found = [turned_ref[pl.ds(ids_ref[c * chunk + at + k], 1), :] for k in range(32)]
                for k in range(32):
                    rows_ref[pl.ds(at + k, 1), :] = found[k]
                return inner

            lax.fori_loop(0, chunk // 32, body, 0)
            start = pl.multiple_of(c * chunk, chunk)
            out_ref[pl.ds(start, chunk), :] = rows_ref[:, :features].astype(low)
            return carry

        lax.fori_loop(0, tokens // chunk, piece, 0)


def lookup(ids, table):
    features, vocab = table.shape
    width = -(-vocab // (4 * LANES)) * LANES
    steps = -(-vocab // width)
    return pl.pallas_call(
        lookup_kernel,
        grid=(steps,),
        in_specs=[smem(), pl.BlockSpec((features, width), lambda s: (0, s))],
        out_specs=pl.BlockSpec((ids.shape[0], features), lambda s: (0, 0)),
        out_shape=jax.ShapeDtypeStruct((ids.shape[0], features), low),
        scratch_shapes=[pltpu.VMEM((steps * width, LANES), full), pltpu.VMEM((1024, LANES), full)],
        compiler_params=params(56),
        cost_estimate=cost(19),
        name="lookup",
    )(ids, table)


def collect_kernel(place_ref, ids_ref, grads_ref, out_ref, square_ref, *scratch,
                   span, tokens, features, vocab):
    sums, rows_ref = scratch[:-1], scratch[-1]
    step = pl.program_id(0)
    last = pl.num_programs(0) - 1
    streams = len(sums)
    batch = 4 * streams

    @pl.when(step == 0)
    def _():
        for total in sums:
            total[...] = jnp.zeros_like(total)

    group = ids_ref[0] // span
    grads = grads_ref[0].astype(full)
    pad = jnp.zeros((WIDTH - features, tokens), full)
    pieces = []
    for at in range(GROUPS):
        pieces += [jnp.where(group == at, grads, 0.0), pad]
    rows_ref[...] = jnp.concatenate(pieces, axis=0).T

    def body(i, carry):
        for base in range(0, batch, streams):
            at = i * batch + base
            places = [pl.ds(place_ref[0, 0, at + k], 1) for k in range(streams)]
            olds = [sums[k][places[k], :] for k in range(streams)]
            news = [rows_ref[pl.ds(at + k, 1), :] for k in range(streams)]
            for k in range(streams):
                sums[k][places[k], :] = olds[k] + news[k]
        return carry

    lax.fori_loop(0, tokens // batch, body, 0)

    @pl.when(step == last)
    def _():
        def flush(b, total):
            at = pl.multiple_of(b * LANES, LANES)
            block = sums[0][pl.ds(at, LANES), :]
            for k in range(1, streams):
                block += sums[k][pl.ds(at, LANES), :]
            turned = block.T
            for g in range(GROUPS):
                piece = turned[g * WIDTH:g * WIDTH + features]

                @pl.when(g * span + at < vocab)
                def _():
                    out_ref[:, pl.ds(pl.multiple_of(g * span + at, LANES), LANES)] = piece.astype(low)

            return total + block * block

        total = lax.fori_loop(0, span // LANES, flush, jnp.zeros((LANES, LANES), full))
        square_ref[...] = jnp.broadcast_to(jnp.sum(total, keepdims=True), square_ref.shape)


def collect(ids, grads, vocab, tokens):
    sources, features = grads.shape[:2]
    span = -(-vocab // (GROUPS * LANES)) * LANES
    return pl.pallas_call(
        partial(collect_kernel, span=span, tokens=tokens, features=features, vocab=vocab),
        grid=(sources,),
        in_specs=[
            pl.BlockSpec((1, 1, tokens), lambda s: (s, 0, 0), memory_space=pltpu.SMEM),
            pl.BlockSpec((1, 1, tokens), lambda s: (s, 0, 0)),
            pl.BlockSpec((1, features, tokens), lambda s: (s, 0, 0)),
        ],
        out_specs=[
            pl.BlockSpec((features, vocab), lambda s: (0, 0)),
            pl.BlockSpec((8, LANES), lambda s: (0, 0)),
        ],
        out_shape=[
            jax.ShapeDtypeStruct((features, vocab), low),
            jax.ShapeDtypeStruct((8, LANES), full),
        ],
        scratch_shapes=[pltpu.VMEM((span, LANES), full)] * 8 + [pltpu.VMEM((tokens, LANES), full)],
        compiler_params=params(56),
        cost_estimate=cost(49),
        name="collect",
    )((ids % span)[:, None, :], ids[:, None, :], grads)


def moment_kernel(info_ref, factor_ref, grad_ref, old_ref, moment_ref, gram_ref, *, piece, block):
    factor = factor_ref[0]
    for at in range(old_ref.shape[0] // piece):
        source = pl.multiple_of(info_ref[2 + at] * piece, piece)
        rows = slice(at * piece, (at + 1) * piece)
        moment_ref[rows] = muon_beta * old_ref[rows] + factor * grad_ref[pl.ds(source, piece)].astype(full)
    gram_ref[...] = jnp.zeros_like(gram_ref)

    def body(b, carry):
        slot = (b * block >= info_ref[0]).astype(jnp.int32)
        high, small = halves(moment_ref[pl.ds(pl.multiple_of(b * block, block), block)])
        for at, (i, j) in enumerate(TILES):
            left, right = slice(i * BLOCK, (i + 1) * BLOCK), slice(j * BLOCK, (j + 1) * BLOCK)
            gram_ref[slot, at] += dot32(
                jnp.concatenate([high[:, left], high[:, left], small[:, left]], axis=0),
                jnp.concatenate([high[:, right], small[:, right], high[:, right]], axis=0),
                0,
                0,
            )
        return carry

    lax.fori_loop(0, old_ref.shape[0] // block, body, 0)


def moment_and_gram(info, factor, grad, old, piece, block):
    return pl.pallas_call(
        partial(moment_kernel, piece=piece, block=block),
        in_specs=[smem(), smem(), vmem(), vmem(), vmem()][:4],
        out_specs=[vmem(), vmem()],
        out_shape=[
            jax.ShapeDtypeStruct(old.shape, full),
            jax.ShapeDtypeStruct((2, len(TILES), BLOCK, BLOCK), full),
        ],
        compiler_params=params(56),
        cost_estimate=cost(10),
        name="moment",
    )(info, factor, grad, old)


def even_product(left, right, put):
    (lh, ll), (rh, rl) = left, right
    for i in range(D // BLOCK):
        rows = slice(i * BLOCK, (i + 1) * BLOCK)
        panel = jnp.concatenate([lh[rows], lh[rows], ll[rows]], axis=1)
        for j in range(i, D // BLOCK):
            cols = slice(j * BLOCK, (j + 1) * BLOCK)
            other = jnp.concatenate([rh[:, cols], rl[:, cols], rh[:, cols]], axis=0)
            put(rows, cols, dot32(panel, other, 1, 0))


def keep(pair):
    def put(rows, cols, value):
        pair[0][rows, cols], pair[1][rows, cols] = halves(value)
        if rows != cols:
            pair[0][cols, rows], pair[1][cols, rows] = halves(value.T)

    return put


def chain_kernel(gram_ref, out_ref, a_ref, *parts):
    a, q, p, t = [parts[2 * i:2 * i + 2] for i in range(4)]

    def diagonal(size):
        shape = (size, size)
        return lax.broadcasted_iota(jnp.int32, shape, 0) == lax.broadcasted_iota(jnp.int32, shape, 1)

    def put_a(rows, cols, value):
        a_ref[rows, cols] = value
        keep(a)(rows, cols, value)

    once = diagonal(BLOCK)
    trace = 0.0
    for at, (i, j) in enumerate(TILES):
        if i == j:
            trace = trace + jnp.sum(jnp.where(once, gram_ref[at], 0.0))
    scale = jnp.sqrt(trace) + 1e-07
    for at, (i, j) in enumerate(TILES):
        rows, cols = slice(i * BLOCK, (i + 1) * BLOCK), slice(j * BLOCK, (j + 1) * BLOCK)
        put_a(rows, cols, gram_ref[at] * (1.0 / (scale * scale)))

    def put_q(rows, cols, value):
        new = 2.0315 * value - 4.775 * a_ref[rows, cols]
        keep(q)(rows, cols, new + jnp.where(once, 3.4445, 0.0) if rows == cols else new)

    def put_out(rows, cols, value):
        value = value * (1.0 / scale)
        out_ref[rows, cols] = value
        if rows != cols:
            out_ref[cols, rows] = value.T

    def turn(k, carry):
        even_product(a, a, put_q)

        @pl.when(k == 0)
        def _():
            p[0][...], p[1][...] = q[0][...], q[1][...]

        @pl.when((k > 0) & (k < NS_TURNS - 1))
        def _():
            even_product(p, q, keep(t))
            p[0][...], p[1][...] = t[0][...], t[1][...]

        @pl.when(k == NS_TURNS - 1)
        def _():
            even_product(p, q, put_out)

        @pl.when(k < NS_TURNS - 1)
        def _():
            even_product(a, q, keep(t))
            even_product(t, q, put_a)

        return carry

    lax.fori_loop(0, NS_TURNS, turn, 0)


def chain(gram):
    return pl.pallas_call(
        chain_kernel,
        in_specs=[vmem()],
        out_specs=vmem(),
        out_shape=jax.ShapeDtypeStruct((D, D), full),
        scratch_shapes=[pltpu.VMEM((D, D), full)] + [pltpu.VMEM((D, D), low)] * 8,
        compiler_params=params(40),
        cost_estimate=cost(36),
        name="chain",
    )(gram)


def apply_kernel(info_ref, gain_ref, first_ref, second_ref, moment_ref, master_ref, new_ref, copy_ref,
                 *, block):
    split = info_ref[0] // block

    def over(slot, p_ref, start, stop):
        p = halves(p_ref[...])
        gain = gain_ref[slot] * muon_rate

        def body(b, carry):
            rows = pl.ds(pl.multiple_of(b * block, block), block)
            ortho = dot_split(halves(moment_ref[rows]), p)
            new = master_ref[rows] * (1.0 - muon_rate * muon_decay) - gain * ortho
            new_ref[rows] = new
            copy_ref[rows] = new.astype(low)
            return carry

        lax.fori_loop(start, stop, body, 0)

    over(0, first_ref, 0, split)
    total = moment_ref.shape[0] // block

    @pl.when(split < total)
    def _():
        over(1, second_ref, split, total)


def apply_chain(info, gains, first, second, moment, master, block):
    return pl.pallas_call(
        partial(apply_kernel, block=block),
        in_specs=[smem(), smem(), vmem(), vmem(), vmem(), vmem()],
        out_specs=[vmem(), vmem()],
        out_shape=[
            jax.ShapeDtypeStruct(moment.shape, full),
            jax.ShapeDtypeStruct(moment.shape, low),
        ],
        compiler_params=params(48),
        cost_estimate=cost(10),
        name="apply",
    )(info, gains, first, second, moment, master)


def chains(grams, wide_at, first_matrix, second_matrix, rider):
    wide = lax.axis_size("wide")
    if wide != 8:
        which = jnp.arange(4)
        slots = (which == first_matrix).astype(full)[:, None, None, None] * grams[0]
        slots = slots + (which == second_matrix).astype(full)[:, None, None, None] * grams[1]
        total = lax.psum(slots, "wide")
        return (
            chain(lax.dynamic_index_in_dim(total, first_matrix, 0, keepdims=False)),
            chain(lax.dynamic_index_in_dim(total, second_matrix, 0, keepdims=False)),
            rider,
        )
    half = len(TILES) // 2
    gram0, gram1 = grams[0], grams[1]
    pairs = [(i, i ^ 1) for i in range(8)]
    lower = wide_at % 2 == 0
    mine = jnp.where(wide_at == 2, gram1, gram0)
    moved = lax.ppermute(gram1[:half], "wide", [(5, 4)])
    chip = mine + lax.ppermute(mine, "wide", pairs)
    up_send = jnp.where(lower, chip[:half], chip[half:])
    down_send = jnp.where(wide_at == 4, moved, jnp.where(wide_at == 5, gram1[half:], up_send))
    up = up_send + lax.ppermute(up_send, "wide", [(2, 4), (4, 2), (3, 5), (5, 3)])
    down = down_send + lax.ppermute(down_send, "wide", [(4, 6), (6, 4), (5, 7), (7, 5)])
    send = jnp.where((wide_at == 4), down, up)
    send = jnp.where(wide_at >= 6, down, send)
    swap = lax.ppermute(send, "wide", [(2, 3), (4, 5), (6, 7), (7, 6)])
    back = lax.ppermute(up, "wide", [(5, 4)])
    kept = jnp.where(wide_at >= 5, down, up)
    other = jnp.where(wide_at == 4, back, swap)
    whole = jnp.concatenate([jnp.where(lower, kept, other), jnp.where(lower, other, kept)])
    gram = jnp.where(wide_at < 2, chip, jnp.where(wide_at == 2, gram0, whole))
    gram, rider = lax.optimization_barrier((gram, rider))
    own = chain(gram)
    come = lax.ppermute(own, "wide", [(3, 2), (4, 5)])
    return jnp.where(wide_at == 5, come, own), jnp.where(wide_at == 5, own, come), rider


def layout(lengths):
    row_ends = jnp.cumsum(lengths)
    starts = row_ends - lengths
    places = jnp.arange(SEQ, dtype=jnp.int32)
    segment = jnp.sum((places[:, None] >= row_ends[None, :]).astype(jnp.int32), axis=1)
    chosen = segment[:, None] == jnp.arange(SLOTS, dtype=jnp.int32)[None, :]
    start_at = jnp.sum(jnp.where(chosen, starts[None, :], 0), axis=1)
    length_at = jnp.sum(jnp.where(chosen, lengths[None, :], 0), axis=1)
    position = places - start_at
    second = (2 * position >= length_at).astype(jnp.int32)
    return (chosen.astype(full), position, second, segment)


def norm_forward(hidden, gain, bias):
    center = hidden - jnp.mean(hidden, axis=-1, keepdims=True)
    inverse = lax.rsqrt(jnp.mean(center * center, axis=-1, keepdims=True) + norm_eps)
    scaled = center * inverse
    return (scaled * gain + bias, scaled, inverse)


def norm_backward(upstream, scaled, inverse, gain):
    weighted = upstream * gain
    back = inverse * (
        weighted
        - jnp.mean(weighted, axis=-1, keepdims=True)
        - scaled * jnp.mean(weighted * scaled, axis=-1, keepdims=True)
    )
    return (back, jnp.sum(upstream * scaled, axis=0), jnp.sum(upstream, axis=0))


def project(left, right):
    return jnp.dot(left, right, preferred_element_type=full)


def task_loss(logits, scores, tasks, labels, negatives, counts):
    logprob = jax.nn.log_softmax(logits, axis=-1)
    picked = jnp.sum(
        jnp.where(labels[:, :, None] == jnp.arange(3, dtype=jnp.int32), logprob, 0.0), axis=2
    )
    chosen = negatives[:, :, :, None] == jnp.arange(scores.shape[1], dtype=jnp.int32)
    rivals = jnp.sum(jnp.where(chosen, scores[:, None, None, :], 0.0), axis=3)
    together = jnp.concatenate([scores[:, :, None], rivals], axis=2)
    ranking = jax.nn.logsumexp(together, axis=2) - scores
    first_part = jnp.sum(jnp.where(tasks == 0, -picked, 0.0)) / counts[0]
    return first_part + jnp.sum(jnp.where(tasks == 1, ranking, 0.0)) / counts[1]


def adam(weight, grad, first, second, step, rate):
    first = beta_one * first + (1.0 - beta_one) * grad
    second = beta_two * second + (1.0 - beta_two) * grad * grad
    unbiased = first / (1.0 - beta_one**step)
    spread = second / (1.0 - beta_two**step)
    return (
        weight - rate * (unbiased / (jnp.sqrt(spread) + adam_eps) + adam_decay * weight),
        first,
        second,
    )


def broadcast_all(x):
    count = lax.axis_size("narrow") * lax.axis_size("wide")
    return lax.all_to_all(
        jnp.broadcast_to(x[None], (count,) + x.shape), BOTH, split_axis=0, concat_axis=0, tiled=True
    )


def sides(wide):
    return [list(range(0, wide, 2)), list(range(1, wide, 2))]


def chip_mates(wide):
    return [(i, i ^ 1) for i in range(wide)]


def by_owner(grad, spans, parts):
    pieces = [
        grad[lo:hi].reshape(parts, (hi - lo) // parts, D) for lo, hi in spans
    ]
    return jnp.concatenate(pieces, axis=1).reshape(-1, D).astype(low)


def gather_weights(master, narrow_at, wide_at, first):
    wide = lax.axis_size("wide")
    if wide != 8:
        whole = lax.all_gather(master.astype(low), "wide", axis=0, tiled=True)
        return first, list(whole.reshape(wide, -1, D))
    share = master.shape[0] // lax.axis_size("narrow")
    mine = lax.dynamic_slice_in_dim(master, narrow_at * share, share, 0).astype(low)
    near = lax.all_gather(mine, "wide", axis=0, tiled=False, axis_index_groups=sides(wide))
    near, first = lax.optimization_barrier((near, first))
    return first, [
        lax.all_gather(part, "narrow", axis=1, tiled=True)
        for part in (near[: wide // 4], near[wide // 4 :])
    ]


def both_cores(held, wide_at):
    owners = []
    other = lax.ppermute(held, "wide", chip_mates(lax.axis_size("wide")))
    side = wide_at % 2
    even = jnp.where(side == 0, held, other)
    odd = jnp.where(side == 0, other, held)
    for at in range(held.shape[0]):
        owners += [even[at], odd[at]]
    return owners


def rows_of(owners, matrix):
    rows = owners[0].shape[0]
    lo, hi = BOUNDS[matrix], BOUNDS[matrix + 1]
    pieces = []
    for at in range(lo // rows, -(-hi // rows)):
        pieces.append(owners[at][max(lo - at * rows, 0) : min(hi - at * rows, rows)])
    return jnp.concatenate(pieces) if len(pieces) > 1 else pieces[0]


def shards(
    token_ids,
    seq_lengths,
    task_ids,
    labels,
    negatives,
    step_count,
    hidden_master,
    hidden_momentum,
    table_master,
    table_first,
    table_second,
    pos_types,
    pos_first,
    pos_second,
    vectors,
    vec_first,
    vec_second,
):
    wide_at = lax.axis_index("wide")
    narrow_at = lax.axis_index("narrow")
    wide = lax.axis_size("wide")
    narrow = lax.axis_size("narrow")
    count = wide * narrow
    device_at = narrow_at * wide + wide_at
    micro_count, rows_each = token_ids.shape[:2]
    batch = micro_count * rows_each
    tokens = batch * SEQ
    shard = hidden_master.shape[0]
    vocab = table_master.shape[1]
    features = table_master.shape[0] // narrow
    pairs_each = rows_each * SLOTS

    parts = [token_ids, task_ids, labels, negatives]
    sizes = [part.size for part in parts]
    packed = jnp.concatenate([part.reshape(-1) for part in parts])
    packed = jnp.pad(packed, (0, -packed.size % LANES))
    gathered = broadcast_all(packed)
    ends = [sum(sizes[: i + 1]) for i in range(len(sizes))]
    ids_all = gathered[:, : ends[0]]

    def pairs_of(lo, hi, tail):
        block = gathered[:, lo:hi].reshape((count, micro_count, pairs_each) + tail)
        return jnp.moveaxis(block, 1, 0).reshape((micro_count, count * pairs_each) + tail)

    tasks_all = pairs_of(ends[0], ends[1], ())
    labels_all = pairs_of(ends[1], ends[2], ())
    negatives_all = pairs_of(ends[2], ends[3], (NEG,))
    counts = jnp.stack(
        [jnp.sum((tasks_all == 0).astype(full)), jnp.sum((tasks_all == 1).astype(full))]
    )


    group_ids = lax.dynamic_slice_in_dim(ids_all, narrow_at * wide, wide, 0).reshape(-1)
    pieces = lookup(group_ids, table_master)
    pieces, gathers = gather_weights(hidden_master, narrow_at, wide_at, pieces)
    simple = wide != 8
    owners = gathers if simple else both_cores(gathers[0], wide_at)
    arrived = lax.all_to_all(
        pieces.reshape(wide, tokens, -1), "wide", split_axis=0, concat_axis=0, tiled=True
    )
    token_rows = jnp.moveaxis(arrived, 0, 1).reshape(tokens, D)

    lengths = seq_lengths.reshape(batch, SLOTS)
    member, position, second, segment = jax.vmap(layout)(lengths)
    flat_position = position.reshape(-1)
    flat_second = second.reshape(-1)
    embed = token_rows.astype(full) + pos_types[flat_position]
    embed = embed + jnp.where(flat_second[:, None] == 1, pos_types[SEQ + 1], pos_types[SEQ])
    normed0, scaled0, inverse0 = norm_forward(embed, vectors[0], vectors[1])
    input0 = normed0.astype(low)
    qkv_bias = jnp.concatenate([vectors[6], jnp.zeros_like(vectors[6]), vectors[7]])
    weight_qkv, weight_out = rows_of(owners, 0), rows_of(owners, 1)
    mixed = (project(input0, weight_qkv.T) + qkv_bias).astype(low)
    context_low, logsum = attend(mixed, segment)
    if not simple:
        rest, context_low = lax.optimization_barrier((gathers[1], context_low))
        owners = owners + both_cores(rest, wide_at)
    weight_up, weight_down = rows_of(owners, 2), rows_of(owners, 3)
    attended = project(context_low, weight_out.T) + vectors[8]
    normed1, scaled1, inverse1 = norm_forward(normed0 + attended, vectors[2], vectors[3])
    input1 = normed1.astype(low)
    inner = project(input1, weight_up.T) + vectors[14:].reshape(-1)
    cdf = 0.5 * (1.0 + lax.erf(inner * math.sqrt(0.5)))
    active = (inner * cdf).astype(low)
    slope = cdf + inner * (jnp.exp(-0.5 * inner * inner) * (1.0 / math.sqrt(2.0 * math.pi)))
    branch = project(active, weight_down) + vectors[9]
    normed2, scaled2, inverse2 = norm_forward(normed1 + branch, vectors[4], vectors[5])
    share = member / lengths.astype(full)[:, None, :]
    pooled = jnp.einsum("rps,rpd->rsd", share, normed2.reshape(batch, SEQ, D), precision=highest)
    flat_pooled = pooled.reshape(-1, D)
    heads = vectors[10:14]
    head_out = jnp.dot(flat_pooled, heads.T, precision=highest)

    sent = jnp.pad(head_out.reshape(-1), (0, -head_out.size % LANES))
    head_all = broadcast_all(sent)[:, : head_out.size]
    head_all = head_all.reshape(count, micro_count, pairs_each, 4)
    head_all = jnp.moveaxis(head_all, 1, 0).reshape(micro_count, count * pairs_each, 4)

    def objective(every):
        return task_loss(every[:, :, :3], every[:, :, 3], tasks_all, labels_all, negatives_all, counts)

    loss, pullback = jax.vjp(objective, head_all)
    head_grads = pullback(jnp.ones_like(loss))[0]
    output_grads = lax.dynamic_slice_in_dim(head_grads, device_at * pairs_each, pairs_each, 1)
    output_grads = output_grads.reshape(-1, 4)
    heads_grad = jnp.dot(output_grads.T, flat_pooled, precision=highest)
    pooled_grads = jnp.dot(output_grads, heads, precision=highest).reshape(pooled.shape)

    spread = jnp.einsum("rps,rsd->rpd", share, pooled_grads, precision=highest).reshape(-1, D)
    sum2_grad, gain2, bias2 = norm_backward(spread, scaled2, inverse2, vectors[4])
    branch_grad = sum2_grad.astype(low)
    down_grad = project(active.T, branch_grad)
    spans_down = [(0, 768), (768, 1920), (1920, 3072)]
    spans_up = [(0, 384), (384, 1536), (1536, 2688), (2688, 3072)]
    spans_front = [(0, 1152), (1152, 2304), (2304, 3072)]

    side = wide_at % 2

    def ready(grad, spans):
        if simple:
            return grad.astype(low)
        grad = by_owner(grad, spans, narrow)
        left, right = grad[:, : D // 2], grad[:, D // 2 :]
        stays = jnp.where(side == 0, left, right)
        leaves = jnp.where(side == 0, right, left)
        return stays, leaves

    def between_cores(grad):
        if simple:
            return grad
        stays, leaves = grad
        return stays, lax.ppermute(leaves, "wide", chip_mates(wide))

    def slices(grad):
        if simple:
            return [grad]
        stays, comes = grad
        chip = (stays.astype(full) + comes.astype(full)).astype(low).reshape(narrow, -1, D // 2)
        return [chip[narrow_at ^ turn] for turn in range(narrow)]

    def over_narrow(parts):
        return parts[:1] + [
            lax.ppermute(part, "narrow", [(i, i ^ (turn + 1)) for i in range(narrow)])
            for turn, part in enumerate(parts[1:])
        ]

    together = lax.optimization_barrier
    down_send, after_down = together((ready(down_grad, spans_down), branch_grad))
    down_pair = between_cores(down_send)
    active_grad = project(after_down, weight_down.T)
    inner_grad = (active_grad * slope).astype(low)
    up_grad = project(inner_grad.T, input1)
    up_send, down_pair, after_up = together((ready(up_grad, spans_up), down_pair, inner_grad))
    up_pair = between_cores(up_send)
    down_cut, after_up = together((slices(down_pair), after_up))
    down_part = over_narrow(down_cut)
    normed1_grad = sum2_grad + project(after_up, weight_up)
    sum1_grad, gain1, bias1 = norm_backward(normed1_grad, scaled1, inverse1, vectors[2])
    attended_grad = sum1_grad.astype(low)
    up_pair, attended_grad = together((up_pair, attended_grad))
    out_grad = project(attended_grad.T, context_low)
    context_grad = project(attended_grad, weight_out).astype(low)
    up_cut, context_grad = together((slices(up_pair), context_grad))
    up_part = over_narrow(up_cut)
    mixed_grad = attend_back(mixed, context_grad, logsum, segment)
    mixed_grad, up_part, down_part = together((mixed_grad, up_part, down_part))
    qkv_grad = project(mixed_grad.T, input0)
    front_grad = jnp.concatenate([qkv_grad.astype(low), out_grad.astype(low)])
    front_send, after_front = together((ready(front_grad, spans_front), mixed_grad))
    front_pair = between_cores(front_send)
    normed0_grad = sum1_grad + project(after_front, weight_qkv)
    embed_grad, gain0, bias0 = norm_backward(normed0_grad, scaled0, inverse0, vectors[0])
    mixed_sum = jnp.sum(mixed_grad.astype(full), axis=0)
    small_rows = jnp.stack(
        [
            gain0,
            bias0,
            gain1,
            bias1,
            gain2,
            bias2,
            mixed_sum[:D],
            mixed_sum[2 * D :],
            jnp.sum(attended_grad.astype(full), axis=0),
            jnp.sum(branch_grad.astype(full), axis=0),
        ]
    )
    up_rows = jnp.sum(inner_grad.astype(full), axis=0).reshape(-1, D)

    places = jnp.arange(SEQ, dtype=jnp.int32)[:, None]
    row_hot = jnp.concatenate(
        [
            flat_position[None] == places,
            jnp.stack([flat_second == 0, flat_second == 1]),
        ]
    ).astype(low)
    high_part, low_part = halves(embed_grad)
    pos_grad = project(jnp.concatenate([row_hot, row_hot], axis=1), jnp.concatenate([high_part, low_part]))
    small = jnp.concatenate([pos_grad, small_rows, heads_grad, up_rows])
    small_count = small.shape[0]
    small = jnp.pad(small, ((0, count * features - small_count), (0, 0)))

    embed_low, front_pair = together((embed_grad.astype(low), front_pair))
    front_part = over_narrow(slices(front_pair))
    table_send = embed_low.T.reshape(wide, narrow, features, tokens)
    table_send = jnp.moveaxis(table_send, 1, 0).reshape(count, features, tokens)
    come = lax.all_to_all(table_send, BOTH, split_axis=0, concat_axis=0, tiled=True)

    def added(parts):
        return sum(part.astype(full) for part in parts).astype(low)

    joined = jnp.concatenate([added(front_part), added(up_part), added(down_part)])
    small_send = small.astype(low).reshape(count, features, D)
    joined, come, small_send = together((joined, come, small_send))
    small_come = lax.all_to_all(small_send, BOTH, split_axis=0, concat_axis=0, tiled=True)
    table_part, table_square = collect(ids_all, come, vocab, tokens)
    if simple:
        hidden_part = lax.psum_scatter(joined, "wide", scatter_dimension=0, tiled=True)
        hidden_part = lax.psum_scatter(hidden_part, "narrow", scatter_dimension=0, tiled=True)
        hidden_square = jnp.sum(jnp.square(hidden_part.astype(full)))
    else:
        owned = lax.psum_scatter(
            joined, "wide", scatter_dimension=0, tiled=True, axis_index_groups=sides(wide)
        )
        owned, table_square, small_come = together((owned, table_square, small_come))
        hidden_square = jnp.sum(jnp.square(owned.astype(full)))
        half = owned.shape[0] // 2
        stays = jnp.where(side == 0, owned[:half], owned[half:])
        leaves = jnp.where(side == 0, owned[half:], owned[:half])
        comes = lax.ppermute(leaves, "wide", chip_mates(wide))
        hidden_part = jnp.concatenate(
            [jnp.where(side == 0, stays, comes), jnp.where(side == 0, comes, stays)], axis=1
        )
    small_part = jnp.sum(small_come.astype(full), axis=0)
    square = hidden_square + table_square[0, 0] + jnp.sum(small_part * small_part)
    square, hidden_part = together((square, hidden_part))
    if simple:
        hidden_all = lax.all_gather(hidden_part, "narrow", axis=0, tiled=True)
    else:
        hidden_all = jnp.concatenate(
            [hidden_part]
            + [
                lax.ppermute(hidden_part, "narrow", [(i, i ^ turn) for i in range(narrow)])
                for turn in range(1, narrow)
            ]
        )
    squares = broadcast_all(jnp.broadcast_to(square, (LANES,)))
    squares, hidden_all, table_part = together((squares, hidden_all, table_part))
    table_grad = lax.all_gather(table_part, "narrow", axis=0, tiled=True)
    clip_norm = jnp.sqrt(jnp.sum(squares[:, 0]))
    factor = jnp.minimum(1.0, clip_bound / clip_norm)

    start = wide_at * shard
    bounds = jnp.array(BOUNDS, jnp.int32)
    first_matrix = jnp.sum((start >= bounds[1:4]).astype(jnp.int32))
    second_matrix = jnp.sum((start + shard - 1 >= bounds[1:4]).astype(jnp.int32))
    split = jnp.minimum(bounds[first_matrix + 1] - start, shard)
    block = shard // 3
    piece = shard // 12
    at = jnp.arange(12, dtype=jnp.int32)
    if simple:
        source = at
    else:
        lead = split // piece
        each = lead // narrow
        rest = (12 - lead) // narrow
        in_first = at < lead
        inside = jnp.where(in_first, at, at - lead)
        width = jnp.maximum(jnp.where(in_first, each, rest), 1)
        origin = (inside // width) ^ narrow_at
        source = origin * (12 // narrow) + jnp.where(in_first, 0, each) + inside % width
    info = jnp.concatenate([jnp.stack([split, split]), source]).astype(jnp.int32)
    gains = jnp.array([0.2 * math.sqrt(hi - lo) for lo, hi in zip(BOUNDS, BOUNDS[1:])], full)
    moment, grams = moment_and_gram(info, factor[None], hidden_all, hidden_momentum, piece, block)
    chain0, chain1, (late_small, table_grad) = chains(
        grams, wide_at, first_matrix, second_matrix, (small_part, table_grad)
    )
    small_all = broadcast_all(late_small.astype(low)).reshape(-1, D)[:small_count].astype(full)
    slot_gains = jnp.stack([gains[first_matrix], gains[second_matrix]])
    hidden_new, hidden_copy = apply_chain(info, slot_gains, chain0, chain1, moment, hidden_master, block)

    step = step_count[0].astype(full)
    table_new, table_first_new, table_second_new = adam(
        table_master, factor * table_grad.astype(full), table_first, table_second, step, 0.02
    )
    pos_new, pos_first_new, pos_second_new = adam(
        pos_types, factor * small_all[: SEQ + 2], pos_first, pos_second, step, 0.02
    )
    vectors_new, vec_first_new, vec_second_new = adam(
        vectors, factor * small_all[SEQ + 2 :], vec_first, vec_second, step, 0.2
    )
    return (
        loss,
        clip_norm,
        moment,
        hidden_new,
        hidden_copy,
        table_new,
        table_first_new,
        table_second_new,
        table_new.astype(low),
        pos_new,
        pos_first_new,
        pos_second_new,
        vectors_new,
        vec_first_new,
        vec_second_new,
    )


def solution(mesh):
    rows = P(None, BOTH, None)
    owned = P("wide", None)
    return jax.shard_map(
        shards,
        mesh=mesh,
        in_specs=(rows, rows, rows, rows, P(None, BOTH, None, None), P())
        + (owned,) * 5
        + (P(),) * 6,
        out_specs=(P(), P()) + (owned,) * 7 + (P(),) * 6,
        check_vma=False,
    )
```

```python
from functools import partial
import math

import jax
import jax.numpy as jnp
from jax import lax
from jax.experimental import pallas as pl
from jax.experimental.pallas import tpu as pltpu
from jax.sharding import PartitionSpec as P

D = 768
HEADS = 12
HEAD = 64
FF = 3072
SEQ = 512
SLOTS = 4
NEG = 4
NS_TURNS = 5
LANES = 128
GROUPS = 4
WIDTH = LANES // GROUPS
BLOCK = 256
TILES = [(i, j) for i in range(D // BLOCK) for j in range(i, D // BLOCK)]

BOTH = ("narrow", "wide")
highest = lax.Precision.HIGHEST
clip_bound = 0.002
norm_eps = 1e-06
muon_beta = 0.95
muon_rate = 0.1
muon_decay = 0.01
beta_one = 0.9
beta_two = 0.999
adam_eps = 1e-08
adam_decay = 0.01
BOUNDS = (0, 3 * D, 4 * D, 4 * D + FF, 4 * D + 2 * FF)

low = jnp.bfloat16
full = jnp.float32


def dims(left, right):
    return (((left,), (right,)), ((), ()))


def dot32(left, right, left_dim, right_dim):
    return lax.dot_general(left, right, dims(left_dim, right_dim), preferred_element_type=full)


def halves(x):
    high = x.astype(low)
    return high, (x - high.astype(full)).astype(low)


def dot_split(left, right, left_dim=1, right_dim=0):
    (lh, ll), (rh, rl) = left, right
    return dot32(lh, rh, left_dim, right_dim) + (
        dot32(lh, rl, left_dim, right_dim) + dot32(ll, rh, left_dim, right_dim)
    )


def params(mib):
    return pltpu.CompilerParams(vmem_limit_bytes=mib << 20)


def cost(micros):
    return pl.CostEstimate(flops=micros * 10**9, transcendentals=0, bytes_accessed=1 << 20)


def vmem():
    return pl.BlockSpec(memory_space=pltpu.VMEM)


def smem():
    return pl.BlockSpec(memory_space=pltpu.SMEM)


def attend_kernel(mixed_ref, seg_col_ref, seg_row_ref, context_ref, logsum_ref):
    same = seg_col_ref[0] == seg_row_ref[0]

    def pair(step, carry):
        at = pl.multiple_of(step * LANES, LANES)
        queries = mixed_ref[:, pl.ds(at, LANES)]
        keys = mixed_ref[:, pl.ds(D + at, LANES)]
        values = mixed_ref[:, pl.ds(2 * D + at, LANES)]
        outs = []
        for half in range(2):
            cut = slice(half * HEAD, (half + 1) * HEAD)
            raw = dot32(keys[:, cut], queries[:, cut], 1, 1)
            scores = jnp.where(same, raw * (1.0 / math.sqrt(HEAD)), -1e30)
            peak = jnp.max(scores, axis=0, keepdims=True)
            lifted = jnp.exp(scores - peak)
            total = jnp.sum(lifted, axis=0, keepdims=True)
            probs = (lifted * (1.0 / total)).astype(low)
            outs.append(dot32(values[:, cut], probs, 0, 0))
            logsum_ref[0, pl.ds(2 * step + half, 1), :] = peak + jnp.log(total)
        context_ref[:, pl.ds(at, LANES)] = jnp.concatenate(outs, axis=0).T.astype(low)
        return carry

    lax.fori_loop(0, HEADS // 2, pair, 0)


def attend(mixed, segment):
    rows = segment.shape[0]
    return pl.pallas_call(
        attend_kernel,
        grid=(rows,),
        in_specs=[
            pl.BlockSpec((SEQ, 3 * D), lambda b: (b, 0)),
            pl.BlockSpec((1, SEQ, 1), lambda b: (b, 0, 0)),
            pl.BlockSpec((1, 1, SEQ), lambda b: (b, 0, 0)),
        ],
        out_specs=[
            pl.BlockSpec((SEQ, D), lambda b: (b, 0)),
            pl.BlockSpec((1, 16, SEQ), lambda b: (b, 0, 0)),
        ],
        out_shape=[
            jax.ShapeDtypeStruct((rows * SEQ, D), low),
            jax.ShapeDtypeStruct((rows, 16, SEQ), full),
        ],
        compiler_params=params(48),
        cost_estimate=cost(19),
        name="attend",
    )(mixed, segment[:, :, None], segment[:, None, :])


def attend_back_kernel(mixed_ref, grad_ref, logsum_ref, seg_col_ref, seg_row_ref, out_ref):
    same = seg_col_ref[0] == seg_row_ref[0]
    scale = 1.0 / math.sqrt(HEAD)

    def pair(step, carry):
        at = pl.multiple_of(step * LANES, LANES)
        queries = mixed_ref[:, pl.ds(at, LANES)]
        keys = mixed_ref[:, pl.ds(D + at, LANES)]
        values = mixed_ref[:, pl.ds(2 * D + at, LANES)]
        upstream = grad_ref[:, pl.ds(at, LANES)]
        query_grads, key_grads, value_grads = [], [], []
        for half in range(2):
            cut = slice(half * HEAD, (half + 1) * HEAD)
            logsum = logsum_ref[0, pl.ds(2 * step + half, 1), :]
            raw = dot32(keys[:, cut], queries[:, cut], 1, 1)
            probs = jnp.exp(jnp.where(same, raw * scale, -1e30) - logsum)
            prob_grads = dot32(values[:, cut], upstream[:, cut], 1, 1)
            value_grads.append(dot32(probs.astype(low), upstream[:, cut], 1, 0))
            moved = jnp.sum(prob_grads * probs, axis=0, keepdims=True)
            back = (probs * (prob_grads - moved) * scale).astype(low)
            key_grads.append(dot32(back, queries[:, cut], 1, 0))
            query_grads.append(dot32(keys[:, cut], back, 0, 0))
        out_ref[:, pl.ds(at, LANES)] = jnp.concatenate(query_grads, axis=0).T.astype(low)
        out_ref[:, pl.ds(D + at, LANES)] = jnp.concatenate(key_grads, axis=1).astype(low)
        out_ref[:, pl.ds(2 * D + at, LANES)] = jnp.concatenate(value_grads, axis=1).astype(low)
        return carry

    lax.fori_loop(0, HEADS // 2, pair, 0)


def attend_back(mixed, context_grad, logsum, segment):
    rows = segment.shape[0]
    return pl.pallas_call(
        attend_back_kernel,
        grid=(rows,),
        in_specs=[
            pl.BlockSpec((SEQ, 3 * D), lambda b: (b, 0)),
            pl.BlockSpec((SEQ, D), lambda b: (b, 0)),
            pl.BlockSpec((1, 16, SEQ), lambda b: (b, 0, 0)),
            pl.BlockSpec((1, SEQ, 1), lambda b: (b, 0, 0)),
            pl.BlockSpec((1, 1, SEQ), lambda b: (b, 0, 0)),
        ],
        out_specs=pl.BlockSpec((SEQ, 3 * D), lambda b: (b, 0)),
        out_shape=jax.ShapeDtypeStruct((rows * SEQ, 3 * D), low),
        compiler_params=params(56),
        cost_estimate=cost(28),
        name="attend_back",
    )(mixed, context_grad, logsum, segment[:, :, None], segment[:, None, :])


def lookup_kernel(ids_ref, table_ref, out_ref, turned_ref, rows_ref):
    step = pl.program_id(0)
    features, width = table_ref.shape
    tokens, chunk = out_ref.shape[0], rows_ref.shape[0]
    block = table_ref[...].astype(low).astype(full)
    block = jnp.concatenate([block, jnp.zeros((LANES - features, width), full)], axis=0)
    turned_ref[pl.ds(pl.multiple_of(step * width, width), width), :] = block.T

    @pl.when(step == pl.num_programs(0) - 1)
    def _():
        def piece(c, carry):
            def body(i, inner):
                at = i * 32
                found = [turned_ref[pl.ds(ids_ref[c * chunk + at + k], 1), :] for k in range(32)]
                for k in range(32):
                    rows_ref[pl.ds(at + k, 1), :] = found[k]
                return inner

            lax.fori_loop(0, chunk // 32, body, 0)
            start = pl.multiple_of(c * chunk, chunk)
            out_ref[pl.ds(start, chunk), :] = rows_ref[:, :features].astype(low)
            return carry

        lax.fori_loop(0, tokens // chunk, piece, 0)


def lookup(ids, table):
    features, vocab = table.shape
    width = -(-vocab // (4 * LANES)) * LANES
    steps = -(-vocab // width)
    return pl.pallas_call(
        lookup_kernel,
        grid=(steps,),
        in_specs=[smem(), pl.BlockSpec((features, width), lambda s: (0, s))],
        out_specs=pl.BlockSpec((ids.shape[0], features), lambda s: (0, 0)),
        out_shape=jax.ShapeDtypeStruct((ids.shape[0], features), low),
        scratch_shapes=[pltpu.VMEM((steps * width, LANES), full), pltpu.VMEM((1024, LANES), full)],
        compiler_params=params(56),
        cost_estimate=cost(19),
        name="lookup",
    )(ids, table)


def collect_kernel(place_ref, ids_ref, grads_ref, out_ref, square_ref, *scratch,
                   span, tokens, features, vocab):
    sums, rows_ref = scratch[:-1], scratch[-1]
    step = pl.program_id(0)
    last = pl.num_programs(0) - 1
    streams = len(sums)
    batch = 4 * streams

    @pl.when(step == 0)
    def _():
        for total in sums:
            total[...] = jnp.zeros_like(total)

    group = ids_ref[0] // span
    grads = grads_ref[0].astype(full)
    pad = jnp.zeros((WIDTH - features, tokens), full)
    pieces = []
    for at in range(GROUPS):
        pieces += [jnp.where(group == at, grads, 0.0), pad]
    rows_ref[...] = jnp.concatenate(pieces, axis=0).T

    def body(i, carry):
        for base in range(0, batch, streams):
            at = i * batch + base
            places = [pl.ds(place_ref[0, 0, at + k], 1) for k in range(streams)]
            olds = [sums[k][places[k], :] for k in range(streams)]
            news = [rows_ref[pl.ds(at + k, 1), :] for k in range(streams)]
            for k in range(streams):
                sums[k][places[k], :] = olds[k] + news[k]
        return carry

    lax.fori_loop(0, tokens // batch, body, 0)

    @pl.when(step == last)
    def _():
        def flush(b, total):
            at = pl.multiple_of(b * LANES, LANES)
            block = sums[0][pl.ds(at, LANES), :]
            for k in range(1, streams):
                block += sums[k][pl.ds(at, LANES), :]
            turned = block.T
            for g in range(GROUPS):
                piece = turned[g * WIDTH:g * WIDTH + features]

                @pl.when(g * span + at < vocab)
                def _():
                    out_ref[:, pl.ds(pl.multiple_of(g * span + at, LANES), LANES)] = piece.astype(low)

            return total + block * block

        total = lax.fori_loop(0, span // LANES, flush, jnp.zeros((LANES, LANES), full))
        square_ref[...] = jnp.broadcast_to(jnp.sum(total, keepdims=True), square_ref.shape)


def collect(ids, grads, vocab, tokens):
    sources, features = grads.shape[:2]
    span = -(-vocab // (GROUPS * LANES)) * LANES
    return pl.pallas_call(
        partial(collect_kernel, span=span, tokens=tokens, features=features, vocab=vocab),
        grid=(sources,),
        in_specs=[
            pl.BlockSpec((1, 1, tokens), lambda s: (s, 0, 0), memory_space=pltpu.SMEM),
            pl.BlockSpec((1, 1, tokens), lambda s: (s, 0, 0)),
            pl.BlockSpec((1, features, tokens), lambda s: (s, 0, 0)),
        ],
        out_specs=[
            pl.BlockSpec((features, vocab), lambda s: (0, 0)),
            pl.BlockSpec((8, LANES), lambda s: (0, 0)),
        ],
        out_shape=[
            jax.ShapeDtypeStruct((features, vocab), low),
            jax.ShapeDtypeStruct((8, LANES), full),
        ],
        scratch_shapes=[pltpu.VMEM((span, LANES), full)] * 8 + [pltpu.VMEM((tokens, LANES), full)],
        compiler_params=params(56),
        cost_estimate=cost(150),
        name="collect",
    )((ids % span)[:, None, :], ids[:, None, :], grads)


def moment_kernel(info_ref, factor_ref, grad_ref, old_ref, moment_ref, mine_ref, other_ref,
                  *, piece, block):
    factor = factor_ref[0]
    for at in range(old_ref.shape[0] // piece):
        source = pl.multiple_of(info_ref[2 + at] * piece, piece)
        rows = slice(at * piece, (at + 1) * piece)
        moment_ref[rows] = muon_beta * old_ref[rows] + factor * grad_ref[pl.ds(source, piece)].astype(full)

    def grams(out_ref, start, stop):
        out_ref[...] = jnp.zeros_like(out_ref)

        def body(b, carry):
            high, small = halves(moment_ref[pl.ds(pl.multiple_of(b * block, block), block)])
            for at, (i, j) in enumerate(TILES):
                left, right = slice(i * BLOCK, (i + 1) * BLOCK), slice(j * BLOCK, (j + 1) * BLOCK)
                out_ref[at] += dot32(
                    jnp.concatenate([high[:, left], high[:, left], small[:, left]], axis=0),
                    jnp.concatenate([high[:, right], small[:, right], high[:, right]], axis=0),
                    0,
                    0,
                )
            return carry

        lax.fori_loop(start, stop, body, 0)

    lead, total = info_ref[0] // block, old_ref.shape[0] // block
    swap = info_ref[1] == 1
    grams(mine_ref, jnp.where(swap, lead, 0), jnp.where(swap, total, lead))
    grams(other_ref, jnp.where(swap, 0, lead), jnp.where(swap, lead, total))


def moment_and_grams(info, factor, grad, old, piece, block):
    tiles = jax.ShapeDtypeStruct((len(TILES), BLOCK, BLOCK), full)
    return pl.pallas_call(
        partial(moment_kernel, piece=piece, block=block),
        in_specs=[smem(), smem(), vmem(), vmem()],
        out_specs=[vmem()] * 3,
        out_shape=[jax.ShapeDtypeStruct(old.shape, full), tiles, tiles],
        compiler_params=params(48),
        cost_estimate=cost(10),
        name="moment",
    )(info, factor, grad, old)


def even_product(left, right, put):
    (lh, ll), (rh, rl) = left, right
    for i in range(D // BLOCK):
        rows = slice(i * BLOCK, (i + 1) * BLOCK)
        panel = jnp.concatenate([lh[rows], lh[rows], ll[rows]], axis=1)
        for j in range(i, D // BLOCK):
            cols = slice(j * BLOCK, (j + 1) * BLOCK)
            other = jnp.concatenate([rh[:, cols], rl[:, cols], rh[:, cols]], axis=0)
            put(rows, cols, dot32(panel, other, 1, 0))


def keep(pair):
    def put(rows, cols, value):
        pair[0][rows, cols], pair[1][rows, cols] = halves(value)
        if rows != cols:
            pair[0][cols, rows], pair[1][cols, rows] = halves(value.T)

    return put


def chain_kernel(kind_ref, factor_ref, debias_ref, chip_ref, other_ref, kept_ref, got_ref,
                 grad_ref, weight_ref, first_ref, second_ref,
                 out_ref, weight_new_ref, first_new_ref, second_new_ref, copy_ref,
                 a_ref, scale_ref, *parts, chunks):
    a, q, p, t = [parts[2 * i:2 * i + 2] for i in range(4)]
    step = pl.program_id(0)
    shape = (BLOCK, BLOCK)
    once = lax.broadcasted_iota(jnp.int32, shape, 0) == lax.broadcasted_iota(jnp.int32, shape, 1)

    def put_q(rows, cols, value):
        new = 2.0315 * value - 4.775 * a_ref[rows, cols]
        keep(q)(rows, cols, new + jnp.where(once, 3.4445, 0.0) if rows == cols else new)

    def put_a(rows, cols, value):
        a_ref[rows, cols] = value
        keep(a)(rows, cols, value)

    def put_out(rows, cols, value):
        value = value * (1.0 / scale_ref[0])
        out_ref[rows, cols] = value
        if rows != cols:
            out_ref[cols, rows] = value.T

    @pl.when(step == 0)
    def _():
        half = len(TILES) // 2
        lower = kind_ref[1] == 1
        trace = 0.0
        for at, (i, j) in enumerate(TILES):
            side = kept_ref[at % half], got_ref[at % half]
            near, far = side if at < half else side[::-1]
            tile = jnp.where(lower, near, far)
            tile = jnp.where(kind_ref[0] == 0, chip_ref[at], tile)
            tile = jnp.where(kind_ref[0] == 1, other_ref[at], tile)
            a_ref[i * BLOCK:(i + 1) * BLOCK, j * BLOCK:(j + 1) * BLOCK] = tile
            if i == j:
                trace = trace + jnp.sum(jnp.where(once, tile, 0.0))
        scale = jnp.sqrt(trace) + 1e-07
        scale_ref[0] = scale
        for i, j in TILES:
            rows, cols = slice(i * BLOCK, (i + 1) * BLOCK), slice(j * BLOCK, (j + 1) * BLOCK)
            put_a(rows, cols, a_ref[rows, cols] * (1.0 / (scale * scale)))

    turn = lax.rem(step + 1, 4)
    last = 4 * NS_TURNS - 4

    @pl.when((step == 0) | (turn == 0))
    def _():
        even_product(a, a, put_q)

    @pl.when(step == 0)
    def _():
        p[0][...], p[1][...] = q[0][...], q[1][...]

    @pl.when((turn == 1) & (step > 0) & (step < last))
    def _():
        even_product(p, q, keep(t))
        p[0][...], p[1][...] = t[0][...], t[1][...]

    @pl.when(step == last)
    def _():
        even_product(p, q, put_out)

    @pl.when(turn == 2)
    def _():
        even_product(a, q, keep(t))

    @pl.when(turn == 3)
    def _():
        even_product(t, q, put_a)

    @pl.when(step < chunks)
    def _():
        grad = factor_ref[0] * grad_ref[...].astype(full)
        weight = weight_ref[...]
        first = beta_one * first_ref[...] + (1.0 - beta_one) * grad
        second = beta_two * second_ref[...] + (1.0 - beta_two) * grad * grad
        move = (first * debias_ref[0]) / (jnp.sqrt(second * debias_ref[1]) + adam_eps)
        new = weight - 0.02 * (move + adam_decay * weight)
        weight_new_ref[...] = new
        first_new_ref[...] = first
        second_new_ref[...] = second
        copy_ref[...] = new.astype(low)


def chain(kind, factor, debias, grams, table):
    steps = 4 * NS_TURNS - 3
    features, vocab = table[1].shape
    width = -(-vocab // ((steps - 1) * LANES)) * LANES
    chunks = -(-vocab // width)
    part = pl.BlockSpec((features, width), lambda g: (0, jnp.minimum(g, chunks - 1)))
    whole = jax.ShapeDtypeStruct((features, vocab), full)
    return pl.pallas_call(
        partial(chain_kernel, chunks=chunks),
        grid=(steps,),
        in_specs=[smem(), smem(), smem()] + [vmem()] * 4 + [part] * 4,
        out_specs=[pl.BlockSpec((D, D), lambda g: (0, 0))] + [part] * 4,
        out_shape=[
            jax.ShapeDtypeStruct((D, D), full),
            whole,
            whole,
            whole,
            jax.ShapeDtypeStruct((features, vocab), low),
        ],
        scratch_shapes=[pltpu.VMEM((D, D), full), pltpu.SMEM((1,), full)]
        + [pltpu.VMEM((D, D), low)] * 8,
        compiler_params=params(56),
        cost_estimate=cost(48),
        name="chain",
    )(kind, factor, debias, *grams, *table)


def apply_kernel(info_ref, gain_ref, first_ref, second_ref, moment_ref, master_ref, new_ref, copy_ref,
                 *, block):
    split = info_ref[0] // block

    def over(slot, p_ref, start, stop):
        p = halves(p_ref[...])
        gain = gain_ref[slot] * muon_rate

        def body(b, carry):
            rows = pl.ds(pl.multiple_of(b * block, block), block)
            ortho = dot_split(halves(moment_ref[rows]), p)
            new = master_ref[rows] * (1.0 - muon_rate * muon_decay) - gain * ortho
            new_ref[rows] = new
            copy_ref[rows] = new.astype(low)
            return carry

        lax.fori_loop(start, stop, body, 0)

    over(0, first_ref, 0, split)
    total = moment_ref.shape[0] // block

    @pl.when(split < total)
    def _():
        over(1, second_ref, split, total)


def apply_chain(info, gains, first, second, moment, master, block):
    return pl.pallas_call(
        partial(apply_kernel, block=block),
        in_specs=[smem(), smem(), vmem(), vmem(), vmem(), vmem()],
        out_specs=[vmem(), vmem()],
        out_shape=[
            jax.ShapeDtypeStruct(moment.shape, full),
            jax.ShapeDtypeStruct(moment.shape, low),
        ],
        compiler_params=params(48),
        cost_estimate=cost(10),
        name="apply",
    )(info, gains, first, second, moment, master)


def chains(mine, other, wide_at, first_matrix, second_matrix, factor, debias, table, rider):
    wide = lax.axis_size("wide")
    if wide != 8:
        which = jnp.arange(4)
        slots = (which == first_matrix).astype(full)[:, None, None, None] * mine
        slots = slots + (which == second_matrix).astype(full)[:, None, None, None] * other
        total = lax.psum(slots, "wide")
        kind = jnp.zeros((2,), jnp.int32)
        outs = []
        for matrix in (first_matrix, second_matrix):
            gram = lax.dynamic_index_in_dim(total, matrix, 0, keepdims=False)
            half = gram[: len(TILES) // 2]
            outs.append(chain(kind, factor, debias, (gram, gram, half, half), table))
        return outs[0][0], outs[1][0], outs[0][1:], rider
    half = len(TILES) // 2
    pairs = [(i, i ^ 1) for i in range(8)]
    lower = wide_at % 2 == 0
    moved = lax.ppermute(other[:half], "wide", [(5, 4)])
    chip = mine + lax.ppermute(mine, "wide", pairs)
    up_send = jnp.where(lower, chip[:half], chip[half:])
    down_send = jnp.where(wide_at == 4, moved, jnp.where(wide_at == 5, other[half:], up_send))
    up = up_send + lax.ppermute(up_send, "wide", [(2, 4), (4, 2), (3, 5), (5, 3)])
    down = down_send + lax.ppermute(down_send, "wide", [(4, 6), (6, 4), (5, 7), (7, 5)])
    send = jnp.where((wide_at == 4) | (wide_at >= 6), down, up)
    swap = lax.ppermute(send, "wide", [(2, 3), (4, 5), (6, 7), (7, 6)])
    back = lax.ppermute(up, "wide", [(5, 4)])
    kept = jnp.where(wide_at >= 5, down, up)
    got = jnp.where(wide_at == 4, back, swap)
    kind = jnp.where(wide_at < 2, 0, jnp.where(wide_at == 2, 1, 2))
    kind = jnp.stack([kind, lower.astype(jnp.int32)]).astype(jnp.int32)
    got, rider = lax.optimization_barrier((got, rider))
    own, *table_new = chain(kind, factor, debias, (chip, other, kept, got), table)
    come = lax.ppermute(own, "wide", [(3, 2), (4, 5)])
    return jnp.where(wide_at == 5, come, own), jnp.where(wide_at == 5, own, come), table_new, rider


def layout(lengths):
    row_ends = jnp.cumsum(lengths)
    starts = row_ends - lengths
    places = jnp.arange(SEQ, dtype=jnp.int32)
    segment = jnp.sum((places[:, None] >= row_ends[None, :]).astype(jnp.int32), axis=1)
    chosen = segment[:, None] == jnp.arange(SLOTS, dtype=jnp.int32)[None, :]
    start_at = jnp.sum(jnp.where(chosen, starts[None, :], 0), axis=1)
    length_at = jnp.sum(jnp.where(chosen, lengths[None, :], 0), axis=1)
    position = places - start_at
    second = (2 * position >= length_at).astype(jnp.int32)
    return (chosen.astype(full), position, second, segment)


def norm_forward(hidden, gain, bias):
    center = hidden - jnp.mean(hidden, axis=-1, keepdims=True)
    inverse = lax.rsqrt(jnp.mean(center * center, axis=-1, keepdims=True) + norm_eps)
    scaled = center * inverse
    return (scaled * gain + bias, scaled, inverse)


def norm_backward(upstream, scaled, inverse, gain):
    weighted = upstream * gain
    back = inverse * (
        weighted
        - jnp.mean(weighted, axis=-1, keepdims=True)
        - scaled * jnp.mean(weighted * scaled, axis=-1, keepdims=True)
    )
    return (back, jnp.sum(upstream * scaled, axis=0), jnp.sum(upstream, axis=0))


def project(left, right):
    return jnp.dot(left, right, preferred_element_type=full)


def task_loss(logits, scores, tasks, labels, negatives, counts):
    logprob = jax.nn.log_softmax(logits, axis=-1)
    picked = jnp.sum(
        jnp.where(labels[:, :, None] == jnp.arange(3, dtype=jnp.int32), logprob, 0.0), axis=2
    )
    chosen = negatives[:, :, :, None] == jnp.arange(scores.shape[1], dtype=jnp.int32)
    rivals = jnp.sum(jnp.where(chosen, scores[:, None, None, :], 0.0), axis=3)
    together = jnp.concatenate([scores[:, :, None], rivals], axis=2)
    ranking = jax.nn.logsumexp(together, axis=2) - scores
    first_part = jnp.sum(jnp.where(tasks == 0, -picked, 0.0)) / counts[0]
    return first_part + jnp.sum(jnp.where(tasks == 1, ranking, 0.0)) / counts[1]


def adam(weight, grad, first, second, step, rate):
    first = beta_one * first + (1.0 - beta_one) * grad
    second = beta_two * second + (1.0 - beta_two) * grad * grad
    unbiased = first / (1.0 - beta_one**step)
    spread = second / (1.0 - beta_two**step)
    return (
        weight - rate * (unbiased / (jnp.sqrt(spread) + adam_eps) + adam_decay * weight),
        first,
        second,
    )


def broadcast_all(x):
    count = lax.axis_size("narrow") * lax.axis_size("wide")
    return lax.all_to_all(
        jnp.broadcast_to(x[None], (count,) + x.shape), BOTH, split_axis=0, concat_axis=0, tiled=True
    )


def sides(wide):
    return [list(range(0, wide, 2)), list(range(1, wide, 2))]


def chip_mates(wide):
    return [(i, i ^ 1) for i in range(wide)]


def by_owner(grad, spans, parts):
    pieces = [
        grad[lo:hi].reshape(parts, (hi - lo) // parts, D) for lo, hi in spans
    ]
    return jnp.concatenate(pieces, axis=1).reshape(-1, D).astype(low)


def gather_weights(master, narrow_at, wide_at, first):
    wide = lax.axis_size("wide")
    if wide != 8:
        whole = lax.all_gather(master.astype(low), "wide", axis=0, tiled=True)
        return first, list(whole.reshape(wide, -1, D))
    share = master.shape[0] // lax.axis_size("narrow")
    mine = lax.dynamic_slice_in_dim(master, narrow_at * share, share, 0).astype(low)
    near = lax.all_gather(mine, "wide", axis=0, tiled=False, axis_index_groups=sides(wide))
    near, first = lax.optimization_barrier((near, first))
    return first, [
        lax.all_gather(part, "narrow", axis=1, tiled=True)
        for part in (near[: wide // 4], near[wide // 4 :])
    ]


def both_cores(held, wide_at):
    owners = []
    other = lax.ppermute(held, "wide", chip_mates(lax.axis_size("wide")))
    side = wide_at % 2
    even = jnp.where(side == 0, held, other)
    odd = jnp.where(side == 0, other, held)
    for at in range(held.shape[0]):
        owners += [even[at], odd[at]]
    return owners


def rows_of(owners, matrix):
    rows = owners[0].shape[0]
    lo, hi = BOUNDS[matrix], BOUNDS[matrix + 1]
    pieces = []
    for at in range(lo // rows, -(-hi // rows)):
        pieces.append(owners[at][max(lo - at * rows, 0) : min(hi - at * rows, rows)])
    return jnp.concatenate(pieces) if len(pieces) > 1 else pieces[0]


def shards(
    token_ids,
    seq_lengths,
    task_ids,
    labels,
    negatives,
    step_count,
    hidden_master,
    hidden_momentum,
    table_master,
    table_first,
    table_second,
    pos_types,
    pos_first,
    pos_second,
    vectors,
    vec_first,
    vec_second,
):
    wide_at = lax.axis_index("wide")
    narrow_at = lax.axis_index("narrow")
    wide = lax.axis_size("wide")
    narrow = lax.axis_size("narrow")
    count = wide * narrow
    device_at = narrow_at * wide + wide_at
    micro_count, rows_each = token_ids.shape[:2]
    batch = micro_count * rows_each
    tokens = batch * SEQ
    shard = hidden_master.shape[0]
    vocab = table_master.shape[1]
    features = table_master.shape[0] // narrow
    pairs_each = rows_each * SLOTS

    parts = [token_ids, task_ids, labels, negatives]
    sizes = [part.size for part in parts]
    packed = jnp.concatenate([part.reshape(-1) for part in parts])
    packed = jnp.pad(packed, (0, -packed.size % LANES))
    gathered = broadcast_all(packed)
    ends = [sum(sizes[: i + 1]) for i in range(len(sizes))]
    ids_all = gathered[:, : ends[0]]

    def pairs_of(lo, hi, tail):
        block = gathered[:, lo:hi].reshape((count, micro_count, pairs_each) + tail)
        return jnp.moveaxis(block, 1, 0).reshape((micro_count, count * pairs_each) + tail)

    tasks_all = pairs_of(ends[0], ends[1], ())
    labels_all = pairs_of(ends[1], ends[2], ())
    negatives_all = pairs_of(ends[2], ends[3], (NEG,))
    counts = jnp.stack(
        [jnp.sum((tasks_all == 0).astype(full)), jnp.sum((tasks_all == 1).astype(full))]
    )


    group_ids = lax.dynamic_slice_in_dim(ids_all, narrow_at * wide, wide, 0).reshape(-1)
    pieces = lookup(group_ids, table_master)
    pieces, gathers = gather_weights(hidden_master, narrow_at, wide_at, pieces)
    simple = wide != 8
    arrived = lax.all_to_all(
        pieces.reshape(wide, tokens, -1), "wide", split_axis=0, concat_axis=0, tiled=True
    )
    token_rows = jnp.moveaxis(arrived, 0, 1).reshape(tokens, D)

    lengths = seq_lengths.reshape(batch, SLOTS)
    member, position, second, segment = jax.vmap(layout)(lengths)
    flat_position = position.reshape(-1)
    flat_second = second.reshape(-1)
    place_rows = pos_types[flat_position]
    place_rows = place_rows + jnp.where(flat_second[:, None] == 1, pos_types[SEQ + 1], pos_types[SEQ])
    if simple:
        owners = gathers
    else:
        place_rows, held = lax.optimization_barrier((place_rows, gathers[0]))
        owners = both_cores(held, wide_at)
    embed = token_rows.astype(full) + place_rows
    normed0, scaled0, inverse0 = norm_forward(embed, vectors[0], vectors[1])
    input0 = normed0.astype(low)
    qkv_bias = jnp.concatenate([vectors[6], jnp.zeros_like(vectors[6]), vectors[7]])
    weight_qkv, weight_out = rows_of(owners, 0), rows_of(owners, 1)
    mixed = (project(input0, weight_qkv.T) + qkv_bias).astype(low)
    context_low, logsum = attend(mixed, segment)
    if not simple:
        rest, context_low = lax.optimization_barrier((gathers[1], context_low))
        owners = owners + both_cores(rest, wide_at)
    weight_up, weight_down = rows_of(owners, 2), rows_of(owners, 3)
    attended = project(context_low, weight_out.T) + vectors[8]
    normed1, scaled1, inverse1 = norm_forward(normed0 + attended, vectors[2], vectors[3])
    input1 = normed1.astype(low)
    inner = project(input1, weight_up.T) + vectors[14:].reshape(-1)
    cdf = 0.5 * (1.0 + lax.erf(inner * math.sqrt(0.5)))
    active = (inner * cdf).astype(low)
    slope = cdf + inner * (jnp.exp(-0.5 * inner * inner) * (1.0 / math.sqrt(2.0 * math.pi)))
    branch = project(active, weight_down) + vectors[9]
    normed2, scaled2, inverse2 = norm_forward(normed1 + branch, vectors[4], vectors[5])
    share = member / lengths.astype(full)[:, None, :]
    pooled = jnp.einsum("rps,rpd->rsd", share, normed2.reshape(batch, SEQ, D), precision=highest)
    flat_pooled = pooled.reshape(-1, D)
    heads = vectors[10:14]
    head_out = jnp.dot(flat_pooled, heads.T, precision=highest)

    sent = jnp.pad(head_out.reshape(-1), (0, -head_out.size % LANES))
    head_all = broadcast_all(sent)[:, : head_out.size]
    head_all = head_all.reshape(count, micro_count, pairs_each, 4)
    head_all = jnp.moveaxis(head_all, 1, 0).reshape(micro_count, count * pairs_each, 4)

    def objective(every):
        return task_loss(every[:, :, :3], every[:, :, 3], tasks_all, labels_all, negatives_all, counts)

    loss, pullback = jax.vjp(objective, head_all)
    head_grads = pullback(jnp.ones_like(loss))[0]
    output_grads = lax.dynamic_slice_in_dim(head_grads, device_at * pairs_each, pairs_each, 1)
    output_grads = output_grads.reshape(-1, 4)
    heads_grad = jnp.dot(output_grads.T, flat_pooled, precision=highest)
    pooled_grads = jnp.dot(output_grads, heads, precision=highest).reshape(pooled.shape)

    spread = jnp.einsum("rps,rsd->rpd", share, pooled_grads, precision=highest).reshape(-1, D)
    sum2_grad, gain2, bias2 = norm_backward(spread, scaled2, inverse2, vectors[4])
    branch_grad = sum2_grad.astype(low)
    down_grad = project(active.T, branch_grad)
    spans_down = [(0, 768), (768, 1920), (1920, 3072)]
    spans_up = [(0, 384), (384, 1536), (1536, 2688), (2688, 3072)]
    spans_front = [(0, 1152), (1152, 2304), (2304, 3072)]

    side = wide_at % 2

    def ready(grad, spans):
        if simple:
            return grad.astype(low)
        grad = by_owner(grad, spans, narrow)
        left, right = grad[:, : D // 2], grad[:, D // 2 :]
        stays = jnp.where(side == 0, left, right)
        leaves = jnp.where(side == 0, right, left)
        return stays, leaves

    def between_cores(grad):
        if simple:
            return grad
        stays, leaves = grad
        return stays, lax.ppermute(leaves, "wide", chip_mates(wide))

    def slices(grad):
        if simple:
            return [grad]
        stays, comes = grad
        chip = (stays.astype(full) + comes.astype(full)).astype(low).reshape(narrow, -1, D // 2)
        return [chip[narrow_at ^ turn] for turn in range(narrow)]

    def over_narrow(parts):
        return parts[:1] + [
            lax.ppermute(part, "narrow", [(i, i ^ (turn + 1)) for i in range(narrow)])
            for turn, part in enumerate(parts[1:])
        ]

    together = lax.optimization_barrier
    down_send, after_down = together((ready(down_grad, spans_down), branch_grad))
    down_pair = between_cores(down_send)
    active_grad = project(after_down, weight_down.T)
    inner_grad = (active_grad * slope).astype(low)
    up_grad = project(inner_grad.T, input1)
    up_send, down_pair, after_up = together((ready(up_grad, spans_up), down_pair, inner_grad))
    up_pair = between_cores(up_send)
    down_cut, after_up = together((slices(down_pair), after_up))
    down_part = over_narrow(down_cut)
    normed1_grad = sum2_grad + project(after_up, weight_up)
    sum1_grad, gain1, bias1 = norm_backward(normed1_grad, scaled1, inverse1, vectors[2])
    attended_grad = sum1_grad.astype(low)
    up_pair, attended_grad = together((up_pair, attended_grad))
    out_grad = project(attended_grad.T, context_low)
    context_grad = project(attended_grad, weight_out).astype(low)
    up_cut, context_grad = together((slices(up_pair), context_grad))
    up_part = over_narrow(up_cut)
    mixed_grad = attend_back(mixed, context_grad, logsum, segment)
    mixed_grad, up_part, down_part = together((mixed_grad, up_part, down_part))
    normed0_grad = sum1_grad + project(mixed_grad, weight_qkv)
    embed_grad, gain0, bias0 = norm_backward(normed0_grad, scaled0, inverse0, vectors[0])

    table_send = embed_grad.astype(low).T.reshape(wide, narrow, features, tokens)
    table_send = jnp.moveaxis(table_send, 1, 0).reshape(count, features, tokens)
    table_send, mixed_grad = together((table_send, mixed_grad))
    come = lax.all_to_all(table_send, BOTH, split_axis=0, concat_axis=0, tiled=True)

    qkv_grad = project(mixed_grad.T, input0)
    front_grad = jnp.concatenate([qkv_grad.astype(low), out_grad.astype(low)])
    front_send, embed_grad, mixed_grad = together(
        (ready(front_grad, spans_front), embed_grad, mixed_grad)
    )
    front_part = over_narrow(slices(between_cores(front_send)))
    mixed_sum = jnp.sum(mixed_grad.astype(full), axis=0)
    small_rows = jnp.stack(
        [
            gain0,
            bias0,
            gain1,
            bias1,
            gain2,
            bias2,
            mixed_sum[:D],
            mixed_sum[2 * D :],
            jnp.sum(attended_grad.astype(full), axis=0),
            jnp.sum(branch_grad.astype(full), axis=0),
        ]
    )
    up_rows = jnp.sum(inner_grad.astype(full), axis=0).reshape(-1, D)

    places = jnp.arange(SEQ, dtype=jnp.int32)[:, None]
    row_hot = jnp.concatenate(
        [
            flat_position[None] == places,
            jnp.stack([flat_second == 0, flat_second == 1]),
        ]
    ).astype(low)
    high_part, low_part = halves(embed_grad)
    pos_grad = project(jnp.concatenate([row_hot, row_hot], axis=1), jnp.concatenate([high_part, low_part]))
    small = jnp.concatenate([pos_grad, small_rows, heads_grad, up_rows])
    small_count = small.shape[0]
    small = jnp.pad(small, ((0, count * features - small_count), (0, 0)))

    def added(parts):
        return sum(part.astype(full) for part in parts).astype(low)

    joined = jnp.concatenate([added(front_part), added(up_part), added(down_part)])
    small_send = small.astype(low).reshape(count, features, D)
    come, small_send = together((come, small_send))
    small_come = lax.all_to_all(small_send, BOTH, split_axis=0, concat_axis=0, tiled=True)
    table_part, table_square = collect(ids_all, come, vocab, tokens)
    if simple:
        hidden_part = lax.psum_scatter(joined, "wide", scatter_dimension=0, tiled=True)
        hidden_part = lax.psum_scatter(hidden_part, "narrow", scatter_dimension=0, tiled=True)
        hidden_square = jnp.sum(jnp.square(hidden_part.astype(full)))
    else:
        owned = lax.psum_scatter(
            joined, "wide", scatter_dimension=0, tiled=True, axis_index_groups=sides(wide)
        )
        owned, table_square, small_come = together((owned, table_square, small_come))
        hidden_square = jnp.sum(jnp.square(owned.astype(full)))
        half = owned.shape[0] // 2
        stays = jnp.where(side == 0, owned[:half], owned[half:])
        leaves = jnp.where(side == 0, owned[half:], owned[:half])
        comes = lax.ppermute(leaves, "wide", chip_mates(wide))
        hidden_part = jnp.concatenate(
            [jnp.where(side == 0, stays, comes), jnp.where(side == 0, comes, stays)], axis=1
        )
    small_part = jnp.sum(small_come.astype(full), axis=0)
    square = hidden_square + table_square[0, 0] + jnp.sum(small_part * small_part)
    square, hidden_part = together((square, hidden_part))
    if simple:
        hidden_all = lax.all_gather(hidden_part, "narrow", axis=0, tiled=True)
    else:
        hidden_all = jnp.concatenate(
            [hidden_part]
            + [
                lax.ppermute(hidden_part, "narrow", [(i, i ^ turn) for i in range(narrow)])
                for turn in range(1, narrow)
            ]
        )
    squares = broadcast_all(jnp.broadcast_to(square, (LANES,)))
    squares, hidden_all, table_part = together((squares, hidden_all, table_part))
    table_grad = lax.all_gather(table_part, "narrow", axis=0, tiled=True)
    clip_norm = jnp.sqrt(jnp.sum(squares[:, 0]))
    factor = jnp.minimum(1.0, clip_bound / clip_norm)

    start = wide_at * shard
    bounds = jnp.array(BOUNDS, jnp.int32)
    first_matrix = jnp.sum((start >= bounds[1:4]).astype(jnp.int32))
    second_matrix = jnp.sum((start + shard - 1 >= bounds[1:4]).astype(jnp.int32))
    split = jnp.minimum(bounds[first_matrix + 1] - start, shard)
    block = shard // 3
    piece = shard // 12
    at = jnp.arange(12, dtype=jnp.int32)
    if simple:
        source = at
    else:
        lead = split // piece
        each = lead // narrow
        rest = (12 - lead) // narrow
        in_first = at < lead
        inside = jnp.where(in_first, at, at - lead)
        width = jnp.maximum(jnp.where(in_first, each, rest), 1)
        origin = (inside // width) ^ narrow_at
        source = origin * (12 // narrow) + jnp.where(in_first, 0, each) + inside % width
    swap = (wide_at == 2).astype(jnp.int32) * (0 if simple else 1)
    info = jnp.concatenate([jnp.stack([split, swap]), source]).astype(jnp.int32)
    gains = jnp.array([0.2 * math.sqrt(hi - lo) for lo, hi in zip(BOUNDS, BOUNDS[1:])], full)
    moment, mine, other = moment_and_grams(
        info, factor[None], hidden_all, hidden_momentum, piece, block
    )
    step = step_count[0].astype(full)
    debias = jnp.stack([1.0 / (1.0 - beta_one**step), 1.0 / (1.0 - beta_two**step)])
    chain0, chain1, (table_new, table_first_new, table_second_new, table_copy), late_small = chains(
        mine,
        other,
        wide_at,
        first_matrix,
        second_matrix,
        factor[None],
        debias,
        (table_grad, table_master, table_first, table_second),
        small_part,
    )
    small_all = broadcast_all(late_small.astype(low)).reshape(-1, D)[:small_count].astype(full)
    slot_gains = jnp.stack([gains[first_matrix], gains[second_matrix]])
    hidden_new, hidden_copy = apply_chain(info, slot_gains, chain0, chain1, moment, hidden_master, block)

    pos_new, pos_first_new, pos_second_new = adam(
        pos_types, factor * small_all[: SEQ + 2], pos_first, pos_second, step, 0.02
    )
    vectors_new, vec_first_new, vec_second_new = adam(
        vectors, factor * small_all[SEQ + 2 :], vec_first, vec_second, step, 0.2
    )
    return (
        loss,
        clip_norm,
        moment,
        hidden_new,
        hidden_copy,
        table_new,
        table_first_new,
        table_second_new,
        table_copy,
        pos_new,
        pos_first_new,
        pos_second_new,
        vectors_new,
        vec_first_new,
        vec_second_new,
    )


def solution(mesh):
    rows = P(None, BOTH, None)
    owned = P("wide", None)
    return jax.shard_map(
        shards,
        mesh=mesh,
        in_specs=(rows, rows, rows, rows, P(None, BOTH, None, None), P())
        + (owned,) * 5
        + (P(),) * 6,
        out_specs=(P(), P()) + (owned,) * 7 + (P(),) * 6,
        check_vma=False,
    )
```

```python
from functools import partial
import math

import jax
import jax.numpy as jnp
from jax import lax
from jax.experimental import pallas as pl
from jax.experimental.pallas import tpu as pltpu
from jax.sharding import PartitionSpec as P

D = 768
HEADS = 12
HEAD = 64
FF = 3072
SEQ = 512
SLOTS = 4
NEG = 4
NS_TURNS = 5
LANES = 128
GROUPS = 4
WIDTH = LANES // GROUPS
BLOCK = 256
TILES = [(i, j) for i in range(D // BLOCK) for j in range(i, D // BLOCK)]

BOTH = ("narrow", "wide")
highest = lax.Precision.HIGHEST
clip_bound = 0.002
norm_eps = 1e-06
muon_beta = 0.95
muon_rate = 0.1
muon_decay = 0.01
beta_one = 0.9
beta_two = 0.999
adam_eps = 1e-08
adam_decay = 0.01
BOUNDS = (0, 3 * D, 4 * D, 4 * D + FF, 4 * D + 2 * FF)

low = jnp.bfloat16
full = jnp.float32


def dims(left, right):
    return (((left,), (right,)), ((), ()))


def dot32(left, right, left_dim, right_dim):
    return lax.dot_general(left, right, dims(left_dim, right_dim), preferred_element_type=full)


def halves(x):
    high = x.astype(low)
    return high, (x - high.astype(full)).astype(low)


def dot_split(left, right, left_dim=1, right_dim=0):
    (lh, ll), (rh, rl) = left, right
    return dot32(lh, rh, left_dim, right_dim) + (
        dot32(lh, rl, left_dim, right_dim) + dot32(ll, rh, left_dim, right_dim)
    )


def params(mib):
    return pltpu.CompilerParams(vmem_limit_bytes=mib << 20)


def cost(micros):
    return pl.CostEstimate(flops=micros * 10**9, transcendentals=0, bytes_accessed=1 << 20)


def vmem():
    return pl.BlockSpec(memory_space=pltpu.VMEM)


def smem():
    return pl.BlockSpec(memory_space=pltpu.SMEM)


def attend_kernel(mixed_ref, seg_col_ref, seg_row_ref, context_ref, logsum_ref):
    same = seg_col_ref[0] == seg_row_ref[0]

    def pair(step, carry):
        at = pl.multiple_of(step * LANES, LANES)
        queries = mixed_ref[:, pl.ds(at, LANES)]
        keys = mixed_ref[:, pl.ds(D + at, LANES)]
        values = mixed_ref[:, pl.ds(2 * D + at, LANES)]
        outs = []
        for half in range(2):
            cut = slice(half * HEAD, (half + 1) * HEAD)
            raw = dot32(keys[:, cut], queries[:, cut], 1, 1)
            scores = jnp.where(same, raw * (1.0 / math.sqrt(HEAD)), -1e30)
            peak = jnp.max(scores, axis=0, keepdims=True)
            lifted = jnp.exp(scores - peak)
            total = jnp.sum(lifted, axis=0, keepdims=True)
            probs = (lifted * (1.0 / total)).astype(low)
            outs.append(dot32(values[:, cut], probs, 0, 0))
            logsum_ref[0, pl.ds(2 * step + half, 1), :] = peak + jnp.log(total)
        context_ref[:, pl.ds(at, LANES)] = jnp.concatenate(outs, axis=0).T.astype(low)
        return carry

    lax.fori_loop(0, HEADS // 2, pair, 0)


def attend(mixed, segment):
    rows = segment.shape[0]
    return pl.pallas_call(
        attend_kernel,
        grid=(rows,),
        in_specs=[
            pl.BlockSpec((SEQ, 3 * D), lambda b: (b, 0)),
            pl.BlockSpec((1, SEQ, 1), lambda b: (b, 0, 0)),
            pl.BlockSpec((1, 1, SEQ), lambda b: (b, 0, 0)),
        ],
        out_specs=[
            pl.BlockSpec((SEQ, D), lambda b: (b, 0)),
            pl.BlockSpec((1, 16, SEQ), lambda b: (b, 0, 0)),
        ],
        out_shape=[
            jax.ShapeDtypeStruct((rows * SEQ, D), low),
            jax.ShapeDtypeStruct((rows, 16, SEQ), full),
        ],
        compiler_params=params(48),
        cost_estimate=cost(19),
        name="attend",
    )(mixed, segment[:, :, None], segment[:, None, :])


def attend_back_kernel(mixed_ref, grad_ref, logsum_ref, seg_col_ref, seg_row_ref, out_ref):
    same = seg_col_ref[0] == seg_row_ref[0]
    scale = 1.0 / math.sqrt(HEAD)

    def pair(step, carry):
        at = pl.multiple_of(step * LANES, LANES)
        queries = mixed_ref[:, pl.ds(at, LANES)]
        keys = mixed_ref[:, pl.ds(D + at, LANES)]
        values = mixed_ref[:, pl.ds(2 * D + at, LANES)]
        upstream = grad_ref[:, pl.ds(at, LANES)]
        query_grads, key_grads, value_grads = [], [], []
        for half in range(2):
            cut = slice(half * HEAD, (half + 1) * HEAD)
            logsum = logsum_ref[0, pl.ds(2 * step + half, 1), :]
            raw = dot32(keys[:, cut], queries[:, cut], 1, 1)
            probs = jnp.exp(jnp.where(same, raw * scale, -1e30) - logsum)
            prob_grads = dot32(values[:, cut], upstream[:, cut], 1, 1)
            value_grads.append(dot32(probs.astype(low), upstream[:, cut], 1, 0))
            moved = jnp.sum(prob_grads * probs, axis=0, keepdims=True)
            back = (probs * (prob_grads - moved) * scale).astype(low)
            key_grads.append(dot32(back, queries[:, cut], 1, 0))
            query_grads.append(dot32(keys[:, cut], back, 0, 0))
        out_ref[:, pl.ds(at, LANES)] = jnp.concatenate(query_grads, axis=0).T.astype(low)
        out_ref[:, pl.ds(D + at, LANES)] = jnp.concatenate(key_grads, axis=1).astype(low)
        out_ref[:, pl.ds(2 * D + at, LANES)] = jnp.concatenate(value_grads, axis=1).astype(low)
        return carry

    lax.fori_loop(0, HEADS // 2, pair, 0)


def attend_back(mixed, context_grad, logsum, segment):
    rows = segment.shape[0]
    return pl.pallas_call(
        attend_back_kernel,
        grid=(rows,),
        in_specs=[
            pl.BlockSpec((SEQ, 3 * D), lambda b: (b, 0)),
            pl.BlockSpec((SEQ, D), lambda b: (b, 0)),
            pl.BlockSpec((1, 16, SEQ), lambda b: (b, 0, 0)),
            pl.BlockSpec((1, SEQ, 1), lambda b: (b, 0, 0)),
            pl.BlockSpec((1, 1, SEQ), lambda b: (b, 0, 0)),
        ],
        out_specs=pl.BlockSpec((SEQ, 3 * D), lambda b: (b, 0)),
        out_shape=jax.ShapeDtypeStruct((rows * SEQ, 3 * D), low),
        compiler_params=params(56),
        cost_estimate=cost(28),
        name="attend_back",
    )(mixed, context_grad, logsum, segment[:, :, None], segment[:, None, :])


def lookup_kernel(ids_ref, table_ref, out_ref, turned_ref, rows_ref):
    step = pl.program_id(0)
    features, width = table_ref.shape
    tokens, chunk = out_ref.shape[0], rows_ref.shape[0]
    block = table_ref[...].astype(low).astype(full)
    block = jnp.concatenate([block, jnp.zeros((LANES - features, width), full)], axis=0)
    turned_ref[pl.ds(pl.multiple_of(step * width, width), width), :] = block.T

    @pl.when(step == pl.num_programs(0) - 1)
    def _():
        def piece(c, carry):
            def body(i, inner):
                at = i * 32
                found = [turned_ref[pl.ds(ids_ref[c * chunk + at + k], 1), :] for k in range(32)]
                for k in range(32):
                    rows_ref[pl.ds(at + k, 1), :] = found[k]
                return inner

            lax.fori_loop(0, chunk // 32, body, 0)
            start = pl.multiple_of(c * chunk, chunk)
            out_ref[pl.ds(start, chunk), :] = rows_ref[:, :features].astype(low)
            return carry

        lax.fori_loop(0, tokens // chunk, piece, 0)


def lookup(ids, table):
    features, vocab = table.shape
    width = -(-vocab // (4 * LANES)) * LANES
    steps = -(-vocab // width)
    return pl.pallas_call(
        lookup_kernel,
        grid=(steps,),
        in_specs=[smem(), pl.BlockSpec((features, width), lambda s: (0, s))],
        out_specs=pl.BlockSpec((ids.shape[0], features), lambda s: (0, 0)),
        out_shape=jax.ShapeDtypeStruct((ids.shape[0], features), low),
        scratch_shapes=[pltpu.VMEM((steps * width, LANES), full), pltpu.VMEM((1024, LANES), full)],
        compiler_params=params(56),
        cost_estimate=cost(19),
        name="lookup",
    )(ids, table)


def collect_kernel(place_ref, ids_ref, grads_ref, out_ref, square_ref, *scratch,
                   span, tokens, features, vocab):
    sums, rows_ref = scratch[:-1], scratch[-1]
    step = pl.program_id(0)
    last = pl.num_programs(0) - 1
    streams = len(sums)
    batch = 4 * streams

    @pl.when(step == 0)
    def _():
        for total in sums:
            total[...] = jnp.zeros_like(total)

    group = ids_ref[0] // span
    grads = grads_ref[0].astype(full)
    pad = jnp.zeros((WIDTH - features, tokens), full)
    pieces = []
    for at in range(GROUPS):
        pieces += [jnp.where(group == at, grads, 0.0), pad]
    rows_ref[...] = jnp.concatenate(pieces, axis=0).T

    def body(i, carry):
        for base in range(0, batch, streams):
            at = i * batch + base
            places = [pl.ds(place_ref[0, 0, at + k], 1) for k in range(streams)]
            olds = [sums[k][places[k], :] for k in range(streams)]
            news = [rows_ref[pl.ds(at + k, 1), :] for k in range(streams)]
            for k in range(streams):
                sums[k][places[k], :] = olds[k] + news[k]
        return carry

    lax.fori_loop(0, tokens // batch, body, 0)

    @pl.when(step == last)
    def _():
        def flush(b, total):
            at = pl.multiple_of(b * LANES, LANES)
            block = sums[0][pl.ds(at, LANES), :]
            for k in range(1, streams):
                block += sums[k][pl.ds(at, LANES), :]
            turned = block.T
            for g in range(GROUPS):
                piece = turned[g * WIDTH:g * WIDTH + features]

                @pl.when(g * span + at < vocab)
                def _():
                    out_ref[:, pl.ds(pl.multiple_of(g * span + at, LANES), LANES)] = piece.astype(low)

            return total + block * block

        total = lax.fori_loop(0, span // LANES, flush, jnp.zeros((LANES, LANES), full))
        square_ref[...] = jnp.broadcast_to(jnp.sum(total, keepdims=True), square_ref.shape)


def collect(ids, grads, vocab, tokens):
    sources, features = grads.shape[:2]
    span = -(-vocab // (GROUPS * LANES)) * LANES
    return pl.pallas_call(
        partial(collect_kernel, span=span, tokens=tokens, features=features, vocab=vocab),
        grid=(sources,),
        in_specs=[
            pl.BlockSpec((1, 1, tokens), lambda s: (s, 0, 0), memory_space=pltpu.SMEM),
            pl.BlockSpec((1, 1, tokens), lambda s: (s, 0, 0)),
            pl.BlockSpec((1, features, tokens), lambda s: (s, 0, 0)),
        ],
        out_specs=[
            pl.BlockSpec((features, vocab), lambda s: (0, 0)),
            pl.BlockSpec((8, LANES), lambda s: (0, 0)),
        ],
        out_shape=[
            jax.ShapeDtypeStruct((features, vocab), low),
            jax.ShapeDtypeStruct((8, LANES), full),
        ],
        scratch_shapes=[pltpu.VMEM((span, LANES), full)] * 8 + [pltpu.VMEM((tokens, LANES), full)],
        compiler_params=params(56),
        cost_estimate=cost(150),
        name="collect",
    )((ids % span)[:, None, :], ids[:, None, :], grads)


def moment_kernel(info_ref, factor_ref, grad_ref, old_ref, moment_ref, mine_ref, other_ref,
                  *, piece, block):
    factor = factor_ref[0]
    for at in range(old_ref.shape[0] // piece):
        source = pl.multiple_of(info_ref[2 + at] * piece, piece)
        rows = slice(at * piece, (at + 1) * piece)
        moment_ref[rows] = muon_beta * old_ref[rows] + factor * grad_ref[pl.ds(source, piece)].astype(full)

    def grams(out_ref, start, stop):
        out_ref[...] = jnp.zeros_like(out_ref)

        def body(b, carry):
            high, small = halves(moment_ref[pl.ds(pl.multiple_of(b * block, block), block)])
            for at, (i, j) in enumerate(TILES):
                left, right = slice(i * BLOCK, (i + 1) * BLOCK), slice(j * BLOCK, (j + 1) * BLOCK)
                out_ref[at] += dot32(
                    jnp.concatenate([high[:, left], high[:, left], small[:, left]], axis=0),
                    jnp.concatenate([high[:, right], small[:, right], high[:, right]], axis=0),
                    0,
                    0,
                )
            return carry

        lax.fori_loop(start, stop, body, 0)

    lead, total = info_ref[0] // block, old_ref.shape[0] // block
    swap = info_ref[1] == 1
    grams(mine_ref, jnp.where(swap, lead, 0), jnp.where(swap, total, lead))
    grams(other_ref, jnp.where(swap, 0, lead), jnp.where(swap, lead, total))


def moment_and_grams(info, factor, grad, old, piece, block):
    tiles = jax.ShapeDtypeStruct((len(TILES), BLOCK, BLOCK), full)
    return pl.pallas_call(
        partial(moment_kernel, piece=piece, block=block),
        in_specs=[smem(), smem(), vmem(), vmem()],
        out_specs=[vmem()] * 3,
        out_shape=[jax.ShapeDtypeStruct(old.shape, full), tiles, tiles],
        compiler_params=params(48),
        cost_estimate=cost(10),
        name="moment",
    )(info, factor, grad, old)


def even_product(left, right, put):
    (lh, ll), (rh, rl) = left, right
    for i in range(D // BLOCK):
        rows = slice(i * BLOCK, (i + 1) * BLOCK)
        panel = jnp.concatenate([lh[rows], lh[rows], ll[rows]], axis=1)
        for j in range(i, D // BLOCK):
            cols = slice(j * BLOCK, (j + 1) * BLOCK)
            other = jnp.concatenate([rh[:, cols], rl[:, cols], rh[:, cols]], axis=0)
            put(rows, cols, dot32(panel, other, 1, 0))


def keep(pair):
    def put(rows, cols, value):
        pair[0][rows, cols], pair[1][rows, cols] = halves(value)
        if rows != cols:
            pair[0][cols, rows], pair[1][cols, rows] = halves(value.T)

    return put


def chain_kernel(kind_ref, factor_ref, debias_ref, chip_ref, other_ref, kept_ref, got_ref,
                 grad_ref, weight_ref, first_ref, second_ref,
                 out_ref, weight_new_ref, first_new_ref, second_new_ref, copy_ref,
                 a_ref, scale_ref, *parts, chunks):
    a, q, p, t = [parts[2 * i:2 * i + 2] for i in range(4)]
    step = pl.program_id(0)
    shape = (BLOCK, BLOCK)
    once = lax.broadcasted_iota(jnp.int32, shape, 0) == lax.broadcasted_iota(jnp.int32, shape, 1)

    def put_q(rows, cols, value):
        new = 2.0315 * value - 4.775 * a_ref[rows, cols]
        keep(q)(rows, cols, new + jnp.where(once, 3.4445, 0.0) if rows == cols else new)

    def put_a(rows, cols, value):
        a_ref[rows, cols] = value
        keep(a)(rows, cols, value)

    def put_out(rows, cols, value):
        value = value * (1.0 / scale_ref[0])
        out_ref[rows, cols] = value
        if rows != cols:
            out_ref[cols, rows] = value.T

    @pl.when(step == 0)
    def _():
        half = len(TILES) // 2
        lower = kind_ref[1] == 1
        trace = 0.0
        for at, (i, j) in enumerate(TILES):
            side = kept_ref[at % half], got_ref[at % half]
            near, far = side if at < half else side[::-1]
            tile = jnp.where(lower, near, far)
            tile = jnp.where(kind_ref[0] == 0, chip_ref[at], tile)
            tile = jnp.where(kind_ref[0] == 1, other_ref[at], tile)
            a_ref[i * BLOCK:(i + 1) * BLOCK, j * BLOCK:(j + 1) * BLOCK] = tile
            if i == j:
                trace = trace + jnp.sum(jnp.where(once, tile, 0.0))
        scale = jnp.sqrt(trace) + 1e-07
        scale_ref[0] = scale
        for i, j in TILES:
            rows, cols = slice(i * BLOCK, (i + 1) * BLOCK), slice(j * BLOCK, (j + 1) * BLOCK)
            put_a(rows, cols, a_ref[rows, cols] * (1.0 / (scale * scale)))

    turn = lax.rem(step + 1, 4)
    last = 4 * NS_TURNS - 4

    @pl.when((step == 0) | (turn == 0))
    def _():
        even_product(a, a, put_q)

    @pl.when(step == 0)
    def _():
        p[0][...], p[1][...] = q[0][...], q[1][...]

    @pl.when((turn == 1) & (step > 0) & (step < last))
    def _():
        even_product(p, q, keep(t))
        p[0][...], p[1][...] = t[0][...], t[1][...]

    @pl.when(step == last)
    def _():
        even_product(p, q, put_out)

    @pl.when(turn == 2)
    def _():
        even_product(a, q, keep(t))

    @pl.when(turn == 3)
    def _():
        even_product(t, q, put_a)

    @pl.when(step < chunks)
    def _():
        grad = factor_ref[0] * grad_ref[...].astype(full)
        weight = weight_ref[...]
        first = beta_one * first_ref[...] + (1.0 - beta_one) * grad
        second = beta_two * second_ref[...] + (1.0 - beta_two) * grad * grad
        move = (first * debias_ref[0]) / (jnp.sqrt(second * debias_ref[1]) + adam_eps)
        new = weight - 0.02 * (move + adam_decay * weight)
        weight_new_ref[...] = new
        first_new_ref[...] = first
        second_new_ref[...] = second
        copy_ref[...] = new.astype(low)


def chain(kind, factor, debias, grams, table):
    steps = 4 * NS_TURNS - 3
    features, vocab = table[1].shape
    width = -(-vocab // ((steps - 1) * LANES)) * LANES
    chunks = -(-vocab // width)
    part = pl.BlockSpec((features, width), lambda g: (0, jnp.minimum(g, chunks - 1)))
    whole = jax.ShapeDtypeStruct((features, vocab), full)
    return pl.pallas_call(
        partial(chain_kernel, chunks=chunks),
        grid=(steps,),
        in_specs=[smem(), smem(), smem()] + [vmem()] * 4 + [part] * 4,
        out_specs=[pl.BlockSpec((D, D), lambda g: (0, 0))] + [part] * 4,
        out_shape=[
            jax.ShapeDtypeStruct((D, D), full),
            whole,
            whole,
            whole,
            jax.ShapeDtypeStruct((features, vocab), low),
        ],
        scratch_shapes=[pltpu.VMEM((D, D), full), pltpu.SMEM((1,), full)]
        + [pltpu.VMEM((D, D), low)] * 8,
        compiler_params=params(56),
        cost_estimate=cost(48),
        name="chain",
    )(kind, factor, debias, *grams, *table)


def apply_kernel(info_ref, gain_ref, first_ref, second_ref, moment_ref, master_ref, new_ref, copy_ref,
                 *, block):
    split = info_ref[0] // block

    def over(slot, p_ref, start, stop):
        p = halves(p_ref[...])
        gain = gain_ref[slot] * muon_rate

        def body(b, carry):
            rows = pl.ds(pl.multiple_of(b * block, block), block)
            ortho = dot_split(halves(moment_ref[rows]), p)
            new = master_ref[rows] * (1.0 - muon_rate * muon_decay) - gain * ortho
            new_ref[rows] = new
            copy_ref[rows] = new.astype(low)
            return carry

        lax.fori_loop(start, stop, body, 0)

    over(0, first_ref, 0, split)
    total = moment_ref.shape[0] // block

    @pl.when(split < total)
    def _():
        over(1, second_ref, split, total)


def apply_chain(info, gains, first, second, moment, master, block):
    return pl.pallas_call(
        partial(apply_kernel, block=block),
        in_specs=[smem(), smem(), vmem(), vmem(), vmem(), vmem()],
        out_specs=[vmem(), vmem()],
        out_shape=[
            jax.ShapeDtypeStruct(moment.shape, full),
            jax.ShapeDtypeStruct(moment.shape, low),
        ],
        compiler_params=params(48),
        cost_estimate=cost(10),
        name="apply",
    )(info, gains, first, second, moment, master)


def chains(mine, other, wide_at, first_matrix, second_matrix, factor, debias, table, rider):
    wide = lax.axis_size("wide")
    if wide != 8:
        which = jnp.arange(4)
        slots = (which == first_matrix).astype(full)[:, None, None, None] * mine
        slots = slots + (which == second_matrix).astype(full)[:, None, None, None] * other
        total = lax.psum(slots, "wide")
        kind = jnp.zeros((2,), jnp.int32)
        outs = []
        for matrix in (first_matrix, second_matrix):
            gram = lax.dynamic_index_in_dim(total, matrix, 0, keepdims=False)
            half = gram[: len(TILES) // 2]
            outs.append(chain(kind, factor, debias, (gram, gram, half, half), table))
        return outs[0][0], outs[1][0], outs[0][1:], rider
    half = len(TILES) // 2
    pairs = [(i, i ^ 1) for i in range(8)]
    lower = wide_at % 2 == 0
    moved = lax.ppermute(other[:half], "wide", [(5, 4)])
    chip = mine + lax.ppermute(mine, "wide", pairs)
    up_send = jnp.where(lower, chip[:half], chip[half:])
    down_send = jnp.where(wide_at == 4, moved, jnp.where(wide_at == 5, other[half:], up_send))
    up = up_send + lax.ppermute(up_send, "wide", [(2, 4), (4, 2), (3, 5), (5, 3)])
    down = down_send + lax.ppermute(down_send, "wide", [(4, 6), (6, 4), (5, 7), (7, 5)])
    send = jnp.where((wide_at == 4) | (wide_at >= 6), down, up)
    swap = lax.ppermute(send, "wide", [(2, 3), (4, 5), (6, 7), (7, 6)])
    back = lax.ppermute(up, "wide", [(5, 4)])
    kept = jnp.where(wide_at >= 5, down, up)
    got = jnp.where(wide_at == 4, back, swap)
    kind = jnp.where(wide_at < 2, 0, jnp.where(wide_at == 2, 1, 2))
    kind = jnp.stack([kind, lower.astype(jnp.int32)]).astype(jnp.int32)
    got, rider = lax.optimization_barrier((got, rider))
    own, *table_new = chain(kind, factor, debias, (chip, other, kept, got), table)
    come = lax.ppermute(own, "wide", [(3, 2), (4, 5)])
    return jnp.where(wide_at == 5, come, own), jnp.where(wide_at == 5, own, come), table_new, rider


def scale_rows(hidden):
    center = hidden - jnp.mean(hidden, axis=-1, keepdims=True)
    inverse = lax.rsqrt(jnp.mean(center * center, axis=-1, keepdims=True) + norm_eps)
    return center * inverse, inverse


def unscale_rows(upstream, scaled, inverse, gain):
    weighted = upstream * gain
    return inverse * (
        weighted
        - jnp.mean(weighted, axis=-1, keepdims=True)
        - scaled * jnp.mean(weighted * scaled, axis=-1, keepdims=True)
    )


def forward_kernel(context_ref, normed0_ref, share_ref, vectors_ref, bias_ref, out_w_ref, up_w_ref, down_w_ref,
                   scaled1_ref, inverse1_ref, input1_ref, active_ref, slope_ref,
                   scaled2_ref, inverse2_ref, pooled_ref, normed1_ref, sum_ref):
    step = pl.program_id(0)

    @pl.when(step == 0)
    def _():
        attended = dot32(context_ref[...], out_w_ref[...], 1, 1) + vectors_ref[8:9]
        scaled, inverse = scale_rows(normed0_ref[...] + attended)
        scaled1_ref[...], inverse1_ref[...] = scaled, inverse
        normed1_ref[...] = scaled * vectors_ref[2:3] + vectors_ref[3:4]
        input1_ref[...] = normed1_ref[...].astype(low)
        sum_ref[...] = normed1_ref[...] + vectors_ref[9:10]

    inner = dot32(input1_ref[...], up_w_ref[...], 1, 1) + bias_ref[...]
    cdf = 0.5 * (1.0 + lax.erf(inner * math.sqrt(0.5)))
    active = (inner * cdf).astype(low)
    active_ref[...] = active
    slope_ref[...] = cdf + inner * (jnp.exp(-0.5 * inner * inner) * (1.0 / math.sqrt(2.0 * math.pi)))
    sum_ref[...] += dot32(active, down_w_ref[...], 1, 0)

    @pl.when(step == pl.num_programs(0) - 1)
    def _():
        scaled, inverse = scale_rows(sum_ref[...])
        scaled2_ref[...], inverse2_ref[...] = scaled, inverse
        normed2 = scaled * vectors_ref[4:5] + vectors_ref[5:6]
        pooled_ref[...] = jnp.dot(share_ref[...], normed2, precision=highest)


CHUNK = 512


def same(shape):
    return pl.BlockSpec(shape, lambda c: (0,) * len(shape))


def forward_rest(context, normed0, share, vectors, out_w, up_w, down_w):
    tokens = context.shape[0]
    pairs = share.shape[0]
    wide_rows = jax.ShapeDtypeStruct((tokens, D), full)
    column = jax.ShapeDtypeStruct((tokens, 1), full)
    return pl.pallas_call(
        forward_kernel,
        grid=(FF // CHUNK,),
        in_specs=[
            same((tokens, D)),
            same((tokens, D)),
            same((pairs, tokens)),
            same(vectors.shape),
            pl.BlockSpec((1, CHUNK), lambda c: (0, c)),
            same((D, D)),
            pl.BlockSpec((CHUNK, D), lambda c: (c, 0)),
            pl.BlockSpec((CHUNK, D), lambda c: (c, 0)),
        ],
        out_specs=[
            same((tokens, D)),
            same((tokens, 1)),
            same((tokens, D)),
            pl.BlockSpec((tokens, CHUNK), lambda c: (0, c)),
            pl.BlockSpec((tokens, CHUNK), lambda c: (0, c)),
            same((tokens, D)),
            same((tokens, 1)),
            same((pairs, D)),
        ],
        out_shape=[
            wide_rows,
            column,
            jax.ShapeDtypeStruct((tokens, D), low),
            jax.ShapeDtypeStruct((tokens, FF), low),
            jax.ShapeDtypeStruct((tokens, FF), full),
            wide_rows,
            column,
            jax.ShapeDtypeStruct((pairs, D), full),
        ],
        scratch_shapes=[pltpu.VMEM((tokens, D), full)] * 2,
        compiler_params=params(58),
        cost_estimate=cost(25),
        name="forward_rest",
    )(context, normed0, share, vectors, vectors[14:].reshape(1, -1), out_w, up_w, down_w)


def backward_kernel(pooled_ref, share_ref, vectors_ref, scaled2_ref, inverse2_ref, active_ref, slope_ref,
                    input1_ref, scaled1_ref, inverse1_ref, context_ref, out_w_ref, up_w_ref, down_w_ref,
                    down_grad_ref, up_grad_ref, out_grad_ref, sum1_ref, context_grad_ref, sums_ref, up_sums_ref,
                    branch_ref, total_ref):
    step = pl.program_id(0)

    def over_tokens(x):
        return jnp.sum(x, axis=0, keepdims=True)

    @pl.when(step == 0)
    def _():
        spread = lax.dot_general(
            share_ref[...], pooled_ref[...], dims(0, 0), precision=highest, preferred_element_type=full
        )
        scaled = scaled2_ref[...]
        back = unscale_rows(spread, scaled, inverse2_ref[...], vectors_ref[4:5])
        total_ref[...] = back
        branch = back.astype(low)
        branch_ref[...] = branch
        sums_ref[2:3] = over_tokens(spread * scaled)
        sums_ref[3:4] = over_tokens(spread)
        sums_ref[5:6] = over_tokens(branch.astype(full))

    branch = branch_ref[...]
    inner_grad = (dot32(branch, down_w_ref[...], 1, 1) * slope_ref[...]).astype(low)
    down_grad_ref[...] = dot32(active_ref[...], branch, 0, 0).astype(low)
    up_grad_ref[...] = dot32(inner_grad, input1_ref[...], 0, 0).astype(low)
    up_sums_ref[...] = over_tokens(inner_grad.astype(full))
    total_ref[...] += dot32(inner_grad, up_w_ref[...], 1, 0)

    @pl.when(step == pl.num_programs(0) - 1)
    def _():
        upstream = total_ref[...]
        scaled = scaled1_ref[...]
        back = unscale_rows(upstream, scaled, inverse1_ref[...], vectors_ref[2:3])
        sum1_ref[...] = back
        attended = back.astype(low)
        sums_ref[0:1] = over_tokens(upstream * scaled)
        sums_ref[1:2] = over_tokens(upstream)
        sums_ref[4:5] = over_tokens(attended.astype(full))
        out_grad_ref[...] = dot32(attended, context_ref[...], 0, 0).astype(low)
        context_grad_ref[...] = dot32(attended, out_w_ref[...], 1, 0).astype(low)


def backward_rest(pooled_grads, share, vectors, kept, context, out_w, up_w, down_w):
    scaled1, inverse1, input1, active, slope, scaled2, inverse2 = kept
    tokens = context.shape[0]
    pairs = share.shape[0]
    rows = pl.BlockSpec((CHUNK, D), lambda c: (c, 0))
    cols = pl.BlockSpec((tokens, CHUNK), lambda c: (0, c))
    return pl.pallas_call(
        backward_kernel,
        grid=(FF // CHUNK,),
        in_specs=[
            same((pairs, D)),
            same((pairs, tokens)),
            same(vectors.shape),
            same((tokens, D)),
            same((tokens, 1)),
            cols,
            cols,
            same((tokens, D)),
            same((tokens, D)),
            same((tokens, 1)),
            same((tokens, D)),
            same((D, D)),
            rows,
            rows,
        ],
        out_specs=[
            rows,
            rows,
            same((D, D)),
            same((tokens, D)),
            same((tokens, D)),
            same((8, D)),
            pl.BlockSpec((1, CHUNK), lambda c: (0, c)),
        ],
        out_shape=[
            jax.ShapeDtypeStruct((FF, D), low),
            jax.ShapeDtypeStruct((FF, D), low),
            jax.ShapeDtypeStruct((D, D), low),
            jax.ShapeDtypeStruct((tokens, D), full),
            jax.ShapeDtypeStruct((tokens, D), low),
            jax.ShapeDtypeStruct((8, D), full),
            jax.ShapeDtypeStruct((1, FF), full),
        ],
        scratch_shapes=[pltpu.VMEM((tokens, D), low), pltpu.VMEM((tokens, D), full)],
        compiler_params=params(58),
        cost_estimate=cost(35),
        name="backward_rest",
    )(pooled_grads, share, vectors, scaled2, inverse2, active, slope, input1, scaled1, inverse1, context,
      out_w, up_w, down_w)


def layout(lengths):
    row_ends = jnp.cumsum(lengths)
    starts = row_ends - lengths
    places = jnp.arange(SEQ, dtype=jnp.int32)
    segment = jnp.sum((places[:, None] >= row_ends[None, :]).astype(jnp.int32), axis=1)
    chosen = segment[:, None] == jnp.arange(SLOTS, dtype=jnp.int32)[None, :]
    start_at = jnp.sum(jnp.where(chosen, starts[None, :], 0), axis=1)
    length_at = jnp.sum(jnp.where(chosen, lengths[None, :], 0), axis=1)
    position = places - start_at
    second = (2 * position >= length_at).astype(jnp.int32)
    return (chosen.astype(full), position, second, segment)


def norm_forward(hidden, gain, bias):
    center = hidden - jnp.mean(hidden, axis=-1, keepdims=True)
    inverse = lax.rsqrt(jnp.mean(center * center, axis=-1, keepdims=True) + norm_eps)
    scaled = center * inverse
    return (scaled * gain + bias, scaled, inverse)


def norm_backward(upstream, scaled, inverse, gain):
    weighted = upstream * gain
    back = inverse * (
        weighted
        - jnp.mean(weighted, axis=-1, keepdims=True)
        - scaled * jnp.mean(weighted * scaled, axis=-1, keepdims=True)
    )
    return (back, jnp.sum(upstream * scaled, axis=0), jnp.sum(upstream, axis=0))


def project(left, right):
    return jnp.dot(left, right, preferred_element_type=full)


def task_loss(logits, scores, tasks, labels, negatives, counts):
    logprob = jax.nn.log_softmax(logits, axis=-1)
    picked = jnp.sum(
        jnp.where(labels[:, :, None] == jnp.arange(3, dtype=jnp.int32), logprob, 0.0), axis=2
    )
    chosen = negatives[:, :, :, None] == jnp.arange(scores.shape[1], dtype=jnp.int32)
    rivals = jnp.sum(jnp.where(chosen, scores[:, None, None, :], 0.0), axis=3)
    together = jnp.concatenate([scores[:, :, None], rivals], axis=2)
    ranking = jax.nn.logsumexp(together, axis=2) - scores
    first_part = jnp.sum(jnp.where(tasks == 0, -picked, 0.0)) / counts[0]
    return first_part + jnp.sum(jnp.where(tasks == 1, ranking, 0.0)) / counts[1]


def adam(weight, grad, first, second, step, rate):
    first = beta_one * first + (1.0 - beta_one) * grad
    second = beta_two * second + (1.0 - beta_two) * grad * grad
    unbiased = first / (1.0 - beta_one**step)
    spread = second / (1.0 - beta_two**step)
    return (
        weight - rate * (unbiased / (jnp.sqrt(spread) + adam_eps) + adam_decay * weight),
        first,
        second,
    )


def broadcast_all(x):
    count = lax.axis_size("narrow") * lax.axis_size("wide")
    return lax.all_to_all(
        jnp.broadcast_to(x[None], (count,) + x.shape), BOTH, split_axis=0, concat_axis=0, tiled=True
    )


def sides(wide):
    return [list(range(0, wide, 2)), list(range(1, wide, 2))]


def chip_mates(wide):
    return [(i, i ^ 1) for i in range(wide)]


def by_owner(grad, spans, parts):
    pieces = [
        grad[lo:hi].reshape(parts, (hi - lo) // parts, D) for lo, hi in spans
    ]
    return jnp.concatenate(pieces, axis=1).reshape(-1, D).astype(low)


def gather_weights(master, narrow_at, wide_at, first):
    wide = lax.axis_size("wide")
    if wide != 8:
        whole = lax.all_gather(master.astype(low), "wide", axis=0, tiled=True)
        return first, list(whole.reshape(wide, -1, D))
    share = master.shape[0] // lax.axis_size("narrow")
    mine = lax.dynamic_slice_in_dim(master, narrow_at * share, share, 0).astype(low)
    near = lax.all_gather(mine, "wide", axis=0, tiled=False, axis_index_groups=sides(wide))
    near, first = lax.optimization_barrier((near, first))
    return first, [
        lax.all_gather(part, "narrow", axis=1, tiled=True)
        for part in (near[: wide // 4], near[wide // 4 :])
    ]


def both_cores(held, wide_at):
    owners = []
    other = lax.ppermute(held, "wide", chip_mates(lax.axis_size("wide")))
    side = wide_at % 2
    even = jnp.where(side == 0, held, other)
    odd = jnp.where(side == 0, other, held)
    for at in range(held.shape[0]):
        owners += [even[at], odd[at]]
    return owners


def rows_of(owners, matrix):
    rows = owners[0].shape[0]
    lo, hi = BOUNDS[matrix], BOUNDS[matrix + 1]
    pieces = []
    for at in range(lo // rows, -(-hi // rows)):
        pieces.append(owners[at][max(lo - at * rows, 0) : min(hi - at * rows, rows)])
    return jnp.concatenate(pieces) if len(pieces) > 1 else pieces[0]


def shards(
    token_ids,
    seq_lengths,
    task_ids,
    labels,
    negatives,
    step_count,
    hidden_master,
    hidden_momentum,
    table_master,
    table_first,
    table_second,
    pos_types,
    pos_first,
    pos_second,
    vectors,
    vec_first,
    vec_second,
):
    wide_at = lax.axis_index("wide")
    narrow_at = lax.axis_index("narrow")
    wide = lax.axis_size("wide")
    narrow = lax.axis_size("narrow")
    count = wide * narrow
    device_at = narrow_at * wide + wide_at
    micro_count, rows_each = token_ids.shape[:2]
    batch = micro_count * rows_each
    tokens = batch * SEQ
    shard = hidden_master.shape[0]
    vocab = table_master.shape[1]
    features = table_master.shape[0] // narrow
    pairs_each = rows_each * SLOTS

    parts = [token_ids, task_ids, labels, negatives]
    sizes = [part.size for part in parts]
    packed = jnp.concatenate([part.reshape(-1) for part in parts])
    packed = jnp.pad(packed, (0, -packed.size % LANES))
    gathered = broadcast_all(packed)
    ends = [sum(sizes[: i + 1]) for i in range(len(sizes))]
    ids_all = gathered[:, : ends[0]]

    def pairs_of(lo, hi, tail):
        block = gathered[:, lo:hi].reshape((count, micro_count, pairs_each) + tail)
        return jnp.moveaxis(block, 1, 0).reshape((micro_count, count * pairs_each) + tail)

    tasks_all = pairs_of(ends[0], ends[1], ())
    labels_all = pairs_of(ends[1], ends[2], ())
    negatives_all = pairs_of(ends[2], ends[3], (NEG,))
    counts = jnp.stack(
        [jnp.sum((tasks_all == 0).astype(full)), jnp.sum((tasks_all == 1).astype(full))]
    )


    group_ids = lax.dynamic_slice_in_dim(ids_all, narrow_at * wide, wide, 0).reshape(-1)
    pieces = lookup(group_ids, table_master)
    pieces, gathers = gather_weights(hidden_master, narrow_at, wide_at, pieces)
    simple = wide != 8
    arrived = lax.all_to_all(
        pieces.reshape(wide, tokens, -1), "wide", split_axis=0, concat_axis=0, tiled=True
    )
    token_rows = jnp.moveaxis(arrived, 0, 1).reshape(tokens, D)

    lengths = seq_lengths.reshape(batch, SLOTS)
    member, position, second, segment = jax.vmap(layout)(lengths)
    flat_position = position.reshape(-1)
    flat_second = second.reshape(-1)
    place_rows = pos_types[flat_position]
    place_rows = place_rows + jnp.where(flat_second[:, None] == 1, pos_types[SEQ + 1], pos_types[SEQ])
    if simple:
        owners = gathers
    else:
        place_rows, held = lax.optimization_barrier((place_rows, gathers[0]))
        owners = both_cores(held, wide_at)
    embed = token_rows.astype(full) + place_rows
    normed0, scaled0, inverse0 = norm_forward(embed, vectors[0], vectors[1])
    input0 = normed0.astype(low)
    qkv_bias = jnp.concatenate([vectors[6], jnp.zeros_like(vectors[6]), vectors[7]])
    weight_qkv, weight_out = rows_of(owners, 0), rows_of(owners, 1)
    mixed = (project(input0, weight_qkv.T) + qkv_bias).astype(low)
    context_low, logsum = attend(mixed, segment)
    if not simple:
        rest, context_low = lax.optimization_barrier((gathers[1], context_low))
        owners = owners + both_cores(rest, wide_at)
    weight_up, weight_down = rows_of(owners, 2), rows_of(owners, 3)
    pair_at = (jnp.arange(batch, dtype=jnp.int32)[:, None] * SLOTS + segment).reshape(1, -1)
    pairs = jnp.arange(batch * SLOTS, dtype=jnp.int32)[:, None]
    share = jnp.where(pair_at == pairs, 1.0 / lengths.astype(full).reshape(-1, 1), 0.0)
    scaled1, inverse1, input1, active, slope, scaled2, inverse2, flat_pooled = forward_rest(
        context_low, normed0, share, vectors, weight_out, weight_up, weight_down
    )
    heads = vectors[10:14]
    head_out = jnp.dot(flat_pooled, heads.T, precision=highest)

    sent = jnp.pad(head_out.reshape(-1), (0, -head_out.size % LANES))
    head_all = broadcast_all(sent)[:, : head_out.size]
    head_all = head_all.reshape(count, micro_count, pairs_each, 4)
    head_all = jnp.moveaxis(head_all, 1, 0).reshape(micro_count, count * pairs_each, 4)

    def objective(every):
        return task_loss(every[:, :, :3], every[:, :, 3], tasks_all, labels_all, negatives_all, counts)

    loss, pullback = jax.vjp(objective, head_all)
    head_grads = pullback(jnp.ones_like(loss))[0]
    output_grads = lax.dynamic_slice_in_dim(head_grads, device_at * pairs_each, pairs_each, 1)
    output_grads = output_grads.reshape(-1, 4)
    heads_grad = jnp.dot(output_grads.T, flat_pooled, precision=highest)
    pooled_grads = jnp.dot(output_grads, heads, precision=highest)

    spans_down = [(0, 768), (768, 1920), (1920, 3072)]
    spans_up = [(0, 384), (384, 1536), (1536, 2688), (2688, 3072)]
    spans_front = [(0, 1152), (1152, 2304), (2304, 3072)]

    side = wide_at % 2

    def ready(grad, spans):
        if simple:
            return grad.astype(low)
        grad = by_owner(grad, spans, narrow)
        left, right = grad[:, : D // 2], grad[:, D // 2 :]
        stays = jnp.where(side == 0, left, right)
        leaves = jnp.where(side == 0, right, left)
        return stays, leaves

    def between_cores(grad):
        if simple:
            return grad
        stays, leaves = grad
        return stays, lax.ppermute(leaves, "wide", chip_mates(wide))

    def slices(grad):
        if simple:
            return [grad]
        stays, comes = grad
        chip = (stays.astype(full) + comes.astype(full)).astype(low).reshape(narrow, -1, D // 2)
        return [chip[narrow_at ^ turn] for turn in range(narrow)]

    def over_narrow(parts):
        return parts[:1] + [
            lax.ppermute(part, "narrow", [(i, i ^ (turn + 1)) for i in range(narrow)])
            for turn, part in enumerate(parts[1:])
        ]

    together = lax.optimization_barrier
    kept = (scaled1, inverse1, input1, active, slope, scaled2, inverse2)
    down_grad, up_grad, out_grad, sum1_grad, context_grad, sums, up_sums = backward_rest(
        pooled_grads, share, vectors, kept, context_low, weight_out, weight_up, weight_down
    )
    down_pair = between_cores(ready(down_grad, spans_down))
    up_pair = between_cores(ready(up_grad, spans_up))
    down_cut, up_pair, context_grad = together((slices(down_pair), up_pair, context_grad))
    down_part = over_narrow(down_cut)
    up_cut, context_grad = together((slices(up_pair), context_grad))
    up_part = over_narrow(up_cut)
    mixed_grad = attend_back(mixed, context_grad, logsum, segment)
    mixed_grad, down_part = together((mixed_grad, down_part))
    normed0_grad = sum1_grad + project(mixed_grad, weight_qkv)
    embed_grad, gain0, bias0 = norm_backward(normed0_grad, scaled0, inverse0, vectors[0])

    table_send = embed_grad.astype(low).T.reshape(wide, narrow, features, tokens)
    table_send = jnp.moveaxis(table_send, 1, 0).reshape(count, features, tokens)
    table_send, mixed_grad = together((table_send, mixed_grad))
    come = lax.all_to_all(table_send, BOTH, split_axis=0, concat_axis=0, tiled=True)

    qkv_grad = project(mixed_grad.T, input0)
    front_grad = jnp.concatenate([qkv_grad.astype(low), out_grad.astype(low)])
    front_send, embed_grad, mixed_grad, up_part = together(
        (ready(front_grad, spans_front), embed_grad, mixed_grad, up_part)
    )
    front_part = over_narrow(slices(between_cores(front_send)))
    mixed_sum = jnp.sum(mixed_grad.astype(full), axis=0)
    small_rows = jnp.concatenate(
        [
            jnp.stack([gain0, bias0]),
            sums[:4],
            jnp.stack([mixed_sum[:D], mixed_sum[2 * D :]]),
            sums[4:6],
        ]
    )
    up_rows = up_sums.reshape(-1, D)

    places = jnp.arange(SEQ, dtype=jnp.int32)[:, None]
    row_hot = jnp.concatenate(
        [
            flat_position[None] == places,
            jnp.stack([flat_second == 0, flat_second == 1]),
        ]
    ).astype(low)
    high_part, low_part = halves(embed_grad)
    pos_grad = project(jnp.concatenate([row_hot, row_hot], axis=1), jnp.concatenate([high_part, low_part]))
    small = jnp.concatenate([pos_grad, small_rows, heads_grad, up_rows])
    small_count = small.shape[0]
    small = jnp.pad(small, ((0, count * features - small_count), (0, 0)))

    def added(parts):
        return sum(part.astype(full) for part in parts).astype(low)

    joined = jnp.concatenate([added(front_part), added(up_part), added(down_part)])
    small_send = small.astype(low).reshape(count, features, D)
    come, small_send = together((come, small_send))
    small_come = lax.all_to_all(small_send, BOTH, split_axis=0, concat_axis=0, tiled=True)
    table_part, table_square = collect(ids_all, come, vocab, tokens)
    if simple:
        hidden_part = lax.psum_scatter(joined, "wide", scatter_dimension=0, tiled=True)
        hidden_part = lax.psum_scatter(hidden_part, "narrow", scatter_dimension=0, tiled=True)
        hidden_square = jnp.sum(jnp.square(hidden_part.astype(full)))
    else:
        owned = lax.psum_scatter(
            joined, "wide", scatter_dimension=0, tiled=True, axis_index_groups=sides(wide)
        )
        owned, table_square, small_come = together((owned, table_square, small_come))
        hidden_square = jnp.sum(jnp.square(owned.astype(full)))
        half = owned.shape[0] // 2
        stays = jnp.where(side == 0, owned[:half], owned[half:])
        leaves = jnp.where(side == 0, owned[half:], owned[:half])
        comes = lax.ppermute(leaves, "wide", chip_mates(wide))
        hidden_part = jnp.concatenate(
            [jnp.where(side == 0, stays, comes), jnp.where(side == 0, comes, stays)], axis=1
        )
    small_part = jnp.sum(small_come.astype(full), axis=0)
    square = hidden_square + table_square[0, 0] + jnp.sum(small_part * small_part)
    square, hidden_part = together((square, hidden_part))
    if simple:
        hidden_all = lax.all_gather(hidden_part, "narrow", axis=0, tiled=True)
    else:
        hidden_all = jnp.concatenate(
            [hidden_part]
            + [
                lax.ppermute(hidden_part, "narrow", [(i, i ^ turn) for i in range(narrow)])
                for turn in range(1, narrow)
            ]
        )
    squares = broadcast_all(jnp.broadcast_to(square, (LANES,)))
    squares, hidden_all, table_part = together((squares, hidden_all, table_part))
    table_grad = lax.all_gather(table_part, "narrow", axis=0, tiled=True)
    clip_norm = jnp.sqrt(jnp.sum(squares[:, 0]))
    factor = jnp.minimum(1.0, clip_bound / clip_norm)

    start = wide_at * shard
    bounds = jnp.array(BOUNDS, jnp.int32)
    first_matrix = jnp.sum((start >= bounds[1:4]).astype(jnp.int32))
    second_matrix = jnp.sum((start + shard - 1 >= bounds[1:4]).astype(jnp.int32))
    split = jnp.minimum(bounds[first_matrix + 1] - start, shard)
    block = shard // 3
    piece = shard // 12
    at = jnp.arange(12, dtype=jnp.int32)
    if simple:
        source = at
    else:
        lead = split // piece
        each = lead // narrow
        rest = (12 - lead) // narrow
        in_first = at < lead
        inside = jnp.where(in_first, at, at - lead)
        width = jnp.maximum(jnp.where(in_first, each, rest), 1)
        origin = (inside // width) ^ narrow_at
        source = origin * (12 // narrow) + jnp.where(in_first, 0, each) + inside % width
    swap = (wide_at == 2).astype(jnp.int32) * (0 if simple else 1)
    info = jnp.concatenate([jnp.stack([split, swap]), source]).astype(jnp.int32)
    gains = jnp.array([0.2 * math.sqrt(hi - lo) for lo, hi in zip(BOUNDS, BOUNDS[1:])], full)
    moment, mine, other = moment_and_grams(
        info, factor[None], hidden_all, hidden_momentum, piece, block
    )
    step = step_count[0].astype(full)
    debias = jnp.stack([1.0 / (1.0 - beta_one**step), 1.0 / (1.0 - beta_two**step)])
    chain0, chain1, (table_new, table_first_new, table_second_new, table_copy), late_small = chains(
        mine,
        other,
        wide_at,
        first_matrix,
        second_matrix,
        factor[None],
        debias,
        (table_grad, table_master, table_first, table_second),
        small_part,
    )
    small_all = broadcast_all(late_small.astype(low)).reshape(-1, D)[:small_count].astype(full)
    slot_gains = jnp.stack([gains[first_matrix], gains[second_matrix]])
    hidden_new, hidden_copy = apply_chain(info, slot_gains, chain0, chain1, moment, hidden_master, block)

    pos_new, pos_first_new, pos_second_new = adam(
        pos_types, factor * small_all[: SEQ + 2], pos_first, pos_second, step, 0.02
    )
    vectors_new, vec_first_new, vec_second_new = adam(
        vectors, factor * small_all[SEQ + 2 :], vec_first, vec_second, step, 0.2
    )
    return (
        loss,
        clip_norm,
        moment,
        hidden_new,
        hidden_copy,
        table_new,
        table_first_new,
        table_second_new,
        table_copy,
        pos_new,
        pos_first_new,
        pos_second_new,
        vectors_new,
        vec_first_new,
        vec_second_new,
    )


def solution(mesh):
    rows = P(None, BOTH, None)
    owned = P("wide", None)
    return jax.shard_map(
        shards,
        mesh=mesh,
        in_specs=(rows, rows, rows, rows, P(None, BOTH, None, None), P())
        + (owned,) * 5
        + (P(),) * 6,
        out_specs=(P(), P()) + (owned,) * 7 + (P(),) * 6,
        check_vma=False,
    )
```

```python
from functools import partial
import math

import jax
import jax.numpy as jnp
from jax import lax
from jax.experimental import pallas as pl
from jax.experimental.pallas import tpu as pltpu
from jax.sharding import PartitionSpec as P

D = 768
HEADS = 12
HEAD = 64
FF = 3072
SEQ = 512
SLOTS = 4
NEG = 4
NS_TURNS = 5
LANES = 128
GROUPS = 4
WIDTH = LANES // GROUPS
BLOCK = 256
TILES = [(i, j) for i in range(D // BLOCK) for j in range(i, D // BLOCK)]

BOTH = ("narrow", "wide")
highest = lax.Precision.HIGHEST
clip_bound = 0.002
norm_eps = 1e-06
muon_beta = 0.95
muon_rate = 0.1
muon_decay = 0.01
beta_one = 0.9
beta_two = 0.999
adam_eps = 1e-08
adam_decay = 0.01
BOUNDS = (0, 3 * D, 4 * D, 4 * D + FF, 4 * D + 2 * FF)

low = jnp.bfloat16
full = jnp.float32


def dims(left, right):
    return (((left,), (right,)), ((), ()))


def dot32(left, right, left_dim, right_dim):
    return lax.dot_general(left, right, dims(left_dim, right_dim), preferred_element_type=full)


def halves(x):
    high = x.astype(low)
    return high, (x - high.astype(full)).astype(low)


def dot_split(left, right, left_dim=1, right_dim=0):
    (lh, ll), (rh, rl) = left, right
    return dot32(lh, rh, left_dim, right_dim) + (
        dot32(lh, rl, left_dim, right_dim) + dot32(ll, rh, left_dim, right_dim)
    )


def params(mib):
    return pltpu.CompilerParams(vmem_limit_bytes=mib << 20)


def cost(micros):
    return pl.CostEstimate(flops=micros * 10**9, transcendentals=0, bytes_accessed=1 << 20)


def vmem():
    return pl.BlockSpec(memory_space=pltpu.VMEM)


def smem():
    return pl.BlockSpec(memory_space=pltpu.SMEM)


def attend_kernel(mixed_ref, seg_col_ref, seg_row_ref, context_ref, logsum_ref):
    same = seg_col_ref[0] == seg_row_ref[0]

    def pair(step, carry):
        at = pl.multiple_of(step * LANES, LANES)
        queries = mixed_ref[:, pl.ds(at, LANES)]
        keys = mixed_ref[:, pl.ds(D + at, LANES)]
        values = mixed_ref[:, pl.ds(2 * D + at, LANES)]
        outs = []
        for half in range(2):
            cut = slice(half * HEAD, (half + 1) * HEAD)
            raw = dot32(keys[:, cut], queries[:, cut], 1, 1)
            scores = jnp.where(same, raw * (1.0 / math.sqrt(HEAD)), -1e30)
            peak = jnp.max(scores, axis=0, keepdims=True)
            lifted = jnp.exp(scores - peak)
            total = jnp.sum(lifted, axis=0, keepdims=True)
            probs = (lifted * (1.0 / total)).astype(low)
            outs.append(dot32(values[:, cut], probs, 0, 0))
            logsum_ref[0, pl.ds(2 * step + half, 1), :] = peak + jnp.log(total)
        context_ref[:, pl.ds(at, LANES)] = jnp.concatenate(outs, axis=0).T.astype(low)
        return carry

    lax.fori_loop(0, HEADS // 2, pair, 0)


def attend(mixed, segment):
    rows = segment.shape[0]
    return pl.pallas_call(
        attend_kernel,
        grid=(rows,),
        in_specs=[
            pl.BlockSpec((SEQ, 3 * D), lambda b: (b, 0)),
            pl.BlockSpec((1, SEQ, 1), lambda b: (b, 0, 0)),
            pl.BlockSpec((1, 1, SEQ), lambda b: (b, 0, 0)),
        ],
        out_specs=[
            pl.BlockSpec((SEQ, D), lambda b: (b, 0)),
            pl.BlockSpec((1, 16, SEQ), lambda b: (b, 0, 0)),
        ],
        out_shape=[
            jax.ShapeDtypeStruct((rows * SEQ, D), low),
            jax.ShapeDtypeStruct((rows, 16, SEQ), full),
        ],
        compiler_params=params(48),
        cost_estimate=cost(19),
        name="attend",
    )(mixed, segment[:, :, None], segment[:, None, :])


def attend_back_kernel(mixed_ref, grad_ref, logsum_ref, seg_col_ref, seg_row_ref, out_ref):
    same = seg_col_ref[0] == seg_row_ref[0]
    scale = 1.0 / math.sqrt(HEAD)

    def pair(step, carry):
        at = pl.multiple_of(step * LANES, LANES)
        queries = mixed_ref[:, pl.ds(at, LANES)]
        keys = mixed_ref[:, pl.ds(D + at, LANES)]
        values = mixed_ref[:, pl.ds(2 * D + at, LANES)]
        upstream = grad_ref[:, pl.ds(at, LANES)]
        query_grads, key_grads, value_grads = [], [], []
        for half in range(2):
            cut = slice(half * HEAD, (half + 1) * HEAD)
            logsum = logsum_ref[0, pl.ds(2 * step + half, 1), :]
            raw = dot32(keys[:, cut], queries[:, cut], 1, 1)
            probs = jnp.exp(jnp.where(same, raw * scale, -1e30) - logsum)
            prob_grads = dot32(values[:, cut], upstream[:, cut], 1, 1)
            value_grads.append(dot32(probs.astype(low), upstream[:, cut], 1, 0))
            moved = jnp.sum(prob_grads * probs, axis=0, keepdims=True)
            back = (probs * (prob_grads - moved) * scale).astype(low)
            key_grads.append(dot32(back, queries[:, cut], 1, 0))
            query_grads.append(dot32(keys[:, cut], back, 0, 0))
        out_ref[:, pl.ds(at, LANES)] = jnp.concatenate(query_grads, axis=0).T.astype(low)
        out_ref[:, pl.ds(D + at, LANES)] = jnp.concatenate(key_grads, axis=1).astype(low)
        out_ref[:, pl.ds(2 * D + at, LANES)] = jnp.concatenate(value_grads, axis=1).astype(low)
        return carry

    lax.fori_loop(0, HEADS // 2, pair, 0)


def attend_back(mixed, context_grad, logsum, segment):
    rows = segment.shape[0]
    return pl.pallas_call(
        attend_back_kernel,
        grid=(rows,),
        in_specs=[
            pl.BlockSpec((SEQ, 3 * D), lambda b: (b, 0)),
            pl.BlockSpec((SEQ, D), lambda b: (b, 0)),
            pl.BlockSpec((1, 16, SEQ), lambda b: (b, 0, 0)),
            pl.BlockSpec((1, SEQ, 1), lambda b: (b, 0, 0)),
            pl.BlockSpec((1, 1, SEQ), lambda b: (b, 0, 0)),
        ],
        out_specs=pl.BlockSpec((SEQ, 3 * D), lambda b: (b, 0)),
        out_shape=jax.ShapeDtypeStruct((rows * SEQ, 3 * D), low),
        compiler_params=params(56),
        cost_estimate=cost(28),
        name="attend_back",
    )(mixed, context_grad, logsum, segment[:, :, None], segment[:, None, :])


def lookup_kernel(ids_ref, table_ref, out_ref, turned_ref, rows_ref):
    step = pl.program_id(0)
    features, width = table_ref.shape
    tokens, chunk = out_ref.shape[0], rows_ref.shape[0]
    block = table_ref[...].astype(low).astype(full)
    block = jnp.concatenate([block, jnp.zeros((LANES - features, width), full)], axis=0)
    turned_ref[pl.ds(pl.multiple_of(step * width, width), width), :] = block.T

    @pl.when(step == pl.num_programs(0) - 1)
    def _():
        def piece(c, carry):
            def body(i, inner):
                at = i * 32
                found = [turned_ref[pl.ds(ids_ref[c * chunk + at + k], 1), :] for k in range(32)]
                for k in range(32):
                    rows_ref[pl.ds(at + k, 1), :] = found[k]
                return inner

            lax.fori_loop(0, chunk // 32, body, 0)
            start = pl.multiple_of(c * chunk, chunk)
            out_ref[pl.ds(start, chunk), :] = rows_ref[:, :features].astype(low)
            return carry

        lax.fori_loop(0, tokens // chunk, piece, 0)


def lookup(ids, table):
    features, vocab = table.shape
    width = -(-vocab // (4 * LANES)) * LANES
    steps = -(-vocab // width)
    return pl.pallas_call(
        lookup_kernel,
        grid=(steps,),
        in_specs=[smem(), pl.BlockSpec((features, width), lambda s: (0, s))],
        out_specs=pl.BlockSpec((ids.shape[0], features), lambda s: (0, 0)),
        out_shape=jax.ShapeDtypeStruct((ids.shape[0], features), low),
        scratch_shapes=[pltpu.VMEM((steps * width, LANES), full), pltpu.VMEM((1024, LANES), full)],
        compiler_params=params(56),
        cost_estimate=cost(19),
        name="lookup",
    )(ids, table)


def collect_kernel(place_ref, ids_ref, grads_ref, out_ref, square_ref, *scratch,
                   span, tokens, features, vocab):
    sums, rows_ref = scratch[:-1], scratch[-1]
    step = pl.program_id(0)
    last = pl.num_programs(0) - 1
    streams = len(sums)
    batch = 4 * streams

    @pl.when(step == 0)
    def _():
        for total in sums:
            total[...] = jnp.zeros_like(total)

    group = ids_ref[0] // span
    grads = grads_ref[0].astype(full)
    pad = jnp.zeros((WIDTH - features, tokens), full)
    pieces = []
    for at in range(GROUPS):
        pieces += [jnp.where(group == at, grads, 0.0), pad]
    rows_ref[...] = jnp.concatenate(pieces, axis=0).T

    def body(i, carry):
        for base in range(0, batch, streams):
            at = i * batch + base
            places = [pl.ds(place_ref[0, 0, at + k], 1) for k in range(streams)]
            olds = [sums[k][places[k], :] for k in range(streams)]
            news = [rows_ref[pl.ds(at + k, 1), :] for k in range(streams)]
            for k in range(streams):
                sums[k][places[k], :] = olds[k] + news[k]
        return carry

    lax.fori_loop(0, tokens // batch, body, 0)

    @pl.when(step == last)
    def _():
        def flush(b, total):
            at = pl.multiple_of(b * LANES, LANES)
            block = sums[0][pl.ds(at, LANES), :]
            for k in range(1, streams):
                block += sums[k][pl.ds(at, LANES), :]
            turned = block.T
            for g in range(GROUPS):
                piece = turned[g * WIDTH:g * WIDTH + features]

                @pl.when(g * span + at < vocab)
                def _():
                    out_ref[:, pl.ds(pl.multiple_of(g * span + at, LANES), LANES)] = piece.astype(low)

            return total + block * block

        total = lax.fori_loop(0, span // LANES, flush, jnp.zeros((LANES, LANES), full))
        square_ref[...] = jnp.broadcast_to(jnp.sum(total, keepdims=True), square_ref.shape)


def collect(ids, grads, vocab, tokens):
    sources, features = grads.shape[:2]
    span = -(-vocab // (GROUPS * LANES)) * LANES
    return pl.pallas_call(
        partial(collect_kernel, span=span, tokens=tokens, features=features, vocab=vocab),
        grid=(sources,),
        in_specs=[
            pl.BlockSpec((1, 1, tokens), lambda s: (s, 0, 0), memory_space=pltpu.SMEM),
            pl.BlockSpec((1, 1, tokens), lambda s: (s, 0, 0)),
            pl.BlockSpec((1, features, tokens), lambda s: (s, 0, 0)),
        ],
        out_specs=[
            pl.BlockSpec((features, vocab), lambda s: (0, 0)),
            pl.BlockSpec((8, LANES), lambda s: (0, 0)),
        ],
        out_shape=[
            jax.ShapeDtypeStruct((features, vocab), low),
            jax.ShapeDtypeStruct((8, LANES), full),
        ],
        scratch_shapes=[pltpu.VMEM((span, LANES), full)] * 8 + [pltpu.VMEM((tokens, LANES), full)],
        compiler_params=params(56),
        cost_estimate=cost(150),
        name="collect",
    )((ids % span)[:, None, :], ids[:, None, :], grads)


def moment_kernel(info_ref, factor_ref, grad_ref, old_ref, moment_ref, mine_ref, other_ref,
                  *, piece, block):
    factor = factor_ref[0]
    for at in range(old_ref.shape[0] // piece):
        source = pl.multiple_of(info_ref[2 + at] * piece, piece)
        rows = slice(at * piece, (at + 1) * piece)
        moment_ref[rows] = muon_beta * old_ref[rows] + factor * grad_ref[pl.ds(source, piece)].astype(full)

    def grams(out_ref, start, stop):
        out_ref[...] = jnp.zeros_like(out_ref)

        def body(b, carry):
            high, small = halves(moment_ref[pl.ds(pl.multiple_of(b * block, block), block)])
            for at, (i, j) in enumerate(TILES):
                left, right = slice(i * BLOCK, (i + 1) * BLOCK), slice(j * BLOCK, (j + 1) * BLOCK)
                out_ref[at] += dot32(
                    jnp.concatenate([high[:, left], high[:, left], small[:, left]], axis=0),
                    jnp.concatenate([high[:, right], small[:, right], high[:, right]], axis=0),
                    0,
                    0,
                )
            return carry

        lax.fori_loop(start, stop, body, 0)

    lead, total = info_ref[0] // block, old_ref.shape[0] // block
    swap = info_ref[1] == 1
    grams(mine_ref, jnp.where(swap, lead, 0), jnp.where(swap, total, lead))
    grams(other_ref, jnp.where(swap, 0, lead), jnp.where(swap, lead, total))


def moment_and_grams(info, factor, grad, old, piece, block):
    tiles = jax.ShapeDtypeStruct((len(TILES), BLOCK, BLOCK), full)
    return pl.pallas_call(
        partial(moment_kernel, piece=piece, block=block),
        in_specs=[smem(), smem(), vmem(), vmem()],
        out_specs=[vmem()] * 3,
        out_shape=[jax.ShapeDtypeStruct(old.shape, full), tiles, tiles],
        compiler_params=params(48),
        cost_estimate=cost(10),
        name="moment",
    )(info, factor, grad, old)


def even_product(left, right, put):
    (lh, ll), (rh, rl) = left, right
    for i in range(D // BLOCK):
        rows = slice(i * BLOCK, (i + 1) * BLOCK)
        panel = jnp.concatenate([lh[rows], lh[rows], ll[rows]], axis=1)
        for j in range(i, D // BLOCK):
            cols = slice(j * BLOCK, (j + 1) * BLOCK)
            other = jnp.concatenate([rh[:, cols], rl[:, cols], rh[:, cols]], axis=0)
            put(rows, cols, dot32(panel, other, 1, 0))


def keep(pair):
    def put(rows, cols, value):
        pair[0][rows, cols], pair[1][rows, cols] = halves(value)
        if rows != cols:
            pair[0][cols, rows], pair[1][cols, rows] = halves(value.T)

    return put


def chain_kernel(kind_ref, factor_ref, debias_ref, chip_ref, other_ref, kept_ref, got_ref,
                 grad_ref, weight_ref, first_ref, second_ref,
                 out_ref, weight_new_ref, first_new_ref, second_new_ref, copy_ref,
                 a_ref, scale_ref, *parts, chunks):
    a, q, p, t = [parts[2 * i:2 * i + 2] for i in range(4)]
    step = pl.program_id(0)
    shape = (BLOCK, BLOCK)
    once = lax.broadcasted_iota(jnp.int32, shape, 0) == lax.broadcasted_iota(jnp.int32, shape, 1)

    def put_q(rows, cols, value):
        new = 2.0315 * value - 4.775 * a_ref[rows, cols]
        keep(q)(rows, cols, new + jnp.where(once, 3.4445, 0.0) if rows == cols else new)

    def put_a(rows, cols, value):
        a_ref[rows, cols] = value
        keep(a)(rows, cols, value)

    def put_out(rows, cols, value):
        value = value * (1.0 / scale_ref[0])
        out_ref[rows, cols] = value
        if rows != cols:
            out_ref[cols, rows] = value.T

    @pl.when(step == 0)
    def _():
        half = len(TILES) // 2
        lower = kind_ref[1] == 1
        trace = 0.0
        for at, (i, j) in enumerate(TILES):
            side = kept_ref[at % half], got_ref[at % half]
            near, far = side if at < half else side[::-1]
            tile = jnp.where(lower, near, far)
            tile = jnp.where(kind_ref[0] == 0, chip_ref[at], tile)
            tile = jnp.where(kind_ref[0] == 1, other_ref[at], tile)
            a_ref[i * BLOCK:(i + 1) * BLOCK, j * BLOCK:(j + 1) * BLOCK] = tile
            if i == j:
                trace = trace + jnp.sum(jnp.where(once, tile, 0.0))
        scale = jnp.sqrt(trace) + 1e-07
        scale_ref[0] = scale
        for i, j in TILES:
            rows, cols = slice(i * BLOCK, (i + 1) * BLOCK), slice(j * BLOCK, (j + 1) * BLOCK)
            put_a(rows, cols, a_ref[rows, cols] * (1.0 / (scale * scale)))

    turn = lax.rem(step + 1, 4)
    last = 4 * NS_TURNS - 4

    @pl.when((step == 0) | (turn == 0))
    def _():
        even_product(a, a, put_q)

    @pl.when(step == 0)
    def _():
        p[0][...], p[1][...] = q[0][...], q[1][...]

    @pl.when((turn == 1) & (step > 0) & (step < last))
    def _():
        even_product(p, q, keep(t))
        p[0][...], p[1][...] = t[0][...], t[1][...]

    @pl.when(step == last)
    def _():
        even_product(p, q, put_out)

    @pl.when(turn == 2)
    def _():
        even_product(a, q, keep(t))

    @pl.when(turn == 3)
    def _():
        even_product(t, q, put_a)

    @pl.when(step < chunks)
    def _():
        grad = factor_ref[0] * grad_ref[...].astype(full)
        weight = weight_ref[...]
        first = beta_one * first_ref[...] + (1.0 - beta_one) * grad
        second = beta_two * second_ref[...] + (1.0 - beta_two) * grad * grad
        move = (first * debias_ref[0]) / (jnp.sqrt(second * debias_ref[1]) + adam_eps)
        new = weight - 0.02 * (move + adam_decay * weight)
        weight_new_ref[...] = new
        first_new_ref[...] = first
        second_new_ref[...] = second
        copy_ref[...] = new.astype(low)


def chain(kind, factor, debias, grams, table):
    steps = 4 * NS_TURNS - 3
    features, vocab = table[1].shape
    width = -(-vocab // ((steps - 1) * LANES)) * LANES
    chunks = -(-vocab // width)
    part = pl.BlockSpec((features, width), lambda g: (0, jnp.minimum(g, chunks - 1)))
    whole = jax.ShapeDtypeStruct((features, vocab), full)
    return pl.pallas_call(
        partial(chain_kernel, chunks=chunks),
        grid=(steps,),
        in_specs=[smem(), smem(), smem()] + [vmem()] * 4 + [part] * 4,
        out_specs=[pl.BlockSpec((D, D), lambda g: (0, 0))] + [part] * 4,
        out_shape=[
            jax.ShapeDtypeStruct((D, D), full),
            whole,
            whole,
            whole,
            jax.ShapeDtypeStruct((features, vocab), low),
        ],
        scratch_shapes=[pltpu.VMEM((D, D), full), pltpu.SMEM((1,), full)]
        + [pltpu.VMEM((D, D), low)] * 8,
        compiler_params=params(56),
        cost_estimate=cost(48),
        name="chain",
    )(kind, factor, debias, *grams, *table)


def apply_kernel(info_ref, gain_ref, first_ref, second_ref, moment_ref, master_ref, new_ref, copy_ref,
                 *, block):
    split = info_ref[0] // block

    def over(slot, p_ref, start, stop):
        p = halves(p_ref[...])
        gain = gain_ref[slot] * muon_rate

        def body(b, carry):
            rows = pl.ds(pl.multiple_of(b * block, block), block)
            ortho = dot_split(halves(moment_ref[rows]), p)
            new = master_ref[rows] * (1.0 - muon_rate * muon_decay) - gain * ortho
            new_ref[rows] = new
            copy_ref[rows] = new.astype(low)
            return carry

        lax.fori_loop(start, stop, body, 0)

    over(0, first_ref, 0, split)
    total = moment_ref.shape[0] // block

    @pl.when(split < total)
    def _():
        over(1, second_ref, split, total)


def apply_chain(info, gains, first, second, moment, master, block):
    return pl.pallas_call(
        partial(apply_kernel, block=block),
        in_specs=[smem(), smem(), vmem(), vmem(), vmem(), vmem()],
        out_specs=[vmem(), vmem()],
        out_shape=[
            jax.ShapeDtypeStruct(moment.shape, full),
            jax.ShapeDtypeStruct(moment.shape, low),
        ],
        compiler_params=params(48),
        cost_estimate=cost(10),
        name="apply",
    )(info, gains, first, second, moment, master)


def chains(mine, other, wide_at, first_matrix, second_matrix, factor, debias, table, rider):
    wide = lax.axis_size("wide")
    if wide != 8:
        which = jnp.arange(4)
        slots = (which == first_matrix).astype(full)[:, None, None, None] * mine
        slots = slots + (which == second_matrix).astype(full)[:, None, None, None] * other
        total = lax.psum(slots, "wide")
        kind = jnp.zeros((2,), jnp.int32)
        outs = []
        for matrix in (first_matrix, second_matrix):
            gram = lax.dynamic_index_in_dim(total, matrix, 0, keepdims=False)
            half = gram[: len(TILES) // 2]
            outs.append(chain(kind, factor, debias, (gram, gram, half, half), table))
        return outs[0][0], outs[1][0], outs[0][1:], rider
    half = len(TILES) // 2
    pairs = [(i, i ^ 1) for i in range(8)]
    lower = wide_at % 2 == 0
    moved = lax.ppermute(other[:half], "wide", [(5, 4)])
    chip = mine + lax.ppermute(mine, "wide", pairs)
    up_send = jnp.where(lower, chip[:half], chip[half:])
    down_send = jnp.where(wide_at == 4, moved, jnp.where(wide_at == 5, other[half:], up_send))
    up = up_send + lax.ppermute(up_send, "wide", [(2, 4), (4, 2), (3, 5), (5, 3)])
    down = down_send + lax.ppermute(down_send, "wide", [(4, 6), (6, 4), (5, 7), (7, 5)])
    send = jnp.where((wide_at == 4) | (wide_at >= 6), down, up)
    swap = lax.ppermute(send, "wide", [(2, 3), (4, 5), (6, 7), (7, 6)])
    back = lax.ppermute(up, "wide", [(5, 4)])
    kept = jnp.where(wide_at >= 5, down, up)
    got = jnp.where(wide_at == 4, back, swap)
    kind = jnp.where(wide_at < 2, 0, jnp.where(wide_at == 2, 1, 2))
    kind = jnp.stack([kind, lower.astype(jnp.int32)]).astype(jnp.int32)
    got, rider = lax.optimization_barrier((got, rider))
    own, *table_new = chain(kind, factor, debias, (chip, other, kept, got), table)
    come = lax.ppermute(own, "wide", [(3, 2), (4, 5)])
    return jnp.where(wide_at == 5, come, own), jnp.where(wide_at == 5, own, come), table_new, rider


def scale_rows(hidden):
    center = hidden - jnp.mean(hidden, axis=-1, keepdims=True)
    inverse = lax.rsqrt(jnp.mean(center * center, axis=-1, keepdims=True) + norm_eps)
    return center * inverse, inverse


def unscale_rows(upstream, scaled, inverse, gain):
    weighted = upstream * gain
    return inverse * (
        weighted
        - jnp.mean(weighted, axis=-1, keepdims=True)
        - scaled * jnp.mean(weighted * scaled, axis=-1, keepdims=True)
    )


def forward_kernel(context_ref, normed0_ref, share_ref, vectors_ref, bias_ref, out_w_ref, up_w_ref, down_w_ref,
                   scaled1_ref, inverse1_ref, input1_ref, active_ref, slope_ref,
                   scaled2_ref, inverse2_ref, pooled_ref, normed1_ref, sum_ref):
    step = pl.program_id(0)

    @pl.when(step == 0)
    def _():
        attended = dot32(context_ref[...], out_w_ref[...], 1, 1) + vectors_ref[8:9]
        scaled, inverse = scale_rows(normed0_ref[...] + attended)
        scaled1_ref[...], inverse1_ref[...] = scaled, inverse
        normed1_ref[...] = scaled * vectors_ref[2:3] + vectors_ref[3:4]
        input1_ref[...] = normed1_ref[...].astype(low)
        sum_ref[...] = normed1_ref[...] + vectors_ref[9:10]

    inner = dot32(input1_ref[...], up_w_ref[...], 1, 1) + bias_ref[...]
    cdf = 0.5 * (1.0 + lax.erf(inner * math.sqrt(0.5)))
    active = (inner * cdf).astype(low)
    active_ref[...] = active
    slope_ref[...] = cdf + inner * (jnp.exp(-0.5 * inner * inner) * (1.0 / math.sqrt(2.0 * math.pi)))
    sum_ref[...] += dot32(active, down_w_ref[...], 1, 0)

    @pl.when(step == pl.num_programs(0) - 1)
    def _():
        scaled, inverse = scale_rows(sum_ref[...])
        scaled2_ref[...], inverse2_ref[...] = scaled, inverse
        normed2 = scaled * vectors_ref[4:5] + vectors_ref[5:6]
        pooled_ref[...] = jnp.dot(share_ref[...], normed2, precision=highest)


CHUNK = 512


def same(shape):
    return pl.BlockSpec(shape, lambda c: (0,) * len(shape))


def forward_rest(context, normed0, share, vectors, out_w, up_w, down_w):
    tokens = context.shape[0]
    pairs = share.shape[0]
    wide_rows = jax.ShapeDtypeStruct((tokens, D), full)
    column = jax.ShapeDtypeStruct((tokens, 1), full)
    return pl.pallas_call(
        forward_kernel,
        grid=(FF // CHUNK,),
        in_specs=[
            same((tokens, D)),
            same((tokens, D)),
            same((pairs, tokens)),
            same(vectors.shape),
            pl.BlockSpec((1, CHUNK), lambda c: (0, c)),
            same((D, D)),
            pl.BlockSpec((CHUNK, D), lambda c: (c, 0)),
            pl.BlockSpec((CHUNK, D), lambda c: (c, 0)),
        ],
        out_specs=[
            same((tokens, D)),
            same((tokens, 1)),
            same((tokens, D)),
            pl.BlockSpec((tokens, CHUNK), lambda c: (0, c)),
            pl.BlockSpec((tokens, CHUNK), lambda c: (0, c)),
            same((tokens, D)),
            same((tokens, 1)),
            same((pairs, D)),
        ],
        out_shape=[
            wide_rows,
            column,
            jax.ShapeDtypeStruct((tokens, D), low),
            jax.ShapeDtypeStruct((tokens, FF), low),
            jax.ShapeDtypeStruct((tokens, FF), full),
            wide_rows,
            column,
            jax.ShapeDtypeStruct((pairs, D), full),
        ],
        scratch_shapes=[pltpu.VMEM((tokens, D), full)] * 2,
        compiler_params=params(58),
        cost_estimate=cost(25),
        name="forward_rest",
    )(context, normed0, share, vectors, vectors[14:].reshape(1, -1), out_w, up_w, down_w)


def backward_kernel(side_ref, pooled_ref, share_ref, vectors_ref, scaled2_ref, inverse2_ref, active_ref, slope_ref,
                    input1_ref, scaled1_ref, inverse1_ref, context_ref, out_w_ref, up_w_ref, down_w_ref,
                    down_stays_ref, down_leaves_ref, up_stays_ref, up_leaves_ref, out_grad_ref, sum1_ref, context_grad_ref, sums_ref, up_sums_ref,
                    branch_ref, total_ref):
    step = pl.program_id(0)

    def over_tokens(x):
        return jnp.sum(x, axis=0, keepdims=True)

    @pl.when(step == 0)
    def _():
        spread = lax.dot_general(
            share_ref[...], pooled_ref[...], dims(0, 0), precision=highest, preferred_element_type=full
        )
        scaled = scaled2_ref[...]
        back = unscale_rows(spread, scaled, inverse2_ref[...], vectors_ref[4:5])
        total_ref[...] = back
        branch = back.astype(low)
        branch_ref[...] = branch
        sums_ref[2:3] = over_tokens(spread * scaled)
        sums_ref[3:4] = over_tokens(spread)
        sums_ref[5:6] = over_tokens(branch.astype(full))

    branch = branch_ref[...]
    inner_grad = (dot32(branch, down_w_ref[...], 1, 1) * slope_ref[...]).astype(low)

    def halve(grad, stays_ref, leaves_ref):
        left, right = grad[:, : D // 2], grad[:, D // 2 :]
        stays_ref[...] = jnp.where(side_ref[0] == 0, left, right).astype(low)
        leaves_ref[...] = jnp.where(side_ref[0] == 0, right, left).astype(low)

    halve(dot32(active_ref[...], branch, 0, 0), down_stays_ref, down_leaves_ref)
    halve(dot32(inner_grad, input1_ref[...], 0, 0), up_stays_ref, up_leaves_ref)
    up_sums_ref[...] = over_tokens(inner_grad.astype(full))
    total_ref[...] += dot32(inner_grad, up_w_ref[...], 1, 0)

    @pl.when(step == pl.num_programs(0) - 1)
    def _():
        upstream = total_ref[...]
        scaled = scaled1_ref[...]
        back = unscale_rows(upstream, scaled, inverse1_ref[...], vectors_ref[2:3])
        sum1_ref[...] = back
        attended = back.astype(low)
        sums_ref[0:1] = over_tokens(upstream * scaled)
        sums_ref[1:2] = over_tokens(upstream)
        sums_ref[4:5] = over_tokens(attended.astype(full))
        out_grad_ref[...] = dot32(attended, context_ref[...], 0, 0).astype(low)
        context_grad_ref[...] = dot32(attended, out_w_ref[...], 1, 0).astype(low)


def backward_rest(side, pooled_grads, share, vectors, kept, context, out_w, up_w, down_w):
    scaled1, inverse1, input1, active, slope, scaled2, inverse2 = kept
    tokens = context.shape[0]
    pairs = share.shape[0]
    rows = pl.BlockSpec((CHUNK, D), lambda c: (c, 0))
    cols = pl.BlockSpec((tokens, CHUNK), lambda c: (0, c))
    return pl.pallas_call(
        backward_kernel,
        grid=(FF // CHUNK,),
        in_specs=[
            smem(),
            same((pairs, D)),
            same((pairs, tokens)),
            same(vectors.shape),
            same((tokens, D)),
            same((tokens, 1)),
            cols,
            cols,
            same((tokens, D)),
            same((tokens, D)),
            same((tokens, 1)),
            same((tokens, D)),
            same((D, D)),
            rows,
            rows,
        ],
        out_specs=[pl.BlockSpec((CHUNK, D // 2), lambda c: (c, 0))] * 4
        + [
            same((D, D)),
            same((tokens, D)),
            same((tokens, D)),
            same((8, D)),
            pl.BlockSpec((1, CHUNK), lambda c: (0, c)),
        ],
        out_shape=[jax.ShapeDtypeStruct((FF, D // 2), low)] * 4
        + [
            jax.ShapeDtypeStruct((D, D), low),
            jax.ShapeDtypeStruct((tokens, D), full),
            jax.ShapeDtypeStruct((tokens, D), low),
            jax.ShapeDtypeStruct((8, D), full),
            jax.ShapeDtypeStruct((1, FF), full),
        ],
        scratch_shapes=[pltpu.VMEM((tokens, D), low), pltpu.VMEM((tokens, D), full)],
        compiler_params=params(58),
        cost_estimate=cost(35),
        name="backward_rest",
    )(side, pooled_grads, share, vectors, scaled2, inverse2, active, slope, input1, scaled1, inverse1, context,
      out_w, up_w, down_w)


def embed_back_kernel(mixed_ref, sum1_ref, scaled_ref, inverse_ref, vectors_ref, weight_ref,
                      embed_ref, send_ref, sums_ref, mixed_sum_ref, *, narrow, wide):
    upstream = sum1_ref[...] + dot32(mixed_ref[...], weight_ref[...], 1, 0)
    scaled = scaled_ref[...]
    back = unscale_rows(upstream, scaled, inverse_ref[...], vectors_ref[0:1])
    embed_ref[...] = back
    turned = back.T.astype(low)
    features = send_ref.shape[1]
    for n in range(narrow):
        for w in range(wide):
            start = (w * narrow + n) * features
            send_ref[n * wide + w] = turned[start:start + features]

    @pl.when(pl.program_id(0) == 0)
    def _():
        sums_ref[...] = jnp.zeros_like(sums_ref)
        mixed_sum_ref[...] = jnp.zeros_like(mixed_sum_ref)

    sums_ref[0:1] += jnp.sum(upstream * scaled, axis=0, keepdims=True)
    sums_ref[1:2] += jnp.sum(upstream, axis=0, keepdims=True)
    mixed_sum_ref[...] += jnp.sum(mixed_ref[...].astype(full), axis=0, keepdims=True)


def embed_back(mixed_grad, sum1_grad, scaled0, inverse0, vectors, weight, narrow, wide):
    tokens = mixed_grad.shape[0]
    count = narrow * wide
    block = pl.BlockSpec((SEQ, D), lambda b: (b, 0))
    return pl.pallas_call(
        partial(embed_back_kernel, narrow=narrow, wide=wide),
        grid=(tokens // SEQ,),
        in_specs=[
            pl.BlockSpec((SEQ, 3 * D), lambda b: (b, 0)),
            block,
            block,
            pl.BlockSpec((SEQ, 1), lambda b: (b, 0)),
            same(vectors.shape),
            same((3 * D, D)),
        ],
        out_specs=[
            block,
            pl.BlockSpec((count, D // count, SEQ), lambda b: (0, 0, b)),
            same((8, D)),
            same((1, 3 * D)),
        ],
        out_shape=[
            jax.ShapeDtypeStruct((tokens, D), full),
            jax.ShapeDtypeStruct((count, D // count, tokens), low),
            jax.ShapeDtypeStruct((8, D), full),
            jax.ShapeDtypeStruct((1, 3 * D), full),
        ],
        compiler_params=params(48),
        cost_estimate=cost(10),
        name="embed_back",
    )(mixed_grad, sum1_grad, scaled0, inverse0, vectors, weight)


def layout(lengths):
    row_ends = jnp.cumsum(lengths)
    starts = row_ends - lengths
    places = jnp.arange(SEQ, dtype=jnp.int32)
    segment = jnp.sum((places[:, None] >= row_ends[None, :]).astype(jnp.int32), axis=1)
    chosen = segment[:, None] == jnp.arange(SLOTS, dtype=jnp.int32)[None, :]
    start_at = jnp.sum(jnp.where(chosen, starts[None, :], 0), axis=1)
    length_at = jnp.sum(jnp.where(chosen, lengths[None, :], 0), axis=1)
    position = places - start_at
    second = (2 * position >= length_at).astype(jnp.int32)
    return (chosen.astype(full), position, second, segment)


def norm_forward(hidden, gain, bias):
    center = hidden - jnp.mean(hidden, axis=-1, keepdims=True)
    inverse = lax.rsqrt(jnp.mean(center * center, axis=-1, keepdims=True) + norm_eps)
    scaled = center * inverse
    return (scaled * gain + bias, scaled, inverse)


def norm_backward(upstream, scaled, inverse, gain):
    weighted = upstream * gain
    back = inverse * (
        weighted
        - jnp.mean(weighted, axis=-1, keepdims=True)
        - scaled * jnp.mean(weighted * scaled, axis=-1, keepdims=True)
    )
    return (back, jnp.sum(upstream * scaled, axis=0), jnp.sum(upstream, axis=0))


def project(left, right):
    return jnp.dot(left, right, preferred_element_type=full)


def task_loss(logits, scores, tasks, labels, negatives, counts):
    logprob = jax.nn.log_softmax(logits, axis=-1)
    picked = jnp.sum(
        jnp.where(labels[:, :, None] == jnp.arange(3, dtype=jnp.int32), logprob, 0.0), axis=2
    )
    chosen = negatives[:, :, :, None] == jnp.arange(scores.shape[1], dtype=jnp.int32)
    rivals = jnp.sum(jnp.where(chosen, scores[:, None, None, :], 0.0), axis=3)
    together = jnp.concatenate([scores[:, :, None], rivals], axis=2)
    ranking = jax.nn.logsumexp(together, axis=2) - scores
    first_part = jnp.sum(jnp.where(tasks == 0, -picked, 0.0)) / counts[0]
    return first_part + jnp.sum(jnp.where(tasks == 1, ranking, 0.0)) / counts[1]


def adam(weight, grad, first, second, step, rate):
    first = beta_one * first + (1.0 - beta_one) * grad
    second = beta_two * second + (1.0 - beta_two) * grad * grad
    unbiased = first / (1.0 - beta_one**step)
    spread = second / (1.0 - beta_two**step)
    return (
        weight - rate * (unbiased / (jnp.sqrt(spread) + adam_eps) + adam_decay * weight),
        first,
        second,
    )


def broadcast_all(x):
    count = lax.axis_size("narrow") * lax.axis_size("wide")
    return lax.all_to_all(
        jnp.broadcast_to(x[None], (count,) + x.shape), BOTH, split_axis=0, concat_axis=0, tiled=True
    )


def sides(wide):
    return [list(range(0, wide, 2)), list(range(1, wide, 2))]


def chip_mates(wide):
    return [(i, i ^ 1) for i in range(wide)]


def gather_weights(master, narrow_at, wide_at, first):
    wide = lax.axis_size("wide")
    if wide != 8:
        whole = lax.all_gather(master.astype(low), "wide", axis=0, tiled=True)
        return first, list(whole.reshape(wide, -1, D))
    share = master.shape[0] // lax.axis_size("narrow")
    mine = lax.dynamic_slice_in_dim(master, narrow_at * share, share, 0).astype(low)
    near = lax.all_gather(mine, "wide", axis=0, tiled=False, axis_index_groups=sides(wide))
    near, first = lax.optimization_barrier((near, first))
    return first, [
        lax.all_gather(part, "narrow", axis=1, tiled=True)
        for part in (near[: wide // 4], near[wide // 4 :])
    ]


def both_cores(held, wide_at):
    owners = []
    other = lax.ppermute(held, "wide", chip_mates(lax.axis_size("wide")))
    side = wide_at % 2
    even = jnp.where(side == 0, held, other)
    odd = jnp.where(side == 0, other, held)
    for at in range(held.shape[0]):
        owners += [even[at], odd[at]]
    return owners


def rows_of(owners, matrix):
    rows = owners[0].shape[0]
    lo, hi = BOUNDS[matrix], BOUNDS[matrix + 1]
    pieces = []
    for at in range(lo // rows, -(-hi // rows)):
        pieces.append(owners[at][max(lo - at * rows, 0) : min(hi - at * rows, rows)])
    return jnp.concatenate(pieces) if len(pieces) > 1 else pieces[0]


def shards(
    token_ids,
    seq_lengths,
    task_ids,
    labels,
    negatives,
    step_count,
    hidden_master,
    hidden_momentum,
    table_master,
    table_first,
    table_second,
    pos_types,
    pos_first,
    pos_second,
    vectors,
    vec_first,
    vec_second,
):
    wide_at = lax.axis_index("wide")
    narrow_at = lax.axis_index("narrow")
    wide = lax.axis_size("wide")
    narrow = lax.axis_size("narrow")
    count = wide * narrow
    device_at = narrow_at * wide + wide_at
    micro_count, rows_each = token_ids.shape[:2]
    batch = micro_count * rows_each
    tokens = batch * SEQ
    shard = hidden_master.shape[0]
    vocab = table_master.shape[1]
    features = table_master.shape[0] // narrow
    pairs_each = rows_each * SLOTS

    parts = [token_ids, task_ids, labels, negatives]
    sizes = [part.size for part in parts]
    packed = jnp.concatenate([part.reshape(-1) for part in parts])
    packed = jnp.pad(packed, (0, -packed.size % LANES))
    gathered = broadcast_all(packed)
    ends = [sum(sizes[: i + 1]) for i in range(len(sizes))]
    ids_all = gathered[:, : ends[0]]

    def pairs_of(lo, hi, tail):
        block = gathered[:, lo:hi].reshape((count, micro_count, pairs_each) + tail)
        return jnp.moveaxis(block, 1, 0).reshape((micro_count, count * pairs_each) + tail)

    tasks_all = pairs_of(ends[0], ends[1], ())
    labels_all = pairs_of(ends[1], ends[2], ())
    negatives_all = pairs_of(ends[2], ends[3], (NEG,))
    counts = jnp.stack(
        [jnp.sum((tasks_all == 0).astype(full)), jnp.sum((tasks_all == 1).astype(full))]
    )


    group_ids = lax.dynamic_slice_in_dim(ids_all, narrow_at * wide, wide, 0).reshape(-1)
    pieces = lookup(group_ids, table_master)
    pieces, gathers = gather_weights(hidden_master, narrow_at, wide_at, pieces)
    simple = wide != 8
    arrived = lax.all_to_all(
        pieces.reshape(wide, tokens, -1), "wide", split_axis=0, concat_axis=0, tiled=True
    )
    token_rows = jnp.moveaxis(arrived, 0, 1).reshape(tokens, D)

    lengths = seq_lengths.reshape(batch, SLOTS)
    member, position, second, segment = jax.vmap(layout)(lengths)
    flat_position = position.reshape(-1)
    flat_second = second.reshape(-1)
    place_rows = pos_types[flat_position]
    place_rows = place_rows + jnp.where(flat_second[:, None] == 1, pos_types[SEQ + 1], pos_types[SEQ])
    if simple:
        owners = gathers
    else:
        place_rows, held = lax.optimization_barrier((place_rows, gathers[0]))
        owners = both_cores(held, wide_at)
    embed = token_rows.astype(full) + place_rows
    normed0, scaled0, inverse0 = norm_forward(embed, vectors[0], vectors[1])
    input0 = normed0.astype(low)
    qkv_bias = jnp.concatenate([vectors[6], jnp.zeros_like(vectors[6]), vectors[7]])
    weight_qkv, weight_out = rows_of(owners, 0), rows_of(owners, 1)
    mixed = (project(input0, weight_qkv.T) + qkv_bias).astype(low)
    context_low, logsum = attend(mixed, segment)
    if not simple:
        rest, context_low = lax.optimization_barrier((gathers[1], context_low))
        owners = owners + both_cores(rest, wide_at)
    weight_up, weight_down = rows_of(owners, 2), rows_of(owners, 3)
    pair_at = (jnp.arange(batch, dtype=jnp.int32)[:, None] * SLOTS + segment).reshape(1, -1)
    pairs = jnp.arange(batch * SLOTS, dtype=jnp.int32)[:, None]
    share = jnp.where(pair_at == pairs, 1.0 / lengths.astype(full).reshape(-1, 1), 0.0)
    scaled1, inverse1, input1, active, slope, scaled2, inverse2, flat_pooled = forward_rest(
        context_low, normed0, share, vectors, weight_out, weight_up, weight_down
    )
    heads = vectors[10:14]
    head_out = jnp.dot(flat_pooled, heads.T, precision=highest)

    sent = jnp.pad(head_out.reshape(-1), (0, -head_out.size % LANES))
    head_all = broadcast_all(sent)[:, : head_out.size]
    head_all = head_all.reshape(count, micro_count, pairs_each, 4)
    head_all = jnp.moveaxis(head_all, 1, 0).reshape(micro_count, count * pairs_each, 4)

    def objective(every):
        return task_loss(every[:, :, :3], every[:, :, 3], tasks_all, labels_all, negatives_all, counts)

    loss, pullback = jax.vjp(objective, head_all)
    head_grads = pullback(jnp.ones_like(loss))[0]
    output_grads = lax.dynamic_slice_in_dim(head_grads, device_at * pairs_each, pairs_each, 1)
    output_grads = output_grads.reshape(-1, 4)
    heads_grad = jnp.dot(output_grads.T, flat_pooled, precision=highest)
    pooled_grads = jnp.dot(output_grads, heads, precision=highest)

    spans_down = [(0, 768), (768, 1920), (1920, 3072)]
    spans_up = [(0, 384), (384, 1536), (1536, 2688), (2688, 3072)]
    spans_front = [(0, 1152), (1152, 2304), (2304, 3072)]

    side = wide_at % 2

    def between_cores(grad):
        stays, leaves = grad
        if simple:
            return stays, leaves
        return stays, lax.ppermute(leaves, "wide", chip_mates(wide))

    def slices(grad, spans):
        stays, comes = grad
        if simple:
            return [jnp.concatenate([stays, comes], axis=1)]
        chip = (stays.astype(full) + comes.astype(full)).astype(low)
        parts = []
        for turn in range(narrow):
            pieces = []
            for lo, hi in spans:
                share_rows = (hi - lo) // narrow
                start = lo + (narrow_at ^ turn) * share_rows
                pieces.append(lax.dynamic_slice_in_dim(chip, start, share_rows, 0))
            parts.append(jnp.concatenate(pieces))
        return parts

    def over_narrow(parts):
        return parts[:1] + [
            lax.ppermute(part, "narrow", [(i, i ^ (turn + 1)) for i in range(narrow)])
            for turn, part in enumerate(parts[1:])
        ]

    together = lax.optimization_barrier
    kept = (scaled1, inverse1, input1, active, slope, scaled2, inverse2)
    *sides_of, out_grad, sum1_grad, context_grad, sums, up_sums = backward_rest(
        side[None] if not simple else jnp.zeros((1,), jnp.int32),
        pooled_grads, share, vectors, kept, context_low, weight_out, weight_up, weight_down
    )
    down_pair = between_cores(sides_of[:2])
    up_pair = between_cores(sides_of[2:])
    down_cut, up_pair, context_grad = together((slices(down_pair, spans_down), up_pair, context_grad))
    down_part = over_narrow(down_cut)
    up_cut, context_grad = together((slices(up_pair, spans_up), context_grad))
    up_part = over_narrow(up_cut)
    mixed_grad = attend_back(mixed, context_grad, logsum, segment)
    mixed_grad, down_part = together((mixed_grad, down_part))
    if simple:
        normed0_grad = sum1_grad + project(mixed_grad, weight_qkv)
        embed_grad, gain0, bias0 = norm_backward(normed0_grad, scaled0, inverse0, vectors[0])
        table_send = embed_grad.astype(low).T.reshape(wide, narrow, features, tokens)
        table_send = jnp.moveaxis(table_send, 1, 0).reshape(count, features, tokens)
        mixed_sum = jnp.sum(mixed_grad.astype(full), axis=0)
    else:
        embed_grad, table_send, first_sums, mixed_sum = embed_back(
            mixed_grad, sum1_grad, scaled0, inverse0, vectors, weight_qkv, narrow, wide
        )
        gain0, bias0, mixed_sum = first_sums[0], first_sums[1], mixed_sum[0]
    table_send, mixed_grad = together((table_send, mixed_grad))
    come = lax.all_to_all(table_send, BOTH, split_axis=0, concat_axis=0, tiled=True)

    qkv_grad = project(mixed_grad.T, input0)
    front_grad = jnp.concatenate([qkv_grad.astype(low), out_grad.astype(low)])
    front_halves = (front_grad[:, : D // 2], front_grad[:, D // 2 :])
    if not simple:
        left, right = front_halves
        front_halves = (jnp.where(side == 0, left, right), jnp.where(side == 0, right, left))
    front_send, embed_grad, mixed_grad, up_part = together(
        (front_halves, embed_grad, mixed_grad, up_part)
    )
    front_part = over_narrow(slices(between_cores(front_send), spans_front))
    small_rows = jnp.concatenate(
        [
            jnp.stack([gain0, bias0]),
            sums[:4],
            jnp.stack([mixed_sum[:D], mixed_sum[2 * D :]]),
            sums[4:6],
        ]
    )
    up_rows = up_sums.reshape(-1, D)

    places = jnp.arange(SEQ, dtype=jnp.int32)[:, None]
    row_hot = jnp.concatenate(
        [
            flat_position[None] == places,
            jnp.stack([flat_second == 0, flat_second == 1]),
        ]
    ).astype(low)
    high_part, low_part = halves(embed_grad)
    pos_grad = project(jnp.concatenate([row_hot, row_hot], axis=1), jnp.concatenate([high_part, low_part]))
    small = jnp.concatenate([pos_grad, small_rows, heads_grad, up_rows])
    small_count = small.shape[0]
    small = jnp.pad(small, ((0, count * features - small_count), (0, 0)))

    def added(parts):
        return sum(part.astype(full) for part in parts).astype(low)

    joined = jnp.concatenate([added(front_part), added(up_part), added(down_part)])
    small_send = small.astype(low).reshape(count, features, D)
    come, small_send = together((come, small_send))
    small_come = lax.all_to_all(small_send, BOTH, split_axis=0, concat_axis=0, tiled=True)
    table_part, table_square = collect(ids_all, come, vocab, tokens)
    if simple:
        hidden_part = lax.psum_scatter(joined, "wide", scatter_dimension=0, tiled=True)
        hidden_part = lax.psum_scatter(hidden_part, "narrow", scatter_dimension=0, tiled=True)
        hidden_square = jnp.sum(jnp.square(hidden_part.astype(full)))
    else:
        owned = lax.psum_scatter(
            joined, "wide", scatter_dimension=0, tiled=True, axis_index_groups=sides(wide)
        )
        owned, table_square, small_come = together((owned, table_square, small_come))
        hidden_square = jnp.sum(jnp.square(owned.astype(full)))
        half = owned.shape[0] // 2
        stays = jnp.where(side == 0, owned[:half], owned[half:])
        leaves = jnp.where(side == 0, owned[half:], owned[:half])
        comes = lax.ppermute(leaves, "wide", chip_mates(wide))
        hidden_part = jnp.concatenate(
            [jnp.where(side == 0, stays, comes), jnp.where(side == 0, comes, stays)], axis=1
        )
    small_part = jnp.sum(small_come.astype(full), axis=0)
    square = hidden_square + table_square[0, 0] + jnp.sum(small_part * small_part)
    square, hidden_part = together((square, hidden_part))
    if simple:
        hidden_all = lax.all_gather(hidden_part, "narrow", axis=0, tiled=True)
    else:
        hidden_all = jnp.concatenate(
            [hidden_part]
            + [
                lax.ppermute(hidden_part, "narrow", [(i, i ^ turn) for i in range(narrow)])
                for turn in range(1, narrow)
            ]
        )
    squares = broadcast_all(jnp.broadcast_to(square, (LANES,)))
    squares, hidden_all, table_part = together((squares, hidden_all, table_part))
    table_grad = lax.all_gather(table_part, "narrow", axis=0, tiled=True)
    clip_norm = jnp.sqrt(jnp.sum(squares[:, 0]))
    factor = jnp.minimum(1.0, clip_bound / clip_norm)

    start = wide_at * shard
    bounds = jnp.array(BOUNDS, jnp.int32)
    first_matrix = jnp.sum((start >= bounds[1:4]).astype(jnp.int32))
    second_matrix = jnp.sum((start + shard - 1 >= bounds[1:4]).astype(jnp.int32))
    split = jnp.minimum(bounds[first_matrix + 1] - start, shard)
    block = shard // 3
    piece = shard // 12
    at = jnp.arange(12, dtype=jnp.int32)
    if simple:
        source = at
    else:
        lead = split // piece
        each = lead // narrow
        rest = (12 - lead) // narrow
        in_first = at < lead
        inside = jnp.where(in_first, at, at - lead)
        width = jnp.maximum(jnp.where(in_first, each, rest), 1)
        origin = (inside // width) ^ narrow_at
        source = origin * (12 // narrow) + jnp.where(in_first, 0, each) + inside % width
    swap = (wide_at == 2).astype(jnp.int32) * (0 if simple else 1)
    info = jnp.concatenate([jnp.stack([split, swap]), source]).astype(jnp.int32)
    gains = jnp.array([0.2 * math.sqrt(hi - lo) for lo, hi in zip(BOUNDS, BOUNDS[1:])], full)
    moment, mine, other = moment_and_grams(
        info, factor[None], hidden_all, hidden_momentum, piece, block
    )
    step = step_count[0].astype(full)
    debias = jnp.stack([1.0 / (1.0 - beta_one**step), 1.0 / (1.0 - beta_two**step)])
    chain0, chain1, (table_new, table_first_new, table_second_new, table_copy), late_small = chains(
        mine,
        other,
        wide_at,
        first_matrix,
        second_matrix,
        factor[None],
        debias,
        (table_grad, table_master, table_first, table_second),
        small_part,
    )
    small_all = broadcast_all(late_small.astype(low)).reshape(-1, D)[:small_count].astype(full)
    slot_gains = jnp.stack([gains[first_matrix], gains[second_matrix]])
    hidden_new, hidden_copy = apply_chain(info, slot_gains, chain0, chain1, moment, hidden_master, block)

    pos_new, pos_first_new, pos_second_new = adam(
        pos_types, factor * small_all[: SEQ + 2], pos_first, pos_second, step, 0.02
    )
    vectors_new, vec_first_new, vec_second_new = adam(
        vectors, factor * small_all[SEQ + 2 :], vec_first, vec_second, step, 0.2
    )
    return (
        loss,
        clip_norm,
        moment,
        hidden_new,
        hidden_copy,
        table_new,
        table_first_new,
        table_second_new,
        table_copy,
        pos_new,
        pos_first_new,
        pos_second_new,
        vectors_new,
        vec_first_new,
        vec_second_new,
    )


def solution(mesh):
    rows = P(None, BOTH, None)
    owned = P("wide", None)
    return jax.shard_map(
        shards,
        mesh=mesh,
        in_specs=(rows, rows, rows, rows, P(None, BOTH, None, None), P())
        + (owned,) * 5
        + (P(),) * 6,
        out_specs=(P(), P()) + (owned,) * 7 + (P(),) * 6,
        check_vma=False,
    )
```

```python
from functools import partial
import math

import jax
import jax.numpy as jnp
from jax import lax
from jax.experimental import pallas as pl
from jax.experimental.pallas import tpu as pltpu
from jax.sharding import PartitionSpec as P

D = 768
HEADS = 12
HEAD = 64
FF = 3072
SEQ = 512
SLOTS = 4
NEG = 4
NS_TURNS = 5
LANES = 128
GROUPS = 4
WIDTH = LANES // GROUPS
BLOCK = 256
TILES = [(i, j) for i in range(D // BLOCK) for j in range(i, D // BLOCK)]

BOTH = ("narrow", "wide")
highest = lax.Precision.HIGHEST
clip_bound = 0.002
norm_eps = 1e-06
muon_beta = 0.95
muon_rate = 0.1
muon_decay = 0.01
beta_one = 0.9
beta_two = 0.999
adam_eps = 1e-08
adam_decay = 0.01
BOUNDS = (0, 3 * D, 4 * D, 4 * D + FF, 4 * D + 2 * FF)

low = jnp.bfloat16
full = jnp.float32


def dims(left, right):
    return (((left,), (right,)), ((), ()))


def dot32(left, right, left_dim, right_dim):
    return lax.dot_general(left, right, dims(left_dim, right_dim), preferred_element_type=full)


def halves(x):
    high = x.astype(low)
    return high, (x - high.astype(full)).astype(low)


def dot_split(left, right, left_dim=1, right_dim=0):
    (lh, ll), (rh, rl) = left, right
    return dot32(lh, rh, left_dim, right_dim) + (
        dot32(lh, rl, left_dim, right_dim) + dot32(ll, rh, left_dim, right_dim)
    )


def params(mib):
    return pltpu.CompilerParams(vmem_limit_bytes=mib << 20)


def cost(micros):
    return pl.CostEstimate(flops=micros * 10**9, transcendentals=0, bytes_accessed=1 << 20)


def vmem():
    return pl.BlockSpec(memory_space=pltpu.VMEM)


def smem():
    return pl.BlockSpec(memory_space=pltpu.SMEM)


def attend_kernel(mixed_ref, seg_col_ref, seg_row_ref, context_ref, logsum_ref):
    same = seg_col_ref[0] == seg_row_ref[0]

    def pair(step, carry):
        at = pl.multiple_of(step * LANES, LANES)
        queries = mixed_ref[:, pl.ds(at, LANES)]
        keys = mixed_ref[:, pl.ds(D + at, LANES)]
        values = mixed_ref[:, pl.ds(2 * D + at, LANES)]
        outs = []
        for half in range(2):
            cut = slice(half * HEAD, (half + 1) * HEAD)
            raw = dot32(keys[:, cut], queries[:, cut], 1, 1)
            scores = jnp.where(same, raw * (1.0 / math.sqrt(HEAD)), -1e30)
            peak = jnp.max(scores, axis=0, keepdims=True)
            lifted = jnp.exp(scores - peak)
            total = jnp.sum(lifted, axis=0, keepdims=True)
            probs = (lifted * (1.0 / total)).astype(low)
            outs.append(dot32(values[:, cut], probs, 0, 0))
            logsum_ref[0, pl.ds(2 * step + half, 1), :] = peak + jnp.log(total)
        context_ref[:, pl.ds(at, LANES)] = jnp.concatenate(outs, axis=0).T.astype(low)
        return carry

    lax.fori_loop(0, HEADS // 2, pair, 0, unroll=3)


def attend(mixed, segment):
    rows = segment.shape[0]
    return pl.pallas_call(
        attend_kernel,
        grid=(rows,),
        in_specs=[
            pl.BlockSpec((SEQ, 3 * D), lambda b: (b, 0)),
            pl.BlockSpec((1, SEQ, 1), lambda b: (b, 0, 0)),
            pl.BlockSpec((1, 1, SEQ), lambda b: (b, 0, 0)),
        ],
        out_specs=[
            pl.BlockSpec((SEQ, D), lambda b: (b, 0)),
            pl.BlockSpec((1, 16, SEQ), lambda b: (b, 0, 0)),
        ],
        out_shape=[
            jax.ShapeDtypeStruct((rows * SEQ, D), low),
            jax.ShapeDtypeStruct((rows, 16, SEQ), full),
        ],
        compiler_params=params(48),
        cost_estimate=cost(19),
        name="attend",
    )(mixed, segment[:, :, None], segment[:, None, :])


def attend_back_kernel(mixed_ref, grad_ref, logsum_ref, seg_col_ref, seg_row_ref, out_ref):
    same = seg_col_ref[0] == seg_row_ref[0]
    scale = 1.0 / math.sqrt(HEAD)

    def pair(step, carry):
        at = pl.multiple_of(step * LANES, LANES)
        queries = mixed_ref[:, pl.ds(at, LANES)]
        keys = mixed_ref[:, pl.ds(D + at, LANES)]
        values = mixed_ref[:, pl.ds(2 * D + at, LANES)]
        upstream = grad_ref[:, pl.ds(at, LANES)]
        query_grads, key_grads, value_grads = [], [], []
        for half in range(2):
            cut = slice(half * HEAD, (half + 1) * HEAD)
            logsum = logsum_ref[0, pl.ds(2 * step + half, 1), :]
            raw = dot32(keys[:, cut], queries[:, cut], 1, 1)
            probs = jnp.exp(jnp.where(same, raw * scale, -1e30) - logsum)
            prob_grads = dot32(values[:, cut], upstream[:, cut], 1, 1)
            value_grads.append(dot32(probs.astype(low), upstream[:, cut], 1, 0))
            moved = jnp.sum(prob_grads * probs, axis=0, keepdims=True)
            back = (probs * (prob_grads - moved) * scale).astype(low)
            key_grads.append(dot32(back, queries[:, cut], 1, 0))
            query_grads.append(dot32(keys[:, cut], back, 0, 0))
        out_ref[:, pl.ds(at, LANES)] = jnp.concatenate(query_grads, axis=0).T.astype(low)
        out_ref[:, pl.ds(D + at, LANES)] = jnp.concatenate(key_grads, axis=1).astype(low)
        out_ref[:, pl.ds(2 * D + at, LANES)] = jnp.concatenate(value_grads, axis=1).astype(low)
        return carry

    lax.fori_loop(0, HEADS // 2, pair, 0, unroll=3)


def attend_back(mixed, context_grad, logsum, segment):
    rows = segment.shape[0]
    return pl.pallas_call(
        attend_back_kernel,
        grid=(rows,),
        in_specs=[
            pl.BlockSpec((SEQ, 3 * D), lambda b: (b, 0)),
            pl.BlockSpec((SEQ, D), lambda b: (b, 0)),
            pl.BlockSpec((1, 16, SEQ), lambda b: (b, 0, 0)),
            pl.BlockSpec((1, SEQ, 1), lambda b: (b, 0, 0)),
            pl.BlockSpec((1, 1, SEQ), lambda b: (b, 0, 0)),
        ],
        out_specs=pl.BlockSpec((SEQ, 3 * D), lambda b: (b, 0)),
        out_shape=jax.ShapeDtypeStruct((rows * SEQ, 3 * D), low),
        compiler_params=params(56),
        cost_estimate=cost(28),
        name="attend_back",
    )(mixed, context_grad, logsum, segment[:, :, None], segment[:, None, :])


def lookup_kernel(ids_ref, table_ref, out_ref, turned_ref, rows_ref):
    step = pl.program_id(0)
    features, width = table_ref.shape
    tokens, chunk = out_ref.shape[0], rows_ref.shape[0]
    block = table_ref[...].astype(low).astype(full)
    block = jnp.concatenate([block, jnp.zeros((LANES - features, width), full)], axis=0)
    turned_ref[pl.ds(pl.multiple_of(step * width, width), width), :] = block.T

    @pl.when(step == pl.num_programs(0) - 1)
    def _():
        def piece(c, carry):
            def body(i, inner):
                at = i * 32
                found = [turned_ref[pl.ds(ids_ref[c * chunk + at + k], 1), :] for k in range(32)]
                for k in range(32):
                    rows_ref[pl.ds(at + k, 1), :] = found[k]
                return inner

            lax.fori_loop(0, chunk // 32, body, 0)
            start = pl.multiple_of(c * chunk, chunk)
            out_ref[pl.ds(start, chunk), :] = rows_ref[:, :features].astype(low)
            return carry

        lax.fori_loop(0, tokens // chunk, piece, 0)


def lookup(ids, table):
    features, vocab = table.shape
    width = -(-vocab // (4 * LANES)) * LANES
    steps = -(-vocab // width)
    return pl.pallas_call(
        lookup_kernel,
        grid=(steps,),
        in_specs=[smem(), pl.BlockSpec((features, width), lambda s: (0, s))],
        out_specs=pl.BlockSpec((ids.shape[0], features), lambda s: (0, 0)),
        out_shape=jax.ShapeDtypeStruct((ids.shape[0], features), low),
        scratch_shapes=[pltpu.VMEM((steps * width, LANES), full), pltpu.VMEM((1024, LANES), full)],
        compiler_params=params(56),
        cost_estimate=cost(19),
        name="lookup",
    )(ids, table)


def collect_kernel(place_ref, ids_ref, grads_ref, out_ref, square_ref, *scratch,
                   span, tokens, features, vocab):
    sums, rows_ref = scratch[:-1], scratch[-1]
    step = pl.program_id(0)
    last = pl.num_programs(0) - 1
    streams = len(sums)
    batch = 4 * streams

    @pl.when(step == 0)
    def _():
        for total in sums:
            total[...] = jnp.zeros_like(total)

    group = ids_ref[0] // span
    grads = grads_ref[0].astype(full)
    pad = jnp.zeros((WIDTH - features, tokens), full)
    pieces = []
    for at in range(GROUPS):
        pieces += [jnp.where(group == at, grads, 0.0), pad]
    rows_ref[...] = jnp.concatenate(pieces, axis=0).T

    def body(i, carry):
        for base in range(0, batch, streams):
            at = i * batch + base
            places = [pl.ds(place_ref[0, 0, at + k], 1) for k in range(streams)]
            olds = [sums[k][places[k], :] for k in range(streams)]
            news = [rows_ref[pl.ds(at + k, 1), :] for k in range(streams)]
            for k in range(streams):
                sums[k][places[k], :] = olds[k] + news[k]
        return carry

    lax.fori_loop(0, tokens // batch, body, 0)

    @pl.when(step == last)
    def _():
        def flush(b, total):
            at = pl.multiple_of(b * LANES, LANES)
            block = sums[0][pl.ds(at, LANES), :]
            for k in range(1, streams):
                block += sums[k][pl.ds(at, LANES), :]
            turned = block.T
            for g in range(GROUPS):
                piece = turned[g * WIDTH:g * WIDTH + features]

                @pl.when(g * span + at < vocab)
                def _():
                    out_ref[:, pl.ds(pl.multiple_of(g * span + at, LANES), LANES)] = piece.astype(low)

            return total + block * block

        total = lax.fori_loop(0, span // LANES, flush, jnp.zeros((LANES, LANES), full))
        square_ref[...] = jnp.broadcast_to(jnp.sum(total, keepdims=True), square_ref.shape)


def collect(ids, grads, vocab, tokens):
    sources, features = grads.shape[:2]
    span = -(-vocab // (GROUPS * LANES)) * LANES
    return pl.pallas_call(
        partial(collect_kernel, span=span, tokens=tokens, features=features, vocab=vocab),
        grid=(sources,),
        in_specs=[
            pl.BlockSpec((1, 1, tokens), lambda s: (s, 0, 0), memory_space=pltpu.SMEM),
            pl.BlockSpec((1, 1, tokens), lambda s: (s, 0, 0)),
            pl.BlockSpec((1, features, tokens), lambda s: (s, 0, 0)),
        ],
        out_specs=[
            pl.BlockSpec((features, vocab), lambda s: (0, 0)),
            pl.BlockSpec((8, LANES), lambda s: (0, 0)),
        ],
        out_shape=[
            jax.ShapeDtypeStruct((features, vocab), low),
            jax.ShapeDtypeStruct((8, LANES), full),
        ],
        scratch_shapes=[pltpu.VMEM((span, LANES), full)] * 8 + [pltpu.VMEM((tokens, LANES), full)],
        compiler_params=params(56),
        cost_estimate=cost(150),
        name="collect",
    )((ids % span)[:, None, :], ids[:, None, :], grads)


def moment_kernel(info_ref, factor_ref, grad_ref, old_ref, moment_ref, mine_ref, other_ref,
                  *, piece, block):
    factor = factor_ref[0]
    for at in range(old_ref.shape[0] // piece):
        source = pl.multiple_of(info_ref[2 + at] * piece, piece)
        rows = slice(at * piece, (at + 1) * piece)
        moment_ref[rows] = muon_beta * old_ref[rows] + factor * grad_ref[pl.ds(source, piece)].astype(full)

    def grams(out_ref, start, stop):
        out_ref[...] = jnp.zeros_like(out_ref)

        def body(b, carry):
            high, small = halves(moment_ref[pl.ds(pl.multiple_of(b * block, block), block)])
            for at, (i, j) in enumerate(TILES):
                left, right = slice(i * BLOCK, (i + 1) * BLOCK), slice(j * BLOCK, (j + 1) * BLOCK)
                out_ref[at] += dot32(
                    jnp.concatenate([high[:, left], high[:, left], small[:, left]], axis=0),
                    jnp.concatenate([high[:, right], small[:, right], high[:, right]], axis=0),
                    0,
                    0,
                )
            return carry

        lax.fori_loop(start, stop, body, 0)

    lead, total = info_ref[0] // block, old_ref.shape[0] // block
    swap = info_ref[1] == 1
    grams(mine_ref, jnp.where(swap, lead, 0), jnp.where(swap, total, lead))
    grams(other_ref, jnp.where(swap, 0, lead), jnp.where(swap, lead, total))


def moment_and_grams(info, factor, grad, old, piece, block):
    tiles = jax.ShapeDtypeStruct((len(TILES), BLOCK, BLOCK), full)
    return pl.pallas_call(
        partial(moment_kernel, piece=piece, block=block),
        in_specs=[smem(), smem(), vmem(), vmem()],
        out_specs=[vmem()] * 3,
        out_shape=[jax.ShapeDtypeStruct(old.shape, full), tiles, tiles],
        compiler_params=params(48),
        cost_estimate=cost(10),
        name="moment",
    )(info, factor, grad, old)


def even_product(left, right, put):
    (lh, ll), (rh, rl) = left, right
    for i in range(D // BLOCK):
        rows = slice(i * BLOCK, (i + 1) * BLOCK)
        panel = jnp.concatenate([lh[rows], lh[rows], ll[rows]], axis=1)
        for j in range(i, D // BLOCK):
            cols = slice(j * BLOCK, (j + 1) * BLOCK)
            other = jnp.concatenate([rh[:, cols], rl[:, cols], rh[:, cols]], axis=0)
            put(rows, cols, dot32(panel, other, 1, 0))


def keep(pair):
    def put(rows, cols, value):
        pair[0][rows, cols], pair[1][rows, cols] = halves(value)
        if rows != cols:
            pair[0][cols, rows], pair[1][cols, rows] = halves(value.T)

    return put


def chain_kernel(kind_ref, factor_ref, debias_ref, chip_ref, other_ref, kept_ref, got_ref,
                 grad_ref, weight_ref, first_ref, second_ref,
                 out_ref, weight_new_ref, first_new_ref, second_new_ref, copy_ref,
                 a_ref, scale_ref, *parts, chunks):
    a, q, p, t = [parts[2 * i:2 * i + 2] for i in range(4)]
    step = pl.program_id(0)
    shape = (BLOCK, BLOCK)
    once = lax.broadcasted_iota(jnp.int32, shape, 0) == lax.broadcasted_iota(jnp.int32, shape, 1)

    def put_q(rows, cols, value):
        new = 2.0315 * value - 4.775 * a_ref[rows, cols]
        keep(q)(rows, cols, new + jnp.where(once, 3.4445, 0.0) if rows == cols else new)

    def put_a(rows, cols, value):
        a_ref[rows, cols] = value
        keep(a)(rows, cols, value)

    def put_out(rows, cols, value):
        value = value * (1.0 / scale_ref[0])
        out_ref[rows, cols] = value
        if rows != cols:
            out_ref[cols, rows] = value.T

    @pl.when(step == 0)
    def _():
        half = len(TILES) // 2
        lower = kind_ref[1] == 1
        trace = 0.0
        for at, (i, j) in enumerate(TILES):
            side = kept_ref[at % half], got_ref[at % half]
            near, far = side if at < half else side[::-1]
            tile = jnp.where(lower, near, far)
            tile = jnp.where(kind_ref[0] == 0, chip_ref[at], tile)
            tile = jnp.where(kind_ref[0] == 1, other_ref[at], tile)
            a_ref[i * BLOCK:(i + 1) * BLOCK, j * BLOCK:(j + 1) * BLOCK] = tile
            if i == j:
                trace = trace + jnp.sum(jnp.where(once, tile, 0.0))
        scale = jnp.sqrt(trace) + 1e-07
        scale_ref[0] = scale
        for i, j in TILES:
            rows, cols = slice(i * BLOCK, (i + 1) * BLOCK), slice(j * BLOCK, (j + 1) * BLOCK)
            put_a(rows, cols, a_ref[rows, cols] * (1.0 / (scale * scale)))

    turn = lax.rem(step + 1, 4)
    last = 4 * NS_TURNS - 4

    @pl.when((step == 0) | (turn == 0))
    def _():
        even_product(a, a, put_q)

    @pl.when(step == 0)
    def _():
        p[0][...], p[1][...] = q[0][...], q[1][...]

    @pl.when((turn == 1) & (step > 0) & (step < last))
    def _():
        even_product(p, q, keep(t))
        p[0][...], p[1][...] = t[0][...], t[1][...]

    @pl.when(step == last)
    def _():
        even_product(p, q, put_out)

    @pl.when(turn == 2)
    def _():
        even_product(a, q, keep(t))

    @pl.when(turn == 3)
    def _():
        even_product(t, q, put_a)

    @pl.when(step < chunks)
    def _():
        grad = factor_ref[0] * grad_ref[...].astype(full)
        weight = weight_ref[...]
        first = beta_one * first_ref[...] + (1.0 - beta_one) * grad
        second = beta_two * second_ref[...] + (1.0 - beta_two) * grad * grad
        move = (first * debias_ref[0]) / (jnp.sqrt(second * debias_ref[1]) + adam_eps)
        new = weight - 0.02 * (move + adam_decay * weight)
        weight_new_ref[...] = new
        first_new_ref[...] = first
        second_new_ref[...] = second
        copy_ref[...] = new.astype(low)


def chain(kind, factor, debias, grams, table):
    steps = 4 * NS_TURNS - 3
    features, vocab = table[1].shape
    width = -(-vocab // ((steps - 1) * LANES)) * LANES
    chunks = -(-vocab // width)
    part = pl.BlockSpec((features, width), lambda g: (0, jnp.minimum(g, chunks - 1)))
    whole = jax.ShapeDtypeStruct((features, vocab), full)
    return pl.pallas_call(
        partial(chain_kernel, chunks=chunks),
        grid=(steps,),
        in_specs=[smem(), smem(), smem()] + [vmem()] * 4 + [part] * 4,
        out_specs=[pl.BlockSpec((D, D), lambda g: (0, 0))] + [part] * 4,
        out_shape=[
            jax.ShapeDtypeStruct((D, D), full),
            whole,
            whole,
            whole,
            jax.ShapeDtypeStruct((features, vocab), low),
        ],
        scratch_shapes=[pltpu.VMEM((D, D), full), pltpu.SMEM((1,), full)]
        + [pltpu.VMEM((D, D), low)] * 8,
        compiler_params=params(56),
        cost_estimate=cost(48),
        name="chain",
    )(kind, factor, debias, *grams, *table)


def apply_kernel(info_ref, gain_ref, own_ref, come_ref, moment_ref, master_ref, new_ref, copy_ref,
                 *, block):
    lead, total = info_ref[0] // block, moment_ref.shape[0] // block
    late = info_ref[2]

    def over(p_ref, start, stop, slot):
        p = halves(p_ref[...])
        gain = gain_ref[slot] * muon_rate

        def body(b, carry):
            rows = pl.ds(pl.multiple_of(b * block, block), block)
            ortho = dot_split(halves(moment_ref[rows]), p)
            new = master_ref[rows] * (1.0 - muon_rate * muon_decay) - gain * ortho
            new_ref[rows] = new
            copy_ref[rows] = new.astype(low)
            return carry

        lax.fori_loop(start, stop, body, 0)

    over(own_ref, jnp.where(late == 1, lead, 0), jnp.where(late == 1, total, lead), late)

    @pl.when(lead < total)
    def _():
        over(come_ref, jnp.where(late == 1, 0, lead), jnp.where(late == 1, lead, total), 1 - late)


def apply_chain(info, gains, own, come, moment, master, block):
    return pl.pallas_call(
        partial(apply_kernel, block=block),
        in_specs=[smem(), smem(), vmem(), vmem(), vmem(), vmem()],
        out_specs=[vmem(), vmem()],
        out_shape=[
            jax.ShapeDtypeStruct(moment.shape, full),
            jax.ShapeDtypeStruct(moment.shape, low),
        ],
        compiler_params=params(48),
        cost_estimate=cost(10),
        name="apply",
    )(info, gains, own, come, moment, master)


def chains(mine, other, wide_at, first_matrix, second_matrix, factor, debias, table, rider):
    wide = lax.axis_size("wide")
    if wide != 8:
        which = jnp.arange(4)
        slots = (which == first_matrix).astype(full)[:, None, None, None] * mine
        slots = slots + (which == second_matrix).astype(full)[:, None, None, None] * other
        total = lax.psum(slots, "wide")
        kind = jnp.zeros((2,), jnp.int32)
        outs = []
        for matrix in (first_matrix, second_matrix):
            gram = lax.dynamic_index_in_dim(total, matrix, 0, keepdims=False)
            half = gram[: len(TILES) // 2]
            outs.append(chain(kind, factor, debias, (gram, gram, half, half), table))
        return outs[0][0], outs[1][0], outs[0][1:], rider
    half = len(TILES) // 2
    pairs = [(i, i ^ 1) for i in range(8)]
    lower = wide_at % 2 == 0
    moved = lax.ppermute(other[:half], "wide", [(5, 4)])
    chip = mine + lax.ppermute(mine, "wide", pairs)
    up_send = jnp.where(lower, chip[:half], chip[half:])
    down_send = jnp.where(wide_at == 4, moved, jnp.where(wide_at == 5, other[half:], up_send))
    up = up_send + lax.ppermute(up_send, "wide", [(2, 4), (4, 2), (3, 5), (5, 3)])
    down = down_send + lax.ppermute(down_send, "wide", [(4, 6), (6, 4), (5, 7), (7, 5)])
    send = jnp.where((wide_at == 4) | (wide_at >= 6), down, up)
    swap = lax.ppermute(send, "wide", [(2, 3), (4, 5), (6, 7), (7, 6)])
    back = lax.ppermute(up, "wide", [(5, 4)])
    kept = jnp.where(wide_at >= 5, down, up)
    got = jnp.where(wide_at == 4, back, swap)
    kind = jnp.where(wide_at < 2, 0, jnp.where(wide_at == 2, 1, 2))
    kind = jnp.stack([kind, lower.astype(jnp.int32)]).astype(jnp.int32)
    got, rider = lax.optimization_barrier((got, rider))
    own, *table_new = chain(kind, factor, debias, (chip, other, kept, got), table)
    come = lax.ppermute(own, "wide", [(3, 2), (4, 5)])
    return own, come, table_new, rider


def scale_rows(hidden):
    center = hidden - jnp.mean(hidden, axis=-1, keepdims=True)
    inverse = lax.rsqrt(jnp.mean(center * center, axis=-1, keepdims=True) + norm_eps)
    return center * inverse, inverse


def unscale_rows(upstream, scaled, inverse, gain):
    weighted = upstream * gain
    return inverse * (
        weighted
        - jnp.mean(weighted, axis=-1, keepdims=True)
        - scaled * jnp.mean(weighted * scaled, axis=-1, keepdims=True)
    )


def forward_kernel(context_ref, normed0_ref, share_ref, vectors_ref, bias_ref, out_w_ref, up_w_ref, down_w_ref,
                   scaled1_ref, inverse1_ref, input1_ref, active_ref, slope_ref,
                   scaled2_ref, inverse2_ref, pooled_ref, normed1_ref, sum_ref):
    step = pl.program_id(0)

    @pl.when(step == 0)
    def _():
        attended = dot32(context_ref[...], out_w_ref[...], 1, 1) + vectors_ref[8:9]
        scaled, inverse = scale_rows(normed0_ref[...] + attended)
        scaled1_ref[...], inverse1_ref[...] = scaled, inverse
        normed1_ref[...] = scaled * vectors_ref[2:3] + vectors_ref[3:4]
        input1_ref[...] = normed1_ref[...].astype(low)
        sum_ref[...] = normed1_ref[...] + vectors_ref[9:10]

    inner = dot32(input1_ref[...], up_w_ref[...], 1, 1) + bias_ref[...]
    cdf = 0.5 * (1.0 + lax.erf(inner * math.sqrt(0.5)))
    active = (inner * cdf).astype(low)
    active_ref[...] = active
    slope_ref[...] = cdf + inner * (jnp.exp(-0.5 * inner * inner) * (1.0 / math.sqrt(2.0 * math.pi)))
    sum_ref[...] += dot32(active, down_w_ref[...], 1, 0)

    @pl.when(step == pl.num_programs(0) - 1)
    def _():
        scaled, inverse = scale_rows(sum_ref[...])
        scaled2_ref[...], inverse2_ref[...] = scaled, inverse
        normed2 = scaled * vectors_ref[4:5] + vectors_ref[5:6]
        pooled_ref[...] = jnp.dot(share_ref[...], normed2, precision=highest)


CHUNK = 512


def same(shape):
    return pl.BlockSpec(shape, lambda c: (0,) * len(shape))


def forward_rest(context, normed0, share, vectors, out_w, up_w, down_w):
    tokens = context.shape[0]
    pairs = share.shape[0]
    wide_rows = jax.ShapeDtypeStruct((tokens, D), full)
    column = jax.ShapeDtypeStruct((tokens, 1), full)
    return pl.pallas_call(
        forward_kernel,
        grid=(FF // CHUNK,),
        in_specs=[
            same((tokens, D)),
            same((tokens, D)),
            same((pairs, tokens)),
            same(vectors.shape),
            pl.BlockSpec((1, CHUNK), lambda c: (0, c)),
            same((D, D)),
            pl.BlockSpec((CHUNK, D), lambda c: (c, 0)),
            pl.BlockSpec((CHUNK, D), lambda c: (c, 0)),
        ],
        out_specs=[
            same((tokens, D)),
            same((tokens, 1)),
            same((tokens, D)),
            pl.BlockSpec((tokens, CHUNK), lambda c: (0, c)),
            pl.BlockSpec((tokens, CHUNK), lambda c: (0, c)),
            same((tokens, D)),
            same((tokens, 1)),
            same((pairs, D)),
        ],
        out_shape=[
            wide_rows,
            column,
            jax.ShapeDtypeStruct((tokens, D), low),
            jax.ShapeDtypeStruct((tokens, FF), low),
            jax.ShapeDtypeStruct((tokens, FF), full),
            wide_rows,
            column,
            jax.ShapeDtypeStruct((pairs, D), full),
        ],
        scratch_shapes=[pltpu.VMEM((tokens, D), full)] * 2,
        compiler_params=params(58),
        cost_estimate=cost(25),
        name="forward_rest",
    )(context, normed0, share, vectors, vectors[14:].reshape(1, -1), out_w, up_w, down_w)


def backward_kernel(side_ref, pooled_ref, share_ref, vectors_ref, scaled2_ref, inverse2_ref, active_ref, slope_ref,
                    input1_ref, scaled1_ref, inverse1_ref, context_ref, out_w_ref, up_w_ref, down_w_ref,
                    down_stays_ref, down_leaves_ref, up_stays_ref, up_leaves_ref, out_grad_ref, sum1_ref, context_grad_ref, sums_ref, up_sums_ref,
                    branch_ref, total_ref):
    step = pl.program_id(0)

    def over_tokens(x):
        return jnp.sum(x, axis=0, keepdims=True)

    @pl.when(step == 0)
    def _():
        spread = lax.dot_general(
            share_ref[...], pooled_ref[...], dims(0, 0), precision=highest, preferred_element_type=full
        )
        scaled = scaled2_ref[...]
        back = unscale_rows(spread, scaled, inverse2_ref[...], vectors_ref[4:5])
        total_ref[...] = back
        branch = back.astype(low)
        branch_ref[...] = branch
        sums_ref[2:3] = over_tokens(spread * scaled)
        sums_ref[3:4] = over_tokens(spread)
        sums_ref[5:6] = over_tokens(branch.astype(full))

    branch = branch_ref[...]
    inner_grad = (dot32(branch, down_w_ref[...], 1, 1) * slope_ref[...]).astype(low)

    def halve(grad, stays_ref, leaves_ref):
        left, right = grad[:, : D // 2], grad[:, D // 2 :]
        stays_ref[...] = jnp.where(side_ref[0] == 0, left, right).astype(low)
        leaves_ref[...] = jnp.where(side_ref[0] == 0, right, left).astype(low)

    halve(dot32(active_ref[...], branch, 0, 0), down_stays_ref, down_leaves_ref)
    halve(dot32(inner_grad, input1_ref[...], 0, 0), up_stays_ref, up_leaves_ref)
    up_sums_ref[...] = over_tokens(inner_grad.astype(full))
    total_ref[...] += dot32(inner_grad, up_w_ref[...], 1, 0)

    @pl.when(step == pl.num_programs(0) - 1)
    def _():
        upstream = total_ref[...]
        scaled = scaled1_ref[...]
        back = unscale_rows(upstream, scaled, inverse1_ref[...], vectors_ref[2:3])
        sum1_ref[...] = back
        attended = back.astype(low)
        sums_ref[0:1] = over_tokens(upstream * scaled)
        sums_ref[1:2] = over_tokens(upstream)
        sums_ref[4:5] = over_tokens(attended.astype(full))
        out_grad_ref[...] = dot32(attended, context_ref[...], 0, 0).astype(low)
        context_grad_ref[...] = dot32(attended, out_w_ref[...], 1, 0).astype(low)


def backward_rest(side, pooled_grads, share, vectors, kept, context, out_w, up_w, down_w):
    scaled1, inverse1, input1, active, slope, scaled2, inverse2 = kept
    tokens = context.shape[0]
    pairs = share.shape[0]
    rows = pl.BlockSpec((CHUNK, D), lambda c: (c, 0))
    cols = pl.BlockSpec((tokens, CHUNK), lambda c: (0, c))
    return pl.pallas_call(
        backward_kernel,
        grid=(FF // CHUNK,),
        in_specs=[
            smem(),
            same((pairs, D)),
            same((pairs, tokens)),
            same(vectors.shape),
            same((tokens, D)),
            same((tokens, 1)),
            cols,
            cols,
            same((tokens, D)),
            same((tokens, D)),
            same((tokens, 1)),
            same((tokens, D)),
            same((D, D)),
            rows,
            rows,
        ],
        out_specs=[pl.BlockSpec((CHUNK, D // 2), lambda c: (c, 0))] * 4
        + [
            same((D, D)),
            same((tokens, D)),
            same((tokens, D)),
            same((8, D)),
            pl.BlockSpec((1, CHUNK), lambda c: (0, c)),
        ],
        out_shape=[jax.ShapeDtypeStruct((FF, D // 2), low)] * 4
        + [
            jax.ShapeDtypeStruct((D, D), low),
            jax.ShapeDtypeStruct((tokens, D), full),
            jax.ShapeDtypeStruct((tokens, D), low),
            jax.ShapeDtypeStruct((8, D), full),
            jax.ShapeDtypeStruct((1, FF), full),
        ],
        scratch_shapes=[pltpu.VMEM((tokens, D), low), pltpu.VMEM((tokens, D), full)],
        compiler_params=params(58),
        cost_estimate=cost(35),
        name="backward_rest",
    )(side, pooled_grads, share, vectors, scaled2, inverse2, active, slope, input1, scaled1, inverse1, context,
      out_w, up_w, down_w)


def front_kernel(side_ref, mixed_ref, input_ref, out_grad_ref, stays_ref, leaves_ref):
    def halve(grad):
        left, right = grad[:, : D // 2], grad[:, D // 2 :]
        stays_ref[...] = jnp.where(side_ref[0] == 0, left, right).astype(low)
        leaves_ref[...] = jnp.where(side_ref[0] == 0, right, left).astype(low)

    @pl.when(pl.program_id(0) < 3)
    def _():
        halve(dot32(mixed_ref[...], input_ref[...], 0, 0))

    @pl.when(pl.program_id(0) == 3)
    def _():
        halve(out_grad_ref[...].astype(full))


def front_grads(side, mixed_grad, input0, out_grad):
    tokens = mixed_grad.shape[0]
    return pl.pallas_call(
        front_kernel,
        grid=(4,),
        in_specs=[
            smem(),
            pl.BlockSpec((tokens, D), lambda c: (0, jnp.minimum(c, 2))),
            same((tokens, D)),
            same((D, D)),
        ],
        out_specs=[pl.BlockSpec((D, D // 2), lambda c: (c, 0))] * 2,
        out_shape=[jax.ShapeDtypeStruct((4 * D, D // 2), low)] * 2,
        compiler_params=params(40),
        cost_estimate=cost(7),
        name="front_grads",
    )(side, mixed_grad, input0, out_grad)


def embed_back_kernel(mixed_ref, sum1_ref, scaled_ref, inverse_ref, vectors_ref, weight_ref,
                      embed_ref, send_ref, sums_ref, mixed_sum_ref, *, narrow, wide):
    upstream = sum1_ref[...] + dot32(mixed_ref[...], weight_ref[...], 1, 0)
    scaled = scaled_ref[...]
    back = unscale_rows(upstream, scaled, inverse_ref[...], vectors_ref[0:1])
    embed_ref[...] = back
    turned = back.T.astype(low)
    features = send_ref.shape[1]
    for n in range(narrow):
        for w in range(wide):
            start = (w * narrow + n) * features
            send_ref[n * wide + w] = turned[start:start + features]

    @pl.when(pl.program_id(0) == 0)
    def _():
        sums_ref[...] = jnp.zeros_like(sums_ref)
        mixed_sum_ref[...] = jnp.zeros_like(mixed_sum_ref)

    sums_ref[0:1] += jnp.sum(upstream * scaled, axis=0, keepdims=True)
    sums_ref[1:2] += jnp.sum(upstream, axis=0, keepdims=True)
    mixed_sum_ref[...] += jnp.sum(mixed_ref[...].astype(full), axis=0, keepdims=True)


def embed_back(mixed_grad, sum1_grad, scaled0, inverse0, vectors, weight, narrow, wide):
    tokens = mixed_grad.shape[0]
    count = narrow * wide
    block = pl.BlockSpec((SEQ, D), lambda b: (b, 0))
    return pl.pallas_call(
        partial(embed_back_kernel, narrow=narrow, wide=wide),
        grid=(tokens // SEQ,),
        in_specs=[
            pl.BlockSpec((SEQ, 3 * D), lambda b: (b, 0)),
            block,
            block,
            pl.BlockSpec((SEQ, 1), lambda b: (b, 0)),
            same(vectors.shape),
            same((3 * D, D)),
        ],
        out_specs=[
            block,
            pl.BlockSpec((count, D // count, SEQ), lambda b: (0, 0, b)),
            same((8, D)),
            same((1, 3 * D)),
        ],
        out_shape=[
            jax.ShapeDtypeStruct((tokens, D), full),
            jax.ShapeDtypeStruct((count, D // count, tokens), low),
            jax.ShapeDtypeStruct((8, D), full),
            jax.ShapeDtypeStruct((1, 3 * D), full),
        ],
        compiler_params=params(48),
        cost_estimate=cost(10),
        name="embed_back",
    )(mixed_grad, sum1_grad, scaled0, inverse0, vectors, weight)


def layout(lengths):
    row_ends = jnp.cumsum(lengths)
    starts = row_ends - lengths
    places = jnp.arange(SEQ, dtype=jnp.int32)
    segment = jnp.sum((places[:, None] >= row_ends[None, :]).astype(jnp.int32), axis=1)
    chosen = segment[:, None] == jnp.arange(SLOTS, dtype=jnp.int32)[None, :]
    start_at = jnp.sum(jnp.where(chosen, starts[None, :], 0), axis=1)
    length_at = jnp.sum(jnp.where(chosen, lengths[None, :], 0), axis=1)
    position = places - start_at
    second = (2 * position >= length_at).astype(jnp.int32)
    return (chosen.astype(full), position, second, segment)


def norm_forward(hidden, gain, bias):
    center = hidden - jnp.mean(hidden, axis=-1, keepdims=True)
    inverse = lax.rsqrt(jnp.mean(center * center, axis=-1, keepdims=True) + norm_eps)
    scaled = center * inverse
    return (scaled * gain + bias, scaled, inverse)


def norm_backward(upstream, scaled, inverse, gain):
    weighted = upstream * gain
    back = inverse * (
        weighted
        - jnp.mean(weighted, axis=-1, keepdims=True)
        - scaled * jnp.mean(weighted * scaled, axis=-1, keepdims=True)
    )
    return (back, jnp.sum(upstream * scaled, axis=0), jnp.sum(upstream, axis=0))


def project(left, right):
    return jnp.dot(left, right, preferred_element_type=full)


def task_loss(logits, scores, tasks, labels, negatives, counts):
    logprob = jax.nn.log_softmax(logits, axis=-1)
    picked = jnp.sum(
        jnp.where(labels[:, :, None] == jnp.arange(3, dtype=jnp.int32), logprob, 0.0), axis=2
    )
    chosen = negatives[:, :, :, None] == jnp.arange(scores.shape[1], dtype=jnp.int32)
    rivals = jnp.sum(jnp.where(chosen, scores[:, None, None, :], 0.0), axis=3)
    together = jnp.concatenate([scores[:, :, None], rivals], axis=2)
    ranking = jax.nn.logsumexp(together, axis=2) - scores
    first_part = jnp.sum(jnp.where(tasks == 0, -picked, 0.0)) / counts[0]
    return first_part + jnp.sum(jnp.where(tasks == 1, ranking, 0.0)) / counts[1]


def adam(weight, grad, first, second, step, rate):
    first = beta_one * first + (1.0 - beta_one) * grad
    second = beta_two * second + (1.0 - beta_two) * grad * grad
    unbiased = first / (1.0 - beta_one**step)
    spread = second / (1.0 - beta_two**step)
    return (
        weight - rate * (unbiased / (jnp.sqrt(spread) + adam_eps) + adam_decay * weight),
        first,
        second,
    )


def broadcast_all(x):
    count = lax.axis_size("narrow") * lax.axis_size("wide")
    return lax.all_to_all(
        jnp.broadcast_to(x[None], (count,) + x.shape), BOTH, split_axis=0, concat_axis=0, tiled=True
    )


def sides(wide):
    return [list(range(0, wide, 2)), list(range(1, wide, 2))]


def chip_mates(wide):
    return [(i, i ^ 1) for i in range(wide)]


def gather_weights(master, narrow_at, wide_at, first):
    wide = lax.axis_size("wide")
    if wide != 8:
        whole = lax.all_gather(master.astype(low), "wide", axis=0, tiled=True)
        return first, list(whole.reshape(wide, -1, D))
    share = master.shape[0] // lax.axis_size("narrow")
    mine = lax.dynamic_slice_in_dim(master, narrow_at * share, share, 0).astype(low)
    near = lax.all_gather(mine, "wide", axis=0, tiled=False, axis_index_groups=sides(wide))
    near, first = lax.optimization_barrier((near, first))
    return first, [
        lax.all_gather(part, "narrow", axis=1, tiled=True)
        for part in (near[: wide // 4], near[wide // 4 :])
    ]


def both_cores(held, wide_at):
    owners = []
    other = lax.ppermute(held, "wide", chip_mates(lax.axis_size("wide")))
    side = wide_at % 2
    even = jnp.where(side == 0, held, other)
    odd = jnp.where(side == 0, other, held)
    for at in range(held.shape[0]):
        owners += [even[at], odd[at]]
    return owners


def rows_of(owners, matrix):
    rows = owners[0].shape[0]
    lo, hi = BOUNDS[matrix], BOUNDS[matrix + 1]
    pieces = []
    for at in range(lo // rows, -(-hi // rows)):
        pieces.append(owners[at][max(lo - at * rows, 0) : min(hi - at * rows, rows)])
    return jnp.concatenate(pieces) if len(pieces) > 1 else pieces[0]


def shards(
    token_ids,
    seq_lengths,
    task_ids,
    labels,
    negatives,
    step_count,
    hidden_master,
    hidden_momentum,
    table_master,
    table_first,
    table_second,
    pos_types,
    pos_first,
    pos_second,
    vectors,
    vec_first,
    vec_second,
):
    wide_at = lax.axis_index("wide")
    narrow_at = lax.axis_index("narrow")
    wide = lax.axis_size("wide")
    narrow = lax.axis_size("narrow")
    count = wide * narrow
    device_at = narrow_at * wide + wide_at
    micro_count, rows_each = token_ids.shape[:2]
    batch = micro_count * rows_each
    tokens = batch * SEQ
    shard = hidden_master.shape[0]
    vocab = table_master.shape[1]
    features = table_master.shape[0] // narrow
    pairs_each = rows_each * SLOTS

    parts = [token_ids, task_ids, labels, negatives]
    sizes = [part.size for part in parts]
    packed = jnp.concatenate([part.reshape(-1) for part in parts])
    packed = jnp.pad(packed, (0, -packed.size % LANES))
    gathered = broadcast_all(packed)
    ends = [sum(sizes[: i + 1]) for i in range(len(sizes))]
    ids_all = gathered[:, : ends[0]]

    def pairs_of(lo, hi, tail):
        block = gathered[:, lo:hi].reshape((count, micro_count, pairs_each) + tail)
        return jnp.moveaxis(block, 1, 0).reshape((micro_count, count * pairs_each) + tail)

    tasks_all = pairs_of(ends[0], ends[1], ())
    labels_all = pairs_of(ends[1], ends[2], ())
    negatives_all = pairs_of(ends[2], ends[3], (NEG,))
    counts = jnp.stack(
        [jnp.sum((tasks_all == 0).astype(full)), jnp.sum((tasks_all == 1).astype(full))]
    )


    group_ids = lax.dynamic_slice_in_dim(ids_all, narrow_at * wide, wide, 0).reshape(-1)
    pieces = lookup(group_ids, table_master)
    pieces, gathers = gather_weights(hidden_master, narrow_at, wide_at, pieces)
    simple = wide != 8
    arrived = lax.all_to_all(
        pieces.reshape(wide, tokens, -1), "wide", split_axis=0, concat_axis=0, tiled=True
    )
    token_rows = jnp.moveaxis(arrived, 0, 1).reshape(tokens, D)

    lengths = seq_lengths.reshape(batch, SLOTS)
    member, position, second, segment = jax.vmap(layout)(lengths)
    flat_position = position.reshape(-1)
    flat_second = second.reshape(-1)
    place_rows = pos_types[flat_position]
    place_rows = place_rows + jnp.where(flat_second[:, None] == 1, pos_types[SEQ + 1], pos_types[SEQ])
    if simple:
        owners = gathers
    else:
        place_rows, held = lax.optimization_barrier((place_rows, gathers[0]))
        owners = both_cores(held, wide_at)
    embed = token_rows.astype(full) + place_rows
    normed0, scaled0, inverse0 = norm_forward(embed, vectors[0], vectors[1])
    input0 = normed0.astype(low)
    qkv_bias = jnp.concatenate([vectors[6], jnp.zeros_like(vectors[6]), vectors[7]])
    weight_qkv, weight_out = rows_of(owners, 0), rows_of(owners, 1)
    mixed = (project(input0, weight_qkv.T) + qkv_bias).astype(low)
    context_low, logsum = attend(mixed, segment)
    if not simple:
        rest, context_low = lax.optimization_barrier((gathers[1], context_low))
        owners = owners + both_cores(rest, wide_at)
    weight_up, weight_down = rows_of(owners, 2), rows_of(owners, 3)
    pair_at = (jnp.arange(batch, dtype=jnp.int32)[:, None] * SLOTS + segment).reshape(1, -1)
    pairs = jnp.arange(batch * SLOTS, dtype=jnp.int32)[:, None]
    share = jnp.where(pair_at == pairs, 1.0 / lengths.astype(full).reshape(-1, 1), 0.0)
    scaled1, inverse1, input1, active, slope, scaled2, inverse2, flat_pooled = forward_rest(
        context_low, normed0, share, vectors, weight_out, weight_up, weight_down
    )
    heads = vectors[10:14]
    head_out = jnp.dot(flat_pooled, heads.T, precision=highest)

    sent = jnp.pad(head_out.reshape(-1), (0, -head_out.size % LANES))
    head_all = broadcast_all(sent)[:, : head_out.size]
    head_all = head_all.reshape(count, micro_count, pairs_each, 4)
    head_all = jnp.moveaxis(head_all, 1, 0).reshape(micro_count, count * pairs_each, 4)

    def objective(every):
        return task_loss(every[:, :, :3], every[:, :, 3], tasks_all, labels_all, negatives_all, counts)

    loss, pullback = jax.vjp(objective, head_all)
    head_grads = pullback(jnp.ones_like(loss))[0]
    output_grads = lax.dynamic_slice_in_dim(head_grads, device_at * pairs_each, pairs_each, 1)
    output_grads = output_grads.reshape(-1, 4)
    heads_grad = jnp.dot(output_grads.T, flat_pooled, precision=highest)
    pooled_grads = jnp.dot(output_grads, heads, precision=highest)

    spans_down = [(0, 768), (768, 1920), (1920, 3072)]
    spans_up = [(0, 384), (384, 1536), (1536, 2688), (2688, 3072)]
    spans_front = [(0, 1152), (1152, 2304), (2304, 3072)]

    side = wide_at % 2

    def between_cores(grad):
        stays, leaves = grad
        if simple:
            return stays, leaves
        return stays, lax.ppermute(leaves, "wide", chip_mates(wide))

    def slices(grad, spans):
        stays, comes = grad
        if simple:
            return [jnp.concatenate([stays, comes], axis=1)]
        chip = (stays.astype(full) + comes.astype(full)).astype(low)
        parts = []
        for turn in range(narrow):
            pieces = []
            for lo, hi in spans:
                share_rows = (hi - lo) // narrow
                start = lo + (narrow_at ^ turn) * share_rows
                pieces.append(lax.dynamic_slice_in_dim(chip, start, share_rows, 0))
            parts.append(jnp.concatenate(pieces))
        return parts

    def over_narrow(parts):
        return parts[:1] + [
            lax.ppermute(part, "narrow", [(i, i ^ (turn + 1)) for i in range(narrow)])
            for turn, part in enumerate(parts[1:])
        ]

    together = lax.optimization_barrier
    kept = (scaled1, inverse1, input1, active, slope, scaled2, inverse2)
    *sides_of, out_grad, sum1_grad, context_grad, sums, up_sums = backward_rest(
        side[None] if not simple else jnp.zeros((1,), jnp.int32),
        pooled_grads, share, vectors, kept, context_low, weight_out, weight_up, weight_down
    )
    down_pair = between_cores(sides_of[:2])
    up_pair = between_cores(sides_of[2:])
    down_cut, up_pair, context_grad = together((slices(down_pair, spans_down), up_pair, context_grad))
    down_part = over_narrow(down_cut)
    up_cut, context_grad = together((slices(up_pair, spans_up), context_grad))
    up_part = over_narrow(up_cut)
    mixed_grad = attend_back(mixed, context_grad, logsum, segment)
    mixed_grad, down_part = together((mixed_grad, down_part))
    if simple:
        normed0_grad = sum1_grad + project(mixed_grad, weight_qkv)
        embed_grad, gain0, bias0 = norm_backward(normed0_grad, scaled0, inverse0, vectors[0])
        table_send = embed_grad.astype(low).T.reshape(wide, narrow, features, tokens)
        table_send = jnp.moveaxis(table_send, 1, 0).reshape(count, features, tokens)
        mixed_sum = jnp.sum(mixed_grad.astype(full), axis=0)
    else:
        embed_grad, table_send, first_sums, mixed_sum = embed_back(
            mixed_grad, sum1_grad, scaled0, inverse0, vectors, weight_qkv, narrow, wide
        )
        gain0, bias0, mixed_sum = first_sums[0], first_sums[1], mixed_sum[0]
    table_send, mixed_grad = together((table_send, mixed_grad))
    come = lax.all_to_all(table_send, BOTH, split_axis=0, concat_axis=0, tiled=True)

    if simple:
        front_grad = jnp.concatenate([project(mixed_grad.T, input0).astype(low), out_grad])
        front_halves = (front_grad[:, : D // 2], front_grad[:, D // 2 :])
    else:
        front_halves = tuple(front_grads(side[None], mixed_grad, input0, out_grad))
    front_send, embed_grad, mixed_grad, up_part = together(
        (front_halves, embed_grad, mixed_grad, up_part)
    )
    front_part = over_narrow(slices(between_cores(front_send), spans_front))
    small_rows = jnp.concatenate(
        [
            jnp.stack([gain0, bias0]),
            sums[:4],
            jnp.stack([mixed_sum[:D], mixed_sum[2 * D :]]),
            sums[4:6],
        ]
    )
    up_rows = up_sums.reshape(-1, D)

    places = jnp.arange(SEQ, dtype=jnp.int32)[:, None]
    row_hot = jnp.concatenate(
        [
            flat_position[None] == places,
            jnp.stack([flat_second == 0, flat_second == 1]),
        ]
    ).astype(low)
    high_part, low_part = halves(embed_grad)
    pos_grad = project(jnp.concatenate([row_hot, row_hot], axis=1), jnp.concatenate([high_part, low_part]))
    small = jnp.concatenate([pos_grad, small_rows, heads_grad, up_rows])
    small_count = small.shape[0]
    small = jnp.pad(small, ((0, count * features - small_count), (0, 0)))

    def added(parts):
        return sum(part.astype(full) for part in parts).astype(low)

    joined = jnp.concatenate([added(front_part), added(up_part), added(down_part)])
    small_send = small.astype(low).reshape(count, features, D)
    come, small_send = together((come, small_send))
    small_come = lax.all_to_all(small_send, BOTH, split_axis=0, concat_axis=0, tiled=True)
    table_part, table_square = collect(ids_all, come, vocab, tokens)
    if simple:
        hidden_part = lax.psum_scatter(joined, "wide", scatter_dimension=0, tiled=True)
        hidden_part = lax.psum_scatter(hidden_part, "narrow", scatter_dimension=0, tiled=True)
        hidden_square = jnp.sum(jnp.square(hidden_part.astype(full)))
    else:
        owned = lax.psum_scatter(
            joined, "wide", scatter_dimension=0, tiled=True, axis_index_groups=sides(wide)
        )
        owned, table_square, small_come = together((owned, table_square, small_come))
        hidden_square = jnp.sum(jnp.square(owned.astype(full)))
        half = owned.shape[0] // 2
        stays = jnp.where(side == 0, owned[:half], owned[half:])
        leaves = jnp.where(side == 0, owned[half:], owned[:half])
        comes = lax.ppermute(leaves, "wide", chip_mates(wide))
        hidden_part = jnp.concatenate(
            [jnp.where(side == 0, stays, comes), jnp.where(side == 0, comes, stays)], axis=1
        )
    small_part = jnp.sum(small_come.astype(full), axis=0)
    square = hidden_square + table_square[0, 0] + jnp.sum(small_part * small_part)
    square, hidden_part = together((square, hidden_part))
    if simple:
        hidden_all = lax.all_gather(hidden_part, "narrow", axis=0, tiled=True)
    else:
        hidden_all = jnp.concatenate(
            [hidden_part]
            + [
                lax.ppermute(hidden_part, "narrow", [(i, i ^ turn) for i in range(narrow)])
                for turn in range(1, narrow)
            ]
        )
    squares = broadcast_all(jnp.broadcast_to(square, (LANES,)))
    squares, hidden_all, table_part = together((squares, hidden_all, table_part))
    table_grad = lax.all_gather(table_part, "narrow", axis=0, tiled=True)
    clip_norm = jnp.sqrt(jnp.sum(squares[:, 0]))
    factor = jnp.minimum(1.0, clip_bound / clip_norm)

    start = wide_at * shard
    bounds = jnp.array(BOUNDS, jnp.int32)
    first_matrix = jnp.sum((start >= bounds[1:4]).astype(jnp.int32))
    second_matrix = jnp.sum((start + shard - 1 >= bounds[1:4]).astype(jnp.int32))
    split = jnp.minimum(bounds[first_matrix + 1] - start, shard)
    block = shard // 3
    piece = shard // 12
    at = jnp.arange(12, dtype=jnp.int32)
    if simple:
        source = at
    else:
        lead = split // piece
        each = lead // narrow
        rest = (12 - lead) // narrow
        in_first = at < lead
        inside = jnp.where(in_first, at, at - lead)
        width = jnp.maximum(jnp.where(in_first, each, rest), 1)
        origin = (inside // width) ^ narrow_at
        source = origin * (12 // narrow) + jnp.where(in_first, 0, each) + inside % width
    swap = (wide_at == 2).astype(jnp.int32) * (0 if simple else 1)
    info = jnp.concatenate([jnp.stack([split, swap]), source]).astype(jnp.int32)
    gains = jnp.array([0.2 * math.sqrt(hi - lo) for lo, hi in zip(BOUNDS, BOUNDS[1:])], full)
    moment, mine, other = moment_and_grams(
        info, factor[None], hidden_all, hidden_momentum, piece, block
    )
    step = step_count[0].astype(full)
    debias = jnp.stack([1.0 / (1.0 - beta_one**step), 1.0 / (1.0 - beta_two**step)])
    chain0, chain1, (table_new, table_first_new, table_second_new, table_copy), late_small = chains(
        mine,
        other,
        wide_at,
        first_matrix,
        second_matrix,
        factor[None],
        debias,
        (table_grad, table_master, table_first, table_second),
        small_part,
    )
    small_all = broadcast_all(late_small.astype(low)).reshape(-1, D)[:small_count].astype(full)
    late = (wide_at == 5).astype(jnp.int32) * (0 if simple else 1)
    apply_info = jnp.stack([split, swap, late]).astype(jnp.int32)
    slot_gains = jnp.stack([gains[first_matrix], gains[second_matrix]])
    hidden_new, hidden_copy = apply_chain(apply_info, slot_gains, chain0, chain1, moment, hidden_master, block)

    pos_new, pos_first_new, pos_second_new = adam(
        pos_types, factor * small_all[: SEQ + 2], pos_first, pos_second, step, 0.02
    )
    vectors_new, vec_first_new, vec_second_new = adam(
        vectors, factor * small_all[SEQ + 2 :], vec_first, vec_second, step, 0.2
    )
    return (
        loss,
        clip_norm,
        moment,
        hidden_new,
        hidden_copy,
        table_new,
        table_first_new,
        table_second_new,
        table_copy,
        pos_new,
        pos_first_new,
        pos_second_new,
        vectors_new,
        vec_first_new,
        vec_second_new,
    )


def solution(mesh):
    rows = P(None, BOTH, None)
    owned = P("wide", None)
    return jax.shard_map(
        shards,
        mesh=mesh,
        in_specs=(rows, rows, rows, rows, P(None, BOTH, None, None), P())
        + (owned,) * 5
        + (P(),) * 6,
        out_specs=(P(), P()) + (owned,) * 7 + (P(),) * 6,
        check_vma=False,
    )
```

```python
from functools import partial
import math

import jax
import jax.numpy as jnp
from jax import lax
from jax.experimental import pallas as pl
from jax.experimental.pallas import tpu as pltpu
from jax.sharding import PartitionSpec as P

D = 768
HEADS = 12
HEAD = 64
FF = 3072
SEQ = 512
SLOTS = 4
NEG = 4
NS_TURNS = 5
LANES = 128
GROUPS = 4
WIDTH = LANES // GROUPS
BLOCK = 256
TILES = [(i, j) for i in range(D // BLOCK) for j in range(i, D // BLOCK)]

BOTH = ("narrow", "wide")
highest = lax.Precision.HIGHEST
clip_bound = 0.002
norm_eps = 1e-06
muon_beta = 0.95
muon_rate = 0.1
muon_decay = 0.01
beta_one = 0.9
beta_two = 0.999
adam_eps = 1e-08
adam_decay = 0.01
BOUNDS = (0, 3 * D, 4 * D, 4 * D + FF, 4 * D + 2 * FF)

low = jnp.bfloat16
full = jnp.float32


def dims(left, right):
    return (((left,), (right,)), ((), ()))


def dot32(left, right, left_dim, right_dim):
    return lax.dot_general(left, right, dims(left_dim, right_dim), preferred_element_type=full)


def halves(x):
    high = x.astype(low)
    return high, (x - high.astype(full)).astype(low)


def dot_split(left, right, left_dim=1, right_dim=0):
    (lh, ll), (rh, rl) = left, right
    return dot32(lh, rh, left_dim, right_dim) + (
        dot32(lh, rl, left_dim, right_dim) + dot32(ll, rh, left_dim, right_dim)
    )


def params(mib):
    return pltpu.CompilerParams(vmem_limit_bytes=mib << 20)


def cost(micros):
    return pl.CostEstimate(flops=micros * 10**9, transcendentals=0, bytes_accessed=1 << 20)


def vmem():
    return pl.BlockSpec(memory_space=pltpu.VMEM)


def smem():
    return pl.BlockSpec(memory_space=pltpu.SMEM)


def attend_kernel(mixed_ref, seg_col_ref, seg_row_ref, context_ref, logsum_ref):
    same = seg_col_ref[0] == seg_row_ref[0]

    def pair(step, carry):
        at = pl.multiple_of(step * LANES, LANES)
        queries = mixed_ref[:, pl.ds(at, LANES)]
        keys = mixed_ref[:, pl.ds(D + at, LANES)]
        values = mixed_ref[:, pl.ds(2 * D + at, LANES)]
        outs = []
        for half in range(2):
            cut = slice(half * HEAD, (half + 1) * HEAD)
            raw = dot32(keys[:, cut], queries[:, cut], 1, 1)
            scores = jnp.where(same, raw * (1.0 / math.sqrt(HEAD)), -1e30)
            peak = jnp.max(scores, axis=0, keepdims=True)
            lifted = jnp.exp(scores - peak)
            total = jnp.sum(lifted, axis=0, keepdims=True)
            probs = (lifted * (1.0 / total)).astype(low)
            outs.append(dot32(values[:, cut], probs, 0, 0))
            logsum_ref[0, pl.ds(2 * step + half, 1), :] = peak + jnp.log(total)
        context_ref[:, pl.ds(at, LANES)] = jnp.concatenate(outs, axis=0).T.astype(low)
        return carry

    lax.fori_loop(0, HEADS // 2, pair, 0, unroll=3)


def attend(mixed, segment):
    rows = segment.shape[0]
    return pl.pallas_call(
        attend_kernel,
        grid=(rows,),
        in_specs=[
            pl.BlockSpec((SEQ, 3 * D), lambda b: (b, 0)),
            pl.BlockSpec((1, SEQ, 1), lambda b: (b, 0, 0)),
            pl.BlockSpec((1, 1, SEQ), lambda b: (b, 0, 0)),
        ],
        out_specs=[
            pl.BlockSpec((SEQ, D), lambda b: (b, 0)),
            pl.BlockSpec((1, 16, SEQ), lambda b: (b, 0, 0)),
        ],
        out_shape=[
            jax.ShapeDtypeStruct((rows * SEQ, D), low),
            jax.ShapeDtypeStruct((rows, 16, SEQ), full),
        ],
        compiler_params=params(48),
        cost_estimate=cost(19),
        name="attend",
    )(mixed, segment[:, :, None], segment[:, None, :])


def attend_back_kernel(mixed_ref, grad_ref, logsum_ref, seg_col_ref, seg_row_ref, out_ref):
    same = seg_col_ref[0] == seg_row_ref[0]
    scale = 1.0 / math.sqrt(HEAD)

    def pair(step, carry):
        at = pl.multiple_of(step * LANES, LANES)
        queries = mixed_ref[:, pl.ds(at, LANES)]
        keys = mixed_ref[:, pl.ds(D + at, LANES)]
        values = mixed_ref[:, pl.ds(2 * D + at, LANES)]
        upstream = grad_ref[:, pl.ds(at, LANES)]
        query_grads, key_grads, value_grads = [], [], []
        for half in range(2):
            cut = slice(half * HEAD, (half + 1) * HEAD)
            logsum = logsum_ref[0, pl.ds(2 * step + half, 1), :]
            raw = dot32(keys[:, cut], queries[:, cut], 1, 1)
            probs = jnp.exp(jnp.where(same, raw * scale, -1e30) - logsum)
            prob_grads = dot32(values[:, cut], upstream[:, cut], 1, 1)
            value_grads.append(dot32(probs.astype(low), upstream[:, cut], 1, 0))
            moved = jnp.sum(prob_grads * probs, axis=0, keepdims=True)
            back = (probs * (prob_grads - moved) * scale).astype(low)
            key_grads.append(dot32(back, queries[:, cut], 1, 0))
            query_grads.append(dot32(keys[:, cut], back, 0, 0))
        out_ref[:, pl.ds(at, LANES)] = jnp.concatenate(query_grads, axis=0).T.astype(low)
        out_ref[:, pl.ds(D + at, LANES)] = jnp.concatenate(key_grads, axis=1).astype(low)
        out_ref[:, pl.ds(2 * D + at, LANES)] = jnp.concatenate(value_grads, axis=1).astype(low)
        return carry

    lax.fori_loop(0, HEADS // 2, pair, 0, unroll=3)


def attend_back(mixed, context_grad, logsum, segment):
    rows = segment.shape[0]
    return pl.pallas_call(
        attend_back_kernel,
        grid=(rows,),
        in_specs=[
            pl.BlockSpec((SEQ, 3 * D), lambda b: (b, 0)),
            pl.BlockSpec((SEQ, D), lambda b: (b, 0)),
            pl.BlockSpec((1, 16, SEQ), lambda b: (b, 0, 0)),
            pl.BlockSpec((1, SEQ, 1), lambda b: (b, 0, 0)),
            pl.BlockSpec((1, 1, SEQ), lambda b: (b, 0, 0)),
        ],
        out_specs=pl.BlockSpec((SEQ, 3 * D), lambda b: (b, 0)),
        out_shape=jax.ShapeDtypeStruct((rows * SEQ, 3 * D), low),
        compiler_params=params(56),
        cost_estimate=cost(28),
        name="attend_back",
    )(mixed, context_grad, logsum, segment[:, :, None], segment[:, None, :])


def lookup_kernel(ids_ref, table_ref, out_ref, turned_ref, rows_ref):
    step = pl.program_id(0)
    features, width = table_ref.shape
    tokens, chunk = out_ref.shape[0], rows_ref.shape[0]
    block = table_ref[...].astype(low).astype(full)
    block = jnp.concatenate([block, jnp.zeros((LANES - features, width), full)], axis=0)
    turned_ref[pl.ds(pl.multiple_of(step * width, width), width), :] = block.T

    @pl.when(step == pl.num_programs(0) - 1)
    def _():
        def piece(c, carry):
            def body(i, inner):
                at = i * 32
                found = [turned_ref[pl.ds(ids_ref[c * chunk + at + k], 1), :] for k in range(32)]
                for k in range(32):
                    rows_ref[pl.ds(at + k, 1), :] = found[k]
                return inner

            lax.fori_loop(0, chunk // 32, body, 0)
            start = pl.multiple_of(c * chunk, chunk)
            out_ref[pl.ds(start, chunk), :] = rows_ref[:, :features].astype(low)
            return carry

        lax.fori_loop(0, tokens // chunk, piece, 0)


def lookup(ids, table):
    features, vocab = table.shape
    width = -(-vocab // (4 * LANES)) * LANES
    steps = -(-vocab // width)
    return pl.pallas_call(
        lookup_kernel,
        grid=(steps,),
        in_specs=[smem(), pl.BlockSpec((features, width), lambda s: (0, s))],
        out_specs=pl.BlockSpec((ids.shape[0], features), lambda s: (0, 0)),
        out_shape=jax.ShapeDtypeStruct((ids.shape[0], features), low),
        scratch_shapes=[pltpu.VMEM((steps * width, LANES), full), pltpu.VMEM((1024, LANES), full)],
        compiler_params=params(56),
        cost_estimate=cost(19),
        name="lookup",
    )(ids, table)


def collect_kernel(place_ref, ids_ref, grads_ref, out_ref, square_ref, *scratch,
                   span, tokens, features, vocab):
    sums, rows_ref = scratch[:-1], scratch[-1]
    step = pl.program_id(0)
    last = pl.num_programs(0) - 1
    streams = len(sums)
    batch = 4 * streams

    @pl.when(step == 0)
    def _():
        for total in sums:
            total[...] = jnp.zeros_like(total)

    group = ids_ref[0] // span
    grads = grads_ref[0].astype(full)
    pad = jnp.zeros((WIDTH - features, tokens), full)
    pieces = []
    for at in range(GROUPS):
        pieces += [jnp.where(group == at, grads, 0.0), pad]
    rows_ref[...] = jnp.concatenate(pieces, axis=0).T

    def body(i, carry):
        for base in range(0, batch, streams):
            at = i * batch + base
            places = [pl.ds(place_ref[0, 0, at + k], 1) for k in range(streams)]
            olds = [sums[k][places[k], :] for k in range(streams)]
            news = [rows_ref[pl.ds(at + k, 1), :] for k in range(streams)]
            for k in range(streams):
                sums[k][places[k], :] = olds[k] + news[k]
        return carry

    lax.fori_loop(0, tokens // batch, body, 0)

    @pl.when(step == last)
    def _():
        def flush(b, total):
            at = pl.multiple_of(b * LANES, LANES)
            block = sums[0][pl.ds(at, LANES), :]
            for k in range(1, streams):
                block += sums[k][pl.ds(at, LANES), :]
            turned = block.T
            for g in range(GROUPS):
                piece = turned[g * WIDTH:g * WIDTH + features]

                @pl.when(g * span + at < vocab)
                def _():
                    out_ref[:, pl.ds(pl.multiple_of(g * span + at, LANES), LANES)] = piece.astype(low)

            return total + block * block

        total = lax.fori_loop(0, span // LANES, flush, jnp.zeros((LANES, LANES), full))
        square_ref[...] = jnp.broadcast_to(jnp.sum(total, keepdims=True), square_ref.shape)


def collect(ids, grads, vocab, tokens):
    sources, features = grads.shape[:2]
    span = -(-vocab // (GROUPS * LANES)) * LANES
    return pl.pallas_call(
        partial(collect_kernel, span=span, tokens=tokens, features=features, vocab=vocab),
        grid=(sources,),
        in_specs=[
            pl.BlockSpec((1, 1, tokens), lambda s: (s, 0, 0), memory_space=pltpu.SMEM),
            pl.BlockSpec((1, 1, tokens), lambda s: (s, 0, 0)),
            pl.BlockSpec((1, features, tokens), lambda s: (s, 0, 0)),
        ],
        out_specs=[
            pl.BlockSpec((features, vocab), lambda s: (0, 0)),
            pl.BlockSpec((8, LANES), lambda s: (0, 0)),
        ],
        out_shape=[
            jax.ShapeDtypeStruct((features, vocab), low),
            jax.ShapeDtypeStruct((8, LANES), full),
        ],
        scratch_shapes=[pltpu.VMEM((span, LANES), full)] * 8 + [pltpu.VMEM((tokens, LANES), full)],
        compiler_params=params(56),
        cost_estimate=cost(150),
        name="collect",
    )((ids % span)[:, None, :], ids[:, None, :], grads)


def moment_kernel(info_ref, factor_ref, grad_ref, old_ref, moment_ref, mine_ref, other_ref,
                  *, piece, block):
    factor = factor_ref[0]
    for at in range(old_ref.shape[0] // piece):
        source = pl.multiple_of(info_ref[2 + at] * piece, piece)
        rows = slice(at * piece, (at + 1) * piece)
        moment_ref[rows] = muon_beta * old_ref[rows] + factor * grad_ref[pl.ds(source, piece)].astype(full)

    def grams(out_ref, start, stop):
        out_ref[...] = jnp.zeros_like(out_ref)

        def body(b, carry):
            high, small = halves(moment_ref[pl.ds(pl.multiple_of(b * block, block), block)])
            for at, (i, j) in enumerate(TILES):
                left, right = slice(i * BLOCK, (i + 1) * BLOCK), slice(j * BLOCK, (j + 1) * BLOCK)
                out_ref[at] += dot32(
                    jnp.concatenate([high[:, left], high[:, left], small[:, left]], axis=0),
                    jnp.concatenate([high[:, right], small[:, right], high[:, right]], axis=0),
                    0,
                    0,
                )
            return carry

        lax.fori_loop(start, stop, body, 0)

    lead, total = info_ref[0] // block, old_ref.shape[0] // block
    swap = info_ref[1] == 1
    grams(mine_ref, jnp.where(swap, lead, 0), jnp.where(swap, total, lead))
    grams(other_ref, jnp.where(swap, 0, lead), jnp.where(swap, lead, total))


def moment_and_grams(info, factor, grad, old, piece, block):
    tiles = jax.ShapeDtypeStruct((len(TILES), BLOCK, BLOCK), full)
    return pl.pallas_call(
        partial(moment_kernel, piece=piece, block=block),
        in_specs=[smem(), smem(), vmem(), vmem()],
        out_specs=[vmem()] * 3,
        out_shape=[jax.ShapeDtypeStruct(old.shape, full), tiles, tiles],
        compiler_params=params(48),
        cost_estimate=cost(10),
        name="moment",
    )(info, factor, grad, old)


def even_product(left, right, put):
    (lh, ll), (rh, rl) = left, right
    for i in range(D // BLOCK):
        rows = slice(i * BLOCK, (i + 1) * BLOCK)
        panel = jnp.concatenate([lh[rows], lh[rows], ll[rows]], axis=1)
        for j in range(i, D // BLOCK):
            cols = slice(j * BLOCK, (j + 1) * BLOCK)
            other = jnp.concatenate([rh[:, cols], rl[:, cols], rh[:, cols]], axis=0)
            put(rows, cols, dot32(panel, other, 1, 0))


def keep(pair):
    def put(rows, cols, value):
        pair[0][rows, cols], pair[1][rows, cols] = halves(value)
        if rows != cols:
            pair[0][cols, rows], pair[1][cols, rows] = halves(value.T)

    return put


def chain_kernel(kind_ref, factor_ref, debias_ref, chip_ref, other_ref, kept_ref, got_ref,
                 grad_ref, weight_ref, first_ref, second_ref,
                 out_ref, weight_new_ref, first_new_ref, second_new_ref, copy_ref,
                 a_ref, scale_ref, *parts, chunks):
    a, q, p, t = [parts[2 * i:2 * i + 2] for i in range(4)]
    step = pl.program_id(0)
    shape = (BLOCK, BLOCK)
    once = lax.broadcasted_iota(jnp.int32, shape, 0) == lax.broadcasted_iota(jnp.int32, shape, 1)

    def put_q(rows, cols, value):
        new = 2.0315 * value - 4.775 * a_ref[rows, cols]
        keep(q)(rows, cols, new + jnp.where(once, 3.4445, 0.0) if rows == cols else new)

    def put_a(rows, cols, value):
        a_ref[rows, cols] = value
        keep(a)(rows, cols, value)

    def put_out(rows, cols, value):
        value = value * (1.0 / scale_ref[0])
        out_ref[rows, cols] = value
        if rows != cols:
            out_ref[cols, rows] = value.T

    @pl.when(step == 0)
    def _():
        half = len(TILES) // 2
        lower = kind_ref[1] == 1
        trace = 0.0
        for at, (i, j) in enumerate(TILES):
            side = kept_ref[at % half], got_ref[at % half]
            near, far = side if at < half else side[::-1]
            tile = jnp.where(lower, near, far)
            tile = jnp.where(kind_ref[0] == 0, chip_ref[at], tile)
            tile = jnp.where(kind_ref[0] == 1, other_ref[at], tile)
            a_ref[i * BLOCK:(i + 1) * BLOCK, j * BLOCK:(j + 1) * BLOCK] = tile
            if i == j:
                trace = trace + jnp.sum(jnp.where(once, tile, 0.0))
        scale = jnp.sqrt(trace) + 1e-07
        scale_ref[0] = scale
        for i, j in TILES:
            rows, cols = slice(i * BLOCK, (i + 1) * BLOCK), slice(j * BLOCK, (j + 1) * BLOCK)
            put_a(rows, cols, a_ref[rows, cols] * (1.0 / (scale * scale)))

    turn = lax.rem(step + 1, 4)
    last = 4 * NS_TURNS - 4

    @pl.when((step == 0) | (turn == 0))
    def _():
        even_product(a, a, put_q)

    @pl.when(step == 0)
    def _():
        p[0][...], p[1][...] = q[0][...], q[1][...]

    @pl.when((turn == 1) & (step > 0) & (step < last))
    def _():
        even_product(p, q, keep(t))
        p[0][...], p[1][...] = t[0][...], t[1][...]

    @pl.when(step == last)
    def _():
        even_product(p, q, put_out)

    @pl.when(turn == 2)
    def _():
        even_product(a, q, keep(t))

    @pl.when(turn == 3)
    def _():
        even_product(t, q, put_a)

    @pl.when(step < chunks)
    def _():
        grad = factor_ref[0] * grad_ref[...].astype(full)
        weight = weight_ref[...]
        first = beta_one * first_ref[...] + (1.0 - beta_one) * grad
        second = beta_two * second_ref[...] + (1.0 - beta_two) * grad * grad
        move = (first * debias_ref[0]) / (jnp.sqrt(second * debias_ref[1]) + adam_eps)
        new = weight - 0.02 * (move + adam_decay * weight)
        weight_new_ref[...] = new
        first_new_ref[...] = first
        second_new_ref[...] = second
        copy_ref[...] = new.astype(low)


def chain(kind, factor, debias, grams, table):
    steps = 4 * NS_TURNS - 3
    features, vocab = table[1].shape
    width = -(-vocab // ((steps - 1) * LANES)) * LANES
    chunks = -(-vocab // width)
    part = pl.BlockSpec((features, width), lambda g: (0, jnp.minimum(g, chunks - 1)))
    whole = jax.ShapeDtypeStruct((features, vocab), full)
    return pl.pallas_call(
        partial(chain_kernel, chunks=chunks),
        grid=(steps,),
        in_specs=[smem(), smem(), smem()] + [vmem()] * 4 + [part] * 4,
        out_specs=[pl.BlockSpec((D, D), lambda g: (0, 0))] + [part] * 4,
        out_shape=[
            jax.ShapeDtypeStruct((D, D), full),
            whole,
            whole,
            whole,
            jax.ShapeDtypeStruct((features, vocab), low),
        ],
        scratch_shapes=[pltpu.VMEM((D, D), full), pltpu.SMEM((1,), full)]
        + [pltpu.VMEM((D, D), low)] * 8,
        compiler_params=params(56),
        cost_estimate=cost(48),
        name="chain",
    )(kind, factor, debias, *grams, *table)


def apply_kernel(info_ref, gain_ref, own_ref, come_ref, moment_ref, master_ref, new_ref, copy_ref,
                 *, block):
    lead, total = info_ref[0] // block, moment_ref.shape[0] // block
    late = info_ref[2]

    def over(p_ref, start, stop, slot):
        p = halves(p_ref[...])
        gain = gain_ref[slot] * muon_rate

        def body(b, carry):
            rows = pl.ds(pl.multiple_of(b * block, block), block)
            ortho = dot_split(halves(moment_ref[rows]), p)
            new = master_ref[rows] * (1.0 - muon_rate * muon_decay) - gain * ortho
            new_ref[rows] = new
            copy_ref[rows] = new.astype(low)
            return carry

        lax.fori_loop(start, stop, body, 0)

    over(own_ref, jnp.where(late == 1, lead, 0), jnp.where(late == 1, total, lead), late)

    @pl.when(lead < total)
    def _():
        over(come_ref, jnp.where(late == 1, 0, lead), jnp.where(late == 1, lead, total), 1 - late)


def apply_chain(info, gains, own, come, moment, master, block):
    return pl.pallas_call(
        partial(apply_kernel, block=block),
        in_specs=[smem(), smem(), vmem(), vmem(), vmem(), vmem()],
        out_specs=[vmem(), vmem()],
        out_shape=[
            jax.ShapeDtypeStruct(moment.shape, full),
            jax.ShapeDtypeStruct(moment.shape, low),
        ],
        compiler_params=params(48),
        cost_estimate=cost(10),
        name="apply",
    )(info, gains, own, come, moment, master)


def chains(mine, other, wide_at, first_matrix, second_matrix, factor, debias, table, rider):
    wide = lax.axis_size("wide")
    if wide != 8:
        which = jnp.arange(4)
        slots = (which == first_matrix).astype(full)[:, None, None, None] * mine
        slots = slots + (which == second_matrix).astype(full)[:, None, None, None] * other
        total = lax.psum(slots, "wide")
        kind = jnp.zeros((2,), jnp.int32)
        outs = []
        for matrix in (first_matrix, second_matrix):
            gram = lax.dynamic_index_in_dim(total, matrix, 0, keepdims=False)
            half = gram[: len(TILES) // 2]
            outs.append(chain(kind, factor, debias, (gram, gram, half, half), table))
        return outs[0][0], outs[1][0], outs[0][1:], rider
    half = len(TILES) // 2
    pairs = [(i, i ^ 1) for i in range(8)]
    lower = wide_at % 2 == 0
    moved = lax.ppermute(other[:half], "wide", [(5, 4)])
    chip = mine + lax.ppermute(mine, "wide", pairs)
    up_send = jnp.where(lower, chip[:half], chip[half:])
    down_send = jnp.where(wide_at == 4, moved, jnp.where(wide_at == 5, other[half:], up_send))
    up = up_send + lax.ppermute(up_send, "wide", [(2, 4), (4, 2), (3, 5), (5, 3)])
    down = down_send + lax.ppermute(down_send, "wide", [(4, 6), (6, 4), (5, 7), (7, 5)])
    send = jnp.where((wide_at == 4) | (wide_at >= 6), down, up)
    swap = lax.ppermute(send, "wide", [(2, 3), (4, 5), (6, 7), (7, 6)])
    back = lax.ppermute(up, "wide", [(5, 4)])
    kept = jnp.where(wide_at >= 5, down, up)
    got = jnp.where(wide_at == 4, back, swap)
    kind = jnp.where(wide_at < 2, 0, jnp.where(wide_at == 2, 1, 2))
    kind = jnp.stack([kind, lower.astype(jnp.int32)]).astype(jnp.int32)
    got, rider = lax.optimization_barrier((got, rider))
    own, *table_new = chain(kind, factor, debias, (chip, other, kept, got), table)
    come = lax.ppermute(own, "wide", [(3, 2), (4, 5)])
    return own, come, table_new, rider


def scale_rows(hidden):
    center = hidden - jnp.mean(hidden, axis=-1, keepdims=True)
    inverse = lax.rsqrt(jnp.mean(center * center, axis=-1, keepdims=True) + norm_eps)
    return center * inverse, inverse


def unscale_rows(upstream, scaled, inverse, gain):
    weighted = upstream * gain
    return inverse * (
        weighted
        - jnp.mean(weighted, axis=-1, keepdims=True)
        - scaled * jnp.mean(weighted * scaled, axis=-1, keepdims=True)
    )


def forward_kernel(context_ref, normed0_ref, share_ref, vectors_ref, bias_ref, out_w_ref, up_w_ref, down_w_ref,
                   scaled1_ref, inverse1_ref, input1_ref, active_ref, slope_ref,
                   scaled2_ref, inverse2_ref, pooled_ref, normed1_ref, sum_ref):
    step = pl.program_id(0)

    @pl.when(step == 0)
    def _():
        attended = dot32(context_ref[...], out_w_ref[...], 1, 1) + vectors_ref[8:9]
        scaled, inverse = scale_rows(normed0_ref[...] + attended)
        scaled1_ref[...], inverse1_ref[...] = scaled, inverse
        normed1_ref[...] = scaled * vectors_ref[2:3] + vectors_ref[3:4]
        input1_ref[...] = normed1_ref[...].astype(low)
        sum_ref[...] = normed1_ref[...] + vectors_ref[9:10]

    inner = dot32(input1_ref[...], up_w_ref[...], 1, 1) + bias_ref[...]
    cdf = 0.5 * (1.0 + lax.erf(inner * math.sqrt(0.5)))
    active = (inner * cdf).astype(low)
    active_ref[...] = active
    slope_ref[...] = cdf + inner * (jnp.exp(-0.5 * inner * inner) * (1.0 / math.sqrt(2.0 * math.pi)))
    sum_ref[...] += dot32(active, down_w_ref[...], 1, 0)

    @pl.when(step == pl.num_programs(0) - 1)
    def _():
        scaled, inverse = scale_rows(sum_ref[...])
        scaled2_ref[...], inverse2_ref[...] = scaled, inverse
        normed2 = scaled * vectors_ref[4:5] + vectors_ref[5:6]
        pooled_ref[...] = jnp.dot(share_ref[...], normed2, precision=highest)


CHUNK = 512


def same(shape):
    return pl.BlockSpec(shape, lambda c: (0,) * len(shape))


def forward_rest(context, normed0, share, vectors, out_w, up_w, down_w):
    tokens = context.shape[0]
    pairs = share.shape[0]
    wide_rows = jax.ShapeDtypeStruct((tokens, D), full)
    column = jax.ShapeDtypeStruct((tokens, 1), full)
    return pl.pallas_call(
        forward_kernel,
        grid=(FF // CHUNK,),
        in_specs=[
            same((tokens, D)),
            same((tokens, D)),
            same((pairs, tokens)),
            same(vectors.shape),
            pl.BlockSpec((1, CHUNK), lambda c: (0, c)),
            same((D, D)),
            pl.BlockSpec((CHUNK, D), lambda c: (c, 0)),
            pl.BlockSpec((CHUNK, D), lambda c: (c, 0)),
        ],
        out_specs=[
            same((tokens, D)),
            same((tokens, 1)),
            same((tokens, D)),
            pl.BlockSpec((tokens, CHUNK), lambda c: (0, c)),
            pl.BlockSpec((tokens, CHUNK), lambda c: (0, c)),
            same((tokens, D)),
            same((tokens, 1)),
            same((pairs, D)),
        ],
        out_shape=[
            wide_rows,
            column,
            jax.ShapeDtypeStruct((tokens, D), low),
            jax.ShapeDtypeStruct((tokens, FF), low),
            jax.ShapeDtypeStruct((tokens, FF), full),
            wide_rows,
            column,
            jax.ShapeDtypeStruct((pairs, D), full),
        ],
        scratch_shapes=[pltpu.VMEM((tokens, D), full)] * 2,
        compiler_params=params(58),
        cost_estimate=cost(25),
        name="forward_rest",
    )(context, normed0, share, vectors, vectors[14:].reshape(1, -1), out_w, up_w, down_w)


def backward_kernel(side_ref, pooled_ref, share_ref, vectors_ref, scaled2_ref, inverse2_ref, active_ref, slope_ref,
                    input1_ref, scaled1_ref, inverse1_ref, context_ref, out_w_ref, up_w_ref, down_w_ref,
                    down_stays_ref, down_leaves_ref, up_stays_ref, up_leaves_ref, out_grad_ref, sum1_ref, context_grad_ref, sums_ref, up_sums_ref,
                    branch_ref, total_ref):
    step = pl.program_id(0)

    def over_tokens(x):
        return jnp.sum(x, axis=0, keepdims=True)

    @pl.when(step == 0)
    def _():
        spread = lax.dot_general(
            share_ref[...], pooled_ref[...], dims(0, 0), precision=highest, preferred_element_type=full
        )
        scaled = scaled2_ref[...]
        back = unscale_rows(spread, scaled, inverse2_ref[...], vectors_ref[4:5])
        total_ref[...] = back
        branch = back.astype(low)
        branch_ref[...] = branch
        sums_ref[2:3] = over_tokens(spread * scaled)
        sums_ref[3:4] = over_tokens(spread)
        sums_ref[5:6] = over_tokens(branch.astype(full))

    branch = branch_ref[...]
    inner_grad = (dot32(branch, down_w_ref[...], 1, 1) * slope_ref[...]).astype(low)

    def halve(grad, stays_ref, leaves_ref):
        left, right = grad[:, : D // 2], grad[:, D // 2 :]
        stays_ref[...] = jnp.where(side_ref[0] == 0, left, right).astype(low)
        leaves_ref[...] = jnp.where(side_ref[0] == 0, right, left).astype(low)

    halve(dot32(active_ref[...], branch, 0, 0), down_stays_ref, down_leaves_ref)
    halve(dot32(inner_grad, input1_ref[...], 0, 0), up_stays_ref, up_leaves_ref)
    up_sums_ref[...] = over_tokens(inner_grad.astype(full))
    total_ref[...] += dot32(inner_grad, up_w_ref[...], 1, 0)

    @pl.when(step == pl.num_programs(0) - 1)
    def _():
        upstream = total_ref[...]
        scaled = scaled1_ref[...]
        back = unscale_rows(upstream, scaled, inverse1_ref[...], vectors_ref[2:3])
        sum1_ref[...] = back
        attended = back.astype(low)
        sums_ref[0:1] = over_tokens(upstream * scaled)
        sums_ref[1:2] = over_tokens(upstream)
        sums_ref[4:5] = over_tokens(attended.astype(full))
        out_grad_ref[...] = dot32(attended, context_ref[...], 0, 0).astype(low)
        context_grad_ref[...] = dot32(attended, out_w_ref[...], 1, 0).astype(low)


def backward_rest(side, pooled_grads, share, vectors, kept, context, out_w, up_w, down_w):
    scaled1, inverse1, input1, active, slope, scaled2, inverse2 = kept
    tokens = context.shape[0]
    pairs = share.shape[0]
    rows = pl.BlockSpec((CHUNK, D), lambda c: (c, 0))
    cols = pl.BlockSpec((tokens, CHUNK), lambda c: (0, c))
    return pl.pallas_call(
        backward_kernel,
        grid=(FF // CHUNK,),
        in_specs=[
            smem(),
            same((pairs, D)),
            same((pairs, tokens)),
            same(vectors.shape),
            same((tokens, D)),
            same((tokens, 1)),
            cols,
            cols,
            same((tokens, D)),
            same((tokens, D)),
            same((tokens, 1)),
            same((tokens, D)),
            same((D, D)),
            rows,
            rows,
        ],
        out_specs=[pl.BlockSpec((CHUNK, D // 2), lambda c: (c, 0))] * 4
        + [
            same((D, D)),
            same((tokens, D)),
            same((tokens, D)),
            same((8, D)),
            pl.BlockSpec((1, CHUNK), lambda c: (0, c)),
        ],
        out_shape=[jax.ShapeDtypeStruct((FF, D // 2), low)] * 4
        + [
            jax.ShapeDtypeStruct((D, D), low),
            jax.ShapeDtypeStruct((tokens, D), full),
            jax.ShapeDtypeStruct((tokens, D), low),
            jax.ShapeDtypeStruct((8, D), full),
            jax.ShapeDtypeStruct((1, FF), full),
        ],
        scratch_shapes=[pltpu.VMEM((tokens, D), low), pltpu.VMEM((tokens, D), full)],
        compiler_params=params(58),
        cost_estimate=cost(35),
        name="backward_rest",
    )(side, pooled_grads, share, vectors, scaled2, inverse2, active, slope, input1, scaled1, inverse1, context,
      out_w, up_w, down_w)


def front_kernel(side_ref, mixed_ref, input_ref, out_grad_ref, stays_ref, leaves_ref):
    def halve(grad):
        left, right = grad[:, : D // 2], grad[:, D // 2 :]
        stays_ref[...] = jnp.where(side_ref[0] == 0, left, right).astype(low)
        leaves_ref[...] = jnp.where(side_ref[0] == 0, right, left).astype(low)

    @pl.when(pl.program_id(0) < 3)
    def _():
        halve(dot32(mixed_ref[...], input_ref[...], 0, 0))

    @pl.when(pl.program_id(0) == 3)
    def _():
        halve(out_grad_ref[...].astype(full))


def front_grads(side, mixed_grad, input0, out_grad):
    tokens = mixed_grad.shape[0]
    return pl.pallas_call(
        front_kernel,
        grid=(4,),
        in_specs=[
            smem(),
            pl.BlockSpec((tokens, D), lambda c: (0, jnp.minimum(c, 2))),
            same((tokens, D)),
            same((D, D)),
        ],
        out_specs=[pl.BlockSpec((D, D // 2), lambda c: (c, 0))] * 2,
        out_shape=[jax.ShapeDtypeStruct((4 * D, D // 2), low)] * 2,
        compiler_params=params(40),
        cost_estimate=cost(7),
        name="front_grads",
    )(side, mixed_grad, input0, out_grad)


def embed_back_kernel(mixed_ref, sum1_ref, scaled_ref, inverse_ref, vectors_ref, weight_ref,
                      embed_ref, send_ref, sums_ref, mixed_sum_ref, *, narrow, wide):
    upstream = sum1_ref[...] + dot32(mixed_ref[...], weight_ref[...], 1, 0)
    scaled = scaled_ref[...]
    back = unscale_rows(upstream, scaled, inverse_ref[...], vectors_ref[0:1])
    embed_ref[...] = back
    turned = back.T.astype(low)
    features = send_ref.shape[1]
    for n in range(narrow):
        for w in range(wide):
            start = (w * narrow + n) * features
            send_ref[n * wide + w] = turned[start:start + features]

    @pl.when(pl.program_id(0) == 0)
    def _():
        sums_ref[...] = jnp.zeros_like(sums_ref)
        mixed_sum_ref[...] = jnp.zeros_like(mixed_sum_ref)

    sums_ref[0:1] += jnp.sum(upstream * scaled, axis=0, keepdims=True)
    sums_ref[1:2] += jnp.sum(upstream, axis=0, keepdims=True)
    mixed_sum_ref[...] += jnp.sum(mixed_ref[...].astype(full), axis=0, keepdims=True)


def embed_back(mixed_grad, sum1_grad, scaled0, inverse0, vectors, weight, narrow, wide):
    tokens = mixed_grad.shape[0]
    count = narrow * wide
    block = pl.BlockSpec((SEQ, D), lambda b: (b, 0))
    return pl.pallas_call(
        partial(embed_back_kernel, narrow=narrow, wide=wide),
        grid=(tokens // SEQ,),
        in_specs=[
            pl.BlockSpec((SEQ, 3 * D), lambda b: (b, 0)),
            block,
            block,
            pl.BlockSpec((SEQ, 1), lambda b: (b, 0)),
            same(vectors.shape),
            same((3 * D, D)),
        ],
        out_specs=[
            block,
            pl.BlockSpec((count, D // count, SEQ), lambda b: (0, 0, b)),
            same((8, D)),
            same((1, 3 * D)),
        ],
        out_shape=[
            jax.ShapeDtypeStruct((tokens, D), full),
            jax.ShapeDtypeStruct((count, D // count, tokens), low),
            jax.ShapeDtypeStruct((8, D), full),
            jax.ShapeDtypeStruct((1, 3 * D), full),
        ],
        compiler_params=params(48),
        cost_estimate=cost(10),
        name="embed_back",
    )(mixed_grad, sum1_grad, scaled0, inverse0, vectors, weight)


def layout(lengths):
    row_ends = jnp.cumsum(lengths)
    starts = row_ends - lengths
    places = jnp.arange(SEQ, dtype=jnp.int32)
    segment = jnp.sum((places[:, None] >= row_ends[None, :]).astype(jnp.int32), axis=1)
    chosen = segment[:, None] == jnp.arange(SLOTS, dtype=jnp.int32)[None, :]
    start_at = jnp.sum(jnp.where(chosen, starts[None, :], 0), axis=1)
    length_at = jnp.sum(jnp.where(chosen, lengths[None, :], 0), axis=1)
    position = places - start_at
    second = (2 * position >= length_at).astype(jnp.int32)
    return (chosen.astype(full), position, second, segment)


def norm_forward(hidden, gain, bias):
    center = hidden - jnp.mean(hidden, axis=-1, keepdims=True)
    inverse = lax.rsqrt(jnp.mean(center * center, axis=-1, keepdims=True) + norm_eps)
    scaled = center * inverse
    return (scaled * gain + bias, scaled, inverse)


def norm_backward(upstream, scaled, inverse, gain):
    weighted = upstream * gain
    back = inverse * (
        weighted
        - jnp.mean(weighted, axis=-1, keepdims=True)
        - scaled * jnp.mean(weighted * scaled, axis=-1, keepdims=True)
    )
    return (back, jnp.sum(upstream * scaled, axis=0), jnp.sum(upstream, axis=0))


def project(left, right):
    return jnp.dot(left, right, preferred_element_type=full)


def task_loss(logits, scores, tasks, labels, negatives, counts):
    logprob = jax.nn.log_softmax(logits, axis=-1)
    picked = jnp.sum(
        jnp.where(labels[:, :, None] == jnp.arange(3, dtype=jnp.int32), logprob, 0.0), axis=2
    )
    chosen = negatives[:, :, :, None] == jnp.arange(scores.shape[1], dtype=jnp.int32)
    rivals = jnp.sum(jnp.where(chosen, scores[:, None, None, :], 0.0), axis=3)
    together = jnp.concatenate([scores[:, :, None], rivals], axis=2)
    ranking = jax.nn.logsumexp(together, axis=2) - scores
    first_part = jnp.sum(jnp.where(tasks == 0, -picked, 0.0)) / counts[0]
    return first_part + jnp.sum(jnp.where(tasks == 1, ranking, 0.0)) / counts[1]


def adam(weight, grad, first, second, step, rate):
    first = beta_one * first + (1.0 - beta_one) * grad
    second = beta_two * second + (1.0 - beta_two) * grad * grad
    unbiased = first / (1.0 - beta_one**step)
    spread = second / (1.0 - beta_two**step)
    return (
        weight - rate * (unbiased / (jnp.sqrt(spread) + adam_eps) + adam_decay * weight),
        first,
        second,
    )


def broadcast_all(x):
    count = lax.axis_size("narrow") * lax.axis_size("wide")
    return lax.all_to_all(
        jnp.broadcast_to(x[None], (count,) + x.shape), BOTH, split_axis=0, concat_axis=0, tiled=True
    )


def sides(wide):
    return [list(range(0, wide, 2)), list(range(1, wide, 2))]


def chip_mates(wide):
    return [(i, i ^ 1) for i in range(wide)]


def gather_weights(master, narrow_at, wide_at, first):
    wide = lax.axis_size("wide")
    if wide != 8:
        whole = lax.all_gather(master.astype(low), "wide", axis=0, tiled=True)
        return first, list(whole.reshape(wide, -1, D))
    share = master.shape[0] // lax.axis_size("narrow")
    mine = lax.dynamic_slice_in_dim(master, narrow_at * share, share, 0).astype(low)
    turns = range(wide // 2)
    near = jnp.stack(
        [mine]
        + [
            lax.ppermute(mine, "wide", [(i, i ^ (2 * turn)) for i in range(wide)])
            for turn in turns[1:]
        ]
    )
    near = [near[(wide_at // 2) ^ turn] for turn in turns]
    near, first = lax.optimization_barrier((near, first))
    return first, [
        lax.all_gather(jnp.stack(part), "narrow", axis=1, tiled=True)
        for part in (near[: wide // 4], near[wide // 4 :])
    ]


def both_cores(held, wide_at):
    owners = []
    other = lax.ppermute(held, "wide", chip_mates(lax.axis_size("wide")))
    side = wide_at % 2
    even = jnp.where(side == 0, held, other)
    odd = jnp.where(side == 0, other, held)
    for at in range(held.shape[0]):
        owners += [even[at], odd[at]]
    return owners


def rows_of(owners, matrix):
    rows = owners[0].shape[0]
    lo, hi = BOUNDS[matrix], BOUNDS[matrix + 1]
    pieces = []
    for at in range(lo // rows, -(-hi // rows)):
        pieces.append(owners[at][max(lo - at * rows, 0) : min(hi - at * rows, rows)])
    return jnp.concatenate(pieces) if len(pieces) > 1 else pieces[0]


def shards(
    token_ids,
    seq_lengths,
    task_ids,
    labels,
    negatives,
    step_count,
    hidden_master,
    hidden_momentum,
    table_master,
    table_first,
    table_second,
    pos_types,
    pos_first,
    pos_second,
    vectors,
    vec_first,
    vec_second,
):
    wide_at = lax.axis_index("wide")
    narrow_at = lax.axis_index("narrow")
    wide = lax.axis_size("wide")
    narrow = lax.axis_size("narrow")
    count = wide * narrow
    device_at = narrow_at * wide + wide_at
    micro_count, rows_each = token_ids.shape[:2]
    batch = micro_count * rows_each
    tokens = batch * SEQ
    shard = hidden_master.shape[0]
    vocab = table_master.shape[1]
    features = table_master.shape[0] // narrow
    pairs_each = rows_each * SLOTS

    parts = [token_ids, task_ids, labels, negatives]
    sizes = [part.size for part in parts]
    packed = jnp.concatenate([part.reshape(-1) for part in parts])
    packed = jnp.pad(packed, (0, -packed.size % LANES))
    gathered = broadcast_all(packed)
    ends = [sum(sizes[: i + 1]) for i in range(len(sizes))]
    ids_all = gathered[:, : ends[0]]

    def pairs_of(lo, hi, tail):
        block = gathered[:, lo:hi].reshape((count, micro_count, pairs_each) + tail)
        return jnp.moveaxis(block, 1, 0).reshape((micro_count, count * pairs_each) + tail)

    tasks_all = pairs_of(ends[0], ends[1], ())
    labels_all = pairs_of(ends[1], ends[2], ())
    negatives_all = pairs_of(ends[2], ends[3], (NEG,))
    counts = jnp.stack(
        [jnp.sum((tasks_all == 0).astype(full)), jnp.sum((tasks_all == 1).astype(full))]
    )


    group_ids = lax.dynamic_slice_in_dim(ids_all, narrow_at * wide, wide, 0).reshape(-1)
    group_ids, gathers = gather_weights(hidden_master, narrow_at, wide_at, group_ids)
    pieces = lookup(group_ids, table_master)
    simple = wide != 8
    arrived = lax.all_to_all(
        pieces.reshape(wide, tokens, -1), "wide", split_axis=0, concat_axis=0, tiled=True
    )
    token_rows = jnp.moveaxis(arrived, 0, 1).reshape(tokens, D)

    lengths = seq_lengths.reshape(batch, SLOTS)
    member, position, second, segment = jax.vmap(layout)(lengths)
    flat_position = position.reshape(-1)
    flat_second = second.reshape(-1)
    place_rows = pos_types[flat_position]
    place_rows = place_rows + jnp.where(flat_second[:, None] == 1, pos_types[SEQ + 1], pos_types[SEQ])
    if simple:
        owners = gathers
    else:
        place_rows, held = lax.optimization_barrier((place_rows, gathers[0]))
        owners = both_cores(held, wide_at)
    embed = token_rows.astype(full) + place_rows
    normed0, scaled0, inverse0 = norm_forward(embed, vectors[0], vectors[1])
    input0 = normed0.astype(low)
    qkv_bias = jnp.concatenate([vectors[6], jnp.zeros_like(vectors[6]), vectors[7]])
    weight_qkv, weight_out = rows_of(owners, 0), rows_of(owners, 1)
    mixed = (project(input0, weight_qkv.T) + qkv_bias).astype(low)
    context_low, logsum = attend(mixed, segment)
    if not simple:
        rest, context_low = lax.optimization_barrier((gathers[1], context_low))
        owners = owners + both_cores(rest, wide_at)
    weight_up, weight_down = rows_of(owners, 2), rows_of(owners, 3)
    pair_at = (jnp.arange(batch, dtype=jnp.int32)[:, None] * SLOTS + segment).reshape(1, -1)
    pairs = jnp.arange(batch * SLOTS, dtype=jnp.int32)[:, None]
    share = jnp.where(pair_at == pairs, 1.0 / lengths.astype(full).reshape(-1, 1), 0.0)
    scaled1, inverse1, input1, active, slope, scaled2, inverse2, flat_pooled = forward_rest(
        context_low, normed0, share, vectors, weight_out, weight_up, weight_down
    )
    heads = vectors[10:14]
    head_out = jnp.dot(flat_pooled, heads.T, precision=highest)

    sent = jnp.pad(head_out.reshape(-1), (0, -head_out.size % LANES))
    head_all = broadcast_all(sent)[:, : head_out.size]
    head_all = head_all.reshape(count, micro_count, pairs_each, 4)
    head_all = jnp.moveaxis(head_all, 1, 0).reshape(micro_count, count * pairs_each, 4)

    def objective(every):
        return task_loss(every[:, :, :3], every[:, :, 3], tasks_all, labels_all, negatives_all, counts)

    loss, pullback = jax.vjp(objective, head_all)
    head_grads = pullback(jnp.ones_like(loss))[0]
    output_grads = lax.dynamic_slice_in_dim(head_grads, device_at * pairs_each, pairs_each, 1)
    output_grads = output_grads.reshape(-1, 4)
    heads_grad = jnp.dot(output_grads.T, flat_pooled, precision=highest)
    pooled_grads = jnp.dot(output_grads, heads, precision=highest)

    spans_down = [(0, 768), (768, 1920), (1920, 3072)]
    spans_up = [(0, 384), (384, 1536), (1536, 2688), (2688, 3072)]
    spans_front = [(0, 1152), (1152, 2304), (2304, 3072)]

    side = wide_at % 2

    def between_cores(grad):
        stays, leaves = grad
        if simple:
            return stays, leaves
        return stays, lax.ppermute(leaves, "wide", chip_mates(wide))

    def slices(grad, spans):
        stays, comes = grad
        if simple:
            return [jnp.concatenate([stays, comes], axis=1)]
        chip = (stays.astype(full) + comes.astype(full)).astype(low)
        parts = []
        for turn in range(narrow):
            pieces = []
            for lo, hi in spans:
                share_rows = (hi - lo) // narrow
                start = lo + (narrow_at ^ turn) * share_rows
                pieces.append(lax.dynamic_slice_in_dim(chip, start, share_rows, 0))
            parts.append(jnp.concatenate(pieces))
        return parts

    def over_narrow(parts):
        return parts[:1] + [
            lax.ppermute(part, "narrow", [(i, i ^ (turn + 1)) for i in range(narrow)])
            for turn, part in enumerate(parts[1:])
        ]

    together = lax.optimization_barrier
    kept = (scaled1, inverse1, input1, active, slope, scaled2, inverse2)
    *sides_of, out_grad, sum1_grad, context_grad, sums, up_sums = backward_rest(
        side[None] if not simple else jnp.zeros((1,), jnp.int32),
        pooled_grads, share, vectors, kept, context_low, weight_out, weight_up, weight_down
    )
    down_pair = between_cores(sides_of[:2])
    up_pair = between_cores(sides_of[2:])
    down_cut, up_pair, context_grad = together((slices(down_pair, spans_down), up_pair, context_grad))
    down_part = over_narrow(down_cut)
    up_cut, context_grad = together((slices(up_pair, spans_up), context_grad))
    up_part = over_narrow(up_cut)
    mixed_grad = attend_back(mixed, context_grad, logsum, segment)
    mixed_grad, down_part = together((mixed_grad, down_part))
    if simple:
        normed0_grad = sum1_grad + project(mixed_grad, weight_qkv)
        embed_grad, gain0, bias0 = norm_backward(normed0_grad, scaled0, inverse0, vectors[0])
        table_send = embed_grad.astype(low).T.reshape(wide, narrow, features, tokens)
        table_send = jnp.moveaxis(table_send, 1, 0).reshape(count, features, tokens)
        mixed_sum = jnp.sum(mixed_grad.astype(full), axis=0)
    else:
        embed_grad, table_send, first_sums, mixed_sum = embed_back(
            mixed_grad, sum1_grad, scaled0, inverse0, vectors, weight_qkv, narrow, wide
        )
        gain0, bias0, mixed_sum = first_sums[0], first_sums[1], mixed_sum[0]
    table_send, mixed_grad = together((table_send, mixed_grad))
    come = lax.all_to_all(table_send, BOTH, split_axis=0, concat_axis=0, tiled=True)

    if simple:
        front_grad = jnp.concatenate([project(mixed_grad.T, input0).astype(low), out_grad])
        front_halves = (front_grad[:, : D // 2], front_grad[:, D // 2 :])
    else:
        front_halves = tuple(front_grads(side[None], mixed_grad, input0, out_grad))
    front_send, embed_grad, mixed_grad, up_part = together(
        (front_halves, embed_grad, mixed_grad, up_part)
    )
    front_part = over_narrow(slices(between_cores(front_send), spans_front))
    small_rows = jnp.concatenate(
        [
            jnp.stack([gain0, bias0]),
            sums[:4],
            jnp.stack([mixed_sum[:D], mixed_sum[2 * D :]]),
            sums[4:6],
        ]
    )
    up_rows = up_sums.reshape(-1, D)

    places = jnp.arange(SEQ, dtype=jnp.int32)[:, None]
    row_hot = jnp.concatenate(
        [
            flat_position[None] == places,
            jnp.stack([flat_second == 0, flat_second == 1]),
        ]
    ).astype(low)
    high_part, low_part = halves(embed_grad)
    pos_grad = project(jnp.concatenate([row_hot, row_hot], axis=1), jnp.concatenate([high_part, low_part]))
    small = jnp.concatenate([pos_grad, small_rows, heads_grad, up_rows])
    small_count = small.shape[0]
    small = jnp.pad(small, ((0, count * features - small_count), (0, 0)))

    def added(parts):
        return sum(part.astype(full) for part in parts).astype(low)

    joined = jnp.concatenate([added(front_part), added(up_part), added(down_part)])
    small_send = small.astype(low).reshape(count, features, D)
    come, small_send = together((come, small_send))
    small_come = lax.all_to_all(small_send, BOTH, split_axis=0, concat_axis=0, tiled=True)
    table_part, table_square = collect(ids_all, come, vocab, tokens)
    if simple:
        hidden_part = lax.psum_scatter(joined, "wide", scatter_dimension=0, tiled=True)
        hidden_part = lax.psum_scatter(hidden_part, "narrow", scatter_dimension=0, tiled=True)
        hidden_square = jnp.sum(jnp.square(hidden_part.astype(full)))
    else:
        owned = lax.psum_scatter(
            joined, "wide", scatter_dimension=0, tiled=True, axis_index_groups=sides(wide)
        )
        owned, table_square, small_come = together((owned, table_square, small_come))
        hidden_square = jnp.sum(jnp.square(owned.astype(full)))
        half = owned.shape[0] // 2
        stays = jnp.where(side == 0, owned[:half], owned[half:])
        leaves = jnp.where(side == 0, owned[half:], owned[:half])
        comes = lax.ppermute(leaves, "wide", chip_mates(wide))
        hidden_part = jnp.concatenate(
            [jnp.where(side == 0, stays, comes), jnp.where(side == 0, comes, stays)], axis=1
        )
    small_part = jnp.sum(small_come.astype(full), axis=0)
    square = hidden_square + table_square[0, 0] + jnp.sum(small_part * small_part)
    square, hidden_part = together((square, hidden_part))
    if simple:
        hidden_all = lax.all_gather(hidden_part, "narrow", axis=0, tiled=True)
    else:
        hidden_all = jnp.concatenate(
            [hidden_part]
            + [
                lax.ppermute(hidden_part, "narrow", [(i, i ^ turn) for i in range(narrow)])
                for turn in range(1, narrow)
            ]
        )
    squares = broadcast_all(jnp.broadcast_to(square, (LANES,)))
    squares, hidden_all, table_part = together((squares, hidden_all, table_part))
    table_grad = lax.all_gather(table_part, "narrow", axis=0, tiled=True)
    clip_norm = jnp.sqrt(jnp.sum(squares[:, 0]))
    factor = jnp.minimum(1.0, clip_bound / clip_norm)

    start = wide_at * shard
    bounds = jnp.array(BOUNDS, jnp.int32)
    first_matrix = jnp.sum((start >= bounds[1:4]).astype(jnp.int32))
    second_matrix = jnp.sum((start + shard - 1 >= bounds[1:4]).astype(jnp.int32))
    split = jnp.minimum(bounds[first_matrix + 1] - start, shard)
    block = shard // 3
    piece = shard // 12
    at = jnp.arange(12, dtype=jnp.int32)
    if simple:
        source = at
    else:
        lead = split // piece
        each = lead // narrow
        rest = (12 - lead) // narrow
        in_first = at < lead
        inside = jnp.where(in_first, at, at - lead)
        width = jnp.maximum(jnp.where(in_first, each, rest), 1)
        origin = (inside // width) ^ narrow_at
        source = origin * (12 // narrow) + jnp.where(in_first, 0, each) + inside % width
    swap = (wide_at == 2).astype(jnp.int32) * (0 if simple else 1)
    info = jnp.concatenate([jnp.stack([split, swap]), source]).astype(jnp.int32)
    gains = jnp.array([0.2 * math.sqrt(hi - lo) for lo, hi in zip(BOUNDS, BOUNDS[1:])], full)
    moment, mine, other = moment_and_grams(
        info, factor[None], hidden_all, hidden_momentum, piece, block
    )
    step = step_count[0].astype(full)
    debias = jnp.stack([1.0 / (1.0 - beta_one**step), 1.0 / (1.0 - beta_two**step)])
    chain0, chain1, (table_new, table_first_new, table_second_new, table_copy), late_small = chains(
        mine,
        other,
        wide_at,
        first_matrix,
        second_matrix,
        factor[None],
        debias,
        (table_grad, table_master, table_first, table_second),
        small_part,
    )
    small_all = broadcast_all(late_small.astype(low)).reshape(-1, D)[:small_count].astype(full)
    late = (wide_at == 5).astype(jnp.int32) * (0 if simple else 1)
    apply_info = jnp.stack([split, swap, late]).astype(jnp.int32)
    slot_gains = jnp.stack([gains[first_matrix], gains[second_matrix]])
    hidden_new, hidden_copy = apply_chain(apply_info, slot_gains, chain0, chain1, moment, hidden_master, block)

    pos_new, pos_first_new, pos_second_new = adam(
        pos_types, factor * small_all[: SEQ + 2], pos_first, pos_second, step, 0.02
    )
    vectors_new, vec_first_new, vec_second_new = adam(
        vectors, factor * small_all[SEQ + 2 :], vec_first, vec_second, step, 0.2
    )
    return (
        loss,
        clip_norm,
        moment,
        hidden_new,
        hidden_copy,
        table_new,
        table_first_new,
        table_second_new,
        table_copy,
        pos_new,
        pos_first_new,
        pos_second_new,
        vectors_new,
        vec_first_new,
        vec_second_new,
    )


def solution(mesh):
    rows = P(None, BOTH, None)
    owned = P("wide", None)
    return jax.shard_map(
        shards,
        mesh=mesh,
        in_specs=(rows, rows, rows, rows, P(None, BOTH, None, None), P())
        + (owned,) * 5
        + (P(),) * 6,
        out_specs=(P(), P()) + (owned,) * 7 + (P(),) * 6,
        check_vma=False,
    )
```

```python
from functools import partial
import math

import jax
import jax.numpy as jnp
from jax import lax
from jax.experimental import pallas as pl
from jax.experimental.pallas import tpu as pltpu
from jax.sharding import PartitionSpec as P

D = 768
HEADS = 12
HEAD = 64
FF = 3072
SEQ = 512
SLOTS = 4
NEG = 4
NS_TURNS = 5
LANES = 128
GROUPS = 4
WIDTH = LANES // GROUPS
BLOCK = 256
TILES = [(i, j) for i in range(D // BLOCK) for j in range(i, D // BLOCK)]

BOTH = ("narrow", "wide")
highest = lax.Precision.HIGHEST
clip_bound = 0.002
norm_eps = 1e-06
muon_beta = 0.95
muon_rate = 0.1
muon_decay = 0.01
beta_one = 0.9
beta_two = 0.999
adam_eps = 1e-08
adam_decay = 0.01
BOUNDS = (0, 3 * D, 4 * D, 4 * D + FF, 4 * D + 2 * FF)

low = jnp.bfloat16
full = jnp.float32


def dims(left, right):
    return (((left,), (right,)), ((), ()))


def dot32(left, right, left_dim, right_dim):
    return lax.dot_general(left, right, dims(left_dim, right_dim), preferred_element_type=full)


def halves(x):
    high = x.astype(low)
    return high, (x - high.astype(full)).astype(low)


def dot_split(left, right, left_dim=1, right_dim=0):
    (lh, ll), (rh, rl) = left, right
    return dot32(lh, rh, left_dim, right_dim) + (
        dot32(lh, rl, left_dim, right_dim) + dot32(ll, rh, left_dim, right_dim)
    )


def params(mib):
    return pltpu.CompilerParams(vmem_limit_bytes=mib << 20)


def cost(micros):
    return pl.CostEstimate(flops=micros * 10**9, transcendentals=0, bytes_accessed=1 << 20)


def vmem():
    return pl.BlockSpec(memory_space=pltpu.VMEM)


def smem():
    return pl.BlockSpec(memory_space=pltpu.SMEM)


def attend_kernel(mixed_ref, seg_col_ref, seg_row_ref, context_ref, logsum_ref):
    same = seg_col_ref[0] == seg_row_ref[0]

    def pair(step, carry):
        at = pl.multiple_of(step * LANES, LANES)
        queries = mixed_ref[:, pl.ds(at, LANES)]
        keys = mixed_ref[:, pl.ds(D + at, LANES)]
        values = mixed_ref[:, pl.ds(2 * D + at, LANES)]
        outs = []
        for half in range(2):
            cut = slice(half * HEAD, (half + 1) * HEAD)
            raw = dot32(keys[:, cut], queries[:, cut], 1, 1)
            scores = jnp.where(same, raw * (1.0 / math.sqrt(HEAD)), -1e30)
            peak = jnp.max(scores, axis=0, keepdims=True)
            lifted = jnp.exp(scores - peak)
            total = jnp.sum(lifted, axis=0, keepdims=True)
            probs = (lifted * (1.0 / total)).astype(low)
            outs.append(dot32(values[:, cut], probs, 0, 0))
            logsum_ref[0, pl.ds(2 * step + half, 1), :] = peak + jnp.log(total)
        context_ref[:, pl.ds(at, LANES)] = jnp.concatenate(outs, axis=0).T.astype(low)
        return carry

    lax.fori_loop(0, HEADS // 2, pair, 0, unroll=3)


def attend(mixed, segment):
    rows = segment.shape[0]
    return pl.pallas_call(
        attend_kernel,
        grid=(rows,),
        in_specs=[
            pl.BlockSpec((SEQ, 3 * D), lambda b: (b, 0)),
            pl.BlockSpec((1, SEQ, 1), lambda b: (b, 0, 0)),
            pl.BlockSpec((1, 1, SEQ), lambda b: (b, 0, 0)),
        ],
        out_specs=[
            pl.BlockSpec((SEQ, D), lambda b: (b, 0)),
            pl.BlockSpec((1, 16, SEQ), lambda b: (b, 0, 0)),
        ],
        out_shape=[
            jax.ShapeDtypeStruct((rows * SEQ, D), low),
            jax.ShapeDtypeStruct((rows, 16, SEQ), full),
        ],
        compiler_params=params(48),
        cost_estimate=cost(19),
        name="attend",
    )(mixed, segment[:, :, None], segment[:, None, :])


def attend_back_kernel(mixed_ref, grad_ref, logsum_ref, seg_col_ref, seg_row_ref, out_ref):
    same = seg_col_ref[0] == seg_row_ref[0]
    scale = 1.0 / math.sqrt(HEAD)

    def pair(step, carry):
        at = pl.multiple_of(step * LANES, LANES)
        queries = mixed_ref[:, pl.ds(at, LANES)]
        keys = mixed_ref[:, pl.ds(D + at, LANES)]
        values = mixed_ref[:, pl.ds(2 * D + at, LANES)]
        upstream = grad_ref[:, pl.ds(at, LANES)]
        query_grads, key_grads, value_grads = [], [], []
        for half in range(2):
            cut = slice(half * HEAD, (half + 1) * HEAD)
            logsum = logsum_ref[0, pl.ds(2 * step + half, 1), :]
            raw = dot32(keys[:, cut], queries[:, cut], 1, 1)
            probs = jnp.exp(jnp.where(same, raw * scale, -1e30) - logsum)
            prob_grads = dot32(values[:, cut], upstream[:, cut], 1, 1)
            value_grads.append(dot32(probs.astype(low), upstream[:, cut], 1, 0))
            moved = jnp.sum(prob_grads * probs, axis=0, keepdims=True)
            back = (probs * (prob_grads - moved) * scale).astype(low)
            key_grads.append(dot32(back, queries[:, cut], 1, 0))
            query_grads.append(dot32(keys[:, cut], back, 0, 0))
        out_ref[:, pl.ds(at, LANES)] = jnp.concatenate(query_grads, axis=0).T.astype(low)
        out_ref[:, pl.ds(D + at, LANES)] = jnp.concatenate(key_grads, axis=1).astype(low)
        out_ref[:, pl.ds(2 * D + at, LANES)] = jnp.concatenate(value_grads, axis=1).astype(low)
        return carry

    lax.fori_loop(0, HEADS // 2, pair, 0, unroll=3)


def attend_back(mixed, context_grad, logsum, segment):
    rows = segment.shape[0]
    return pl.pallas_call(
        attend_back_kernel,
        grid=(rows,),
        in_specs=[
            pl.BlockSpec((SEQ, 3 * D), lambda b: (b, 0)),
            pl.BlockSpec((SEQ, D), lambda b: (b, 0)),
            pl.BlockSpec((1, 16, SEQ), lambda b: (b, 0, 0)),
            pl.BlockSpec((1, SEQ, 1), lambda b: (b, 0, 0)),
            pl.BlockSpec((1, 1, SEQ), lambda b: (b, 0, 0)),
        ],
        out_specs=pl.BlockSpec((SEQ, 3 * D), lambda b: (b, 0)),
        out_shape=jax.ShapeDtypeStruct((rows * SEQ, 3 * D), low),
        compiler_params=params(56),
        cost_estimate=cost(28),
        name="attend_back",
    )(mixed, context_grad, logsum, segment[:, :, None], segment[:, None, :])


def lookup_kernel(ids_ref, table_ref, out_ref, turned_ref, rows_ref):
    step = pl.program_id(0)
    features, width = table_ref.shape
    tokens, chunk = out_ref.shape[0], rows_ref.shape[0]
    block = table_ref[...].astype(low).astype(full)
    block = jnp.concatenate([block, jnp.zeros((LANES - features, width), full)], axis=0)
    turned_ref[pl.ds(pl.multiple_of(step * width, width), width), :] = block.T

    @pl.when(step == pl.num_programs(0) - 1)
    def _():
        def piece(c, carry):
            def body(i, inner):
                at = i * 32
                found = [turned_ref[pl.ds(ids_ref[c * chunk + at + k], 1), :] for k in range(32)]
                for k in range(32):
                    rows_ref[pl.ds(at + k, 1), :] = found[k]
                return inner

            lax.fori_loop(0, chunk // 32, body, 0)
            start = pl.multiple_of(c * chunk, chunk)
            out_ref[pl.ds(start, chunk), :] = rows_ref[:, :features].astype(low)
            return carry

        lax.fori_loop(0, tokens // chunk, piece, 0)


def lookup(ids, table):
    features, vocab = table.shape
    width = -(-vocab // (4 * LANES)) * LANES
    steps = -(-vocab // width)
    return pl.pallas_call(
        lookup_kernel,
        grid=(steps,),
        in_specs=[smem(), pl.BlockSpec((features, width), lambda s: (0, s))],
        out_specs=pl.BlockSpec((ids.shape[0], features), lambda s: (0, 0)),
        out_shape=jax.ShapeDtypeStruct((ids.shape[0], features), low),
        scratch_shapes=[pltpu.VMEM((steps * width, LANES), full), pltpu.VMEM((1024, LANES), full)],
        compiler_params=params(56),
        cost_estimate=cost(19),
        name="lookup",
    )(ids, table)


def collect_kernel(place_ref, ids_ref, grads_ref, out_ref, square_ref, *scratch,
                   span, tokens, features, vocab):
    sums, rows_ref = scratch[:-1], scratch[-1]
    step = pl.program_id(0)
    last = pl.num_programs(0) - 1
    streams = len(sums)
    batch = 4 * streams

    @pl.when(step == 0)
    def _():
        for total in sums:
            total[...] = jnp.zeros_like(total)

    group = ids_ref[0] // span
    grads = grads_ref[0].astype(full)
    pad = jnp.zeros((WIDTH - features, tokens), full)
    pieces = []
    for at in range(GROUPS):
        pieces += [jnp.where(group == at, grads, 0.0), pad]
    rows_ref[...] = jnp.concatenate(pieces, axis=0).T

    def body(i, carry):
        for base in range(0, batch, streams):
            at = i * batch + base
            places = [pl.ds(place_ref[0, 0, at + k], 1) for k in range(streams)]
            olds = [sums[k][places[k], :] for k in range(streams)]
            news = [rows_ref[pl.ds(at + k, 1), :] for k in range(streams)]
            for k in range(streams):
                sums[k][places[k], :] = olds[k] + news[k]
        return carry

    lax.fori_loop(0, tokens // batch, body, 0)

    @pl.when(step == last)
    def _():
        def flush(b, total):
            at = pl.multiple_of(b * LANES, LANES)
            block = sums[0][pl.ds(at, LANES), :]
            for k in range(1, streams):
                block += sums[k][pl.ds(at, LANES), :]
            turned = block.T
            for g in range(GROUPS):
                piece = turned[g * WIDTH:g * WIDTH + features]

                @pl.when(g * span + at < vocab)
                def _():
                    out_ref[:, pl.ds(pl.multiple_of(g * span + at, LANES), LANES)] = piece.astype(low)

            return total + block * block

        total = lax.fori_loop(0, span // LANES, flush, jnp.zeros((LANES, LANES), full))
        square_ref[...] = jnp.broadcast_to(jnp.sum(total, keepdims=True), square_ref.shape)


def collect(ids, grads, vocab, tokens):
    sources, features = grads.shape[:2]
    span = -(-vocab // (GROUPS * LANES)) * LANES
    return pl.pallas_call(
        partial(collect_kernel, span=span, tokens=tokens, features=features, vocab=vocab),
        grid=(sources,),
        in_specs=[
            pl.BlockSpec((1, 1, tokens), lambda s: (s, 0, 0), memory_space=pltpu.SMEM),
            pl.BlockSpec((1, 1, tokens), lambda s: (s, 0, 0)),
            pl.BlockSpec((1, features, tokens), lambda s: (s, 0, 0)),
        ],
        out_specs=[
            pl.BlockSpec((features, vocab), lambda s: (0, 0)),
            pl.BlockSpec((8, LANES), lambda s: (0, 0)),
        ],
        out_shape=[
            jax.ShapeDtypeStruct((features, vocab), low),
            jax.ShapeDtypeStruct((8, LANES), full),
        ],
        scratch_shapes=[pltpu.VMEM((span, LANES), full)] * 8 + [pltpu.VMEM((tokens, LANES), full)],
        compiler_params=params(56),
        cost_estimate=cost(150),
        name="collect",
    )((ids % span)[:, None, :], ids[:, None, :], grads)


def moment_kernel(info_ref, factor_ref, grad_ref, old_ref, moment_ref, mine_ref, other_ref,
                  *, piece, block):
    factor = factor_ref[0]
    for at in range(old_ref.shape[0] // piece):
        source = pl.multiple_of(info_ref[2 + at] * piece, piece)
        rows = slice(at * piece, (at + 1) * piece)
        moment_ref[rows] = muon_beta * old_ref[rows] + factor * grad_ref[pl.ds(source, piece)].astype(full)

    def grams(out_ref, start, stop):
        out_ref[...] = jnp.zeros_like(out_ref)

        def body(b, carry):
            high, small = halves(moment_ref[pl.ds(pl.multiple_of(b * block, block), block)])
            for at, (i, j) in enumerate(TILES):
                left, right = slice(i * BLOCK, (i + 1) * BLOCK), slice(j * BLOCK, (j + 1) * BLOCK)
                out_ref[at] += dot32(
                    jnp.concatenate([high[:, left], high[:, left], small[:, left]], axis=0),
                    jnp.concatenate([high[:, right], small[:, right], high[:, right]], axis=0),
                    0,
                    0,
                )
            return carry

        lax.fori_loop(start, stop, body, 0)

    lead, total = info_ref[0] // block, old_ref.shape[0] // block
    swap = info_ref[1] == 1
    grams(mine_ref, jnp.where(swap, lead, 0), jnp.where(swap, total, lead))
    grams(other_ref, jnp.where(swap, 0, lead), jnp.where(swap, lead, total))


def moment_and_grams(info, factor, grad, old, piece, block):
    tiles = jax.ShapeDtypeStruct((len(TILES), BLOCK, BLOCK), full)
    return pl.pallas_call(
        partial(moment_kernel, piece=piece, block=block),
        in_specs=[smem(), smem(), vmem(), vmem()],
        out_specs=[vmem()] * 3,
        out_shape=[jax.ShapeDtypeStruct(old.shape, full), tiles, tiles],
        compiler_params=params(48),
        cost_estimate=cost(10),
        name="moment",
    )(info, factor, grad, old)


def even_product(left, right, put):
    (lh, ll), (rh, rl) = left, right
    for i in range(D // BLOCK):
        rows = slice(i * BLOCK, (i + 1) * BLOCK)
        panel = jnp.concatenate([lh[rows], lh[rows], ll[rows]], axis=1)
        for j in range(i, D // BLOCK):
            cols = slice(j * BLOCK, (j + 1) * BLOCK)
            other = jnp.concatenate([rh[:, cols], rl[:, cols], rh[:, cols]], axis=0)
            put(rows, cols, dot32(panel, other, 1, 0))


def keep(pair):
    def put(rows, cols, value):
        pair[0][rows, cols], pair[1][rows, cols] = halves(value)
        if rows != cols:
            pair[0][cols, rows], pair[1][cols, rows] = halves(value.T)

    return put


def chain_kernel(kind_ref, factor_ref, debias_ref, chip_ref, other_ref, kept_ref, got_ref,
                 grad_ref, weight_ref, first_ref, second_ref,
                 out_ref, weight_new_ref, first_new_ref, second_new_ref, copy_ref,
                 a_ref, scale_ref, *parts, chunks):
    a, q, p, t = [parts[2 * i:2 * i + 2] for i in range(4)]
    step = pl.program_id(0)
    shape = (BLOCK, BLOCK)
    once = lax.broadcasted_iota(jnp.int32, shape, 0) == lax.broadcasted_iota(jnp.int32, shape, 1)

    def put_q(rows, cols, value):
        new = 2.0315 * value - 4.775 * a_ref[rows, cols]
        keep(q)(rows, cols, new + jnp.where(once, 3.4445, 0.0) if rows == cols else new)

    def put_a(rows, cols, value):
        a_ref[rows, cols] = value
        keep(a)(rows, cols, value)

    def put_out(rows, cols, value):
        value = value * (1.0 / scale_ref[0])
        out_ref[rows, cols] = value
        if rows != cols:
            out_ref[cols, rows] = value.T

    @pl.when(step == 0)
    def _():
        half = len(TILES) // 2
        lower = kind_ref[1] == 1
        trace = 0.0
        for at, (i, j) in enumerate(TILES):
            side = kept_ref[at % half], got_ref[at % half]
            near, far = side if at < half else side[::-1]
            tile = jnp.where(lower, near, far)
            tile = jnp.where(kind_ref[0] == 0, chip_ref[at], tile)
            tile = jnp.where(kind_ref[0] == 1, other_ref[at], tile)
            a_ref[i * BLOCK:(i + 1) * BLOCK, j * BLOCK:(j + 1) * BLOCK] = tile
            if i == j:
                trace = trace + jnp.sum(jnp.where(once, tile, 0.0))
        scale = jnp.sqrt(trace) + 1e-07
        scale_ref[0] = scale
        for i, j in TILES:
            rows, cols = slice(i * BLOCK, (i + 1) * BLOCK), slice(j * BLOCK, (j + 1) * BLOCK)
            put_a(rows, cols, a_ref[rows, cols] * (1.0 / (scale * scale)))

    turn = lax.rem(step + 1, 4)
    last = 4 * NS_TURNS - 4

    @pl.when((step == 0) | (turn == 0))
    def _():
        even_product(a, a, put_q)

    @pl.when(step == 0)
    def _():
        p[0][...], p[1][...] = q[0][...], q[1][...]

    @pl.when((turn == 1) & (step > 0) & (step < last))
    def _():
        even_product(p, q, keep(t))
        p[0][...], p[1][...] = t[0][...], t[1][...]

    @pl.when(step == last)
    def _():
        even_product(p, q, put_out)

    @pl.when(turn == 2)
    def _():
        even_product(a, q, keep(t))

    @pl.when(turn == 3)
    def _():
        even_product(t, q, put_a)

    @pl.when(step < chunks)
    def _():
        grad = factor_ref[0] * grad_ref[...].astype(full)
        weight = weight_ref[...]
        first = beta_one * first_ref[...] + (1.0 - beta_one) * grad
        second = beta_two * second_ref[...] + (1.0 - beta_two) * grad * grad
        spread = second * debias_ref[1]
        move = (first * debias_ref[0]) / (spread * lax.rsqrt(spread) + adam_eps)
        new = weight - 0.02 * (move + adam_decay * weight)
        weight_new_ref[...] = new
        first_new_ref[...] = first
        second_new_ref[...] = second
        copy_ref[...] = new.astype(low)


def chain(kind, factor, debias, grams, table):
    steps = 4 * NS_TURNS - 3
    features, vocab = table[1].shape
    width = -(-vocab // ((steps - 1) * LANES)) * LANES
    chunks = -(-vocab // width)
    part = pl.BlockSpec((features, width), lambda g: (0, jnp.minimum(g, chunks - 1)))
    whole = jax.ShapeDtypeStruct((features, vocab), full)
    return pl.pallas_call(
        partial(chain_kernel, chunks=chunks),
        grid=(steps,),
        in_specs=[smem(), smem(), smem()] + [vmem()] * 4 + [part] * 4,
        out_specs=[pl.BlockSpec((D, D), lambda g: (0, 0))] + [part] * 4,
        out_shape=[
            jax.ShapeDtypeStruct((D, D), full),
            whole,
            whole,
            whole,
            jax.ShapeDtypeStruct((features, vocab), low),
        ],
        scratch_shapes=[pltpu.VMEM((D, D), full), pltpu.SMEM((1,), full)]
        + [pltpu.VMEM((D, D), low)] * 8,
        compiler_params=params(56),
        cost_estimate=cost(48),
        name="chain",
    )(kind, factor, debias, *grams, *table)


def apply_kernel(info_ref, gain_ref, own_ref, come_ref, moment_ref, master_ref, new_ref, copy_ref,
                 *, block):
    lead, total = info_ref[0] // block, moment_ref.shape[0] // block
    late = info_ref[2]

    def over(p_ref, start, stop, slot):
        p = halves(p_ref[...])
        gain = gain_ref[slot] * muon_rate

        def body(b, carry):
            rows = pl.ds(pl.multiple_of(b * block, block), block)
            ortho = dot_split(halves(moment_ref[rows]), p)
            new = master_ref[rows] * (1.0 - muon_rate * muon_decay) - gain * ortho
            new_ref[rows] = new
            copy_ref[rows] = new.astype(low)
            return carry

        lax.fori_loop(start, stop, body, 0)

    over(own_ref, jnp.where(late == 1, lead, 0), jnp.where(late == 1, total, lead), late)

    @pl.when(lead < total)
    def _():
        over(come_ref, jnp.where(late == 1, 0, lead), jnp.where(late == 1, lead, total), 1 - late)


def apply_chain(info, gains, own, come, moment, master, block):
    return pl.pallas_call(
        partial(apply_kernel, block=block),
        in_specs=[smem(), smem(), vmem(), vmem(), vmem(), vmem()],
        out_specs=[vmem(), vmem()],
        out_shape=[
            jax.ShapeDtypeStruct(moment.shape, full),
            jax.ShapeDtypeStruct(moment.shape, low),
        ],
        compiler_params=params(48),
        cost_estimate=cost(10),
        name="apply",
    )(info, gains, own, come, moment, master)


def chains(mine, other, wide_at, first_matrix, second_matrix, factor, debias, table, rider):
    wide = lax.axis_size("wide")
    if wide != 8:
        which = jnp.arange(4)
        slots = (which == first_matrix).astype(full)[:, None, None, None] * mine
        slots = slots + (which == second_matrix).astype(full)[:, None, None, None] * other
        total = lax.psum(slots, "wide")
        kind = jnp.zeros((2,), jnp.int32)
        outs = []
        for matrix in (first_matrix, second_matrix):
            gram = lax.dynamic_index_in_dim(total, matrix, 0, keepdims=False)
            half = gram[: len(TILES) // 2]
            outs.append(chain(kind, factor, debias, (gram, gram, half, half), table))
        return outs[0][0], outs[1][0], outs[0][1:], rider
    half = len(TILES) // 2
    pairs = [(i, i ^ 1) for i in range(8)]
    lower = wide_at % 2 == 0
    moved = lax.ppermute(other[:half], "wide", [(5, 4)])
    chip = mine + lax.ppermute(mine, "wide", pairs)
    up_send = jnp.where(lower, chip[:half], chip[half:])
    down_send = jnp.where(wide_at == 4, moved, jnp.where(wide_at == 5, other[half:], up_send))
    up = up_send + lax.ppermute(up_send, "wide", [(2, 4), (4, 2), (3, 5), (5, 3)])
    down = down_send + lax.ppermute(down_send, "wide", [(4, 6), (6, 4), (5, 7), (7, 5)])
    send = jnp.where((wide_at == 4) | (wide_at >= 6), down, up)
    swap = lax.ppermute(send, "wide", [(2, 3), (4, 5), (6, 7), (7, 6)])
    back = lax.ppermute(up, "wide", [(5, 4)])
    kept = jnp.where(wide_at >= 5, down, up)
    got = jnp.where(wide_at == 4, back, swap)
    kind = jnp.where(wide_at < 2, 0, jnp.where(wide_at == 2, 1, 2))
    kind = jnp.stack([kind, lower.astype(jnp.int32)]).astype(jnp.int32)
    got, rider = lax.optimization_barrier((got, rider))
    own, *table_new = chain(kind, factor, debias, (chip, other, kept, got), table)
    come = lax.ppermute(own, "wide", [(3, 2), (4, 5)])
    return own, come, table_new, rider


def scale_rows(hidden):
    center = hidden - jnp.mean(hidden, axis=-1, keepdims=True)
    inverse = lax.rsqrt(jnp.mean(center * center, axis=-1, keepdims=True) + norm_eps)
    return center * inverse, inverse


def unscale_rows(upstream, scaled, inverse, gain):
    weighted = upstream * gain
    return inverse * (
        weighted
        - jnp.mean(weighted, axis=-1, keepdims=True)
        - scaled * jnp.mean(weighted * scaled, axis=-1, keepdims=True)
    )


def forward_kernel(context_ref, normed0_ref, share_ref, vectors_ref, bias_ref, out_w_ref, up_w_ref, down_w_ref,
                   scaled1_ref, inverse1_ref, input1_ref, active_ref, slope_ref,
                   scaled2_ref, inverse2_ref, pooled_ref, normed1_ref, sum_ref):
    step = pl.program_id(0)

    @pl.when(step == 0)
    def _():
        attended = dot32(context_ref[...], out_w_ref[...], 1, 1) + vectors_ref[8:9]
        scaled, inverse = scale_rows(normed0_ref[...] + attended)
        scaled1_ref[...], inverse1_ref[...] = scaled, inverse
        normed1_ref[...] = scaled * vectors_ref[2:3] + vectors_ref[3:4]
        input1_ref[...] = normed1_ref[...].astype(low)
        sum_ref[...] = normed1_ref[...] + vectors_ref[9:10]

    inner = dot32(input1_ref[...], up_w_ref[...], 1, 1) + bias_ref[...]
    cdf = 0.5 * (1.0 + lax.erf(inner * math.sqrt(0.5)))
    active = (inner * cdf).astype(low)
    active_ref[...] = active
    slope_ref[...] = cdf + inner * (jnp.exp(-0.5 * inner * inner) * (1.0 / math.sqrt(2.0 * math.pi)))
    sum_ref[...] += dot32(active, down_w_ref[...], 1, 0)

    @pl.when(step == pl.num_programs(0) - 1)
    def _():
        scaled, inverse = scale_rows(sum_ref[...])
        scaled2_ref[...], inverse2_ref[...] = scaled, inverse
        normed2 = scaled * vectors_ref[4:5] + vectors_ref[5:6]
        pooled_ref[...] = jnp.dot(share_ref[...], normed2, precision=highest)


CHUNK = 512


def same(shape):
    return pl.BlockSpec(shape, lambda c: (0,) * len(shape))


def forward_rest(context, normed0, share, vectors, out_w, up_w, down_w):
    tokens = context.shape[0]
    pairs = share.shape[0]
    wide_rows = jax.ShapeDtypeStruct((tokens, D), full)
    column = jax.ShapeDtypeStruct((tokens, 1), full)
    return pl.pallas_call(
        forward_kernel,
        grid=(FF // CHUNK,),
        in_specs=[
            same((tokens, D)),
            same((tokens, D)),
            same((pairs, tokens)),
            same(vectors.shape),
            pl.BlockSpec((1, CHUNK), lambda c: (0, c)),
            same((D, D)),
            pl.BlockSpec((CHUNK, D), lambda c: (c, 0)),
            pl.BlockSpec((CHUNK, D), lambda c: (c, 0)),
        ],
        out_specs=[
            same((tokens, D)),
            same((tokens, 1)),
            same((tokens, D)),
            pl.BlockSpec((tokens, CHUNK), lambda c: (0, c)),
            pl.BlockSpec((tokens, CHUNK), lambda c: (0, c)),
            same((tokens, D)),
            same((tokens, 1)),
            same((pairs, D)),
        ],
        out_shape=[
            wide_rows,
            column,
            jax.ShapeDtypeStruct((tokens, D), low),
            jax.ShapeDtypeStruct((tokens, FF), low),
            jax.ShapeDtypeStruct((tokens, FF), full),
            wide_rows,
            column,
            jax.ShapeDtypeStruct((pairs, D), full),
        ],
        scratch_shapes=[pltpu.VMEM((tokens, D), full)] * 2,
        compiler_params=params(58),
        cost_estimate=cost(25),
        name="forward_rest",
    )(context, normed0, share, vectors, vectors[14:].reshape(1, -1), out_w, up_w, down_w)


def backward_kernel(side_ref, pooled_ref, share_ref, vectors_ref, scaled2_ref, inverse2_ref, active_ref, slope_ref,
                    input1_ref, scaled1_ref, inverse1_ref, context_ref, out_w_ref, up_w_ref, down_w_ref,
                    down_stays_ref, down_leaves_ref, up_stays_ref, up_leaves_ref, out_grad_ref, sum1_ref, context_grad_ref, sums_ref, up_sums_ref,
                    branch_ref, total_ref):
    step = pl.program_id(0)

    def over_tokens(x):
        return jnp.sum(x, axis=0, keepdims=True)

    @pl.when(step == 0)
    def _():
        spread = lax.dot_general(
            share_ref[...], pooled_ref[...], dims(0, 0), precision=highest, preferred_element_type=full
        )
        scaled = scaled2_ref[...]
        back = unscale_rows(spread, scaled, inverse2_ref[...], vectors_ref[4:5])
        total_ref[...] = back
        branch = back.astype(low)
        branch_ref[...] = branch
        sums_ref[2:3] = over_tokens(spread * scaled)
        sums_ref[3:4] = over_tokens(spread)
        sums_ref[5:6] = over_tokens(branch.astype(full))

    branch = branch_ref[...]
    inner_grad = (dot32(branch, down_w_ref[...], 1, 1) * slope_ref[...]).astype(low)

    def halve(grad, stays_ref, leaves_ref):
        left, right = grad[:, : D // 2], grad[:, D // 2 :]
        stays_ref[...] = jnp.where(side_ref[0] == 0, left, right).astype(low)
        leaves_ref[...] = jnp.where(side_ref[0] == 0, right, left).astype(low)

    halve(dot32(active_ref[...], branch, 0, 0), down_stays_ref, down_leaves_ref)
    halve(dot32(inner_grad, input1_ref[...], 0, 0), up_stays_ref, up_leaves_ref)
    up_sums_ref[...] = over_tokens(inner_grad.astype(full))
    total_ref[...] += dot32(inner_grad, up_w_ref[...], 1, 0)

    @pl.when(step == pl.num_programs(0) - 1)
    def _():
        upstream = total_ref[...]
        scaled = scaled1_ref[...]
        back = unscale_rows(upstream, scaled, inverse1_ref[...], vectors_ref[2:3])
        sum1_ref[...] = back
        attended = back.astype(low)
        sums_ref[0:1] = over_tokens(upstream * scaled)
        sums_ref[1:2] = over_tokens(upstream)
        sums_ref[4:5] = over_tokens(attended.astype(full))
        out_grad_ref[...] = dot32(attended, context_ref[...], 0, 0).astype(low)
        context_grad_ref[...] = dot32(attended, out_w_ref[...], 1, 0).astype(low)


def backward_rest(side, pooled_grads, share, vectors, kept, context, out_w, up_w, down_w):
    scaled1, inverse1, input1, active, slope, scaled2, inverse2 = kept
    tokens = context.shape[0]
    pairs = share.shape[0]
    rows = pl.BlockSpec((CHUNK, D), lambda c: (c, 0))
    cols = pl.BlockSpec((tokens, CHUNK), lambda c: (0, c))
    return pl.pallas_call(
        backward_kernel,
        grid=(FF // CHUNK,),
        in_specs=[
            smem(),
            same((pairs, D)),
            same((pairs, tokens)),
            same(vectors.shape),
            same((tokens, D)),
            same((tokens, 1)),
            cols,
            cols,
            same((tokens, D)),
            same((tokens, D)),
            same((tokens, 1)),
            same((tokens, D)),
            same((D, D)),
            rows,
            rows,
        ],
        out_specs=[pl.BlockSpec((CHUNK, D // 2), lambda c: (c, 0))] * 4
        + [
            same((D, D)),
            same((tokens, D)),
            same((tokens, D)),
            same((8, D)),
            pl.BlockSpec((1, CHUNK), lambda c: (0, c)),
        ],
        out_shape=[jax.ShapeDtypeStruct((FF, D // 2), low)] * 4
        + [
            jax.ShapeDtypeStruct((D, D), low),
            jax.ShapeDtypeStruct((tokens, D), full),
            jax.ShapeDtypeStruct((tokens, D), low),
            jax.ShapeDtypeStruct((8, D), full),
            jax.ShapeDtypeStruct((1, FF), full),
        ],
        scratch_shapes=[pltpu.VMEM((tokens, D), low), pltpu.VMEM((tokens, D), full)],
        compiler_params=params(58),
        cost_estimate=cost(35),
        name="backward_rest",
    )(side, pooled_grads, share, vectors, scaled2, inverse2, active, slope, input1, scaled1, inverse1, context,
      out_w, up_w, down_w)


def front_kernel(side_ref, mixed_ref, input_ref, out_grad_ref, stays_ref, leaves_ref):
    def halve(grad):
        left, right = grad[:, : D // 2], grad[:, D // 2 :]
        stays_ref[...] = jnp.where(side_ref[0] == 0, left, right).astype(low)
        leaves_ref[...] = jnp.where(side_ref[0] == 0, right, left).astype(low)

    @pl.when(pl.program_id(0) < 3)
    def _():
        halve(dot32(mixed_ref[...], input_ref[...], 0, 0))

    @pl.when(pl.program_id(0) == 3)
    def _():
        halve(out_grad_ref[...].astype(full))


def front_grads(side, mixed_grad, input0, out_grad):
    tokens = mixed_grad.shape[0]
    return pl.pallas_call(
        front_kernel,
        grid=(4,),
        in_specs=[
            smem(),
            pl.BlockSpec((tokens, D), lambda c: (0, jnp.minimum(c, 2))),
            same((tokens, D)),
            same((D, D)),
        ],
        out_specs=[pl.BlockSpec((D, D // 2), lambda c: (c, 0))] * 2,
        out_shape=[jax.ShapeDtypeStruct((4 * D, D // 2), low)] * 2,
        compiler_params=params(40),
        cost_estimate=cost(7),
        name="front_grads",
    )(side, mixed_grad, input0, out_grad)


def embed_back_kernel(mixed_ref, sum1_ref, scaled_ref, inverse_ref, vectors_ref, weight_ref,
                      embed_ref, send_ref, sums_ref, mixed_sum_ref, *, narrow, wide):
    upstream = sum1_ref[...] + dot32(mixed_ref[...], weight_ref[...], 1, 0)
    scaled = scaled_ref[...]
    back = unscale_rows(upstream, scaled, inverse_ref[...], vectors_ref[0:1])
    embed_ref[...] = back
    turned = back.T.astype(low)
    features = send_ref.shape[1]
    for n in range(narrow):
        for w in range(wide):
            start = (w * narrow + n) * features
            send_ref[n * wide + w] = turned[start:start + features]

    @pl.when(pl.program_id(0) == 0)
    def _():
        sums_ref[...] = jnp.zeros_like(sums_ref)
        mixed_sum_ref[...] = jnp.zeros_like(mixed_sum_ref)

    sums_ref[0:1] += jnp.sum(upstream * scaled, axis=0, keepdims=True)
    sums_ref[1:2] += jnp.sum(upstream, axis=0, keepdims=True)
    mixed_sum_ref[...] += jnp.sum(mixed_ref[...].astype(full), axis=0, keepdims=True)


def embed_back(mixed_grad, sum1_grad, scaled0, inverse0, vectors, weight, narrow, wide):
    tokens = mixed_grad.shape[0]
    count = narrow * wide
    block = pl.BlockSpec((SEQ, D), lambda b: (b, 0))
    return pl.pallas_call(
        partial(embed_back_kernel, narrow=narrow, wide=wide),
        grid=(tokens // SEQ,),
        in_specs=[
            pl.BlockSpec((SEQ, 3 * D), lambda b: (b, 0)),
            block,
            block,
            pl.BlockSpec((SEQ, 1), lambda b: (b, 0)),
            same(vectors.shape),
            same((3 * D, D)),
        ],
        out_specs=[
            block,
            pl.BlockSpec((count, D // count, SEQ), lambda b: (0, 0, b)),
            same((8, D)),
            same((1, 3 * D)),
        ],
        out_shape=[
            jax.ShapeDtypeStruct((tokens, D), full),
            jax.ShapeDtypeStruct((count, D // count, tokens), low),
            jax.ShapeDtypeStruct((8, D), full),
            jax.ShapeDtypeStruct((1, 3 * D), full),
        ],
        compiler_params=params(48),
        cost_estimate=cost(10),
        name="embed_back",
    )(mixed_grad, sum1_grad, scaled0, inverse0, vectors, weight)


def layout(lengths):
    row_ends = jnp.cumsum(lengths)
    starts = row_ends - lengths
    places = jnp.arange(SEQ, dtype=jnp.int32)
    segment = jnp.sum((places[:, None] >= row_ends[None, :]).astype(jnp.int32), axis=1)
    chosen = segment[:, None] == jnp.arange(SLOTS, dtype=jnp.int32)[None, :]
    start_at = jnp.sum(jnp.where(chosen, starts[None, :], 0), axis=1)
    length_at = jnp.sum(jnp.where(chosen, lengths[None, :], 0), axis=1)
    position = places - start_at
    second = (2 * position >= length_at).astype(jnp.int32)
    return (chosen.astype(full), position, second, segment)


def norm_forward(hidden, gain, bias):
    center = hidden - jnp.mean(hidden, axis=-1, keepdims=True)
    inverse = lax.rsqrt(jnp.mean(center * center, axis=-1, keepdims=True) + norm_eps)
    scaled = center * inverse
    return (scaled * gain + bias, scaled, inverse)


def norm_backward(upstream, scaled, inverse, gain):
    weighted = upstream * gain
    back = inverse * (
        weighted
        - jnp.mean(weighted, axis=-1, keepdims=True)
        - scaled * jnp.mean(weighted * scaled, axis=-1, keepdims=True)
    )
    return (back, jnp.sum(upstream * scaled, axis=0), jnp.sum(upstream, axis=0))


def project(left, right):
    return jnp.dot(left, right, preferred_element_type=full)


def task_loss(logits, scores, tasks, labels, negatives, counts):
    logprob = jax.nn.log_softmax(logits, axis=-1)
    picked = jnp.sum(
        jnp.where(labels[:, :, None] == jnp.arange(3, dtype=jnp.int32), logprob, 0.0), axis=2
    )
    chosen = negatives[:, :, :, None] == jnp.arange(scores.shape[1], dtype=jnp.int32)
    rivals = jnp.sum(jnp.where(chosen, scores[:, None, None, :], 0.0), axis=3)
    together = jnp.concatenate([scores[:, :, None], rivals], axis=2)
    ranking = jax.nn.logsumexp(together, axis=2) - scores
    first_part = jnp.sum(jnp.where(tasks == 0, -picked, 0.0)) / counts[0]
    return first_part + jnp.sum(jnp.where(tasks == 1, ranking, 0.0)) / counts[1]


def adam(weight, grad, first, second, step, rate):
    first = beta_one * first + (1.0 - beta_one) * grad
    second = beta_two * second + (1.0 - beta_two) * grad * grad
    unbiased = first / (1.0 - beta_one**step)
    spread = second / (1.0 - beta_two**step)
    return (
        weight - rate * (unbiased / (jnp.sqrt(spread) + adam_eps) + adam_decay * weight),
        first,
        second,
    )


def broadcast_all(x):
    count = lax.axis_size("narrow") * lax.axis_size("wide")
    return lax.all_to_all(
        jnp.broadcast_to(x[None], (count,) + x.shape), BOTH, split_axis=0, concat_axis=0, tiled=True
    )


def sides(wide):
    return [list(range(0, wide, 2)), list(range(1, wide, 2))]


def chip_mates(wide):
    return [(i, i ^ 1) for i in range(wide)]


def gather_weights(master, narrow_at, wide_at, first):
    wide = lax.axis_size("wide")
    if wide != 8:
        whole = lax.all_gather(master.astype(low), "wide", axis=0, tiled=True)
        return first, list(whole.reshape(wide, -1, D))
    share = master.shape[0] // lax.axis_size("narrow")
    mine = lax.dynamic_slice_in_dim(master, narrow_at * share, share, 0).astype(low)
    near = lax.all_gather(mine, "wide", axis=0, tiled=False, axis_index_groups=sides(wide))
    near, first = lax.optimization_barrier((near, first))
    return first, [
        lax.all_gather(part, "narrow", axis=1, tiled=True)
        for part in (near[: wide // 4], near[wide // 4 :])
    ]


def both_cores(held, wide_at):
    other = lax.ppermute(held, "wide", chip_mates(lax.axis_size("wide")))
    side = wide_at % 2
    return [
        (side == core, held[at], other[at]) for at in range(held.shape[0]) for core in range(2)
    ]


def rows_of(owners, matrix):
    rows = (owners[0][1] if isinstance(owners[0], tuple) else owners[0]).shape[0]
    lo, hi = BOUNDS[matrix], BOUNDS[matrix + 1]
    pieces = []
    for at in range(lo // rows, -(-hi // rows)):
        part = slice(max(lo - at * rows, 0), min(hi - at * rows, rows))
        if isinstance(owners[at], tuple):
            mine, held, other = owners[at]
            pieces.append(jnp.where(mine, held[part], other[part]))
        else:
            pieces.append(owners[at][part])
    return jnp.concatenate(pieces) if len(pieces) > 1 else pieces[0]


def shards(
    token_ids,
    seq_lengths,
    task_ids,
    labels,
    negatives,
    step_count,
    hidden_master,
    hidden_momentum,
    table_master,
    table_first,
    table_second,
    pos_types,
    pos_first,
    pos_second,
    vectors,
    vec_first,
    vec_second,
):
    wide_at = lax.axis_index("wide")
    narrow_at = lax.axis_index("narrow")
    wide = lax.axis_size("wide")
    narrow = lax.axis_size("narrow")
    count = wide * narrow
    device_at = narrow_at * wide + wide_at
    micro_count, rows_each = token_ids.shape[:2]
    batch = micro_count * rows_each
    tokens = batch * SEQ
    shard = hidden_master.shape[0]
    vocab = table_master.shape[1]
    features = table_master.shape[0] // narrow
    pairs_each = rows_each * SLOTS

    parts = [token_ids, task_ids, labels, negatives]
    sizes = [part.size for part in parts]
    packed = jnp.concatenate([part.reshape(-1) for part in parts])
    packed = jnp.pad(packed, (0, -packed.size % LANES))
    gathered = broadcast_all(packed)
    ends = [sum(sizes[: i + 1]) for i in range(len(sizes))]
    ids_all = gathered[:, : ends[0]]

    def pairs_of(lo, hi, tail):
        block = gathered[:, lo:hi].reshape((count, micro_count, pairs_each) + tail)
        return jnp.moveaxis(block, 1, 0).reshape((micro_count, count * pairs_each) + tail)

    tasks_all = pairs_of(ends[0], ends[1], ())
    labels_all = pairs_of(ends[1], ends[2], ())
    negatives_all = pairs_of(ends[2], ends[3], (NEG,))
    counts = jnp.stack(
        [jnp.sum((tasks_all == 0).astype(full)), jnp.sum((tasks_all == 1).astype(full))]
    )


    group_ids = lax.dynamic_slice_in_dim(ids_all, narrow_at * wide, wide, 0).reshape(-1)
    pieces = lookup(group_ids, table_master)
    pieces, gathers = gather_weights(hidden_master, narrow_at, wide_at, pieces)
    simple = wide != 8
    arrived = lax.all_to_all(
        pieces.reshape(wide, tokens, -1), "wide", split_axis=0, concat_axis=0, tiled=True
    )
    token_rows = jnp.moveaxis(arrived, 0, 1).reshape(tokens, D)

    lengths = seq_lengths.reshape(batch, SLOTS)
    member, position, second, segment = jax.vmap(layout)(lengths)
    flat_position = position.reshape(-1)
    flat_second = second.reshape(-1)
    place_rows = pos_types[flat_position]
    place_rows = place_rows + jnp.where(flat_second[:, None] == 1, pos_types[SEQ + 1], pos_types[SEQ])
    if simple:
        owners = gathers
    else:
        place_rows, held = lax.optimization_barrier((place_rows, gathers[0]))
        owners = both_cores(held, wide_at)
    embed = token_rows.astype(full) + place_rows
    normed0, scaled0, inverse0 = norm_forward(embed, vectors[0], vectors[1])
    input0 = normed0.astype(low)
    qkv_bias = jnp.concatenate([vectors[6], jnp.zeros_like(vectors[6]), vectors[7]])
    weight_qkv, weight_out = rows_of(owners, 0), rows_of(owners, 1)
    mixed = (project(input0, weight_qkv.T) + qkv_bias).astype(low)
    context_low, logsum = attend(mixed, segment)
    if not simple:
        rest, context_low = lax.optimization_barrier((gathers[1], context_low))
        owners = owners + both_cores(rest, wide_at)
    weight_up, weight_down = rows_of(owners, 2), rows_of(owners, 3)
    pair_at = (jnp.arange(batch, dtype=jnp.int32)[:, None] * SLOTS + segment).reshape(1, -1)
    pairs = jnp.arange(batch * SLOTS, dtype=jnp.int32)[:, None]
    share = jnp.where(pair_at == pairs, 1.0 / lengths.astype(full).reshape(-1, 1), 0.0)
    scaled1, inverse1, input1, active, slope, scaled2, inverse2, flat_pooled = forward_rest(
        context_low, normed0, share, vectors, weight_out, weight_up, weight_down
    )
    heads = vectors[10:14]
    head_out = jnp.dot(flat_pooled, heads.T, precision=highest)

    sent = jnp.pad(head_out.reshape(-1), (0, -head_out.size % LANES))
    head_all = broadcast_all(sent)[:, : head_out.size]
    head_all = head_all.reshape(count, micro_count, pairs_each, 4)
    head_all = jnp.moveaxis(head_all, 1, 0).reshape(micro_count, count * pairs_each, 4)

    def objective(every):
        return task_loss(every[:, :, :3], every[:, :, 3], tasks_all, labels_all, negatives_all, counts)

    loss, pullback = jax.vjp(objective, head_all)
    head_grads = pullback(jnp.ones_like(loss))[0]
    output_grads = lax.dynamic_slice_in_dim(head_grads, device_at * pairs_each, pairs_each, 1)
    output_grads = output_grads.reshape(-1, 4)
    heads_grad = jnp.dot(output_grads.T, flat_pooled, precision=highest)
    pooled_grads = jnp.dot(output_grads, heads, precision=highest)

    spans_down = [(0, 768), (768, 1920), (1920, 3072)]
    spans_up = [(0, 384), (384, 1536), (1536, 2688), (2688, 3072)]
    spans_front = [(0, 1152), (1152, 2304), (2304, 3072)]

    side = wide_at % 2

    def between_cores(grad):
        stays, leaves = grad
        if simple:
            return stays, leaves
        return stays, lax.ppermute(leaves, "wide", chip_mates(wide))

    def slices(grad, spans):
        stays, comes = grad
        if simple:
            return [jnp.concatenate([stays, comes], axis=1)]
        chip = (stays.astype(full) + comes.astype(full)).astype(low)
        parts = []
        for turn in range(narrow):
            pieces = []
            for lo, hi in spans:
                share_rows = (hi - lo) // narrow
                start = lo + (narrow_at ^ turn) * share_rows
                pieces.append(lax.dynamic_slice_in_dim(chip, start, share_rows, 0))
            parts.append(jnp.concatenate(pieces))
        return parts

    def over_narrow(parts):
        return parts[:1] + [
            lax.ppermute(part, "narrow", [(i, i ^ (turn + 1)) for i in range(narrow)])
            for turn, part in enumerate(parts[1:])
        ]

    together = lax.optimization_barrier
    kept = (scaled1, inverse1, input1, active, slope, scaled2, inverse2)
    *sides_of, out_grad, sum1_grad, context_grad, sums, up_sums = backward_rest(
        side[None] if not simple else jnp.zeros((1,), jnp.int32),
        pooled_grads, share, vectors, kept, context_low, weight_out, weight_up, weight_down
    )
    down_pair = between_cores(sides_of[:2])
    up_pair = between_cores(sides_of[2:])
    down_cut, up_pair, context_grad = together((slices(down_pair, spans_down), up_pair, context_grad))
    down_part = over_narrow(down_cut)
    up_cut, context_grad = together((slices(up_pair, spans_up), context_grad))
    up_part = over_narrow(up_cut)
    mixed_grad = attend_back(mixed, context_grad, logsum, segment)
    mixed_grad, down_part = together((mixed_grad, down_part))
    if simple:
        normed0_grad = sum1_grad + project(mixed_grad, weight_qkv)
        embed_grad, gain0, bias0 = norm_backward(normed0_grad, scaled0, inverse0, vectors[0])
        table_send = embed_grad.astype(low).T.reshape(wide, narrow, features, tokens)
        table_send = jnp.moveaxis(table_send, 1, 0).reshape(count, features, tokens)
        mixed_sum = jnp.sum(mixed_grad.astype(full), axis=0)
    else:
        embed_grad, table_send, first_sums, mixed_sum = embed_back(
            mixed_grad, sum1_grad, scaled0, inverse0, vectors, weight_qkv, narrow, wide
        )
        gain0, bias0, mixed_sum = first_sums[0], first_sums[1], mixed_sum[0]
    table_send, mixed_grad = together((table_send, mixed_grad))
    come = lax.all_to_all(table_send, BOTH, split_axis=0, concat_axis=0, tiled=True)

    if simple:
        front_grad = jnp.concatenate([project(mixed_grad.T, input0).astype(low), out_grad])
        front_halves = (front_grad[:, : D // 2], front_grad[:, D // 2 :])
    else:
        front_halves = tuple(front_grads(side[None], mixed_grad, input0, out_grad))
    front_send, embed_grad, mixed_grad, up_part = together(
        (front_halves, embed_grad, mixed_grad, up_part)
    )
    front_part = over_narrow(slices(between_cores(front_send), spans_front))
    small_rows = jnp.concatenate(
        [
            jnp.stack([gain0, bias0]),
            sums[:4],
            jnp.stack([mixed_sum[:D], mixed_sum[2 * D :]]),
            sums[4:6],
        ]
    )
    up_rows = up_sums.reshape(-1, D)

    places = jnp.arange(SEQ, dtype=jnp.int32)[:, None]
    row_hot = jnp.concatenate(
        [
            flat_position[None] == places,
            jnp.stack([flat_second == 0, flat_second == 1]),
        ]
    ).astype(low)
    high_part, low_part = halves(embed_grad)
    pos_grad = project(jnp.concatenate([row_hot, row_hot], axis=1), jnp.concatenate([high_part, low_part]))
    small = jnp.concatenate([pos_grad, small_rows, heads_grad, up_rows])
    small_count = small.shape[0]
    small = jnp.pad(small, ((0, count * features - small_count), (0, 0)))

    def added(parts):
        return sum(part.astype(full) for part in parts).astype(low)

    joined = jnp.concatenate([added(front_part), added(up_part), added(down_part)])
    small_send = small.astype(low).reshape(count, features, D)
    come, small_send = together((come, small_send))
    small_come = lax.all_to_all(small_send, BOTH, split_axis=0, concat_axis=0, tiled=True)
    table_part, table_square = collect(ids_all, come, vocab, tokens)
    if simple:
        hidden_part = lax.psum_scatter(joined, "wide", scatter_dimension=0, tiled=True)
        hidden_part = lax.psum_scatter(hidden_part, "narrow", scatter_dimension=0, tiled=True)
        hidden_square = jnp.sum(jnp.square(hidden_part.astype(full)))
    else:
        owned = lax.psum_scatter(
            joined, "wide", scatter_dimension=0, tiled=True, axis_index_groups=sides(wide)
        )
        owned, table_square, small_come = together((owned, table_square, small_come))
        hidden_square = jnp.sum(jnp.square(owned.astype(full)))
        half = owned.shape[0] // 2
        stays = jnp.where(side == 0, owned[:half], owned[half:])
        leaves = jnp.where(side == 0, owned[half:], owned[:half])
        comes = lax.ppermute(leaves, "wide", chip_mates(wide))
        hidden_part = jnp.concatenate(
            [jnp.where(side == 0, stays, comes), jnp.where(side == 0, comes, stays)], axis=1
        )
    small_part = jnp.sum(small_come.astype(full), axis=0)
    square = hidden_square + table_square[0, 0] + jnp.sum(small_part * small_part)
    square, hidden_part = together((square, hidden_part))
    if simple:
        hidden_all = lax.all_gather(hidden_part, "narrow", axis=0, tiled=True)
    else:
        hidden_all = jnp.concatenate(
            [hidden_part]
            + [
                lax.ppermute(hidden_part, "narrow", [(i, i ^ turn) for i in range(narrow)])
                for turn in range(1, narrow)
            ]
        )
    squares = broadcast_all(jnp.broadcast_to(square, (LANES,)))
    squares, hidden_all, table_part = together((squares, hidden_all, table_part))
    table_grad = lax.all_gather(table_part, "narrow", axis=0, tiled=True)
    clip_norm = jnp.sqrt(jnp.sum(squares[:, 0]))
    factor = jnp.minimum(1.0, clip_bound / clip_norm)

    start = wide_at * shard
    bounds = jnp.array(BOUNDS, jnp.int32)
    first_matrix = jnp.sum((start >= bounds[1:4]).astype(jnp.int32))
    second_matrix = jnp.sum((start + shard - 1 >= bounds[1:4]).astype(jnp.int32))
    split = jnp.minimum(bounds[first_matrix + 1] - start, shard)
    block = shard // 3
    piece = shard // 12
    at = jnp.arange(12, dtype=jnp.int32)
    if simple:
        source = at
    else:
        lead = split // piece
        each = lead // narrow
        rest = (12 - lead) // narrow
        in_first = at < lead
        inside = jnp.where(in_first, at, at - lead)
        width = jnp.maximum(jnp.where(in_first, each, rest), 1)
        origin = (inside // width) ^ narrow_at
        source = origin * (12 // narrow) + jnp.where(in_first, 0, each) + inside % width
    swap = (wide_at == 2).astype(jnp.int32) * (0 if simple else 1)
    info = jnp.concatenate([jnp.stack([split, swap]), source]).astype(jnp.int32)
    gains = jnp.array([0.2 * math.sqrt(hi - lo) for lo, hi in zip(BOUNDS, BOUNDS[1:])], full)
    moment, mine, other = moment_and_grams(
        info, factor[None], hidden_all, hidden_momentum, piece, block
    )
    step = step_count[0].astype(full)
    debias = jnp.stack([1.0 / (1.0 - beta_one**step), 1.0 / (1.0 - beta_two**step)])
    chain0, chain1, (table_new, table_first_new, table_second_new, table_copy), late_small = chains(
        mine,
        other,
        wide_at,
        first_matrix,
        second_matrix,
        factor[None],
        debias,
        (table_grad, table_master, table_first, table_second),
        small_part,
    )
    small_all = broadcast_all(late_small.astype(low)).reshape(-1, D)[:small_count].astype(full)
    late = (wide_at == 5).astype(jnp.int32) * (0 if simple else 1)
    apply_info = jnp.stack([split, swap, late]).astype(jnp.int32)
    slot_gains = jnp.stack([gains[first_matrix], gains[second_matrix]])
    hidden_new, hidden_copy = apply_chain(apply_info, slot_gains, chain0, chain1, moment, hidden_master, block)

    pos_new, pos_first_new, pos_second_new = adam(
        pos_types, factor * small_all[: SEQ + 2], pos_first, pos_second, step, 0.02
    )
    vectors_new, vec_first_new, vec_second_new = adam(
        vectors, factor * small_all[SEQ + 2 :], vec_first, vec_second, step, 0.2
    )
    return (
        loss,
        clip_norm,
        moment,
        hidden_new,
        hidden_copy,
        table_new,
        table_first_new,
        table_second_new,
        table_copy,
        pos_new,
        pos_first_new,
        pos_second_new,
        vectors_new,
        vec_first_new,
        vec_second_new,
    )


def solution(mesh):
    rows = P(None, BOTH, None)
    owned = P("wide", None)
    return jax.shard_map(
        shards,
        mesh=mesh,
        in_specs=(rows, rows, rows, rows, P(None, BOTH, None, None), P())
        + (owned,) * 5
        + (P(),) * 6,
        out_specs=(P(), P()) + (owned,) * 7 + (P(),) * 6,
        check_vma=False,
    )
```

```python
from functools import partial
import math

import jax
import jax.numpy as jnp
from jax import lax
from jax.experimental import pallas as pl
from jax.experimental.pallas import tpu as pltpu
from jax.sharding import PartitionSpec as P

D = 768
HEADS = 12
HEAD = 64
FF = 3072
SEQ = 512
SLOTS = 4
NEG = 4
NS_TURNS = 5
LANES = 128
GROUPS = 4
WIDTH = LANES // GROUPS
BLOCK = 256
TILES = [(i, j) for i in range(D // BLOCK) for j in range(i, D // BLOCK)]

BOTH = ("narrow", "wide")
highest = lax.Precision.HIGHEST
clip_bound = 0.002
norm_eps = 1e-06
muon_beta = 0.95
muon_rate = 0.1
muon_decay = 0.01
beta_one = 0.9
beta_two = 0.999
adam_eps = 1e-08
adam_decay = 0.01
BOUNDS = (0, 3 * D, 4 * D, 4 * D + FF, 4 * D + 2 * FF)

low = jnp.bfloat16
full = jnp.float32


def dims(left, right):
    return (((left,), (right,)), ((), ()))


def dot32(left, right, left_dim, right_dim):
    return lax.dot_general(left, right, dims(left_dim, right_dim), preferred_element_type=full)


def halves(x):
    high = x.astype(low)
    return high, (x - high.astype(full)).astype(low)


def dot_split(left, right, left_dim=1, right_dim=0):
    (lh, ll), (rh, rl) = left, right
    return dot32(lh, rh, left_dim, right_dim) + (
        dot32(lh, rl, left_dim, right_dim) + dot32(ll, rh, left_dim, right_dim)
    )


def params(mib):
    return pltpu.CompilerParams(vmem_limit_bytes=mib << 20)


def cost(micros):
    return pl.CostEstimate(flops=micros * 10**9, transcendentals=0, bytes_accessed=1 << 20)


def vmem():
    return pl.BlockSpec(memory_space=pltpu.VMEM)


def smem():
    return pl.BlockSpec(memory_space=pltpu.SMEM)


def attend_kernel(mixed_ref, seg_col_ref, seg_row_ref, context_ref, logsum_ref):
    same = seg_col_ref[0] == seg_row_ref[0]

    def pair(step, carry):
        at = pl.multiple_of(step * LANES, LANES)
        queries = mixed_ref[:, pl.ds(at, LANES)]
        keys = mixed_ref[:, pl.ds(D + at, LANES)]
        values = mixed_ref[:, pl.ds(2 * D + at, LANES)]
        outs = []
        for half in range(2):
            cut = slice(half * HEAD, (half + 1) * HEAD)
            raw = dot32(keys[:, cut], queries[:, cut], 1, 1)
            scores = jnp.where(same, raw * (1.0 / math.sqrt(HEAD)), -1e30)
            peak = jnp.max(scores, axis=0, keepdims=True)
            lifted = jnp.exp(scores - peak)
            total = jnp.sum(lifted, axis=0, keepdims=True)
            probs = (lifted * (1.0 / total)).astype(low)
            outs.append(dot32(values[:, cut], probs, 0, 0))
            logsum_ref[0, pl.ds(2 * step + half, 1), :] = peak + jnp.log(total)
        context_ref[:, pl.ds(at, LANES)] = jnp.concatenate(outs, axis=0).T.astype(low)
        return carry

    lax.fori_loop(0, HEADS // 2, pair, 0, unroll=3)


def attend(mixed, segment):
    rows = segment.shape[0]
    return pl.pallas_call(
        attend_kernel,
        grid=(rows,),
        in_specs=[
            pl.BlockSpec((SEQ, 3 * D), lambda b: (b, 0)),
            pl.BlockSpec((1, SEQ, 1), lambda b: (b, 0, 0)),
            pl.BlockSpec((1, 1, SEQ), lambda b: (b, 0, 0)),
        ],
        out_specs=[
            pl.BlockSpec((SEQ, D), lambda b: (b, 0)),
            pl.BlockSpec((1, 16, SEQ), lambda b: (b, 0, 0)),
        ],
        out_shape=[
            jax.ShapeDtypeStruct((rows * SEQ, D), low),
            jax.ShapeDtypeStruct((rows, 16, SEQ), full),
        ],
        compiler_params=params(48),
        cost_estimate=cost(19),
        name="attend",
    )(mixed, segment[:, :, None], segment[:, None, :])


def attend_back_kernel(mixed_ref, grad_ref, logsum_ref, seg_col_ref, seg_row_ref, out_ref):
    same = seg_col_ref[0] == seg_row_ref[0]
    scale = 1.0 / math.sqrt(HEAD)

    def pair(step, carry):
        at = pl.multiple_of(step * LANES, LANES)
        queries = mixed_ref[:, pl.ds(at, LANES)]
        keys = mixed_ref[:, pl.ds(D + at, LANES)]
        values = mixed_ref[:, pl.ds(2 * D + at, LANES)]
        upstream = grad_ref[:, pl.ds(at, LANES)]
        query_grads, key_grads, value_grads = [], [], []
        for half in range(2):
            cut = slice(half * HEAD, (half + 1) * HEAD)
            logsum = logsum_ref[0, pl.ds(2 * step + half, 1), :]
            raw = dot32(keys[:, cut], queries[:, cut], 1, 1)
            probs = jnp.exp(jnp.where(same, raw * scale, -1e30) - logsum)
            prob_grads = dot32(values[:, cut], upstream[:, cut], 1, 1)
            value_grads.append(dot32(probs.astype(low), upstream[:, cut], 1, 0))
            moved = jnp.sum(prob_grads * probs, axis=0, keepdims=True)
            back = (probs * (prob_grads - moved) * scale).astype(low)
            key_grads.append(dot32(back, queries[:, cut], 1, 0))
            query_grads.append(dot32(keys[:, cut], back, 0, 0))
        out_ref[:, pl.ds(at, LANES)] = jnp.concatenate(query_grads, axis=0).T.astype(low)
        out_ref[:, pl.ds(D + at, LANES)] = jnp.concatenate(key_grads, axis=1).astype(low)
        out_ref[:, pl.ds(2 * D + at, LANES)] = jnp.concatenate(value_grads, axis=1).astype(low)
        return carry

    lax.fori_loop(0, HEADS // 2, pair, 0, unroll=3)


def attend_back(mixed, context_grad, logsum, segment):
    rows = segment.shape[0]
    return pl.pallas_call(
        attend_back_kernel,
        grid=(rows,),
        in_specs=[
            pl.BlockSpec((SEQ, 3 * D), lambda b: (b, 0)),
            pl.BlockSpec((SEQ, D), lambda b: (b, 0)),
            pl.BlockSpec((1, 16, SEQ), lambda b: (b, 0, 0)),
            pl.BlockSpec((1, SEQ, 1), lambda b: (b, 0, 0)),
            pl.BlockSpec((1, 1, SEQ), lambda b: (b, 0, 0)),
        ],
        out_specs=pl.BlockSpec((SEQ, 3 * D), lambda b: (b, 0)),
        out_shape=jax.ShapeDtypeStruct((rows * SEQ, 3 * D), low),
        compiler_params=params(56),
        cost_estimate=cost(28),
        name="attend_back",
    )(mixed, context_grad, logsum, segment[:, :, None], segment[:, None, :])


def lookup_kernel(ids_ref, table_ref, out_ref, turned_ref, rows_ref):
    step = pl.program_id(0)
    features, width = table_ref.shape
    tokens, chunk = out_ref.shape[0], rows_ref.shape[0]
    block = table_ref[...].astype(low).astype(full)
    block = jnp.concatenate([block, jnp.zeros((LANES - features, width), full)], axis=0)
    turned_ref[pl.ds(pl.multiple_of(step * width, width), width), :] = block.T

    @pl.when(step == pl.num_programs(0) - 1)
    def _():
        def piece(c, carry):
            def body(i, inner):
                at = i * 32
                found = [turned_ref[pl.ds(ids_ref[c * chunk + at + k], 1), :] for k in range(32)]
                for k in range(32):
                    rows_ref[pl.ds(at + k, 1), :] = found[k]
                return inner

            lax.fori_loop(0, chunk // 32, body, 0)
            start = pl.multiple_of(c * chunk, chunk)
            out_ref[pl.ds(start, chunk), :] = rows_ref[:, :features].astype(low)
            return carry

        lax.fori_loop(0, tokens // chunk, piece, 0)


def lookup(ids, table):
    features, vocab = table.shape
    width = -(-vocab // (4 * LANES)) * LANES
    steps = -(-vocab // width)
    return pl.pallas_call(
        lookup_kernel,
        grid=(steps,),
        in_specs=[smem(), pl.BlockSpec((features, width), lambda s: (0, s))],
        out_specs=pl.BlockSpec((ids.shape[0], features), lambda s: (0, 0)),
        out_shape=jax.ShapeDtypeStruct((ids.shape[0], features), low),
        scratch_shapes=[pltpu.VMEM((steps * width, LANES), full), pltpu.VMEM((1024, LANES), full)],
        compiler_params=params(56),
        cost_estimate=cost(19),
        name="lookup",
    )(ids, table)


def collect_kernel(place_ref, ids_ref, grads_ref, out_ref, square_ref, *scratch,
                   span, tokens, features, vocab):
    sums, rows_ref = scratch[:-1], scratch[-1]
    step = pl.program_id(0)
    last = pl.num_programs(0) - 1
    streams = len(sums)
    batch = 4 * streams

    @pl.when(step == 0)
    def _():
        for total in sums:
            total[...] = jnp.zeros_like(total)

    group = ids_ref[0] // span
    grads = grads_ref[0].astype(full)
    pad = jnp.zeros((WIDTH - features, tokens), full)
    pieces = []
    for at in range(GROUPS):
        pieces += [jnp.where(group == at, grads, 0.0), pad]
    rows_ref[...] = jnp.concatenate(pieces, axis=0).T

    def body(i, carry):
        for base in range(0, batch, streams):
            at = i * batch + base
            places = [pl.ds(place_ref[0, 0, at + k], 1) for k in range(streams)]
            olds = [sums[k][places[k], :] for k in range(streams)]
            news = [rows_ref[pl.ds(at + k, 1), :] for k in range(streams)]
            for k in range(streams):
                sums[k][places[k], :] = olds[k] + news[k]
        return carry

    lax.fori_loop(0, tokens // batch, body, 0)

    @pl.when(step == last)
    def _():
        def flush(b, total):
            at = pl.multiple_of(b * LANES, LANES)
            block = sums[0][pl.ds(at, LANES), :]
            for k in range(1, streams):
                block += sums[k][pl.ds(at, LANES), :]
            turned = block.T
            for g in range(GROUPS):
                piece = turned[g * WIDTH:g * WIDTH + features]

                @pl.when(g * span + at < vocab)
                def _():
                    out_ref[:, pl.ds(pl.multiple_of(g * span + at, LANES), LANES)] = piece.astype(low)

            return total + block * block

        total = lax.fori_loop(0, span // LANES, flush, jnp.zeros((LANES, LANES), full))
        square_ref[...] = jnp.broadcast_to(jnp.sum(total, keepdims=True), square_ref.shape)


def collect(ids, grads, vocab, tokens):
    sources, features = grads.shape[:2]
    span = -(-vocab // (GROUPS * LANES)) * LANES
    return pl.pallas_call(
        partial(collect_kernel, span=span, tokens=tokens, features=features, vocab=vocab),
        grid=(sources,),
        in_specs=[
            pl.BlockSpec((1, 1, tokens), lambda s: (s, 0, 0), memory_space=pltpu.SMEM),
            pl.BlockSpec((1, 1, tokens), lambda s: (s, 0, 0)),
            pl.BlockSpec((1, features, tokens), lambda s: (s, 0, 0)),
        ],
        out_specs=[
            pl.BlockSpec((features, vocab), lambda s: (0, 0)),
            pl.BlockSpec((8, LANES), lambda s: (0, 0)),
        ],
        out_shape=[
            jax.ShapeDtypeStruct((features, vocab), low),
            jax.ShapeDtypeStruct((8, LANES), full),
        ],
        scratch_shapes=[pltpu.VMEM((span, LANES), full)] * 8 + [pltpu.VMEM((tokens, LANES), full)],
        compiler_params=params(56),
        cost_estimate=cost(150),
        name="collect",
    )((ids % span)[:, None, :], ids[:, None, :], grads)


def moment_kernel(info_ref, factor_ref, grad_ref, old_ref, moment_ref, mine_ref, other_ref,
                  *, piece, block):
    factor = factor_ref[0]
    for at in range(old_ref.shape[0] // piece):
        source = pl.multiple_of(info_ref[2 + at] * piece, piece)
        rows = slice(at * piece, (at + 1) * piece)
        moment_ref[rows] = muon_beta * old_ref[rows] + factor * grad_ref[pl.ds(source, piece)].astype(full)

    def grams(out_ref, start, stop):
        out_ref[...] = jnp.zeros_like(out_ref)

        def body(b, carry):
            high, small = halves(moment_ref[pl.ds(pl.multiple_of(b * block, block), block)])
            for at, (i, j) in enumerate(TILES):
                left, right = slice(i * BLOCK, (i + 1) * BLOCK), slice(j * BLOCK, (j + 1) * BLOCK)
                out_ref[at] += dot32(
                    jnp.concatenate([high[:, left], high[:, left], small[:, left]], axis=0),
                    jnp.concatenate([high[:, right], small[:, right], high[:, right]], axis=0),
                    0,
                    0,
                )
            return carry

        lax.fori_loop(start, stop, body, 0)

    lead, total = info_ref[0] // block, old_ref.shape[0] // block
    swap = info_ref[1] == 1
    grams(mine_ref, jnp.where(swap, lead, 0), jnp.where(swap, total, lead))
    grams(other_ref, jnp.where(swap, 0, lead), jnp.where(swap, lead, total))


def moment_and_grams(info, factor, grad, old, piece, block):
    tiles = jax.ShapeDtypeStruct((len(TILES), BLOCK, BLOCK), full)
    return pl.pallas_call(
        partial(moment_kernel, piece=piece, block=block),
        in_specs=[smem(), smem(), vmem(), vmem()],
        out_specs=[vmem()] * 3,
        out_shape=[jax.ShapeDtypeStruct(old.shape, full), tiles, tiles],
        compiler_params=params(48),
        cost_estimate=cost(10),
        name="moment",
    )(info, factor, grad, old)


def even_product(left, right, put):
    (lh, ll), (rh, rl) = left, right
    for i in range(D // BLOCK):
        rows = slice(i * BLOCK, (i + 1) * BLOCK)
        panel = jnp.concatenate([lh[rows], lh[rows], ll[rows]], axis=1)
        for j in range(i, D // BLOCK):
            cols = slice(j * BLOCK, (j + 1) * BLOCK)
            other = jnp.concatenate([rh[:, cols], rl[:, cols], rh[:, cols]], axis=0)
            put(rows, cols, dot32(panel, other, 1, 0))


def keep(pair):
    def put(rows, cols, value):
        pair[0][rows, cols], pair[1][rows, cols] = halves(value)
        if rows != cols:
            pair[0][cols, rows], pair[1][cols, rows] = halves(value.T)

    return put


def chain_kernel(kind_ref, factor_ref, debias_ref, chip_ref, other_ref, kept_ref, got_ref,
                 grad_ref, weight_ref, first_ref, second_ref,
                 out_ref, weight_new_ref, first_new_ref, second_new_ref, copy_ref,
                 a_ref, scale_ref, *parts, chunks):
    a, q, p, t = [parts[2 * i:2 * i + 2] for i in range(4)]
    step = pl.program_id(0)
    shape = (BLOCK, BLOCK)
    once = lax.broadcasted_iota(jnp.int32, shape, 0) == lax.broadcasted_iota(jnp.int32, shape, 1)

    def put_q(rows, cols, value):
        new = 2.0315 * value - 4.775 * a_ref[rows, cols]
        keep(q)(rows, cols, new + jnp.where(once, 3.4445, 0.0) if rows == cols else new)

    def put_a(rows, cols, value):
        a_ref[rows, cols] = value
        keep(a)(rows, cols, value)

    def put_out(rows, cols, value):
        value = value * (1.0 / scale_ref[0])
        out_ref[rows, cols] = value
        if rows != cols:
            out_ref[cols, rows] = value.T

    @pl.when(step == 0)
    def _():
        half = len(TILES) // 2
        lower = kind_ref[1] == 1
        trace = 0.0
        for at, (i, j) in enumerate(TILES):
            side = kept_ref[at % half], got_ref[at % half]
            near, far = side if at < half else side[::-1]
            tile = jnp.where(lower, near, far)
            tile = jnp.where(kind_ref[0] == 0, chip_ref[at], tile)
            tile = jnp.where(kind_ref[0] == 1, other_ref[at], tile)
            a_ref[i * BLOCK:(i + 1) * BLOCK, j * BLOCK:(j + 1) * BLOCK] = tile
            if i == j:
                trace = trace + jnp.sum(jnp.where(once, tile, 0.0))
        scale = jnp.sqrt(trace) + 1e-07
        scale_ref[0] = scale
        for i, j in TILES:
            rows, cols = slice(i * BLOCK, (i + 1) * BLOCK), slice(j * BLOCK, (j + 1) * BLOCK)
            put_a(rows, cols, a_ref[rows, cols] * (1.0 / (scale * scale)))

    turn = lax.rem(step + 1, 4)
    last = 4 * NS_TURNS - 4

    @pl.when((step == 0) | (turn == 0))
    def _():
        even_product(a, a, put_q)

    @pl.when(step == 0)
    def _():
        p[0][...], p[1][...] = q[0][...], q[1][...]

    @pl.when((turn == 1) & (step > 0) & (step < last))
    def _():
        even_product(p, q, keep(t))
        p[0][...], p[1][...] = t[0][...], t[1][...]

    @pl.when(step == last)
    def _():
        even_product(p, q, put_out)

    @pl.when(turn == 2)
    def _():
        even_product(a, q, keep(t))

    @pl.when(turn == 3)
    def _():
        even_product(t, q, put_a)

    @pl.when(step < chunks)
    def _():
        grad = factor_ref[0] * grad_ref[...].astype(full)
        weight = weight_ref[...]
        first = beta_one * first_ref[...] + (1.0 - beta_one) * grad
        second = beta_two * second_ref[...] + (1.0 - beta_two) * grad * grad
        spread = second * debias_ref[1]
        move = (first * debias_ref[0]) / (spread * lax.rsqrt(spread) + adam_eps)
        new = weight - 0.02 * (move + adam_decay * weight)
        weight_new_ref[...] = new
        first_new_ref[...] = first
        second_new_ref[...] = second
        copy_ref[...] = new.astype(low)


def chain(kind, factor, debias, grams, table):
    steps = 4 * NS_TURNS - 3
    features, vocab = table[1].shape
    width = -(-vocab // ((steps - 1) * LANES)) * LANES
    chunks = -(-vocab // width)
    part = pl.BlockSpec((features, width), lambda g: (0, jnp.minimum(g, chunks - 1)))
    whole = jax.ShapeDtypeStruct((features, vocab), full)
    return pl.pallas_call(
        partial(chain_kernel, chunks=chunks),
        grid=(steps,),
        in_specs=[smem(), smem(), smem()] + [vmem()] * 4 + [part] * 4,
        out_specs=[pl.BlockSpec((D, D), lambda g: (0, 0))] + [part] * 4,
        out_shape=[
            jax.ShapeDtypeStruct((D, D), full),
            whole,
            whole,
            whole,
            jax.ShapeDtypeStruct((features, vocab), low),
        ],
        scratch_shapes=[pltpu.VMEM((D, D), full), pltpu.SMEM((1,), full)]
        + [pltpu.VMEM((D, D), low)] * 8,
        compiler_params=params(56),
        cost_estimate=cost(48),
        name="chain",
    )(kind, factor, debias, *grams, *table)


def apply_kernel(info_ref, gain_ref, own_ref, come_ref, moment_ref, master_ref, new_ref, copy_ref,
                 *, block):
    lead, total = info_ref[0] // block, moment_ref.shape[0] // block
    late = info_ref[2]

    def over(p_ref, start, stop, slot):
        p = halves(p_ref[...])
        gain = gain_ref[slot] * muon_rate

        def body(b, carry):
            rows = pl.ds(pl.multiple_of(b * block, block), block)
            ortho = dot_split(halves(moment_ref[rows]), p)
            new = master_ref[rows] * (1.0 - muon_rate * muon_decay) - gain * ortho
            new_ref[rows] = new
            copy_ref[rows] = new.astype(low)
            return carry

        lax.fori_loop(start, stop, body, 0)

    over(own_ref, jnp.where(late == 1, lead, 0), jnp.where(late == 1, total, lead), late)

    @pl.when(lead < total)
    def _():
        over(come_ref, jnp.where(late == 1, 0, lead), jnp.where(late == 1, lead, total), 1 - late)


def apply_chain(info, gains, own, come, moment, master, block):
    return pl.pallas_call(
        partial(apply_kernel, block=block),
        in_specs=[smem(), smem(), vmem(), vmem(), vmem(), vmem()],
        out_specs=[vmem(), vmem()],
        out_shape=[
            jax.ShapeDtypeStruct(moment.shape, full),
            jax.ShapeDtypeStruct(moment.shape, low),
        ],
        compiler_params=params(48),
        cost_estimate=cost(10),
        name="apply",
    )(info, gains, own, come, moment, master)


def chains(mine, other, wide_at, first_matrix, second_matrix, factor, debias, table, rider):
    wide = lax.axis_size("wide")
    if wide != 8:
        which = jnp.arange(4)
        slots = (which == first_matrix).astype(full)[:, None, None, None] * mine
        slots = slots + (which == second_matrix).astype(full)[:, None, None, None] * other
        total = lax.psum(slots, "wide")
        kind = jnp.zeros((2,), jnp.int32)
        outs = []
        for matrix in (first_matrix, second_matrix):
            gram = lax.dynamic_index_in_dim(total, matrix, 0, keepdims=False)
            half = gram[: len(TILES) // 2]
            outs.append(chain(kind, factor, debias, (gram, gram, half, half), table))
        return outs[0][0], outs[1][0], outs[0][1:], rider
    half = len(TILES) // 2
    pairs = [(i, i ^ 1) for i in range(8)]
    lower = wide_at % 2 == 0
    moved = lax.ppermute(other[:half], "wide", [(5, 4)])
    chip = mine + lax.ppermute(mine, "wide", pairs)
    up_send = jnp.where(lower, chip[:half], chip[half:])
    down_send = jnp.where(wide_at == 4, moved, jnp.where(wide_at == 5, other[half:], up_send))
    up = up_send + lax.ppermute(up_send, "wide", [(2, 4), (4, 2), (3, 5), (5, 3)])
    down = down_send + lax.ppermute(down_send, "wide", [(4, 6), (6, 4), (5, 7), (7, 5)])
    send = jnp.where((wide_at == 4) | (wide_at >= 6), down, up)
    swap = lax.ppermute(send, "wide", [(2, 3), (4, 5), (6, 7), (7, 6)])
    back = lax.ppermute(up, "wide", [(5, 4)])
    kept = jnp.where(wide_at >= 5, down, up)
    got = jnp.where(wide_at == 4, back, swap)
    kind = jnp.where(wide_at < 2, 0, jnp.where(wide_at == 2, 1, 2))
    kind = jnp.stack([kind, lower.astype(jnp.int32)]).astype(jnp.int32)
    got, rider = lax.optimization_barrier((got, rider))
    own, *table_new = chain(kind, factor, debias, (chip, other, kept, got), table)
    come = lax.ppermute(own, "wide", [(3, 2), (4, 5)])
    return own, come, table_new, rider


def scale_rows(hidden):
    center = hidden - jnp.mean(hidden, axis=-1, keepdims=True)
    inverse = lax.rsqrt(jnp.mean(center * center, axis=-1, keepdims=True) + norm_eps)
    return center * inverse, inverse


def unscale_rows(upstream, scaled, inverse, gain):
    weighted = upstream * gain
    return inverse * (
        weighted
        - jnp.mean(weighted, axis=-1, keepdims=True)
        - scaled * jnp.mean(weighted * scaled, axis=-1, keepdims=True)
    )


def forward_kernel(context_ref, normed0_ref, share_ref, vectors_ref, bias_ref, out_w_ref, up_w_ref, down_w_ref,
                   scaled1_ref, inverse1_ref, input1_ref, active_ref, slope_ref,
                   scaled2_ref, inverse2_ref, pooled_ref, normed1_ref, sum_ref):
    step = pl.program_id(0)

    @pl.when(step == 0)
    def _():
        attended = dot32(context_ref[...], out_w_ref[...], 1, 1) + vectors_ref[8:9]
        scaled, inverse = scale_rows(normed0_ref[...] + attended)
        scaled1_ref[...], inverse1_ref[...] = scaled, inverse
        normed1_ref[...] = scaled * vectors_ref[2:3] + vectors_ref[3:4]
        input1_ref[...] = normed1_ref[...].astype(low)
        sum_ref[...] = normed1_ref[...] + vectors_ref[9:10]

    inner = dot32(input1_ref[...], up_w_ref[...], 1, 1) + bias_ref[...]
    cdf = 0.5 * (1.0 + lax.erf(inner * math.sqrt(0.5)))
    active = (inner * cdf).astype(low)
    active_ref[...] = active
    slope = cdf + inner * (jnp.exp(-0.5 * inner * inner) * (1.0 / math.sqrt(2.0 * math.pi)))
    slope_ref[...] = slope.astype(low)
    sum_ref[...] += dot32(active, down_w_ref[...], 1, 0)

    @pl.when(step == pl.num_programs(0) - 1)
    def _():
        scaled, inverse = scale_rows(sum_ref[...])
        scaled2_ref[...], inverse2_ref[...] = scaled, inverse
        normed2 = scaled * vectors_ref[4:5] + vectors_ref[5:6]
        pooled_ref[...] = jnp.dot(share_ref[...], normed2, precision=highest)


CHUNK = 512


def same(shape):
    return pl.BlockSpec(shape, lambda c: (0,) * len(shape))


def forward_rest(context, normed0, share, vectors, out_w, up_w, down_w):
    tokens = context.shape[0]
    pairs = share.shape[0]
    wide_rows = jax.ShapeDtypeStruct((tokens, D), full)
    column = jax.ShapeDtypeStruct((tokens, 1), full)
    return pl.pallas_call(
        forward_kernel,
        grid=(FF // CHUNK,),
        in_specs=[
            same((tokens, D)),
            same((tokens, D)),
            same((pairs, tokens)),
            same(vectors.shape),
            pl.BlockSpec((1, CHUNK), lambda c: (0, c)),
            same((D, D)),
            pl.BlockSpec((CHUNK, D), lambda c: (c, 0)),
            pl.BlockSpec((CHUNK, D), lambda c: (c, 0)),
        ],
        out_specs=[
            same((tokens, D)),
            same((tokens, 1)),
            same((tokens, D)),
            pl.BlockSpec((tokens, CHUNK), lambda c: (0, c)),
            pl.BlockSpec((tokens, CHUNK), lambda c: (0, c)),
            same((tokens, D)),
            same((tokens, 1)),
            same((pairs, D)),
        ],
        out_shape=[
            wide_rows,
            column,
            jax.ShapeDtypeStruct((tokens, D), low),
            jax.ShapeDtypeStruct((tokens, FF), low),
            jax.ShapeDtypeStruct((tokens, FF), low),
            wide_rows,
            column,
            jax.ShapeDtypeStruct((pairs, D), full),
        ],
        scratch_shapes=[pltpu.VMEM((tokens, D), full)] * 2,
        compiler_params=params(58),
        cost_estimate=cost(25),
        name="forward_rest",
    )(context, normed0, share, vectors, vectors[14:].reshape(1, -1), out_w, up_w, down_w)


def backward_kernel(side_ref, pooled_ref, share_ref, vectors_ref, scaled2_ref, inverse2_ref, active_ref, slope_ref,
                    input1_ref, scaled1_ref, inverse1_ref, context_ref, out_w_ref, up_w_ref, down_w_ref,
                    down_stays_ref, down_leaves_ref, up_stays_ref, up_leaves_ref, out_grad_ref, sum1_ref, context_grad_ref, sums_ref, up_sums_ref,
                    branch_ref, total_ref):
    step = pl.program_id(0)

    def over_tokens(x):
        return jnp.sum(x, axis=0, keepdims=True)

    @pl.when(step == 0)
    def _():
        spread = lax.dot_general(
            share_ref[...], pooled_ref[...], dims(0, 0), precision=highest, preferred_element_type=full
        )
        scaled = scaled2_ref[...]
        back = unscale_rows(spread, scaled, inverse2_ref[...], vectors_ref[4:5])
        total_ref[...] = back
        branch = back.astype(low)
        branch_ref[...] = branch
        sums_ref[2:3] = over_tokens(spread * scaled)
        sums_ref[3:4] = over_tokens(spread)
        sums_ref[5:6] = over_tokens(branch.astype(full))

    branch = branch_ref[...]
    inner_grad = (dot32(branch, down_w_ref[...], 1, 1) * slope_ref[...].astype(full)).astype(low)

    def halve(grad, stays_ref, leaves_ref):
        left, right = grad[:, : D // 2], grad[:, D // 2 :]
        stays_ref[...] = jnp.where(side_ref[0] == 0, left, right).astype(low)
        leaves_ref[...] = jnp.where(side_ref[0] == 0, right, left).astype(low)

    halve(dot32(active_ref[...], branch, 0, 0), down_stays_ref, down_leaves_ref)
    halve(dot32(inner_grad, input1_ref[...], 0, 0), up_stays_ref, up_leaves_ref)
    up_sums_ref[...] = over_tokens(inner_grad.astype(full))
    total_ref[...] += dot32(inner_grad, up_w_ref[...], 1, 0)

    @pl.when(step == pl.num_programs(0) - 1)
    def _():
        upstream = total_ref[...]
        scaled = scaled1_ref[...]
        back = unscale_rows(upstream, scaled, inverse1_ref[...], vectors_ref[2:3])
        sum1_ref[...] = back
        attended = back.astype(low)
        sums_ref[0:1] = over_tokens(upstream * scaled)
        sums_ref[1:2] = over_tokens(upstream)
        sums_ref[4:5] = over_tokens(attended.astype(full))
        out_grad_ref[...] = dot32(attended, context_ref[...], 0, 0).astype(low)
        context_grad_ref[...] = dot32(attended, out_w_ref[...], 1, 0).astype(low)


def backward_rest(side, pooled_grads, share, vectors, kept, context, out_w, up_w, down_w):
    scaled1, inverse1, input1, active, slope, scaled2, inverse2 = kept
    tokens = context.shape[0]
    pairs = share.shape[0]
    rows = pl.BlockSpec((CHUNK, D), lambda c: (c, 0))
    cols = pl.BlockSpec((tokens, CHUNK), lambda c: (0, c))
    return pl.pallas_call(
        backward_kernel,
        grid=(FF // CHUNK,),
        in_specs=[
            smem(),
            same((pairs, D)),
            same((pairs, tokens)),
            same(vectors.shape),
            same((tokens, D)),
            same((tokens, 1)),
            cols,
            cols,
            same((tokens, D)),
            same((tokens, D)),
            same((tokens, 1)),
            same((tokens, D)),
            same((D, D)),
            rows,
            rows,
        ],
        out_specs=[pl.BlockSpec((CHUNK, D // 2), lambda c: (c, 0))] * 4
        + [
            same((D, D)),
            same((tokens, D)),
            same((tokens, D)),
            same((8, D)),
            pl.BlockSpec((1, CHUNK), lambda c: (0, c)),
        ],
        out_shape=[jax.ShapeDtypeStruct((FF, D // 2), low)] * 4
        + [
            jax.ShapeDtypeStruct((D, D), low),
            jax.ShapeDtypeStruct((tokens, D), full),
            jax.ShapeDtypeStruct((tokens, D), low),
            jax.ShapeDtypeStruct((8, D), full),
            jax.ShapeDtypeStruct((1, FF), full),
        ],
        scratch_shapes=[pltpu.VMEM((tokens, D), low), pltpu.VMEM((tokens, D), full)],
        compiler_params=params(58),
        cost_estimate=cost(35),
        name="backward_rest",
    )(side, pooled_grads, share, vectors, scaled2, inverse2, active, slope, input1, scaled1, inverse1, context,
      out_w, up_w, down_w)


def front_kernel(side_ref, mixed_ref, input_ref, out_grad_ref, stays_ref, leaves_ref):
    def halve(grad):
        left, right = grad[:, : D // 2], grad[:, D // 2 :]
        stays_ref[...] = jnp.where(side_ref[0] == 0, left, right).astype(low)
        leaves_ref[...] = jnp.where(side_ref[0] == 0, right, left).astype(low)

    @pl.when(pl.program_id(0) < 3)
    def _():
        halve(dot32(mixed_ref[...], input_ref[...], 0, 0))

    @pl.when(pl.program_id(0) == 3)
    def _():
        halve(out_grad_ref[...].astype(full))


def front_grads(side, mixed_grad, input0, out_grad):
    tokens = mixed_grad.shape[0]
    return pl.pallas_call(
        front_kernel,
        grid=(4,),
        in_specs=[
            smem(),
            pl.BlockSpec((tokens, D), lambda c: (0, jnp.minimum(c, 2))),
            same((tokens, D)),
            same((D, D)),
        ],
        out_specs=[pl.BlockSpec((D, D // 2), lambda c: (c, 0))] * 2,
        out_shape=[jax.ShapeDtypeStruct((4 * D, D // 2), low)] * 2,
        compiler_params=params(40),
        cost_estimate=cost(7),
        name="front_grads",
    )(side, mixed_grad, input0, out_grad)


def embed_back_kernel(mixed_ref, sum1_ref, scaled_ref, inverse_ref, vectors_ref, weight_ref,
                      embed_ref, send_ref, sums_ref, mixed_sum_ref, *, narrow, wide):
    upstream = sum1_ref[...] + dot32(mixed_ref[...], weight_ref[...], 1, 0)
    scaled = scaled_ref[...]
    back = unscale_rows(upstream, scaled, inverse_ref[...], vectors_ref[0:1])
    embed_ref[...] = back
    turned = back.T.astype(low)
    features = send_ref.shape[1]
    for n in range(narrow):
        for w in range(wide):
            start = (w * narrow + n) * features
            send_ref[n * wide + w] = turned[start:start + features]

    @pl.when(pl.program_id(0) == 0)
    def _():
        sums_ref[...] = jnp.zeros_like(sums_ref)
        mixed_sum_ref[...] = jnp.zeros_like(mixed_sum_ref)

    sums_ref[0:1] += jnp.sum(upstream * scaled, axis=0, keepdims=True)
    sums_ref[1:2] += jnp.sum(upstream, axis=0, keepdims=True)
    mixed_sum_ref[...] += jnp.sum(mixed_ref[...].astype(full), axis=0, keepdims=True)


def embed_back(mixed_grad, sum1_grad, scaled0, inverse0, vectors, weight, narrow, wide):
    tokens = mixed_grad.shape[0]
    count = narrow * wide
    block = pl.BlockSpec((SEQ, D), lambda b: (b, 0))
    return pl.pallas_call(
        partial(embed_back_kernel, narrow=narrow, wide=wide),
        grid=(tokens // SEQ,),
        in_specs=[
            pl.BlockSpec((SEQ, 3 * D), lambda b: (b, 0)),
            block,
            block,
            pl.BlockSpec((SEQ, 1), lambda b: (b, 0)),
            same(vectors.shape),
            same((3 * D, D)),
        ],
        out_specs=[
            block,
            pl.BlockSpec((count, D // count, SEQ), lambda b: (0, 0, b)),
            same((8, D)),
            same((1, 3 * D)),
        ],
        out_shape=[
            jax.ShapeDtypeStruct((tokens, D), full),
            jax.ShapeDtypeStruct((count, D // count, tokens), low),
            jax.ShapeDtypeStruct((8, D), full),
            jax.ShapeDtypeStruct((1, 3 * D), full),
        ],
        compiler_params=params(48),
        cost_estimate=cost(10),
        name="embed_back",
    )(mixed_grad, sum1_grad, scaled0, inverse0, vectors, weight)


def layout(lengths):
    row_ends = jnp.cumsum(lengths)
    starts = row_ends - lengths
    places = jnp.arange(SEQ, dtype=jnp.int32)
    segment = jnp.sum((places[:, None] >= row_ends[None, :]).astype(jnp.int32), axis=1)
    chosen = segment[:, None] == jnp.arange(SLOTS, dtype=jnp.int32)[None, :]
    start_at = jnp.sum(jnp.where(chosen, starts[None, :], 0), axis=1)
    length_at = jnp.sum(jnp.where(chosen, lengths[None, :], 0), axis=1)
    position = places - start_at
    second = (2 * position >= length_at).astype(jnp.int32)
    return (chosen.astype(full), position, second, segment)


def norm_forward(hidden, gain, bias):
    center = hidden - jnp.mean(hidden, axis=-1, keepdims=True)
    inverse = lax.rsqrt(jnp.mean(center * center, axis=-1, keepdims=True) + norm_eps)
    scaled = center * inverse
    return (scaled * gain + bias, scaled, inverse)


def norm_backward(upstream, scaled, inverse, gain):
    weighted = upstream * gain
    back = inverse * (
        weighted
        - jnp.mean(weighted, axis=-1, keepdims=True)
        - scaled * jnp.mean(weighted * scaled, axis=-1, keepdims=True)
    )
    return (back, jnp.sum(upstream * scaled, axis=0), jnp.sum(upstream, axis=0))


def project(left, right):
    return jnp.dot(left, right, preferred_element_type=full)


def task_loss(logits, scores, tasks, labels, negatives, counts):
    logprob = jax.nn.log_softmax(logits, axis=-1)
    picked = jnp.sum(
        jnp.where(labels[:, :, None] == jnp.arange(3, dtype=jnp.int32), logprob, 0.0), axis=2
    )
    chosen = negatives[:, :, :, None] == jnp.arange(scores.shape[1], dtype=jnp.int32)
    rivals = jnp.sum(jnp.where(chosen, scores[:, None, None, :], 0.0), axis=3)
    together = jnp.concatenate([scores[:, :, None], rivals], axis=2)
    ranking = jax.nn.logsumexp(together, axis=2) - scores
    first_part = jnp.sum(jnp.where(tasks == 0, -picked, 0.0)) / counts[0]
    return first_part + jnp.sum(jnp.where(tasks == 1, ranking, 0.0)) / counts[1]


def adam(weight, grad, first, second, step, rate):
    first = beta_one * first + (1.0 - beta_one) * grad
    second = beta_two * second + (1.0 - beta_two) * grad * grad
    unbiased = first / (1.0 - beta_one**step)
    spread = second / (1.0 - beta_two**step)
    return (
        weight - rate * (unbiased / (jnp.sqrt(spread) + adam_eps) + adam_decay * weight),
        first,
        second,
    )


def broadcast_all(x):
    count = lax.axis_size("narrow") * lax.axis_size("wide")
    return lax.all_to_all(
        jnp.broadcast_to(x[None], (count,) + x.shape), BOTH, split_axis=0, concat_axis=0, tiled=True
    )


def sides(wide):
    return [list(range(0, wide, 2)), list(range(1, wide, 2))]


def chip_mates(wide):
    return [(i, i ^ 1) for i in range(wide)]


def gather_weights(master, narrow_at, wide_at, first):
    wide = lax.axis_size("wide")
    if wide != 8:
        whole = lax.all_gather(master.astype(low), "wide", axis=0, tiled=True)
        return first, list(whole.reshape(wide, -1, D))
    share = master.shape[0] // lax.axis_size("narrow")
    mine = lax.dynamic_slice_in_dim(master, narrow_at * share, share, 0).astype(low)
    near = lax.all_gather(mine, "wide", axis=0, tiled=False, axis_index_groups=sides(wide))
    near, first = lax.optimization_barrier((near, first))
    return first, [
        lax.all_gather(part, "narrow", axis=1, tiled=True)
        for part in (near[: wide // 4], near[wide // 4 :])
    ]


def both_cores(held, wide_at):
    other = lax.ppermute(held, "wide", chip_mates(lax.axis_size("wide")))
    side = wide_at % 2
    return [
        (side == core, held[at], other[at]) for at in range(held.shape[0]) for core in range(2)
    ]


def rows_of(owners, matrix):
    rows = (owners[0][1] if isinstance(owners[0], tuple) else owners[0]).shape[0]
    lo, hi = BOUNDS[matrix], BOUNDS[matrix + 1]
    pieces = []
    for at in range(lo // rows, -(-hi // rows)):
        part = slice(max(lo - at * rows, 0), min(hi - at * rows, rows))
        if isinstance(owners[at], tuple):
            mine, held, other = owners[at]
            pieces.append(jnp.where(mine, held[part], other[part]))
        else:
            pieces.append(owners[at][part])
    return jnp.concatenate(pieces) if len(pieces) > 1 else pieces[0]


def shards(
    token_ids,
    seq_lengths,
    task_ids,
    labels,
    negatives,
    step_count,
    hidden_master,
    hidden_momentum,
    table_master,
    table_first,
    table_second,
    pos_types,
    pos_first,
    pos_second,
    vectors,
    vec_first,
    vec_second,
):
    wide_at = lax.axis_index("wide")
    narrow_at = lax.axis_index("narrow")
    wide = lax.axis_size("wide")
    narrow = lax.axis_size("narrow")
    count = wide * narrow
    device_at = narrow_at * wide + wide_at
    micro_count, rows_each = token_ids.shape[:2]
    batch = micro_count * rows_each
    tokens = batch * SEQ
    shard = hidden_master.shape[0]
    vocab = table_master.shape[1]
    features = table_master.shape[0] // narrow
    pairs_each = rows_each * SLOTS

    parts = [token_ids, task_ids, labels, negatives]
    sizes = [part.size for part in parts]
    packed = jnp.concatenate([part.reshape(-1) for part in parts])
    packed = jnp.pad(packed, (0, -packed.size % LANES))
    gathered = broadcast_all(packed)
    ends = [sum(sizes[: i + 1]) for i in range(len(sizes))]
    ids_all = gathered[:, : ends[0]]

    def pairs_of(lo, hi, tail):
        block = gathered[:, lo:hi].reshape((count, micro_count, pairs_each) + tail)
        return jnp.moveaxis(block, 1, 0).reshape((micro_count, count * pairs_each) + tail)

    tasks_all = pairs_of(ends[0], ends[1], ())
    labels_all = pairs_of(ends[1], ends[2], ())
    negatives_all = pairs_of(ends[2], ends[3], (NEG,))
    counts = jnp.stack(
        [jnp.sum((tasks_all == 0).astype(full)), jnp.sum((tasks_all == 1).astype(full))]
    )


    group_ids = lax.dynamic_slice_in_dim(ids_all, narrow_at * wide, wide, 0).reshape(-1)
    pieces = lookup(group_ids, table_master)
    pieces, gathers = gather_weights(hidden_master, narrow_at, wide_at, pieces)
    simple = wide != 8
    arrived = lax.all_to_all(
        pieces.reshape(wide, tokens, -1), "wide", split_axis=0, concat_axis=0, tiled=True
    )
    token_rows = jnp.moveaxis(arrived, 0, 1).reshape(tokens, D)

    lengths = seq_lengths.reshape(batch, SLOTS)
    member, position, second, segment = jax.vmap(layout)(lengths)
    flat_position = position.reshape(-1)
    flat_second = second.reshape(-1)
    place_rows = pos_types[flat_position]
    place_rows = place_rows + jnp.where(flat_second[:, None] == 1, pos_types[SEQ + 1], pos_types[SEQ])
    if simple:
        owners = gathers
    else:
        place_rows, held = lax.optimization_barrier((place_rows, gathers[0]))
        owners = both_cores(held, wide_at)
    embed = token_rows.astype(full) + place_rows
    normed0, scaled0, inverse0 = norm_forward(embed, vectors[0], vectors[1])
    input0 = normed0.astype(low)
    qkv_bias = jnp.concatenate([vectors[6], jnp.zeros_like(vectors[6]), vectors[7]])
    weight_qkv, weight_out = rows_of(owners, 0), rows_of(owners, 1)
    mixed = (project(input0, weight_qkv.T) + qkv_bias).astype(low)
    context_low, logsum = attend(mixed, segment)
    if not simple:
        rest, context_low = lax.optimization_barrier((gathers[1], context_low))
        owners = owners + both_cores(rest, wide_at)
    weight_up, weight_down = rows_of(owners, 2), rows_of(owners, 3)
    pair_at = (jnp.arange(batch, dtype=jnp.int32)[:, None] * SLOTS + segment).reshape(1, -1)
    pairs = jnp.arange(batch * SLOTS, dtype=jnp.int32)[:, None]
    share = jnp.where(pair_at == pairs, 1.0 / lengths.astype(full).reshape(-1, 1), 0.0)
    scaled1, inverse1, input1, active, slope, scaled2, inverse2, flat_pooled = forward_rest(
        context_low, normed0, share, vectors, weight_out, weight_up, weight_down
    )
    heads = vectors[10:14]
    head_out = jnp.dot(flat_pooled, heads.T, precision=highest)

    sent = jnp.pad(head_out.reshape(-1), (0, -head_out.size % LANES))
    head_all = broadcast_all(sent)[:, : head_out.size]
    head_all = head_all.reshape(count, micro_count, pairs_each, 4)
    head_all = jnp.moveaxis(head_all, 1, 0).reshape(micro_count, count * pairs_each, 4)

    def objective(every):
        return task_loss(every[:, :, :3], every[:, :, 3], tasks_all, labels_all, negatives_all, counts)

    loss, pullback = jax.vjp(objective, head_all)
    head_grads = pullback(jnp.ones_like(loss))[0]
    output_grads = lax.dynamic_slice_in_dim(head_grads, device_at * pairs_each, pairs_each, 1)
    output_grads = output_grads.reshape(-1, 4)
    heads_grad = jnp.dot(output_grads.T, flat_pooled, precision=highest)
    pooled_grads = jnp.dot(output_grads, heads, precision=highest)

    spans_down = [(0, 768), (768, 1920), (1920, 3072)]
    spans_up = [(0, 384), (384, 1536), (1536, 2688), (2688, 3072)]
    spans_front = [(0, 1152), (1152, 2304), (2304, 3072)]

    side = wide_at % 2

    def between_cores(grad):
        stays, leaves = grad
        if simple:
            return stays, leaves
        return stays, lax.ppermute(leaves, "wide", chip_mates(wide))

    def slices(grad, spans):
        stays, comes = grad
        if simple:
            return [jnp.concatenate([stays, comes], axis=1)]
        chip = (stays.astype(full) + comes.astype(full)).astype(low)
        parts = []
        for turn in range(narrow):
            pieces = []
            for lo, hi in spans:
                share_rows = (hi - lo) // narrow
                start = lo + (narrow_at ^ turn) * share_rows
                pieces.append(lax.dynamic_slice_in_dim(chip, start, share_rows, 0))
            parts.append(jnp.concatenate(pieces))
        return parts

    def over_narrow(parts):
        return parts[:1] + [
            lax.ppermute(part, "narrow", [(i, i ^ (turn + 1)) for i in range(narrow)])
            for turn, part in enumerate(parts[1:])
        ]

    together = lax.optimization_barrier
    kept = (scaled1, inverse1, input1, active, slope, scaled2, inverse2)
    *sides_of, out_grad, sum1_grad, context_grad, sums, up_sums = backward_rest(
        side[None] if not simple else jnp.zeros((1,), jnp.int32),
        pooled_grads, share, vectors, kept, context_low, weight_out, weight_up, weight_down
    )
    down_pair = between_cores(sides_of[:2])
    up_pair = between_cores(sides_of[2:])
    down_cut, up_pair, context_grad = together((slices(down_pair, spans_down), up_pair, context_grad))
    down_part = over_narrow(down_cut)
    up_cut, context_grad = together((slices(up_pair, spans_up), context_grad))
    up_part = over_narrow(up_cut)
    mixed_grad = attend_back(mixed, context_grad, logsum, segment)
    mixed_grad, down_part = together((mixed_grad, down_part))
    if simple:
        normed0_grad = sum1_grad + project(mixed_grad, weight_qkv)
        embed_grad, gain0, bias0 = norm_backward(normed0_grad, scaled0, inverse0, vectors[0])
        table_send = embed_grad.astype(low).T.reshape(wide, narrow, features, tokens)
        table_send = jnp.moveaxis(table_send, 1, 0).reshape(count, features, tokens)
        mixed_sum = jnp.sum(mixed_grad.astype(full), axis=0)
    else:
        embed_grad, table_send, first_sums, mixed_sum = embed_back(
            mixed_grad, sum1_grad, scaled0, inverse0, vectors, weight_qkv, narrow, wide
        )
        gain0, bias0, mixed_sum = first_sums[0], first_sums[1], mixed_sum[0]
    table_send, mixed_grad = together((table_send, mixed_grad))
    come = lax.all_to_all(table_send, BOTH, split_axis=0, concat_axis=0, tiled=True)

    if simple:
        front_grad = jnp.concatenate([project(mixed_grad.T, input0).astype(low), out_grad])
        front_halves = (front_grad[:, : D // 2], front_grad[:, D // 2 :])
    else:
        front_halves = tuple(front_grads(side[None], mixed_grad, input0, out_grad))
    front_send, embed_grad, mixed_grad, up_part = together(
        (front_halves, embed_grad, mixed_grad, up_part)
    )
    front_part = over_narrow(slices(between_cores(front_send), spans_front))
    small_rows = jnp.concatenate(
        [
            jnp.stack([gain0, bias0]),
            sums[:4],
            jnp.stack([mixed_sum[:D], mixed_sum[2 * D :]]),
            sums[4:6],
        ]
    )
    up_rows = up_sums.reshape(-1, D)

    places = jnp.arange(SEQ, dtype=jnp.int32)[:, None]
    row_hot = jnp.concatenate(
        [
            flat_position[None] == places,
            jnp.stack([flat_second == 0, flat_second == 1]),
        ]
    ).astype(low)
    high_part, low_part = halves(embed_grad)
    pos_grad = project(jnp.concatenate([row_hot, row_hot], axis=1), jnp.concatenate([high_part, low_part]))
    small = jnp.concatenate([pos_grad, small_rows, heads_grad, up_rows])
    small_count = small.shape[0]
    small = jnp.pad(small, ((0, count * features - small_count), (0, 0)))

    def added(parts):
        return sum(part.astype(full) for part in parts).astype(low)

    joined = jnp.concatenate([added(front_part), added(up_part), added(down_part)])
    small_send = small.astype(low).reshape(count, features, D)
    come, small_send = together((come, small_send))
    small_come = lax.all_to_all(small_send, BOTH, split_axis=0, concat_axis=0, tiled=True)
    table_part, table_square = collect(ids_all, come, vocab, tokens)
    if simple:
        hidden_part = lax.psum_scatter(joined, "wide", scatter_dimension=0, tiled=True)
        hidden_part = lax.psum_scatter(hidden_part, "narrow", scatter_dimension=0, tiled=True)
        hidden_square = jnp.sum(jnp.square(hidden_part.astype(full)))
    else:
        owned = lax.psum_scatter(
            joined, "wide", scatter_dimension=0, tiled=True, axis_index_groups=sides(wide)
        )
        owned, table_square, small_come = together((owned, table_square, small_come))
        hidden_square = jnp.sum(jnp.square(owned.astype(full)))
        half = owned.shape[0] // 2
        stays = jnp.where(side == 0, owned[:half], owned[half:])
        leaves = jnp.where(side == 0, owned[half:], owned[:half])
        comes = lax.ppermute(leaves, "wide", chip_mates(wide))
        hidden_part = jnp.concatenate(
            [jnp.where(side == 0, stays, comes), jnp.where(side == 0, comes, stays)], axis=1
        )
    small_part = jnp.sum(small_come.astype(full), axis=0)
    square = hidden_square + table_square[0, 0] + jnp.sum(small_part * small_part)
    square, hidden_part = together((square, hidden_part))
    if simple:
        hidden_all = lax.all_gather(hidden_part, "narrow", axis=0, tiled=True)
    else:
        hidden_all = jnp.concatenate(
            [hidden_part]
            + [
                lax.ppermute(hidden_part, "narrow", [(i, i ^ turn) for i in range(narrow)])
                for turn in range(1, narrow)
            ]
        )
    squares = broadcast_all(jnp.broadcast_to(square, (LANES,)))
    squares, hidden_all, table_part = together((squares, hidden_all, table_part))
    table_grad = lax.all_gather(table_part, "narrow", axis=0, tiled=True)
    clip_norm = jnp.sqrt(jnp.sum(squares[:, 0]))
    factor = jnp.minimum(1.0, clip_bound / clip_norm)

    start = wide_at * shard
    bounds = jnp.array(BOUNDS, jnp.int32)
    first_matrix = jnp.sum((start >= bounds[1:4]).astype(jnp.int32))
    second_matrix = jnp.sum((start + shard - 1 >= bounds[1:4]).astype(jnp.int32))
    split = jnp.minimum(bounds[first_matrix + 1] - start, shard)
    block = shard // 3
    piece = shard // 12
    at = jnp.arange(12, dtype=jnp.int32)
    if simple:
        source = at
    else:
        lead = split // piece
        each = lead // narrow
        rest = (12 - lead) // narrow
        in_first = at < lead
        inside = jnp.where(in_first, at, at - lead)
        width = jnp.maximum(jnp.where(in_first, each, rest), 1)
        origin = (inside // width) ^ narrow_at
        source = origin * (12 // narrow) + jnp.where(in_first, 0, each) + inside % width
    swap = (wide_at == 2).astype(jnp.int32) * (0 if simple else 1)
    info = jnp.concatenate([jnp.stack([split, swap]), source]).astype(jnp.int32)
    gains = jnp.array([0.2 * math.sqrt(hi - lo) for lo, hi in zip(BOUNDS, BOUNDS[1:])], full)
    moment, mine, other = moment_and_grams(
        info, factor[None], hidden_all, hidden_momentum, piece, block
    )
    step = step_count[0].astype(full)
    debias = jnp.stack([1.0 / (1.0 - beta_one**step), 1.0 / (1.0 - beta_two**step)])
    chain0, chain1, (table_new, table_first_new, table_second_new, table_copy), late_small = chains(
        mine,
        other,
        wide_at,
        first_matrix,
        second_matrix,
        factor[None],
        debias,
        (table_grad, table_master, table_first, table_second),
        small_part,
    )
    small_all = broadcast_all(late_small.astype(low)).reshape(-1, D)[:small_count].astype(full)
    late = (wide_at == 5).astype(jnp.int32) * (0 if simple else 1)
    apply_info = jnp.stack([split, swap, late]).astype(jnp.int32)
    slot_gains = jnp.stack([gains[first_matrix], gains[second_matrix]])
    hidden_new, hidden_copy = apply_chain(apply_info, slot_gains, chain0, chain1, moment, hidden_master, block)

    pos_new, pos_first_new, pos_second_new = adam(
        pos_types, factor * small_all[: SEQ + 2], pos_first, pos_second, step, 0.02
    )
    vectors_new, vec_first_new, vec_second_new = adam(
        vectors, factor * small_all[SEQ + 2 :], vec_first, vec_second, step, 0.2
    )
    return (
        loss,
        clip_norm,
        moment,
        hidden_new,
        hidden_copy,
        table_new,
        table_first_new,
        table_second_new,
        table_copy,
        pos_new,
        pos_first_new,
        pos_second_new,
        vectors_new,
        vec_first_new,
        vec_second_new,
    )


def solution(mesh):
    rows = P(None, BOTH, None)
    owned = P("wide", None)
    return jax.shard_map(
        shards,
        mesh=mesh,
        in_specs=(rows, rows, rows, rows, P(None, BOTH, None, None), P())
        + (owned,) * 5
        + (P(),) * 6,
        out_specs=(P(), P()) + (owned,) * 7 + (P(),) * 6,
        check_vma=False,
    )
```
